32 devices in a mesh: seq: 2 (over core), hid: 4 (over y, x), wid: 4 (over z).
Axes of the slice: x: 2, y: 2, z: 4, core: 2. Of those that a mesh axis runs over, the one named last changes fastest.
Arguments:
- inputs: bfloat16 [2048, 1536], P(('seq', 'hid'), 'wid'), may hold values from -6 to 6
- gain_attn: bfloat16 [1536], P('wid'), may hold values from 0.5 to 1.5
- gain_ffn: bfloat16 [1536], P('wid'), may hold values from 0.5 to 1.5
- w_query: bfloat16 [1536, 1536], P(None, 'wid'), may hold values from -0.15625 to 0.15625
- w_key: bfloat16 [1536, 1536], P(None, 'wid'), may hold values from -0.15625 to 0.15625
- w_value: bfloat16 [1536, 1536], P(None, 'wid'), may hold values from -0.15625 to 0.15625
- w_house: bfloat16 [1536, 1536], P(None, 'wid'), may hold values from -0.15625 to 0.15625
- w_beta: bfloat16 [1536, 12], P(None, 'wid'), may hold values from -0.15625 to 0.15625
- w_out: bfloat16 [1536, 1536], P('wid'), may hold values from -0.625 to 0.625
- w_gate: bfloat16 [1536, 4096], P(None, ('hid', 'wid')), may hold values from -0.15625 to 0.15625
- w_up: bfloat16 [1536, 4096], P(None, ('hid', 'wid')), may hold values from -0.15625 to 0.15625
- w_down: bfloat16 [4096, 1536], P(('hid', 'wid')), may hold values from -0.09375 to 0.09375
- lengths: int32 [3], replicated, may hold values from 1 to 1024, 2048 in all
- cotangent: bfloat16 [2048, 1536], P(('seq', 'hid'), 'wid'), may hold values from -6 to 6
Outputs:
- output: bfloat16 [2048, 1536], P(('seq', 'hid'), 'wid')
- d_inputs: float32 [2048, 1536], P(('seq', 'hid'), 'wid')
- d_gain_attn: float32 [1536], P(('seq', 'hid'))
- d_gain_ffn: float32 [1536], P(('seq', 'hid'))
- d_query: float32 [1536, 1536], P(('seq', 'hid'), 'wid')
- d_key: float32 [1536, 1536], P(('seq', 'hid'), 'wid')
- d_value: float32 [1536, 1536], P(('seq', 'hid'), 'wid')
- d_house: float32 [1536, 1536], P(('seq', 'hid'), 'wid')
- d_beta: float32 [1536, 12], P(('seq', 'hid'), 'wid')
- d_out: float32 [1536, 1536], P('wid', ('seq', 'hid'))
- d_gate: float32 [1536, 4096], P('seq', ('hid', 'wid'))
- d_up: float32 [1536, 4096], P('seq', ('hid', 'wid'))
- d_down: float32 [4096, 1536], P(('hid', 'wid'), 'seq')
The draws below stay inside these ranges and needn't reach their ends.
Inputs may be any that keep to these rules, and one draw needn't show every extreme that they name: `lengths`: the 3 documents are packed in order and fill all 2048 tokens; the longest has exactly 1024 tokens.
All inputs are finite; a program needn't handle non-finite values.
Results may differ from the reference program's by a relative error of at most 0.014.
Values may be sent and summed in bfloat16 or wider, within the bound.
A program may use at most 448 MiB of HBM per device.

```python
import math
from functools import partial
import jax
import jax.numpy as jnp
import numpy as np
from jax import lax

D = 1536
HEADS = 12
HDIM = 128
FF = 4096
TOK_DEV = 256
SEQS = 3
TOKENS = 2048
MOST = 1024
HOPS = 4


def steps_of(own_key, shape, shards, low, largest):
    def one(position, parts):
        steps = jax.random.uniform(jax.random.fold_in(jax.random.fold_in(own_key, 6), position), (parts,), jnp.float32, low / len(shards), largest / len(shards))
        return jnp.repeat(jnp.exp(steps), shape[position] // parts).reshape((-1,) + (1,) * (len(shape) - position - 1))

    level = one(*shards[0])
    for cut in shards[1:]:
        level = level * one(*cut)
    return level


def split_up(count, total, limit, lean):
    loads = [(1 << 20) // math.isqrt(grade ** lean) + 1 for grade in range(2, count + 1)]
    spare, counts = total - limit - (count - 1), [1] * (count - 1)
    while spare > 0:
        free = [i for i in range(count - 1) if counts[i] < limit]
        whole, left = sum([loads[i] for i in free]), spare
        for i in free:
            extra = min(limit - counts[i], max(1, left * loads[i] // whole), spare)
            counts[i] = counts[i] + extra
            spare = spare - extra
    return np.array([limit] + counts)


def uneven_parts(stream_key, number_of, total, limit, skew):
    if number_of == 2:
        one = jax.random.randint(stream_key, (), max(1, total - limit), min(limit, total - 1) + 1)
        return jnp.stack([one, total - one])
    sizes = jnp.asarray(split_up(number_of, total, limit, skew), jnp.int32)
    twos = (number_of - 1) // 2
    donor, receiver = sizes[1:1 + 2 * twos:2], sizes[2:2 + 2 * twos:2]
    room = jnp.minimum(donor - 1, limit - receiver)
    moved = jax.random.randint(jax.random.fold_in(stream_key, 1), (twos,), 0, 1 << 20) % (room + 1)
    sizes = sizes.at[1:1 + 2 * twos:2].set(donor - moved).at[2:2 + 2 * twos:2].set(receiver + moved)
    return sizes[jax.random.permutation(jax.random.fold_in(stream_key, 2), number_of)]


def gaussian(key, extent, scale, bound, pieces=(), held_as=jnp.bfloat16):
    values = scale * jax.random.normal(key, extent, jnp.float32)
    if pieces:
        values = values * steps_of(key, extent, pieces, -0.22, 0.18)
    return jnp.clip(values, -bound, bound).astype(held_as)


def setup_inputs(seed: int = 0) -> dict:
    streams_of = jax.random.split(jax.random.key(seed), 15)
    inputs = gaussian(streams_of[0], (TOKENS, D), 1.0, 6.0, ((0, 8), (1, 4)))
    gain_attn = jnp.clip(1.0 + 0.1 * jax.random.normal(streams_of[1], (D,), jnp.float32), 0.5, 1.5).astype(jnp.bfloat16)
    gain_ffn = jnp.clip(1.0 + 0.1 * jax.random.normal(streams_of[2], (D,), jnp.float32), 0.5, 1.5).astype(jnp.bfloat16)
    w_query = gaussian(streams_of[3], (D, D), D ** -0.5, 0.15625, ((1, 4),))
    w_key = gaussian(streams_of[4], (D, D), D ** -0.5, 0.15625, ((1, 4),))
    w_value = gaussian(streams_of[5], (D, D), D ** -0.5, 0.15625, ((1, 4),))
    w_house = gaussian(streams_of[6], (D, D), D ** -0.5, 0.15625, ((1, 4),))
    w_beta = gaussian(streams_of[7], (D, HEADS), D ** -0.5, 0.15625, ((1, 4),))
    w_out = gaussian(streams_of[8], (D, D), (D // 16) ** -0.5, 0.625, ((0, 4),))
    w_gate = gaussian(streams_of[9], (D, FF), D ** -0.5, 0.15625, ((1, 16),))
    w_up = gaussian(streams_of[10], (D, FF), D ** -0.5, 0.15625, ((1, 16),))
    w_down = gaussian(streams_of[11], (FF, D), FF ** -0.5, 0.09375, ((0, 16),))
    lengths = uneven_parts(streams_of[12], SEQS, TOKENS, MOST, 0).astype(jnp.int32)
    cotangent = gaussian(streams_of[13], (TOKENS, D), 1.0, 6.0, ((0, 8), (1, 4)))
    return dict(inputs=inputs, gain_attn=gain_attn, gain_ffn=gain_ffn, w_query=w_query, w_key=w_key, w_value=w_value, w_house=w_house, w_beta=w_beta, w_out=w_out, w_gate=w_gate, w_up=w_up, w_down=w_down, lengths=lengths, cotangent=cotangent)


eps_norm = 1e-06
neg_big = -1e+30
highest = lax.Precision.HIGHEST

@jax.custom_vjp
def low(v):
    return lax.optimization_barrier(v.astype(jnp.bfloat16)).astype(jnp.float32)

@jax.custom_vjp
def low_back(v):
    return v

def low_keep(v):
    return (low(v), None)

def low_pass(kept, grad):
    return (grad,)

def back_keep(v):
    return (v, None)

def back_low(kept, grad):
    return (low(grad),)
low.defvjp(low_keep, low_pass)
low_back.defvjp(back_keep, back_low)

def matmul(left_mat, right_mat):
    return jnp.dot(left_mat.astype(jnp.float32), right_mat.astype(jnp.float32), precision=highest, preferred_element_type=jnp.float32)

def rms_scale(hidden_f, gain_vec):
    return hidden_f * lax.rsqrt(lax.optimization_barrier(jnp.mean(hidden_f * hidden_f, -1, keepdims=True)) + eps_norm) * gain_vec

def lower_solve(matrix, rhs_mat):
    return jax.vmap(partial(jax.scipy.linalg.solve_triangular, lower=True))(matrix, rhs_mat)

def upper_solve(matrix, rhs_mat):
    return jax.vmap(partial(jax.scipy.linalg.solve_triangular, lower=False))(matrix, rhs_mat)

def doc_index(positions, lengths):
    ends_at = jnp.cumsum(lengths)
    return lax.optimization_barrier(jnp.sum((positions[:, None] >= ends_at[None, :]).astype(jnp.int32), 1))

def path_block(queries, key_rows, house_raw, beta_raw):
    length = queries.shape[1]
    head_dim = queries.shape[2]
    beta_vals = 2.0 * jax.nn.sigmoid(beta_raw)
    unit_dirs = house_raw * lax.rsqrt(lax.optimization_barrier(jnp.sum(house_raw * house_raw, -1, keepdims=True)) + eps_norm)
    gram_mat = jnp.einsum('htd,hsd->hts', unit_dirs, unit_dirs, precision=highest)
    identity = jnp.eye(length, dtype=jnp.float32)
    lower_sys = identity + jnp.tril(gram_mat, -1) * beta_vals[:, None, :]
    upper_sys = identity + jnp.triu(gram_mat, 1) * beta_vals[:, None, :]
    unit_keys = jnp.einsum('htd,hjd->htj', unit_dirs, key_rows, precision=highest)
    unit_query = jnp.einsum('htd,hid->hti', unit_dirs, queries, precision=highest)
    carried = lower_solve(lower_sys, jnp.tril(unit_keys, -1))
    forward_part = upper_solve(upper_sys, jnp.triu(unit_query))
    scaled = beta_vals[:, :, None] * unit_dirs
    keys_out = key_rows - jnp.einsum('htj,htd->hjd', carried, scaled, precision=highest)
    query_out = queries - jnp.einsum('hti,htd->hid', forward_part, scaled, precision=highest)
    direct = jnp.einsum('hid,hjd->hij', queries, key_rows, precision=highest)
    through = jnp.einsum('hti,htj->hij', jnp.triu(unit_query), beta_vals[:, :, None] * carried, precision=highest)
    near_raw = direct - through
    solved = lower_solve(lower_sys, unit_dirs)
    product = jnp.eye(head_dim, dtype=jnp.float32) - jnp.einsum('htd,hte->hde', scaled, solved, precision=highest)
    return (query_out, keys_out, near_raw, product)

def attention(queries, key_rows, value_rows, house_rows, beta_rows, lengths):
    blocks_n = TOKENS // TOK_DEV

    def per_block(matrix):
        return matrix.reshape(blocks_n, TOK_DEV, HEADS, HDIM).transpose(0, 2, 1, 3)
    query_b = per_block(queries)
    key_b = per_block(key_rows)
    value_b = per_block(value_rows)
    house_b = per_block(house_rows)
    beta_b = beta_rows.reshape(blocks_n, TOK_DEV, HEADS).transpose(0, 2, 1)
    doc_ids = doc_index(jnp.arange(TOKENS, dtype=jnp.int32), lengths).astype(jnp.int32)
    pad_docs = jnp.concatenate([jnp.full((HOPS * TOK_DEV,), -1, dtype=jnp.int32), doc_ids])
    pad_vals = jnp.concatenate([jnp.zeros((HOPS, HEADS, TOK_DEV, HDIM), jnp.float32), value_b], 0)
    score_scale = HDIM ** (-0.5)
    offsets = jnp.arange(TOK_DEV, dtype=jnp.int32)
    causal = offsets[:, None] >= offsets[None, :]

    def block_step(window, inputs_blk):
        block_idx, query_h, key_h, value_h, house_h, beta_h = inputs_blk
        query_out, keys_out, near_raw, product = path_block(query_h, key_h, house_h, beta_h)
        own_docs = lax.dynamic_slice_in_dim(doc_ids, block_idx.astype(jnp.int32) * TOK_DEV, TOK_DEV)
        far_docs = lax.dynamic_slice_in_dim(pad_docs, block_idx.astype(jnp.int32) * TOK_DEV, HOPS * TOK_DEV)
        near_mask = causal & (own_docs[:, None] == own_docs[None, :])
        far_mask = own_docs[:, None] == far_docs[None, :]
        far_vals = lax.dynamic_slice_in_dim(pad_vals, block_idx.astype(jnp.int32), HOPS, 0)
        far_keys = window.transpose(1, 0, 2, 3).reshape(HEADS, HOPS * TOK_DEV, HDIM)
        far_vals = far_vals.transpose(1, 0, 2, 3).reshape(HEADS, HOPS * TOK_DEV, HDIM)
        far_raw = low_back(jnp.einsum('hid,hjd->hij', low(query_out), far_keys, precision=highest))
        near_scores = jnp.where(near_mask[None], near_raw * score_scale, neg_big)
        far_scores = jnp.where(far_mask[None], far_raw * score_scale, neg_big)
        scores = jnp.concatenate([near_scores, far_scores], 2)
        top_val = lax.optimization_barrier(jnp.max(scores, 2, keepdims=True))
        log_total = top_val + jnp.log(lax.optimization_barrier(jnp.sum(jnp.exp(scores - top_val), 2, keepdims=True)))
        prob_vals = low(jnp.exp(scores - log_total))
        outputs = jnp.einsum('hij,hjd->hid', prob_vals[:, :, :TOK_DEV], value_h, precision=highest)
        outputs = outputs + jnp.einsum('hij,hjd->hid', prob_vals[:, :, TOK_DEV:], far_vals, precision=highest)
        moved = low(jnp.einsum('rhjd,hed->rhje', window[1:], product, precision=highest))
        window = jnp.concatenate([moved, low(keys_out)[None]], 0)
        return (window, outputs)
    init_window = jnp.zeros((HOPS, HEADS, TOK_DEV, HDIM), jnp.float32)
    block_ids = jnp.arange(blocks_n, dtype=jnp.int32)
    last_window, outs_blk = lax.scan(jax.checkpoint(block_step), init_window, (block_ids, query_b, key_b, value_b, house_b, beta_b))
    return outs_blk.transpose(0, 2, 1, 3).reshape(TOKENS, HEADS * HDIM)

def forward(inputs, gain_attn, gain_ffn, w_query, w_key, w_value, w_house, w_beta, w_out, w_gate, w_up, w_down, lengths):
    normed = low(rms_scale(inputs, gain_attn))
    queries = low_back(matmul(normed, w_query))
    key_rows = low_back(matmul(normed, w_key))
    value_rows = low(low_back(matmul(normed, w_value)))
    house_rows = low_back(matmul(normed, w_house))
    beta_rows = low_back(matmul(normed, w_beta))
    attended = low(low_back(attention(queries, key_rows, value_rows, house_rows, beta_rows, lengths)))
    mixed = inputs + low_back(matmul(attended, w_out))
    inner_low = low(rms_scale(mixed, gain_ffn))
    gate_val = low_back(matmul(inner_low, w_gate))
    up_val = low_back(matmul(inner_low, w_up))
    hidden = low(jax.nn.silu(gate_val) * up_val)
    return mixed + low_back(matmul(hidden, w_down))

def reference(inputs, gain_attn, gain_ffn, w_query, w_key, w_value, w_house, w_beta, w_out, w_gate, w_up, w_down, lengths, cotangent):
    floats = [array_in.astype(jnp.float32) for array_in in (inputs, gain_attn, gain_ffn, w_query, w_key, w_value, w_house, w_beta, w_out, w_gate, w_up, w_down)]

    def closed(*params):
        return forward(*params, lengths)
    result, pullback = jax.vjp(closed, *floats)
    gradients = pullback(cotangent.astype(jnp.float32))
    return (result.astype(jnp.bfloat16), gradients[0], gradients[1], gradients[2], gradients[3], gradients[4], gradients[5], gradients[6], gradients[7], gradients[8], gradients[9], gradients[10], gradients[11])
```

```python
import functools

import jax
import jax.numpy as jnp
from jax import lax
from jax.experimental import pallas as pl
from jax.experimental.pallas import tpu as pltpu
from jax.sharding import PartitionSpec as P

HDIM = 128
LEAST = 1024

eps_norm = 1e-06
neg_big = -1e30
BF = jnp.bfloat16
F32 = jnp.float32
VMEM_LIMIT = 60 * 1024 * 1024


def dot(a, b, ca, cb):
    return lax.dot_general(a, b, (((ca,), (cb,)), ((), ())), preferred_element_type=F32)


def split(a):
    hi = a.astype(BF)
    return hi, (a - hi.astype(F32)).astype(BF)


def dot3(a, b, ca, cb):
    return dot(a[0], b[0], ca, cb) + (dot(a[0], b[1], ca, cb) + dot(a[1], b[0], ca, cb))


def dot1(a, b, ca, cb):
    return dot(a.astype(BF), b.astype(BF), ca, cb)


def iotas(n):
    rows = lax.broadcasted_iota(jnp.int32, (n, n), 0)
    cols = lax.broadcasted_iota(jnp.int32, (n, n), 1)
    return rows, cols


def head_cols(h):
    return slice(h * HDIM, (h + 1) * HDIM)


def house_terms(raw, strength, heads, h):
    inv = lax.rsqrt(jnp.sum(raw * raw, -1, keepdims=True) + eps_norm)
    lane = lax.broadcasted_iota(jnp.int32, strength.shape, 1)
    c = jnp.sum(jnp.where(lane == h, strength, 0.0), 1, keepdims=True)
    root = jnp.sqrt(2.0 / (1.0 + jnp.exp(-c)))
    return inv, root


def path_fwd_kernel(heads, q_ref, k_ref, r_ref, c_ref, qt_ref, kt_ref, near_ref, p_ref,
                    u_ref, inv_ref, psi_ref, x_ref, y_ref):
    n = q_ref.shape[0]
    rows, cols = iotas(n)
    strength = c_ref[...]
    us, us2, lows, invs = [], [], [], []
    for h in range(heads):
        raw = r_ref[:, head_cols(h)]
        inv, root = house_terms(raw, strength, heads, h)
        u = raw * (inv * root)
        u_ref[:, head_cols(h)] = u
        u2 = split(u)
        low = jnp.where(rows > cols, dot3(u2, u2, 1, 1), 0.0)
        us.append(u)
        us2.append(u2)
        lows.append(low)
        first = jnp.where(rows == cols, 1.0, 0.0) - jnp.where(rows // 2 == cols // 2, low, 0.0)
        invs.append(first)
    span = 2
    while span < n:
        pick = (rows // (2 * span) == cols // (2 * span)) & (rows // span != cols // span)
        halves = [split(m) for m in invs]
        mids = [dot3(split(jnp.where(pick, lows[h], 0.0)), halves[h], 1, 0) for h in range(heads)]
        invs = [invs[h] - dot3(halves[h], split(mids[h]), 1, 0) for h in range(heads)]
        span = span * 2
    for h in range(heads):
        inv_ref[h] = invs[h]
        kin = split(invs[h])
        q = q_ref[:, head_cols(h)]
        k = k_ref[:, head_cols(h)]
        q2, k2, u2 = split(q), split(k), us2[h]
        a = jnp.where(rows > cols, dot3(u2, k2, 1, 1), 0.0)
        aq = jnp.where(rows < cols, dot3(k2, u2, 1, 1), 0.0)
        fq = jnp.where(rows >= cols, dot3(q2, u2, 1, 1), 0.0)
        fq2 = split(fq)
        x = dot3(kin, u2, 1, 0)
        y = dot3(kin, u2, 0, 0)
        psi = dot3(kin, split(a), 1, 0)
        x2 = split(x)
        x_ref[:, head_cols(h)] = x
        y_ref[:, head_cols(h)] = y
        psi_ref[h] = psi
        qt_ref[:, head_cols(h)] = (q - dot3(fq2, x2, 1, 0)).astype(BF)
        kt_ref[:, head_cols(h)] = (k - dot3(split(aq), split(y), 1, 0)).astype(BF)
        near_ref[h] = dot3(q2, k2, 1, 1) - dot3(fq2, split(psi), 1, 0)
        er, ec = iotas(HDIM)
        p_ref[h] = jnp.where(er == ec, 1.0, 0.0) - dot3(u2, x2, 0, 0)


def path_fwd(q, k, r, c, heads):
    n, width = q.shape
    flat = jax.ShapeDtypeStruct((n, width), F32)
    low = jax.ShapeDtypeStruct((n, width), BF)
    square = jax.ShapeDtypeStruct((heads, n, n), F32)
    return pl.pallas_call(
        functools.partial(path_fwd_kernel, heads),
        out_shape=(low, low, square, jax.ShapeDtypeStruct((heads, HDIM, HDIM), F32),
                   flat, square, square, flat, flat),
        compiler_params=pltpu.CompilerParams(vmem_limit_bytes=VMEM_LIMIT),
        name="path_fwd",
    )(q, k, r, c)


def doc_of(pos, len_ref):
    total = len_ref[0]
    doc = (pos >= total).astype(jnp.int32)
    for i in range(1, len_ref.shape[0]):
        total = total + len_ref[i]
        doc = doc + (pos >= total).astype(jnp.int32)
    return doc


def chain_slot(r, m):
    return r * (r - 1) // 2 + m


def attn_fwd_kernel(heads, hops, len_ref, row_ref, qt_ref, near_ref, v_ref, fk_ref, fv_ref, fp_ref,
                    o_ref, p_ref, chain_ref, s_ref):
    n = qt_ref.shape[0]
    scale = HDIM ** (-0.5)
    row = row_ref[0]
    rows, cols = iotas(n)
    own = doc_of(row * n + rows, len_ref)
    near_ok = (rows >= cols) & (own == doc_of(row * n + cols, len_ref))
    for h in range(heads):
        cs = head_cols(h)
        q = qt_ref[:, cs]
        s = jnp.where(near_ok, near_ref[h] * scale, neg_big)
        s_ref[h, 0] = s
        top = jnp.max(s, 1, keepdims=True)
        for r in range(1, hops + 1):
            keys = fk_ref[r - 1, :, cs]
            chain_ref[chain_slot(r, 0), :, cs] = keys
            for m in range(1, r):
                ph, plo = split(fp_ref[r - m - 1, h])
                keys = (dot(keys, ph, 1, 1) + dot(keys, plo, 1, 1)).astype(BF)
                chain_ref[chain_slot(r, m), :, cs] = keys
            source = row - r
            docs = jnp.where(source >= 0, doc_of(source * n + cols, len_ref), -1)
            s = jnp.where(own == docs, dot(q, keys, 1, 1) * scale, neg_big)
            s_ref[h, r] = s
            top = jnp.maximum(top, jnp.max(s, 1, keepdims=True))
        total = jnp.zeros((n, 1), F32)
        for r in range(hops + 1):
            e = jnp.exp(s_ref[h, r] - top)
            s_ref[h, r] = e
            total = total + jnp.sum(e, 1, keepdims=True)
        recip = 1.0 / total
        out = jnp.zeros((n, HDIM), F32)
        for r in range(hops + 1):
            p = (s_ref[h, r] * recip).astype(BF)
            p_ref[r, h] = p
            vals = v_ref[:, cs] if r == 0 else fv_ref[r - 1, :, cs]
            out = out + dot(p, vals, 1, 0)
        o_ref[:, cs] = out.astype(BF)


def attn_fwd(lengths, my_row, qt, near, v, far_k, far_v, far_p, heads, hops):
    n, width = qt.shape
    slots = hops * (hops + 1) // 2
    smem = pl.BlockSpec(memory_space=pltpu.SMEM)
    vmem = pl.BlockSpec(memory_space=pltpu.VMEM)
    return pl.pallas_call(
        functools.partial(attn_fwd_kernel, heads, hops),
        in_specs=[smem, smem] + [vmem] * 6,
        out_shape=(
            jax.ShapeDtypeStruct((n, width), BF),
            jax.ShapeDtypeStruct((hops + 1, heads, n, n), BF),
            jax.ShapeDtypeStruct((slots, n, width), BF),
        ),
        scratch_shapes=[pltpu.VMEM((heads, hops + 1, n, n), F32)],
        compiler_params=pltpu.CompilerParams(vmem_limit_bytes=VMEM_LIMIT),
        name="attn_fwd",
    )(lengths, my_row, qt, near, v, far_k, far_v, far_p)


def attn_bwd_kernel(heads, hops, p_ref, go_ref, qt_ref, v_ref, fv_ref, fp_ref, chain_ref,
                    gqt_ref, gnear_ref, gv_ref, sendk_ref, sendv_ref, sendp_ref, dp_ref):
    n = qt_ref.shape[0]
    scale = HDIM ** (-0.5)
    for h in range(heads):
        cs = head_cols(h)
        go = go_ref[:, cs]
        q = qt_ref[:, cs]
        delta = jnp.zeros((n, 1), F32)
        for r in range(hops + 1):
            vals = v_ref[:, cs] if r == 0 else fv_ref[r - 1, :, cs]
            dp = dot(go, vals, 1, 1)
            dp_ref[r] = dp
            delta = delta + jnp.sum(p_ref[r, h].astype(F32) * dp, 1, keepdims=True)
            gv = dot(p_ref[r, h], go, 0, 0)
            if r == 0:
                gv_ref[:, cs] = gv
            else:
                sendv_ref[r - 1, :, cs] = gv.astype(BF)
        gnear_ref[h] = p_ref[0, h].astype(F32) * (dp_ref[0] - delta) * scale
        gq = jnp.zeros((n, HDIM), F32)
        gps = [jnp.zeros((HDIM, HDIM), F32) for _ in range(hops - 1)]
        for r in range(1, hops + 1):
            gs = (p_ref[r, h].astype(F32) * (dp_ref[r] - delta) * scale).astype(BF)
            gq = gq + dot(gs, chain_ref[chain_slot(r, r - 1), :, cs], 1, 0)
            gk = dot(gs, q, 0, 0)
            for m in range(r - 1, 0, -1):
                back = r - m - 1
                gkb = gk.astype(BF)
                gps[back] = gps[back] + dot(gkb, chain_ref[chain_slot(r, m - 1), :, cs], 0, 0)
                gk = dot(gkb, fp_ref[back, h].astype(BF), 1, 0)
            sendk_ref[r - 1, :, cs] = gk.astype(BF)
        gqt_ref[:, cs] = gq
        for i in range(hops - 1):
            sendp_ref[i, h] = gps[i].astype(BF)


def attn_bwd(p, go, qt, v, far_v, far_p, chain, heads, hops):
    n, width = qt.shape
    return pl.pallas_call(
        functools.partial(attn_bwd_kernel, heads, hops),
        out_shape=(
            jax.ShapeDtypeStruct((n, width), F32),
            jax.ShapeDtypeStruct((heads, n, n), F32),
            jax.ShapeDtypeStruct((n, width), F32),
            jax.ShapeDtypeStruct((hops, n, width), BF),
            jax.ShapeDtypeStruct((hops, n, width), BF),
            jax.ShapeDtypeStruct((hops - 1, heads, HDIM, HDIM), BF),
        ),
        scratch_shapes=[pltpu.VMEM((hops + 1, n, n), F32)],
        compiler_params=pltpu.CompilerParams(vmem_limit_bytes=VMEM_LIMIT),
        name="attn_bwd",
    )(p, go, qt, v, far_v, far_p, chain)


def path_bwd_kernel(heads, q_ref, k_ref, r_ref, c_ref, u_ref, inv_ref, psi_ref, x_ref, y_ref,
                    gqt_ref, gkt_ref, gnear_ref, gp_ref, gq_ref, gk_ref, gr_ref, gc_ref):
    n = q_ref.shape[0]
    rows, cols = iotas(n)
    strength = c_ref[...]
    lane = lax.broadcasted_iota(jnp.int32, strength.shape, 1)
    gc_all = jnp.zeros(strength.shape, F32)
    for h in range(heads):
        cs = head_cols(h)
        q, k, u = q_ref[:, cs], k_ref[:, cs], u_ref[:, cs]
        qb, kb, ub = q.astype(BF), k.astype(BF), u.astype(BF)
        kin = inv_ref[h].astype(BF)
        psi = psi_ref[h].astype(BF)
        x, y = x_ref[:, cs].astype(BF), y_ref[:, cs].astype(BF)
        gqt, gkt = gqt_ref[:, cs], gkt_ref[:, cs]
        gqtb, gktb = gqt.astype(BF), gkt.astype(BF)
        gs = gnear_ref[h]
        gsb = gs.astype(BF)
        gst = gs.T.astype(BF)
        gp = gp_ref[h].astype(BF)
        f = jnp.where(rows <= cols, dot(ub, qb, 1, 1), 0.0).astype(BF)
        fq = jnp.where(rows >= cols, dot(qb, ub, 1, 1), 0.0).astype(BF)
        a = jnp.where(rows > cols, dot(ub, kb, 1, 1), 0.0).astype(BF)
        gx = -(dot(f, gqtb, 1, 0) + dot(ub, gp, 1, 0))
        gy = -dot(a, gktb, 1, 0)
        phiq = dot(fq, kin, 1, 0).astype(BF)
        back = dot(gst, phiq, 1, 0)
        backb = back.astype(BF)
        gfq = jnp.where(rows >= cols, -(dot(gqtb, x, 1, 1) + dot(gsb, psi, 1, 1)), 0.0)
        gaq = jnp.where(rows < cols, -(dot(gktb, y, 1, 1) + back), 0.0)
        kgx = dot(kin, gx.astype(BF), 0, 0)
        kgy = dot(kin, gy.astype(BF), 1, 0)
        zt = dot(x, kgx.astype(BF), 1, 1) + dot(kgy.astype(BF), y, 1, 1) - dot(psi, backb, 1, 0)
        glt = jnp.where(rows < cols, -zt, 0.0)
        sym = (glt + glt.T).astype(BF)
        gfqb, gaqb = gfq.astype(BF), gaq.astype(BF)
        gu = (kgx + kgy - dot(x, gp, 1, 1) + dot(gfq.T.astype(BF), qb, 1, 0)
              + dot(gaq.T.astype(BF), kb, 1, 0) + dot(sym, ub, 1, 0))
        gq_ref[:, cs] = (gqt + dot(gsb, kb, 1, 0) + dot(gfqb, ub, 1, 0)).astype(BF)
        gk_ref[:, cs] = (gkt + dot(gst, qb, 1, 0) + dot(gaqb, ub, 1, 0)).astype(BF)
        raw = r_ref[:, cs]
        inv, root = house_terms(raw, strength, heads, h)
        gc = jnp.sum(gu * u, 1, keepdims=True) * (1.0 - 0.5 * root * root) * 0.5
        gun = gu * root
        un = raw * inv
        gr = inv * (gun - un * jnp.sum(gun * un, 1, keepdims=True))
        gr_ref[:, cs] = gr.astype(BF)
        gc_all = jnp.where(lane == h, gc, gc_all)
    gc_ref[...] = gc_all.astype(BF)


def path_bwd(q, k, r, c, saved, gqt, gkt, gnear, gp, heads):
    n, width = q.shape
    low = jax.ShapeDtypeStruct((n, width), BF)
    return pl.pallas_call(
        functools.partial(path_bwd_kernel, heads),
        out_shape=(low, low, low, jax.ShapeDtypeStruct((n, heads), BF)),
        compiler_params=pltpu.CompilerParams(vmem_limit_bytes=VMEM_LIMIT),
        name="path_bwd",
    )(q, k, r, c, *saved, gqt, gkt, gnear, gp)


def shifted(array, axis, by):
    peers = lax.axis_size(axis)
    pairs = [(i, i + by) for i in range(peers) if 0 <= i + by < peers]
    return lax.ppermute(array, axis, pairs)


def norm_rows(hidden_f):
    inverse = lax.rsqrt(jnp.mean(hidden_f * hidden_f, -1, keepdims=True) + eps_norm)
    return (hidden_f * inverse, inverse)


def norm_back(grad_out, normed, inverse, gain_vec):
    scaled_grad = grad_out * gain_vec
    grad_gain = jnp.sum(grad_out * normed, 0)
    grad_in = inverse * (scaled_grad - normed * jnp.mean(scaled_grad * normed, -1, keepdims=True))
    return (grad_in, grad_gain)


ROWS = ("seq", "hid")


def body(inputs, gain_attn, gain_ffn, w_query, w_key, w_value, w_house, w_beta, w_out,
         w_gate, w_up, w_down, lengths, cotangent):
    tok, col = inputs.shape
    row_devs = lax.axis_size(ROWS)
    my_row = lax.axis_index(ROWS)
    my_wid = lax.axis_index("wid")
    wid_n = lax.axis_size("wid")
    tokens_all = tok * row_devs
    most_len = max(LEAST, 2 * tokens_all // 5)
    hops = min((most_len - 2) // tok + 1, row_devs - 1)
    heads = w_query.shape[1] // HDIM
    ff = w_gate.shape[1]
    sub = tok // wid_n

    x_all = lax.all_gather(inputs, "wid", axis=1, tiled=True)
    gain_one = lax.all_gather(gain_attn, "wid", axis=0, tiled=True).astype(F32)
    gain_two = lax.all_gather(gain_ffn, "wid", axis=0, tiled=True).astype(F32)
    dy_all = lax.all_gather(cotangent, "wid", axis=1, tiled=True)
    w_gu = lax.all_gather(jnp.concatenate([w_gate, w_up], 1), "hid", axis=0)
    w_dn = lax.all_gather(w_down, "hid", axis=0)
    model = x_all.shape[1]

    residual = x_all.astype(F32)
    normed_one, inverse_one = norm_rows(residual)
    act = (normed_one * gain_one).astype(BF)

    def project(weight):
        return jnp.dot(act, weight, preferred_element_type=F32)

    q, k, r, c = project(w_query), project(w_key), project(w_house), project(w_beta)
    v = project(w_value).astype(BF)
    far_v = jnp.stack([shifted(v, ROWS, i) for i in range(1, hops + 1)])
    qt, kt, near, prod, *saved = path_fwd(q, k, r, c, heads)
    far_k = jnp.stack([shifted(kt, ROWS, i) for i in range(1, hops + 1)])
    far_p = jnp.stack([shifted(prod, ROWS, i) for i in range(1, hops)])
    row_arr = jnp.full((1,), my_row, jnp.int32)
    attended, probs, chain = attn_fwd(lengths, row_arr, qt, near, v, far_k, far_v, far_p, heads, hops)

    attn_part = jnp.dot(attended, w_out, preferred_element_type=F32).astype(BF)
    attn_rows = lax.psum_scatter(attn_part, "wid", scatter_dimension=0, tiled=True)
    x_rows = lax.dynamic_slice_in_dim(x_all, my_wid * sub, sub, 0).astype(F32)
    dy_rows = lax.dynamic_slice_in_dim(dy_all, my_wid * sub, sub, 0).astype(F32)
    mixed = x_rows + attn_rows.astype(F32)
    normed_two, inverse_two = norm_rows(mixed)
    inner = lax.all_gather((normed_two * gain_two).astype(BF), "wid", axis=0, tiled=True)

    pre = jnp.einsum("tc,hcf->htf", inner, w_gu, preferred_element_type=F32)
    gate, up = pre[:, :, :ff], pre[:, :, ff:]
    sig = jax.nn.sigmoid(gate)
    hidden = (gate * sig * up).astype(BF)
    ffn_part = jnp.einsum("htf,hfc->tc", hidden, w_dn, preferred_element_type=F32)
    ffn_part = (ffn_part + attn_part.astype(F32)).astype(BF)
    ffn_cols = lax.psum_scatter(ffn_part, "wid", scatter_dimension=1, tiled=True)
    output = (inputs.astype(F32) + ffn_cols.astype(F32)).astype(BF)

    g_hidden = jnp.einsum("tc,hfc->htf", dy_all, w_dn, preferred_element_type=F32)
    g_gate = g_hidden * up * sig * (1.0 + gate * (1.0 - sig))
    g_up = g_hidden * gate * sig
    g_pre = jnp.concatenate([g_gate, g_up], 2).astype(BF)
    g_inner = jnp.einsum("htf,hcf->tc", g_pre, w_gu, preferred_element_type=F32).astype(BF)
    g_inner = lax.psum_scatter(g_inner, "wid", scatter_dimension=0, tiled=True).astype(F32)
    g_mixed_n, g_gain_two = norm_back(g_inner, normed_two, inverse_two, gain_two)
    g_z = lax.all_gather((dy_rows + g_mixed_n).astype(BF), "wid", axis=0, tiled=True)

    d_gu = jnp.einsum("tc,htf->hcf", inner, g_pre, preferred_element_type=F32).astype(BF)
    d_dn = jnp.einsum("htf,tc->hfc", hidden, dy_all, preferred_element_type=F32).astype(BF)
    d_gu = lax.psum_scatter(d_gu, "seq", scatter_dimension=1, tiled=True)
    d_gu = lax.psum_scatter(d_gu, "hid", scatter_dimension=0)
    d_dn = lax.psum_scatter(d_dn, "seq", scatter_dimension=2, tiled=True)
    d_dn = lax.psum_scatter(d_dn, "hid", scatter_dimension=0)

    g_attn = jnp.einsum("tc,ic->ti", g_z, w_out, preferred_element_type=F32).astype(BF)
    d_out = jnp.einsum("ti,tc->ic", attended, g_z, preferred_element_type=F32).astype(BF)
    g_qt, g_near, gv, send_k, send_v, send_p = attn_bwd(probs, g_attn, qt, v, far_v, far_p, chain, heads, hops)
    g_kt = sum(shifted(send_k[i - 1], ROWS, -i).astype(F32) for i in range(1, hops + 1))
    gv = gv + sum(shifted(send_v[i - 1], ROWS, -i).astype(F32) for i in range(1, hops + 1))
    g_prod = sum(shifted(send_p[i - 1], ROWS, -i).astype(F32) for i in range(1, hops))
    g_q, g_k, g_r, g_c = path_bwd(q, k, r, c, saved, g_qt, g_kt, g_near, g_prod, heads)
    g_v = gv.astype(BF)

    def weight_grad(grad_low):
        return jnp.einsum("tc,ti->ci", act, grad_low, preferred_element_type=F32).astype(BF)

    def input_grad(grad_low, weight):
        return jnp.einsum("ti,ci->tc", grad_low, weight, preferred_element_type=F32)

    g_act = (input_grad(g_q, w_query) + input_grad(g_k, w_key) + input_grad(g_v, w_value)
             + input_grad(g_r, w_house) + input_grad(g_c, w_beta))
    g_act = lax.psum_scatter(g_act.astype(BF), "wid", scatter_dimension=0, tiled=True).astype(F32)
    normed_rows = lax.dynamic_slice_in_dim(normed_one, my_wid * sub, sub, 0)
    inverse_rows = lax.dynamic_slice_in_dim(inverse_one, my_wid * sub, sub, 0)
    g_resid, g_gain_one = norm_back(g_act, normed_rows, inverse_rows, gain_one)
    d_rows = dy_rows + g_mixed_n + g_resid
    d_inputs = lax.all_to_all(d_rows, "wid", split_axis=1, concat_axis=0, tiled=True)

    def scatter(x, dim):
        return lax.psum_scatter(x, ROWS, scatter_dimension=dim, tiled=True)

    gains = lax.psum(jnp.stack([g_gain_one, g_gain_two]), "wid")
    gains = scatter(gains, 1)
    return (
        output,
        d_inputs,
        gains[0],
        gains[1],
        scatter(weight_grad(g_q), 0).astype(F32),
        scatter(weight_grad(g_k), 0).astype(F32),
        scatter(weight_grad(g_v), 0).astype(F32),
        scatter(weight_grad(g_r), 0).astype(F32),
        scatter(weight_grad(g_c), 0).astype(F32),
        scatter(d_out, 1).astype(F32),
        d_gu[:, :ff].astype(F32),
        d_gu[:, ff:].astype(F32),
        d_dn.astype(F32),
    )


def solution(mesh):
    in_specs = (
        P(("seq", "hid"), "wid"), P("wid"), P("wid"),
        P(None, "wid"), P(None, "wid"), P(None, "wid"), P(None, "wid"), P(None, "wid"),
        P("wid", None), P(None, ("hid", "wid")), P(None, ("hid", "wid")), P(("hid", "wid"), None),
        P(), P(("seq", "hid"), "wid"),
    )
    out_specs = (
        P(("seq", "hid"), "wid"), P(("seq", "hid"), "wid"), P(("seq", "hid")), P(("seq", "hid")),
        P(("seq", "hid"), "wid"), P(("seq", "hid"), "wid"), P(("seq", "hid"), "wid"),
        P(("seq", "hid"), "wid"), P(("seq", "hid"), "wid"), P("wid", ("seq", "hid")),
        P("seq", ("hid", "wid")), P("seq", ("hid", "wid")), P(("hid", "wid"), "seq"),
    )
    return jax.shard_map(body, mesh=mesh, in_specs=in_specs, out_specs=out_specs, check_vma=False)
```

```python
import functools

import jax
import jax.numpy as jnp
from jax import lax
from jax.experimental import pallas as pl
from jax.experimental.pallas import tpu as pltpu
from jax.sharding import PartitionSpec as P

HDIM = 128
LEAST = 1024

eps_norm = 1e-06
neg_big = -1e30
BF = jnp.bfloat16
F32 = jnp.float32
VMEM_LIMIT = 60 * 1024 * 1024


def dot(a, b, ca, cb):
    return lax.dot_general(a, b, (((ca,), (cb,)), ((), ())), preferred_element_type=F32)


def split(a):
    hi = a.astype(BF)
    return hi, (a - hi.astype(F32)).astype(BF)


def dot3(a, b, ca, cb):
    return dot(a[0], b[0], ca, cb) + (dot(a[0], b[1], ca, cb) + dot(a[1], b[0], ca, cb))


def dot1(a, b, ca, cb):
    return dot(a.astype(BF), b.astype(BF), ca, cb)


def iotas(n):
    rows = lax.broadcasted_iota(jnp.int32, (n, n), 0)
    cols = lax.broadcasted_iota(jnp.int32, (n, n), 1)
    return rows, cols


def head_cols(h):
    return slice(h * HDIM, (h + 1) * HDIM)


def house_terms(raw, strength, heads, h):
    inv = lax.rsqrt(jnp.sum(raw * raw, -1, keepdims=True) + eps_norm)
    lane = lax.broadcasted_iota(jnp.int32, strength.shape, 1)
    c = jnp.sum(jnp.where(lane == h, strength, 0.0), 1, keepdims=True)
    root = jnp.sqrt(2.0 / (1.0 + jnp.exp(-c)))
    return inv, root


def path_fwd_stage(heads, q_ref, k_ref, r_ref, c_ref, qt_ref, kt_ref, near_ref, p_ref,
                   u_ref, inv_ref, psi_ref, x_ref, y_ref, done=None):
    n = q_ref.shape[0]
    rows, cols = iotas(n)
    strength = c_ref[...]
    us, us2, lows, invs = [], [], [], []
    for h in range(heads):
        raw = r_ref[:, head_cols(h)]
        inv, root = house_terms(raw, strength, heads, h)
        u = raw * (inv * root)
        u_ref[:, head_cols(h)] = u
        u2 = split(u)
        low = jnp.where(rows > cols, dot3(u2, u2, 1, 1), 0.0)
        us.append(u)
        us2.append(u2)
        lows.append(low)
        first = jnp.where(rows == cols, 1.0, 0.0) - jnp.where(rows // 2 == cols // 2, low, 0.0)
        invs.append(first)
    span = 2
    while span < n:
        pick = (rows // (2 * span) == cols // (2 * span)) & (rows // span != cols // span)
        halves = [split(m) for m in invs]
        mids = [dot3(split(jnp.where(pick, lows[h], 0.0)), halves[h], 1, 0) for h in range(heads)]
        invs = [invs[h] - dot3(halves[h], split(mids[h]), 1, 0) for h in range(heads)]
        span = span * 2
    for h in range(heads):
        inv_ref[h] = invs[h]
        kin = split(invs[h])
        q = q_ref[:, head_cols(h)]
        k = k_ref[:, head_cols(h)]
        q2, k2, u2 = split(q), split(k), us2[h]
        a = jnp.where(rows > cols, dot3(u2, k2, 1, 1), 0.0)
        aq = jnp.where(rows < cols, dot3(k2, u2, 1, 1), 0.0)
        fq = jnp.where(rows >= cols, dot3(q2, u2, 1, 1), 0.0)
        fq2 = split(fq)
        x = dot3(kin, u2, 1, 0)
        y = dot3(kin, u2, 0, 0)
        psi = dot3(kin, split(a), 1, 0)
        x2 = split(x)
        x_ref[:, head_cols(h)] = x
        y_ref[:, head_cols(h)] = y
        psi_ref[h] = psi
        qt_ref[:, head_cols(h)] = (q - dot3(fq2, x2, 1, 0)).astype(BF)
        kt_ref[:, head_cols(h)] = (k - dot3(split(aq), split(y), 1, 0)).astype(BF)
        near_ref[h] = dot3(q2, k2, 1, 1) - dot3(fq2, split(psi), 1, 0)
        er, ec = iotas(HDIM)
        p_ref[h] = jnp.where(er == ec, 1.0, 0.0) - dot3(u2, x2, 0, 0)
        if done is not None:
            done(h)


def path_fwd_kernel(heads, *refs):
    path_fwd_stage(heads, *refs)


def path_fwd(q, k, r, c, heads):
    n, width = q.shape
    flat = jax.ShapeDtypeStruct((n, width), F32)
    low = jax.ShapeDtypeStruct((n, width), BF)
    square = jax.ShapeDtypeStruct((heads, n, n), F32)
    return pl.pallas_call(
        functools.partial(path_fwd_kernel, heads),
        out_shape=(low, low, square, jax.ShapeDtypeStruct((heads, HDIM, HDIM), F32),
                   flat, square, square, flat, flat),
        compiler_params=pltpu.CompilerParams(vmem_limit_bytes=VMEM_LIMIT),
        name="path_fwd",
    )(q, k, r, c)


def doc_of(pos, len_ref):
    total = len_ref[0]
    doc = (pos >= total).astype(jnp.int32)
    for i in range(1, len_ref.shape[0]):
        total = total + len_ref[i]
        doc = doc + (pos >= total).astype(jnp.int32)
    return doc


def chain_slot(r, m):
    return r * (r - 1) // 2 + m


def attn_fwd_stage(heads, hops, row, len_ref, qt_ref, near_ref, v_ref, fv_ref, fp_ref, chain_ref,
                   o_ref, p_ref, s_ref, get_k, get_p):
    n = qt_ref.shape[0]
    scale = HDIM ** (-0.5)
    rows, cols = iotas(n)
    own = doc_of(row * n + rows, len_ref)
    near_ok = (rows >= cols) & (own == doc_of(row * n + cols, len_ref))
    for h in range(heads):
        cs = head_cols(h)
        q = qt_ref[:, cs]
        for copy in get_k[h] + get_p[h]:
            copy.wait_recv()
        s = jnp.where(near_ok, near_ref[h] * scale, neg_big)
        s_ref[0] = s
        top = jnp.max(s, 1, keepdims=True)
        for r in range(1, hops + 1):
            keys = chain_ref[chain_slot(r, 0), :, cs]
            for m in range(1, r):
                ph, plo = split(fp_ref[r - m - 1, h])
                keys = (dot(keys, ph, 1, 1) + dot(keys, plo, 1, 1)).astype(BF)
                chain_ref[chain_slot(r, m), :, cs] = keys
            source = row - r
            docs = jnp.where(source >= 0, doc_of(source * n + cols, len_ref), -1)
            s = jnp.where(own == docs, dot(q, keys, 1, 1) * scale, neg_big)
            s_ref[r] = s
            top = jnp.maximum(top, jnp.max(s, 1, keepdims=True))
        total = jnp.zeros((n, 1), F32)
        for r in range(hops + 1):
            e = jnp.exp(s_ref[r] - top)
            s_ref[r] = e
            total = total + jnp.sum(e, 1, keepdims=True)
        recip = 1.0 / total
        out = jnp.zeros((n, HDIM), F32)
        for r in range(hops + 1):
            p = (s_ref[r] * recip).astype(BF)
            p_ref[r, h] = p
            vals = v_ref[:, cs] if r == 0 else fv_ref[r - 1, :, cs]
            out = out + dot(p, vals, 1, 0)
        o_ref[:, cs] = out.astype(BF)

def attn_fwd_kernel(heads, hops, len_ref, row_ref, qt_ref, near_ref, v_ref, fk_ref, fv_ref, fp_ref,
                    o_ref, p_ref, chain_ref, s_ref):
    for r in range(1, hops + 1):
        chain_ref[chain_slot(r, 0)] = fk_ref[r - 1]
    none = [[] for _ in range(heads)]
    attn_fwd_stage(heads, hops, row_ref[0], len_ref, qt_ref, near_ref, v_ref, fv_ref, fp_ref, chain_ref,
                   o_ref, p_ref, s_ref, none, none)


def attn_fwd(lengths, my_row, qt, near, v, far_k, far_v, far_p, heads, hops):
    n, width = qt.shape
    slots = hops * (hops + 1) // 2
    smem = pl.BlockSpec(memory_space=pltpu.SMEM)
    vmem = pl.BlockSpec(memory_space=pltpu.VMEM)
    return pl.pallas_call(
        functools.partial(attn_fwd_kernel, heads, hops),
        in_specs=[smem, smem] + [vmem] * 6,
        out_shape=(
            jax.ShapeDtypeStruct((n, width), BF),
            jax.ShapeDtypeStruct((hops + 1, heads, n, n), BF),
            jax.ShapeDtypeStruct((slots, n, width), BF),
        ),
        scratch_shapes=[pltpu.VMEM((hops + 1, n, n), F32)],
        compiler_params=pltpu.CompilerParams(vmem_limit_bytes=VMEM_LIMIT),
        name="attn_fwd",
    )(lengths, my_row, qt, near, v, far_k, far_v, far_p)


def attn_bwd_kernel(heads, hops, p_ref, go_ref, qt_ref, v_ref, fv_ref, fp_ref, chain_ref,
                    gqt_ref, gnear_ref, gv_ref, sendk_ref, sendv_ref, sendp_ref, dp_ref):
    n = qt_ref.shape[0]
    scale = HDIM ** (-0.5)
    for h in range(heads):
        cs = head_cols(h)
        go = go_ref[:, cs]
        q = qt_ref[:, cs]
        delta = jnp.zeros((n, 1), F32)
        for r in range(hops + 1):
            vals = v_ref[:, cs] if r == 0 else fv_ref[r - 1, :, cs]
            dp = dot(go, vals, 1, 1)
            dp_ref[r] = dp
            delta = delta + jnp.sum(p_ref[r, h].astype(F32) * dp, 1, keepdims=True)
            gv = dot(p_ref[r, h], go, 0, 0)
            if r == 0:
                gv_ref[:, cs] = gv
            else:
                sendv_ref[r - 1, :, cs] = gv.astype(BF)
        gnear_ref[h] = p_ref[0, h].astype(F32) * (dp_ref[0] - delta) * scale
        gq = jnp.zeros((n, HDIM), F32)
        gps = [jnp.zeros((HDIM, HDIM), F32) for _ in range(hops - 1)]
        for r in range(1, hops + 1):
            gs = (p_ref[r, h].astype(F32) * (dp_ref[r] - delta) * scale).astype(BF)
            gq = gq + dot(gs, chain_ref[chain_slot(r, r - 1), :, cs], 1, 0)
            gk = dot(gs, q, 0, 0)
            for m in range(r - 1, 0, -1):
                back = r - m - 1
                gkb = gk.astype(BF)
                gps[back] = gps[back] + dot(gkb, chain_ref[chain_slot(r, m - 1), :, cs], 0, 0)
                gk = dot(gkb, fp_ref[back, h].astype(BF), 1, 0)
            sendk_ref[r - 1, :, cs] = gk.astype(BF)
        gqt_ref[:, cs] = gq
        for i in range(hops - 1):
            sendp_ref[i, h] = gps[i].astype(BF)


def attn_bwd(p, go, qt, v, far_v, far_p, chain, heads, hops):
    n, width = qt.shape
    return pl.pallas_call(
        functools.partial(attn_bwd_kernel, heads, hops),
        out_shape=(
            jax.ShapeDtypeStruct((n, width), F32),
            jax.ShapeDtypeStruct((heads, n, n), F32),
            jax.ShapeDtypeStruct((n, width), F32),
            jax.ShapeDtypeStruct((hops, n, width), BF),
            jax.ShapeDtypeStruct((hops, n, width), BF),
            jax.ShapeDtypeStruct((hops - 1, heads, HDIM, HDIM), BF),
        ),
        scratch_shapes=[pltpu.VMEM((hops + 1, n, n), F32)],
        compiler_params=pltpu.CompilerParams(vmem_limit_bytes=VMEM_LIMIT),
        name="attn_bwd",
    )(p, go, qt, v, far_v, far_p, chain)


def path_bwd_kernel(heads, q_ref, k_ref, r_ref, c_ref, u_ref, inv_ref, psi_ref, x_ref, y_ref,
                    gqt_ref, gkt_ref, gnear_ref, gp_ref, gq_ref, gk_ref, gr_ref, gc_ref):
    n = q_ref.shape[0]
    rows, cols = iotas(n)
    strength = c_ref[...]
    lane = lax.broadcasted_iota(jnp.int32, strength.shape, 1)
    gc_all = jnp.zeros(strength.shape, F32)
    for h in range(heads):
        cs = head_cols(h)
        q, k, u = q_ref[:, cs], k_ref[:, cs], u_ref[:, cs]
        qb, kb, ub = q.astype(BF), k.astype(BF), u.astype(BF)
        kin = inv_ref[h].astype(BF)
        psi = psi_ref[h].astype(BF)
        x, y = x_ref[:, cs].astype(BF), y_ref[:, cs].astype(BF)
        gqt, gkt = gqt_ref[:, cs], gkt_ref[:, cs]
        gqtb, gktb = gqt.astype(BF), gkt.astype(BF)
        gs = gnear_ref[h]
        gsb = gs.astype(BF)
        gst = gs.T.astype(BF)
        gp = gp_ref[h].astype(BF)
        f = jnp.where(rows <= cols, dot(ub, qb, 1, 1), 0.0).astype(BF)
        fq = jnp.where(rows >= cols, dot(qb, ub, 1, 1), 0.0).astype(BF)
        a = jnp.where(rows > cols, dot(ub, kb, 1, 1), 0.0).astype(BF)
        gx = -(dot(f, gqtb, 1, 0) + dot(ub, gp, 1, 0))
        gy = -dot(a, gktb, 1, 0)
        phiq = dot(fq, kin, 1, 0).astype(BF)
        back = dot(gst, phiq, 1, 0)
        backb = back.astype(BF)
        gfq = jnp.where(rows >= cols, -(dot(gqtb, x, 1, 1) + dot(gsb, psi, 1, 1)), 0.0)
        gaq = jnp.where(rows < cols, -(dot(gktb, y, 1, 1) + back), 0.0)
        kgx = dot(kin, gx.astype(BF), 0, 0)
        kgy = dot(kin, gy.astype(BF), 1, 0)
        zt = dot(x, kgx.astype(BF), 1, 1) + dot(kgy.astype(BF), y, 1, 1) - dot(psi, backb, 1, 0)
        glt = jnp.where(rows < cols, -zt, 0.0)
        sym = (glt + glt.T).astype(BF)
        gfqb, gaqb = gfq.astype(BF), gaq.astype(BF)
        gu = (kgx + kgy - dot(x, gp, 1, 1) + dot(gfq.T.astype(BF), qb, 1, 0)
              + dot(gaq.T.astype(BF), kb, 1, 0) + dot(sym, ub, 1, 0))
        gq_ref[:, cs] = (gqt + dot(gsb, kb, 1, 0) + dot(gfqb, ub, 1, 0)).astype(BF)
        gk_ref[:, cs] = (gkt + dot(gst, qb, 1, 0) + dot(gaqb, ub, 1, 0)).astype(BF)
        raw = r_ref[:, cs]
        inv, root = house_terms(raw, strength, heads, h)
        gc = jnp.sum(gu * u, 1, keepdims=True) * (1.0 - 0.5 * root * root) * 0.5
        gun = gu * root
        un = raw * inv
        gr = inv * (gun - un * jnp.sum(gun * un, 1, keepdims=True))
        gr_ref[:, cs] = gr.astype(BF)
        gc_all = jnp.where(lane == h, gc, gc_all)
    gc_ref[...] = gc_all.astype(BF)


def path_bwd(q, k, r, c, saved, gqt, gkt, gnear, gp, heads):
    n, width = q.shape
    low = jax.ShapeDtypeStruct((n, width), BF)
    return pl.pallas_call(
        functools.partial(path_bwd_kernel, heads),
        out_shape=(low, low, low, jax.ShapeDtypeStruct((n, heads), BF)),
        compiler_params=pltpu.CompilerParams(vmem_limit_bytes=VMEM_LIMIT),
        name="path_bwd",
    )(q, k, r, c, *saved, gqt, gkt, gnear, gp)


MESH = pl.DeviceIdType.MESH


class Copies:
    def __init__(self, send, recv):
        self.send, self.recv, self.count = send, recv, 0

    def start(self, src, dst, device):
        i = self.count
        self.count = i + 1
        copy = pltpu.make_async_remote_copy(
            src_ref=src, dst_ref=dst, send_sem=self.send.at[i], recv_sem=self.recv.at[i],
            device_id=device, device_id_type=MESH)
        copy.start()
        return copy


class Loads:
    def __init__(self, sems):
        self.sems, self.count = sems, 0

    def start(self, src, dst):
        copy = pltpu.make_async_copy(src, dst, self.sems.at[self.count])
        self.count = self.count + 1
        copy.start()
        return copy


class Place:
    def __init__(self, sizes):
        self.seq_n, self.hid_n, self.wid_n = sizes
        self.seq = lax.axis_index("seq")
        self.hid = lax.axis_index("hid")
        self.wid = lax.axis_index("wid")
        self.rows_n = self.seq_n * self.hid_n
        self.row = self.seq * self.hid_n + self.hid

    def wid_peer(self, i):
        return lax.rem(self.wid + i, self.wid_n)

    def hid_peer(self, i):
        return lax.rem(self.hid + i, self.hid_n)

    def seq_peer(self, i):
        return lax.rem(self.seq + i, self.seq_n)

    def row_peer(self, i):
        to = lax.rem(self.row + i + self.rows_n, self.rows_n)
        return {"seq": to // self.hid_n, "hid": lax.rem(to, self.hid_n)}

    def barrier(self):
        sem = pltpu.get_barrier_semaphore()
        for i in range(1, self.wid_n):
            pl.semaphore_signal(sem, inc=1, device_id={"wid": self.wid_peer(i)}, device_id_type=MESH)
        for i in range(1, self.rows_n):
            pl.semaphore_signal(sem, inc=1, device_id=self.row_peer(i), device_id_type=MESH)
        pl.semaphore_wait(sem, self.wid_n - 1 + self.rows_n - 1)


def aligned(start, size, step):
    return pl.ds(pl.multiple_of(start, step), size)


def fwd_kernel(cfg, len_ref, x_ref, dy_ref, gain_ref, wq_ref, wk_ref, wv_ref, wr_ref, wb_ref, wo_ref,
               wg_ref, wu_ref, wd_ref,
               act_ref, xall_ref, gall_ref, dyall_ref, q_ref, k_ref, r_ref, c_ref, v_ref,
               qt_ref, u_ref, inv_ref, psi_ref, x1_ref, y1_ref,
               fv_ref, fp_ref, chain_ref, probs_ref, o_ref, mixed_ref, inner_ref,
               hidden_ref, ggate_ref, gup_ref, gin_ref, fsum_ref,
               wq_s, wk_s, wv_s, wr_s, wo_s, wg_s, wu_s, wd_s, kt_s, near_s, prod_s, s_s, part_s, recv_s, row_s,
               load_sem, send_sem, recv_sem):
    heads, hops, sizes = cfg
    place = Place(sizes)
    wid_n, hid_n, seq_n = place.wid_n, place.hid_n, place.seq_n
    n, col = x_ref.shape
    model = act_ref.shape[1]
    ff = wg_ref.shape[1]
    sub = n // wid_n
    copies, loads = Copies(send_sem, recv_sem), Loads(load_sem)
    my_cols = aligned(place.wid * col, col, 128)
    my_rows = aligned(place.wid * sub, sub, sub)

    load_x = [loads.start(x_ref, xall_ref.at[:, my_cols]), loads.start(gain_ref, gall_ref.at[:, my_cols])]
    load_w = [loads.start(a, b) for a, b in ((wv_ref, wv_s), (wq_ref, wq_s), (wk_ref, wk_s), (wr_ref, wr_s))]
    load_dy = loads.start(dy_ref, dyall_ref.at[:, my_cols])
    load_o = loads.start(wo_ref, wo_s)
    load_f = [loads.start(wg_ref, wg_s.at[:, pl.ds(0, ff)]), loads.start(wu_ref, wu_s.at[:, pl.ds(0, ff)]),
              loads.start(wd_ref, wd_s.at[pl.ds(0, ff), :])]
    place.barrier()

    order = sorted(range(1, wid_n), key=lambda i: -min(i, wid_n - i))
    to_wid = [{"wid": place.wid_peer(i)} for i in order]
    get_x = [copies.start(x_ref, xall_ref.at[:, my_cols], d) for d in to_wid]
    get_x += [copies.start(gain_ref, gall_ref.at[:, my_cols], d) for d in to_wid]

    part_c, part_f = model // seq_n, ff // seq_n
    mine_c = aligned(place.seq * part_c, part_c, 16)
    mine_f = aligned(place.seq * part_f, part_f, 16)

    def slot_f(j):
        return aligned(j * ff + place.seq * part_f, part_f, 16)

    get_gu = []
    for src, dst in ((wg_ref, wg_s), (wu_ref, wu_s)):
        get_gu += [copies.start(src.at[mine_c, :], dst.at[mine_c, pl.ds(j * ff, ff)], {"hid": place.hid_peer(j)})
                   for j in range(1, hid_n)]

    for copy in load_x:
        copy.wait()
    for copy in get_x:
        copy.wait_recv()
    get_dy = [copies.start(dy_ref, dyall_ref.at[:, my_cols], d) for d in to_wid]
    xf = xall_ref[...].astype(F32)
    inv_rms = lax.rsqrt(jnp.mean(xf * xf, -1, keepdims=True) + eps_norm)
    act_ref[...] = (xf * inv_rms * gall_ref[0:1, :]).astype(BF)
    for copy in load_w:
        copy.wait()
    act = act_ref[...]
    v_ref[...] = dot(act, wv_s[...], 1, 0).astype(BF)
    get_v = [copies.start(v_ref, fv_ref.at[i - 1], place.row_peer(i)) for i in range(1, hops + 1)]
    q_ref[...] = dot(act, wq_s[...], 1, 0)
    k_ref[...] = dot(act, wk_s[...], 1, 0)
    r_ref[...] = dot(act, wr_s[...], 1, 0)
    c_ref[...] = dot(act, wb_ref[...], 1, 0)

    get_k = [[] for _ in range(heads)]
    get_p = [[] for _ in range(heads)]

    def send_head(h):
        cs = head_cols(h)
        for i in range(1, hops + 1):
            get_k[h].append(copies.start(kt_s.at[:, cs], chain_ref.at[chain_slot(i, 0), :, cs], place.row_peer(i)))
        for i in range(1, hops):
            get_p[h].append(copies.start(prod_s.at[h], fp_ref.at[i - 1, h], place.row_peer(i)))

    path_fwd_stage(heads, q_ref, k_ref, r_ref, c_ref, qt_ref, kt_s, near_s, prod_s,
                   u_ref, inv_ref, psi_ref, x1_ref, y1_ref, send_head)

    for copy in get_gu:
        copy.wait_recv()
    pass_gu = []
    for dst in (wg_s, wu_s):
        for i in range(1, seq_n):
            there = dst.at[mine_c, pl.ds(ff, (hid_n - 1) * ff)]
            pass_gu.append(copies.start(there, there, {"seq": place.seq_peer(i)}))
    get_d = [copies.start(wd_ref.at[mine_f, :], wd_s.at[slot_f(j), :], {"hid": place.hid_peer(j)})
             for j in range(1, hid_n)]

    for copy in get_v:
        copy.wait_recv()
    attn_fwd_stage(heads, hops, place.row, len_ref, qt_ref, near_s, v_ref, fv_ref, fp_ref, chain_ref,
                   o_ref, probs_ref, s_s, get_k, get_p)

    load_o.wait()
    get_a = []
    for slot, i in enumerate(order):
        peer = place.wid_peer(i)
        rows = aligned(peer * sub, sub, sub)
        part_s[rows, :] = dot(o_ref[rows, :], wo_s[...], 1, 0).astype(BF)
        get_a.append(copies.start(part_s.at[rows, :], recv_s.at[slot], {"wid": peer}))
    part_s[my_rows, :] = dot(o_ref[my_rows, :], wo_s[...], 1, 0).astype(BF)
    mixed = xall_ref[my_rows, :].astype(F32) + part_s[my_rows, :].astype(F32)
    for copy in get_d:
        copy.wait_recv()
    pass_d = []
    for i in range(1, seq_n):
        for j in range(1, hid_n):
            there = wd_s.at[slot_f(j), :]
            pass_d.append(copies.start(there, there, {"seq": place.seq_peer(i)}))
    for slot, copy in enumerate(get_a):
        copy.wait_recv()
        mixed = mixed + recv_s[slot].astype(F32)
    mixed_ref[...] = mixed
    inv_two = lax.rsqrt(jnp.mean(mixed * mixed, -1, keepdims=True) + eps_norm)
    row_s[...] = (mixed * inv_two * gall_ref[1:2, :]).astype(BF)
    get_i = [copies.start(row_s, inner_ref.at[my_rows, :], d) for d in to_wid]
    inner_ref[my_rows, :] = row_s[...]
    load_dy.wait()
    for copy in load_f:
        copy.wait()
    for copy in get_dy + pass_gu + pass_d + get_i:
        copy.wait_recv()

    def hidden_tile(t, carry):
        cs = aligned(t * ff, ff, 128)
        gate = dot(inner_ref[...], wg_s[:, cs], 1, 0)
        up = dot(inner_ref[...], wu_s[:, cs], 1, 0)
        g_hidden = dot(dyall_ref[...], wd_s[cs, :], 1, 1)
        sig = 1.0 / (1.0 + jnp.exp(-gate))
        silu = gate * sig
        hidden_ref[:, cs] = (silu * up).astype(BF)
        ggate_ref[:, cs] = (g_hidden * up * sig * (1.0 + gate * (1.0 - sig))).astype(BF)
        gup_ref[:, cs] = (g_hidden * silu).astype(BF)
        return carry

    lax.fori_loop(0, hid_n, hidden_tile, 0)

    def model_tile(t, carry):
        cs = aligned(t * col, col, 128)
        gin_ref[:, cs] = (dot(ggate_ref[...], wg_s[cs, :], 1, 1) + dot(gup_ref[...], wu_s[cs, :], 1, 1)).astype(BF)
        fsum_ref[:, cs] = (dot(hidden_ref[...], wd_s[:, cs], 1, 0) + part_s[:, cs].astype(F32)).astype(BF)
        return carry

    lax.fori_loop(0, wid_n, model_tile, 0)
    every = get_x + get_gu + get_dy + get_v + pass_gu + get_d + get_a + pass_d + get_i
    for h in range(heads):
        every += get_k[h] + get_p[h]
    for copy in every:
        copy.wait_send()


def forward(args, heads, hops, sizes):
    lengths, x, dy, gains, wq, wk, wv, wr, wb, wo, wg, wu, wd = args
    n, col = x.shape
    seq_n, hid_n, wid_n = sizes
    model, ff = wq.shape[0], wg.shape[1]
    width = wq.shape[1]
    sub = n // wid_n
    slots = hops * (hops + 1) // 2
    S = jax.ShapeDtypeStruct
    outs = dict(
        act=S((n, model), BF), xall=S((n, model), BF), gall=S((8, model), F32), dyall=S((n, model), BF),
        q=S((n, width), F32), k=S((n, width), F32), r=S((n, width), F32), c=S((n, heads), F32), v=S((n, width), BF),
        qt=S((n, width), BF), u=S((n, width), F32), inv=S((heads, n, n), F32), psi=S((heads, n, n), F32),
        x1=S((n, width), F32), y1=S((n, width), F32),
        fv=S((hops, n, width), BF), fp=S((hops - 1, heads, HDIM, HDIM), F32), chain=S((slots, n, width), BF),
        probs=S((hops + 1, heads, n, n), BF), o=S((n, width), BF), mixed=S((sub, model), F32),
        inner=S((n, model), BF), hidden=S((n, hid_n * ff), BF), ggate=S((n, hid_n * ff), BF),
        gup=S((n, hid_n * ff), BF), gin=S((n, model), BF), fsum=S((n, model), BF),
    )
    V = pltpu.VMEM
    n_copies = (3 * 3 * (wid_n - 1) + 3 * (hid_n - 1) + (seq_n - 1) * (2 + hid_n - 1)
                + hops + heads * (2 * hops - 1)) + 8
    any_spec = pl.BlockSpec(memory_space=pl.ANY)
    vmem = pl.BlockSpec(memory_space=pltpu.VMEM)
    smem = pl.BlockSpec(memory_space=pltpu.SMEM)
    res = pl.pallas_call(
        functools.partial(fwd_kernel, (heads, hops, sizes)),
        in_specs=[smem, any_spec, any_spec, any_spec] + [any_spec] * 4 + [vmem] + [any_spec] * 4,
        out_shape=tuple(outs.values()),
        out_specs=tuple(vmem for _ in outs),
        scratch_shapes=[
            V((model, width), BF), V((model, width), BF), V((model, width), BF), V((model, width), BF),
            V((width, model), BF),
            V((model, hid_n * ff), BF), V((model, hid_n * ff), BF), V((hid_n * ff, model), BF),
            V((n, width), BF), V((heads, n, n), F32), V((heads, HDIM, HDIM), F32), V((hops + 1, n, n), F32),
            V((n, model), BF), V((wid_n - 1, sub, model), BF), V((sub, model), BF),
            pltpu.SemaphoreType.DMA((11,)), pltpu.SemaphoreType.DMA((n_copies,)),
            pltpu.SemaphoreType.DMA((n_copies,)),
        ],
        compiler_params=pltpu.CompilerParams(
            vmem_limit_bytes=VMEM_LIMIT, collective_id=1, has_side_effects=True),
        name="forward",
    )(lengths, x, dy, gains, wq, wk, wv, wr, wb, wo, wg, wu, wd)
    return dict(zip(outs, res))


def shifted(array, axis, by):
    peers = lax.axis_size(axis)
    pairs = [(i, i + by) for i in range(peers) if 0 <= i + by < peers]
    return lax.ppermute(array, axis, pairs)


def norm_rows(hidden_f):
    inverse = lax.rsqrt(jnp.mean(hidden_f * hidden_f, -1, keepdims=True) + eps_norm)
    return (hidden_f * inverse, inverse)


def norm_back(grad_out, normed, inverse, gain_vec):
    scaled_grad = grad_out * gain_vec
    grad_gain = jnp.sum(grad_out * normed, 0)
    grad_in = inverse * (scaled_grad - normed * jnp.mean(scaled_grad * normed, -1, keepdims=True))
    return (grad_in, grad_gain)


ROWS = ("seq", "hid")


def body(inputs, gain_attn, gain_ffn, w_query, w_key, w_value, w_house, w_beta, w_out,
         w_gate, w_up, w_down, lengths, cotangent):
    tok, col = inputs.shape
    row_devs = lax.axis_size(ROWS)
    my_row = lax.axis_index(ROWS)
    my_wid = lax.axis_index("wid")
    wid_n = lax.axis_size("wid")
    tokens_all = tok * row_devs
    most_len = max(LEAST, 2 * tokens_all // 5)
    hops = min((most_len - 2) // tok + 1, row_devs - 1)
    heads = w_query.shape[1] // HDIM
    ff = w_gate.shape[1]
    sub = tok // wid_n

    x_all = lax.all_gather(inputs, "wid", axis=1, tiled=True)
    gain_one = lax.all_gather(gain_attn, "wid", axis=0, tiled=True).astype(F32)
    gain_two = lax.all_gather(gain_ffn, "wid", axis=0, tiled=True).astype(F32)
    dy_all = lax.all_gather(cotangent, "wid", axis=1, tiled=True)
    w_gu = lax.all_gather(jnp.concatenate([w_gate, w_up], 1), "hid", axis=0)
    w_dn = lax.all_gather(w_down, "hid", axis=0)
    model = x_all.shape[1]

    residual = x_all.astype(F32)
    normed_one, inverse_one = norm_rows(residual)
    act = (normed_one * gain_one).astype(BF)

    def project(weight):
        return jnp.dot(act, weight, preferred_element_type=F32)

    q, k, r, c = project(w_query), project(w_key), project(w_house), project(w_beta)
    v = project(w_value).astype(BF)
    far_v = jnp.stack([shifted(v, ROWS, i) for i in range(1, hops + 1)])
    qt, kt, near, prod, *saved = path_fwd(q, k, r, c, heads)
    far_k = jnp.stack([shifted(kt, ROWS, i) for i in range(1, hops + 1)])
    far_p = jnp.stack([shifted(prod, ROWS, i) for i in range(1, hops)])
    row_arr = jnp.full((1,), my_row, jnp.int32)
    attended, probs, chain = attn_fwd(lengths, row_arr, qt, near, v, far_k, far_v, far_p, heads, hops)

    attn_part = jnp.dot(attended, w_out, preferred_element_type=F32).astype(BF)
    attn_rows = lax.psum_scatter(attn_part, "wid", scatter_dimension=0, tiled=True)
    x_rows = lax.dynamic_slice_in_dim(x_all, my_wid * sub, sub, 0).astype(F32)
    dy_rows = lax.dynamic_slice_in_dim(dy_all, my_wid * sub, sub, 0).astype(F32)
    mixed = x_rows + attn_rows.astype(F32)
    normed_two, inverse_two = norm_rows(mixed)
    inner = lax.all_gather((normed_two * gain_two).astype(BF), "wid", axis=0, tiled=True)

    pre = jnp.einsum("tc,hcf->htf", inner, w_gu, preferred_element_type=F32)
    gate, up = pre[:, :, :ff], pre[:, :, ff:]
    sig = jax.nn.sigmoid(gate)
    hidden = (gate * sig * up).astype(BF)
    ffn_part = jnp.einsum("htf,hfc->tc", hidden, w_dn, preferred_element_type=F32)
    ffn_part = (ffn_part + attn_part.astype(F32)).astype(BF)
    ffn_cols = lax.psum_scatter(ffn_part, "wid", scatter_dimension=1, tiled=True)
    output = (inputs.astype(F32) + ffn_cols.astype(F32)).astype(BF)

    g_hidden = jnp.einsum("tc,hfc->htf", dy_all, w_dn, preferred_element_type=F32)
    g_gate = g_hidden * up * sig * (1.0 + gate * (1.0 - sig))
    g_up = g_hidden * gate * sig
    g_pre = jnp.concatenate([g_gate, g_up], 2).astype(BF)
    g_inner = jnp.einsum("htf,hcf->tc", g_pre, w_gu, preferred_element_type=F32).astype(BF)
    g_inner = lax.psum_scatter(g_inner, "wid", scatter_dimension=0, tiled=True).astype(F32)
    g_mixed_n, g_gain_two = norm_back(g_inner, normed_two, inverse_two, gain_two)
    g_z = lax.all_gather((dy_rows + g_mixed_n).astype(BF), "wid", axis=0, tiled=True)

    d_gu = jnp.einsum("tc,htf->hcf", inner, g_pre, preferred_element_type=F32).astype(BF)
    d_dn = jnp.einsum("htf,tc->hfc", hidden, dy_all, preferred_element_type=F32).astype(BF)
    d_gu = lax.psum_scatter(d_gu, "seq", scatter_dimension=1, tiled=True)
    d_gu = lax.psum_scatter(d_gu, "hid", scatter_dimension=0)
    d_dn = lax.psum_scatter(d_dn, "seq", scatter_dimension=2, tiled=True)
    d_dn = lax.psum_scatter(d_dn, "hid", scatter_dimension=0)

    g_attn = jnp.einsum("tc,ic->ti", g_z, w_out, preferred_element_type=F32).astype(BF)
    d_out = jnp.einsum("ti,tc->ic", attended, g_z, preferred_element_type=F32).astype(BF)
    g_qt, g_near, gv, send_k, send_v, send_p = attn_bwd(probs, g_attn, qt, v, far_v, far_p, chain, heads, hops)
    g_kt = sum(shifted(send_k[i - 1], ROWS, -i).astype(F32) for i in range(1, hops + 1))
    gv = gv + sum(shifted(send_v[i - 1], ROWS, -i).astype(F32) for i in range(1, hops + 1))
    g_prod = sum(shifted(send_p[i - 1], ROWS, -i).astype(F32) for i in range(1, hops))
    g_q, g_k, g_r, g_c = path_bwd(q, k, r, c, saved, g_qt, g_kt, g_near, g_prod, heads)
    g_v = gv.astype(BF)

    def weight_grad(grad_low):
        return jnp.einsum("tc,ti->ci", act, grad_low, preferred_element_type=F32).astype(BF)

    def input_grad(grad_low, weight):
        return jnp.einsum("ti,ci->tc", grad_low, weight, preferred_element_type=F32)

    g_act = (input_grad(g_q, w_query) + input_grad(g_k, w_key) + input_grad(g_v, w_value)
             + input_grad(g_r, w_house) + input_grad(g_c, w_beta))
    g_act = lax.psum_scatter(g_act.astype(BF), "wid", scatter_dimension=0, tiled=True).astype(F32)
    normed_rows = lax.dynamic_slice_in_dim(normed_one, my_wid * sub, sub, 0)
    inverse_rows = lax.dynamic_slice_in_dim(inverse_one, my_wid * sub, sub, 0)
    g_resid, g_gain_one = norm_back(g_act, normed_rows, inverse_rows, gain_one)
    d_rows = dy_rows + g_mixed_n + g_resid
    d_inputs = lax.all_to_all(d_rows, "wid", split_axis=1, concat_axis=0, tiled=True)

    def scatter(x, dim):
        return lax.psum_scatter(x, ROWS, scatter_dimension=dim, tiled=True)

    gains = lax.psum(jnp.stack([g_gain_one, g_gain_two]), "wid")
    gains = scatter(gains, 1)
    return (
        output,
        d_inputs,
        gains[0],
        gains[1],
        scatter(weight_grad(g_q), 0).astype(F32),
        scatter(weight_grad(g_k), 0).astype(F32),
        scatter(weight_grad(g_v), 0).astype(F32),
        scatter(weight_grad(g_r), 0).astype(F32),
        scatter(weight_grad(g_c), 0).astype(F32),
        scatter(d_out, 1).astype(F32),
        d_gu[:, :ff].astype(F32),
        d_gu[:, ff:].astype(F32),
        d_dn.astype(F32),
    )


def fast_body(inputs, gain_attn, gain_ffn, w_query, w_key, w_value, w_house, w_beta, w_out,
              w_gate, w_up, w_down, lengths, cotangent):
    tok, col = inputs.shape
    row_devs = lax.axis_size(ROWS)
    my_wid = lax.axis_index("wid")
    my_hid = lax.axis_index("hid")
    wid_n, hid_n, seq_n = lax.axis_size("wid"), lax.axis_size("hid"), lax.axis_size("seq")
    most_len = max(LEAST, 2 * tok * row_devs // 5)
    hops = min((most_len - 2) // tok + 1, row_devs - 1)
    heads = w_query.shape[1] // HDIM
    ff = w_gate.shape[1]
    sub = tok // wid_n
    gains = jnp.zeros((8, col), F32).at[0].set(gain_attn.astype(F32)).at[1].set(gain_ffn.astype(F32))
    f = forward((lengths, inputs, cotangent, gains, w_query, w_key, w_value, w_house, w_beta, w_out,
                 w_gate, w_up, w_down), heads, hops, (seq_n, hid_n, wid_n))
    gain_one, gain_two = f["gall"][0], f["gall"][1]
    normed_one, inverse_one = norm_rows(f["xall"].astype(F32))
    act, v, qt, fv, fp, chain, probs, attended = (f[i] for i in ("act", "v", "qt", "fv", "fp", "chain", "probs", "o"))
    q, k, r, c = f["q"], f["k"], f["r"], f["c"]
    saved = [f[i] for i in ("u", "inv", "psi", "x1", "y1")]
    dy_all, inner, hidden = f["dyall"], f["inner"], f["hidden"]
    dy_rows = lax.dynamic_slice_in_dim(dy_all, my_wid * sub, sub, 0).astype(F32)
    normed_two, inverse_two = norm_rows(f["mixed"])

    ffn_cols = lax.psum_scatter(f["fsum"], "wid", scatter_dimension=1, tiled=True)
    output = (inputs.astype(F32) + ffn_cols.astype(F32)).astype(BF)
    g_inner = lax.psum_scatter(f["gin"], "wid", scatter_dimension=0, tiled=True).astype(F32)
    g_mixed_n, g_gain_two = norm_back(g_inner, normed_two, inverse_two, gain_two)
    g_z = lax.all_gather((dy_rows + g_mixed_n).astype(BF), "wid", axis=0, tiled=True)

    pick = lax.rem(my_hid - jnp.arange(hid_n) + hid_n, hid_n)

    def slots(x, dim):
        shape = x.shape[:dim] + (hid_n, ff) + x.shape[dim + 1:]
        return jnp.moveaxis(jnp.take(x.reshape(shape), pick, axis=dim), dim, 0)

    def cgrad(g):
        return slots(jnp.einsum("tc,tf->cf", inner, g, preferred_element_type=F32).astype(BF), 1)

    d_gu = jnp.concatenate([cgrad(f["ggate"]), cgrad(f["gup"])], 2)
    d_dn = slots(jnp.einsum("tf,tc->fc", hidden, dy_all, preferred_element_type=F32).astype(BF), 0)
    d_gu = lax.psum_scatter(d_gu, "seq", scatter_dimension=1, tiled=True)
    d_gu = lax.psum_scatter(d_gu, "hid", scatter_dimension=0)
    d_dn = lax.psum_scatter(d_dn, "seq", scatter_dimension=2, tiled=True)
    d_dn = lax.psum_scatter(d_dn, "hid", scatter_dimension=0)

    g_attn = jnp.einsum("tc,ic->ti", g_z, w_out, preferred_element_type=F32).astype(BF)
    d_out = jnp.einsum("ti,tc->ic", attended, g_z, preferred_element_type=F32).astype(BF)
    g_qt, g_near, gv, send_k, send_v, send_p = attn_bwd(probs, g_attn, qt, v, fv, fp, chain, heads, hops)
    g_kt = sum(shifted(send_k[i - 1], ROWS, -i).astype(F32) for i in range(1, hops + 1))
    gv = gv + sum(shifted(send_v[i - 1], ROWS, -i).astype(F32) for i in range(1, hops + 1))
    g_prod = sum(shifted(send_p[i - 1], ROWS, -i).astype(F32) for i in range(1, hops))
    g_q, g_k, g_r, g_c = path_bwd(q, k, r, c, saved, g_qt, g_kt, g_near, g_prod, heads)
    g_v = gv.astype(BF)

    def weight_grad(grad_low):
        return jnp.einsum("tc,ti->ci", act, grad_low, preferred_element_type=F32).astype(BF)

    def input_grad(grad_low, weight):
        return jnp.einsum("ti,ci->tc", grad_low, weight, preferred_element_type=F32)

    g_act = (input_grad(g_q, w_query) + input_grad(g_k, w_key) + input_grad(g_v, w_value)
             + input_grad(g_r, w_house) + input_grad(g_c, w_beta))
    g_act = lax.psum_scatter(g_act.astype(BF), "wid", scatter_dimension=0, tiled=True).astype(F32)
    normed_rows = lax.dynamic_slice_in_dim(normed_one, my_wid * sub, sub, 0)
    inverse_rows = lax.dynamic_slice_in_dim(inverse_one, my_wid * sub, sub, 0)
    g_resid, g_gain_one = norm_back(g_act, normed_rows, inverse_rows, gain_one)
    d_rows = dy_rows + g_mixed_n + g_resid
    d_inputs = lax.all_to_all(d_rows, "wid", split_axis=1, concat_axis=0, tiled=True)

    def scatter(x, dim):
        return lax.psum_scatter(x, ROWS, scatter_dimension=dim, tiled=True)

    gains = lax.psum(jnp.stack([g_gain_one, g_gain_two]), "wid")
    gains = scatter(gains, 1)
    return (
        output,
        d_inputs,
        gains[0],
        gains[1],
        scatter(weight_grad(g_q), 0).astype(F32),
        scatter(weight_grad(g_k), 0).astype(F32),
        scatter(weight_grad(g_v), 0).astype(F32),
        scatter(weight_grad(g_r), 0).astype(F32),
        scatter(weight_grad(g_c), 0).astype(F32),
        scatter(d_out, 1).astype(F32),
        d_gu[:, :ff].astype(F32),
        d_gu[:, ff:].astype(F32),
        d_dn.astype(F32),
    )


def slow(mesh):
    return mesh.shape["seq"] * mesh.shape["hid"] > 8


def solution(mesh):
    in_specs = (
        P(("seq", "hid"), "wid"), P("wid"), P("wid"),
        P(None, "wid"), P(None, "wid"), P(None, "wid"), P(None, "wid"), P(None, "wid"),
        P("wid", None), P(None, ("hid", "wid")), P(None, ("hid", "wid")), P(("hid", "wid"), None),
        P(), P(("seq", "hid"), "wid"),
    )
    out_specs = (
        P(("seq", "hid"), "wid"), P(("seq", "hid"), "wid"), P(("seq", "hid")), P(("seq", "hid")),
        P(("seq", "hid"), "wid"), P(("seq", "hid"), "wid"), P(("seq", "hid"), "wid"),
        P(("seq", "hid"), "wid"), P(("seq", "hid"), "wid"), P("wid", ("seq", "hid")),
        P("seq", ("hid", "wid")), P("seq", ("hid", "wid")), P(("hid", "wid"), "seq"),
    )
    return jax.shard_map(body if slow(mesh) else fast_body, mesh=mesh, in_specs=in_specs, out_specs=out_specs, check_vma=False)
```

```python
import functools
import types

import jax
import jax.numpy as jnp
from jax import lax
from jax.experimental import pallas as pl
from jax.experimental.pallas import tpu as pltpu
from jax.sharding import PartitionSpec as P

HDIM = 128
LEAST = 1024

eps_norm = 1e-06
neg_big = -1e30
BF = jnp.bfloat16
F32 = jnp.float32
VMEM_LIMIT = 60 * 1024 * 1024
VMEM_ALL = 67043328


def dot(a, b, ca, cb):
    return lax.dot_general(a, b, (((ca,), (cb,)), ((), ())), preferred_element_type=F32)


def split(a):
    hi = a.astype(BF)
    return hi, (a - hi.astype(F32)).astype(BF)


def dot3(a, b, ca, cb):
    return dot(a[0], b[0], ca, cb) + (dot(a[0], b[1], ca, cb) + dot(a[1], b[0], ca, cb))


def dot1(a, b, ca, cb):
    return dot(a.astype(BF), b.astype(BF), ca, cb)


def iotas(n):
    rows = lax.broadcasted_iota(jnp.int32, (n, n), 0)
    cols = lax.broadcasted_iota(jnp.int32, (n, n), 1)
    return rows, cols


def head_cols(h):
    return slice(h * HDIM, (h + 1) * HDIM)


def house_terms(raw, strength, heads, h):
    inv = lax.rsqrt(jnp.sum(raw * raw, -1, keepdims=True) + eps_norm)
    lane = lax.broadcasted_iota(jnp.int32, strength.shape, 1)
    c = jnp.sum(jnp.where(lane == h, strength, 0.0), 1, keepdims=True)
    root = jnp.sqrt(2.0 / (1.0 + jnp.exp(-c)))
    return inv, root


def path_fwd_stage(heads, q_ref, k_ref, r_ref, c_ref, qt_ref, kt_ref, near_ref, p_ref,
                   u_ref, inv_ref, psi_ref, x_ref, y_ref, done=None):
    n = q_ref.shape[0]
    rows, cols = iotas(n)
    strength = c_ref[...]
    us, us2, lows, invs = [], [], [], []
    for h in range(heads):
        raw = r_ref[:, head_cols(h)]
        inv, root = house_terms(raw, strength, heads, h)
        u = raw * (inv * root)
        u_ref[:, head_cols(h)] = u
        u2 = split(u)
        low = jnp.where(rows > cols, dot3(u2, u2, 1, 1), 0.0)
        us.append(u)
        us2.append(u2)
        lows.append(low)
        first = jnp.where(rows == cols, 1.0, 0.0) - jnp.where(rows // 2 == cols // 2, low, 0.0)
        invs.append(first)
    span = 2
    while span < n:
        pick = (rows // (2 * span) == cols // (2 * span)) & (rows // span != cols // span)
        halves = [split(m) for m in invs]
        mids = [dot3(split(jnp.where(pick, lows[h], 0.0)), halves[h], 1, 0) for h in range(heads)]
        invs = [invs[h] - dot3(halves[h], split(mids[h]), 1, 0) for h in range(heads)]
        span = span * 2
    for h in range(heads):
        inv_ref[h] = invs[h]
        kin = split(invs[h])
        q = q_ref[:, head_cols(h)]
        k = k_ref[:, head_cols(h)]
        q2, k2, u2 = split(q), split(k), us2[h]
        a = jnp.where(rows > cols, dot3(u2, k2, 1, 1), 0.0)
        aq = jnp.where(rows < cols, dot3(k2, u2, 1, 1), 0.0)
        fq = jnp.where(rows >= cols, dot3(q2, u2, 1, 1), 0.0)
        fq2 = split(fq)
        x = dot3(kin, u2, 1, 0)
        y = dot3(kin, u2, 0, 0)
        psi = dot3(kin, split(a), 1, 0)
        x2 = split(x)
        x_ref[:, head_cols(h)] = x
        y_ref[:, head_cols(h)] = y
        psi_ref[h] = psi
        qt_ref[:, head_cols(h)] = (q - dot3(fq2, x2, 1, 0)).astype(BF)
        kt_ref[:, head_cols(h)] = (k - dot3(split(aq), split(y), 1, 0)).astype(BF)
        near_ref[h] = dot3(q2, k2, 1, 1) - dot3(fq2, split(psi), 1, 0)
        er, ec = iotas(HDIM)
        p_ref[h] = jnp.where(er == ec, 1.0, 0.0) - dot3(u2, x2, 0, 0)
        if done is not None:
            done(h)


def path_fwd_kernel(heads, *refs):
    path_fwd_stage(heads, *refs)


def path_fwd(q, k, r, c, heads):
    n, width = q.shape
    flat = jax.ShapeDtypeStruct((n, width), F32)
    low = jax.ShapeDtypeStruct((n, width), BF)
    square = jax.ShapeDtypeStruct((heads, n, n), F32)
    return pl.pallas_call(
        functools.partial(path_fwd_kernel, heads),
        out_shape=(low, low, square, jax.ShapeDtypeStruct((heads, HDIM, HDIM), F32),
                   flat, square, square, flat, flat),
        compiler_params=pltpu.CompilerParams(vmem_limit_bytes=VMEM_LIMIT),
        name="path_fwd",
    )(q, k, r, c)


def doc_of(pos, len_ref):
    total = len_ref[0]
    doc = (pos >= total).astype(jnp.int32)
    for i in range(1, len_ref.shape[0]):
        total = total + len_ref[i]
        doc = doc + (pos >= total).astype(jnp.int32)
    return doc


def chain_slot(r, m):
    return r * (r - 1) // 2 + m


def attn_fwd_stage(heads, hops, row, len_ref, qt_ref, near_ref, v_ref, fv_ref, fp_ref, chain_ref,
                   o_ref, p_ref, s_ref, get_k, get_p):
    n = qt_ref.shape[0]
    scale = HDIM ** (-0.5)
    rows, cols = iotas(n)
    own = doc_of(row * n + rows, len_ref)
    near_ok = (rows >= cols) & (own == doc_of(row * n + cols, len_ref))
    for h in range(heads):
        cs = head_cols(h)
        q = qt_ref[:, cs]
        for copy in get_k[h] + get_p[h]:
            copy.wait_recv()
        s = jnp.where(near_ok, near_ref[h] * scale, neg_big)
        s_ref[0:n, :] = s
        top = jnp.max(s, 1, keepdims=True)
        for r in range(1, hops + 1):
            keys = chain_ref[chain_slot(r, 0), :, cs]
            for m in range(1, r):
                ph, plo = split(fp_ref[r - m - 1, h])
                keys = (dot(keys, ph, 1, 1) + dot(keys, plo, 1, 1)).astype(BF)
                chain_ref[chain_slot(r, m), :, cs] = keys
            source = row - r
            docs = jnp.where(source >= 0, doc_of(source * n + cols, len_ref), -1)
            s = jnp.where(own == docs, dot(q, keys, 1, 1) * scale, neg_big)
            s_ref[r * n:(r + 1) * n, :] = s
            top = jnp.maximum(top, jnp.max(s, 1, keepdims=True))
        total = jnp.zeros((n, 1), F32)
        for r in range(hops + 1):
            e = jnp.exp(s_ref[r * n:(r + 1) * n, :] - top)
            s_ref[r * n:(r + 1) * n, :] = e
            total = total + jnp.sum(e, 1, keepdims=True)
        recip = 1.0 / total
        out = jnp.zeros((n, HDIM), F32)
        for r in range(hops + 1):
            p = (s_ref[r * n:(r + 1) * n, :] * recip).astype(BF)
            p_ref[r, h] = p
            vals = v_ref[:, cs] if r == 0 else fv_ref[r - 1, :, cs]
            out = out + dot(p, vals, 1, 0)
        o_ref[:, cs] = out.astype(BF)

def attn_fwd_kernel(heads, hops, len_ref, row_ref, qt_ref, near_ref, v_ref, fk_ref, fv_ref, fp_ref,
                    o_ref, p_ref, chain_ref, s_ref):
    for r in range(1, hops + 1):
        chain_ref[chain_slot(r, 0)] = fk_ref[r - 1]
    none = [[] for _ in range(heads)]
    attn_fwd_stage(heads, hops, row_ref[0], len_ref, qt_ref, near_ref, v_ref, fv_ref, fp_ref, chain_ref,
                   o_ref, p_ref, s_ref, none, none)


def attn_fwd(lengths, my_row, qt, near, v, far_k, far_v, far_p, heads, hops):
    n, width = qt.shape
    slots = hops * (hops + 1) // 2
    smem = pl.BlockSpec(memory_space=pltpu.SMEM)
    vmem = pl.BlockSpec(memory_space=pltpu.VMEM)
    return pl.pallas_call(
        functools.partial(attn_fwd_kernel, heads, hops),
        in_specs=[smem, smem] + [vmem] * 6,
        out_shape=(
            jax.ShapeDtypeStruct((n, width), BF),
            jax.ShapeDtypeStruct((hops + 1, heads, n, n), BF),
            jax.ShapeDtypeStruct((slots, n, width), BF),
        ),
        scratch_shapes=[pltpu.VMEM(((hops + 1) * n, n), F32)],
        compiler_params=pltpu.CompilerParams(vmem_limit_bytes=VMEM_LIMIT),
        name="attn_fwd",
    )(lengths, my_row, qt, near, v, far_k, far_v, far_p)


def attn_bwd_kernel(heads, hops, p_ref, go_ref, qt_ref, v_ref, fv_ref, fp_ref, chain_ref,
                    gqt_ref, gnear_ref, gv_ref, sendk_ref, sendv_ref, sendp_ref, dp_ref):
    n = qt_ref.shape[0]
    scale = HDIM ** (-0.5)
    for h in range(heads):
        cs = head_cols(h)
        go = go_ref[:, cs]
        q = qt_ref[:, cs]
        delta = jnp.zeros((n, 1), F32)
        for r in range(hops + 1):
            vals = v_ref[:, cs] if r == 0 else fv_ref[r - 1, :, cs]
            dp = dot(go, vals, 1, 1)
            dp_ref[r] = dp
            delta = delta + jnp.sum(p_ref[r, h].astype(F32) * dp, 1, keepdims=True)
            gv = dot(p_ref[r, h], go, 0, 0)
            if r == 0:
                gv_ref[:, cs] = gv
            else:
                sendv_ref[r - 1, :, cs] = gv.astype(BF)
        gnear_ref[h] = p_ref[0, h].astype(F32) * (dp_ref[0] - delta) * scale
        gq = jnp.zeros((n, HDIM), F32)
        gps = [jnp.zeros((HDIM, HDIM), F32) for _ in range(hops - 1)]
        for r in range(1, hops + 1):
            gs = (p_ref[r, h].astype(F32) * (dp_ref[r] - delta) * scale).astype(BF)
            gq = gq + dot(gs, chain_ref[chain_slot(r, r - 1), :, cs], 1, 0)
            gk = dot(gs, q, 0, 0)
            for m in range(r - 1, 0, -1):
                back = r - m - 1
                gkb = gk.astype(BF)
                gps[back] = gps[back] + dot(gkb, chain_ref[chain_slot(r, m - 1), :, cs], 0, 0)
                gk = dot(gkb, fp_ref[back, h].astype(BF), 1, 0)
            sendk_ref[r - 1, :, cs] = gk.astype(BF)
        gqt_ref[:, cs] = gq
        for i in range(hops - 1):
            sendp_ref[i, h] = gps[i].astype(BF)


def attn_bwd(p, go, qt, v, far_v, far_p, chain, heads, hops):
    n, width = qt.shape
    return pl.pallas_call(
        functools.partial(attn_bwd_kernel, heads, hops),
        out_shape=(
            jax.ShapeDtypeStruct((n, width), F32),
            jax.ShapeDtypeStruct((heads, n, n), F32),
            jax.ShapeDtypeStruct((n, width), F32),
            jax.ShapeDtypeStruct((hops, n, width), BF),
            jax.ShapeDtypeStruct((hops, n, width), BF),
            jax.ShapeDtypeStruct((hops - 1, heads, HDIM, HDIM), BF),
        ),
        scratch_shapes=[pltpu.VMEM((hops + 1, n, n), F32)],
        compiler_params=pltpu.CompilerParams(vmem_limit_bytes=VMEM_LIMIT),
        name="attn_bwd",
    )(p, go, qt, v, far_v, far_p, chain)


def path_bwd_kernel(heads, q_ref, k_ref, r_ref, c_ref, u_ref, inv_ref, psi_ref, x_ref, y_ref,
                    gqt_ref, gkt_ref, gnear_ref, gp_ref, gq_ref, gk_ref, gr_ref, gc_ref):
    n = q_ref.shape[0]
    rows, cols = iotas(n)
    strength = c_ref[...]
    lane = lax.broadcasted_iota(jnp.int32, strength.shape, 1)
    gc_all = jnp.zeros(strength.shape, F32)
    for h in range(heads):
        cs = head_cols(h)
        q, k, u = q_ref[:, cs], k_ref[:, cs], u_ref[:, cs]
        qb, kb, ub = q.astype(BF), k.astype(BF), u.astype(BF)
        kin = inv_ref[h].astype(BF)
        psi = psi_ref[h].astype(BF)
        x, y = x_ref[:, cs].astype(BF), y_ref[:, cs].astype(BF)
        gqt, gkt = gqt_ref[:, cs], gkt_ref[:, cs]
        gqtb, gktb = gqt.astype(BF), gkt.astype(BF)
        gs = gnear_ref[h]
        gsb = gs.astype(BF)
        gst = gs.T.astype(BF)
        gp = gp_ref[h].astype(BF)
        f = jnp.where(rows <= cols, dot(ub, qb, 1, 1), 0.0).astype(BF)
        fq = jnp.where(rows >= cols, dot(qb, ub, 1, 1), 0.0).astype(BF)
        a = jnp.where(rows > cols, dot(ub, kb, 1, 1), 0.0).astype(BF)
        gx = -(dot(f, gqtb, 1, 0) + dot(ub, gp, 1, 0))
        gy = -dot(a, gktb, 1, 0)
        phiq = dot(fq, kin, 1, 0).astype(BF)
        back = dot(gst, phiq, 1, 0)
        backb = back.astype(BF)
        gfq = jnp.where(rows >= cols, -(dot(gqtb, x, 1, 1) + dot(gsb, psi, 1, 1)), 0.0)
        gaq = jnp.where(rows < cols, -(dot(gktb, y, 1, 1) + back), 0.0)
        kgx = dot(kin, gx.astype(BF), 0, 0)
        kgy = dot(kin, gy.astype(BF), 1, 0)
        zt = dot(x, kgx.astype(BF), 1, 1) + dot(kgy.astype(BF), y, 1, 1) - dot(psi, backb, 1, 0)
        glt = jnp.where(rows < cols, -zt, 0.0)
        sym = (glt + glt.T).astype(BF)
        gfqb, gaqb = gfq.astype(BF), gaq.astype(BF)
        gu = (kgx + kgy - dot(x, gp, 1, 1) + dot(gfq.T.astype(BF), qb, 1, 0)
              + dot(gaq.T.astype(BF), kb, 1, 0) + dot(sym, ub, 1, 0))
        gq_ref[:, cs] = (gqt + dot(gsb, kb, 1, 0) + dot(gfqb, ub, 1, 0)).astype(BF)
        gk_ref[:, cs] = (gkt + dot(gst, qb, 1, 0) + dot(gaqb, ub, 1, 0)).astype(BF)
        raw = r_ref[:, cs]
        inv, root = house_terms(raw, strength, heads, h)
        gc = jnp.sum(gu * u, 1, keepdims=True) * (1.0 - 0.5 * root * root) * 0.5
        gun = gu * root
        un = raw * inv
        gr = inv * (gun - un * jnp.sum(gun * un, 1, keepdims=True))
        gr_ref[:, cs] = gr.astype(BF)
        gc_all = jnp.where(lane == h, gc, gc_all)
    gc_ref[...] = gc_all.astype(BF)


def path_bwd(q, k, r, c, saved, gqt, gkt, gnear, gp, heads):
    n, width = q.shape
    low = jax.ShapeDtypeStruct((n, width), BF)
    return pl.pallas_call(
        functools.partial(path_bwd_kernel, heads),
        out_shape=(low, low, low, jax.ShapeDtypeStruct((n, heads), BF)),
        compiler_params=pltpu.CompilerParams(vmem_limit_bytes=VMEM_LIMIT),
        name="path_bwd",
    )(q, k, r, c, *saved, gqt, gkt, gnear, gp)


MESH = pl.DeviceIdType.MESH


class Copies:
    def __init__(self, send, recv):
        self.send, self.recv, self.count, self.open = send, recv, 0, []

    def start(self, src, dst, device):
        i = self.count
        self.count = i + 1
        copy = pltpu.make_async_remote_copy(
            src_ref=src, dst_ref=dst, send_sem=self.send.at[i], recv_sem=self.recv.at[i],
            device_id=device, device_id_type=MESH)
        copy.start()
        self.open.append(copy)
        return copy

    def sent(self, some):
        for copy in some:
            copy.wait_send()
        self.open = [copy for copy in self.open if all(copy is not other for other in some)]


class Loads:
    def __init__(self, sems):
        self.sems, self.count = sems, 0

    def start(self, src, dst):
        copy = pltpu.make_async_copy(src, dst, self.sems.at[self.count])
        self.count = self.count + 1
        copy.start()
        return copy


class Place:
    def __init__(self, sizes):
        self.seq_n, self.hid_n, self.wid_n = sizes
        self.seq = lax.axis_index("seq")
        self.hid = lax.axis_index("hid")
        self.wid = lax.axis_index("wid")
        self.rows_n = self.seq_n * self.hid_n
        self.row = self.seq * self.hid_n + self.hid

    def wid_peer(self, i):
        return lax.rem(self.wid + i, self.wid_n)

    def hid_peer(self, i):
        return lax.rem(self.hid + i, self.hid_n)

    def seq_peer(self, i):
        return lax.rem(self.seq + i, self.seq_n)

    def row_peer(self, i):
        to = lax.rem(self.row + i + self.rows_n, self.rows_n)
        return {"seq": to // self.hid_n, "hid": lax.rem(to, self.hid_n)}

    def barrier(self):
        sem = pltpu.get_barrier_semaphore()
        for i in range(1, self.wid_n):
            pl.semaphore_signal(sem, inc=1, device_id={"wid": self.wid_peer(i)}, device_id_type=MESH)
        for i in range(1, self.rows_n):
            pl.semaphore_signal(sem, inc=1, device_id=self.row_peer(i), device_id_type=MESH)
        pl.semaphore_wait(sem, self.wid_n - 1 + self.rows_n - 1)


def aligned(start, size, step):
    return pl.ds(pl.multiple_of(start, step), size)


def attn_bwd_head(hops, h, p_ref, go, qt_ref, v_ref, fv_ref, fp_ref, chain_ref,
                  gqt_ref, gnear_ref, gv_ref, sendk_ref, sendv_ref, sendp_ref, dp_ref):
    n = qt_ref.shape[0]
    scale = HDIM ** (-0.5)
    cs = head_cols(h)
    q = qt_ref[:, cs]
    delta = jnp.zeros((n, 1), F32)
    for r in range(hops + 1):
        vals = v_ref[:, cs] if r == 0 else fv_ref[r - 1, :, cs]
        dp = dot(go, vals, 1, 1)
        dp_ref[r * n:(r + 1) * n, :] = dp
        delta = delta + jnp.sum(p_ref[r, h].astype(F32) * dp, 1, keepdims=True)
        gv = dot(p_ref[r, h], go, 0, 0)
        if r == 0:
            gv_ref[:, cs] = gv
        else:
            sendv_ref[r - 1, :, cs] = gv.astype(BF)
    gnear_ref[h] = p_ref[0, h].astype(F32) * (dp_ref[0:n, :] - delta) * scale
    gq = jnp.zeros((n, HDIM), F32)
    gps = [jnp.zeros((HDIM, HDIM), F32) for _ in range(hops - 1)]
    for r in range(1, hops + 1):
        gs = (p_ref[r, h].astype(F32) * (dp_ref[r * n:(r + 1) * n, :] - delta) * scale).astype(BF)
        gq = gq + dot(gs, chain_ref[chain_slot(r, r - 1), :, cs], 1, 0)
        gk = dot(gs, q, 0, 0)
        for m in range(r - 1, 0, -1):
            back = r - m - 1
            gkb = gk.astype(BF)
            gps[back] = gps[back] + dot(gkb, chain_ref[chain_slot(r, m - 1), :, cs], 0, 0)
            gk = dot(gkb, fp_ref[back, h].astype(BF), 1, 0)
        sendk_ref[r - 1, :, cs] = gk.astype(BF)
    gqt_ref[:, cs] = gq
    for i in range(hops - 1):
        sendp_ref[i, h] = gps[i].astype(BF)


def path_bwd_head(h, heads, q_ref, k_ref, r_ref, c_ref, u_ref, inv_ref, psi_ref, x_ref, y_ref,
                  gqt, gkt, gs, gp):
    n = q_ref.shape[0]
    rows, cols = iotas(n)
    cs = head_cols(h)
    q, k, u = q_ref[:, cs], k_ref[:, cs], u_ref[:, cs]
    qb, kb, ub = q.astype(BF), k.astype(BF), u.astype(BF)
    kin = inv_ref[h].astype(BF)
    psi = psi_ref[h].astype(BF)
    x, y = x_ref[:, cs].astype(BF), y_ref[:, cs].astype(BF)
    gqtb, gktb = gqt.astype(BF), gkt.astype(BF)
    gsb = gs.astype(BF)
    gst = gs.T.astype(BF)
    gp = gp.astype(BF)
    f = jnp.where(rows <= cols, dot(ub, qb, 1, 1), 0.0).astype(BF)
    fq = jnp.where(rows >= cols, dot(qb, ub, 1, 1), 0.0).astype(BF)
    a = jnp.where(rows > cols, dot(ub, kb, 1, 1), 0.0).astype(BF)
    gx = -(dot(f, gqtb, 1, 0) + dot(ub, gp, 1, 0))
    gy = -dot(a, gktb, 1, 0)
    phiq = dot(fq, kin, 1, 0).astype(BF)
    back = dot(gst, phiq, 1, 0)
    backb = back.astype(BF)
    gfq = jnp.where(rows >= cols, -(dot(gqtb, x, 1, 1) + dot(gsb, psi, 1, 1)), 0.0)
    gaq = jnp.where(rows < cols, -(dot(gktb, y, 1, 1) + back), 0.0)
    kgx = dot(kin, gx.astype(BF), 0, 0)
    kgy = dot(kin, gy.astype(BF), 1, 0)
    zt = dot(x, kgx.astype(BF), 1, 1) + dot(kgy.astype(BF), y, 1, 1) - dot(psi, backb, 1, 0)
    glt = jnp.where(rows < cols, -zt, 0.0)
    sym = (glt + glt.T).astype(BF)
    gfqb, gaqb = gfq.astype(BF), gaq.astype(BF)
    gu = (kgx + kgy - dot(x, gp, 1, 1) + dot(gfq.T.astype(BF), qb, 1, 0)
          + dot(gaq.T.astype(BF), kb, 1, 0) + dot(sym, ub, 1, 0))
    gq = (gqt + dot(gsb, kb, 1, 0) + dot(gfqb, ub, 1, 0)).astype(BF)
    gk = (gkt + dot(gst, qb, 1, 0) + dot(gaqb, ub, 1, 0)).astype(BF)
    raw = r_ref[:, cs]
    inv, root = house_terms(raw, c_ref[...], heads, h)
    gc = jnp.sum(gu * u, 1, keepdims=True) * (1.0 - 0.5 * root * root) * 0.5
    gun = gu * root
    un = raw * inv
    gr = (inv * (gun - un * jnp.sum(gun * un, 1, keepdims=True))).astype(BF)
    return gq, gk, gr, gc


def step_kernel(cfg, names, *refs):
    heads, hops, sizes = cfg
    R = types.SimpleNamespace(**dict(zip(names, refs)))
    place = Place(sizes)
    wid_n, hid_n, seq_n = place.wid_n, place.hid_n, place.seq_n
    n, col = R.x.shape
    model = R.act.shape[1]
    ff = R.wg.shape[1]
    sub = n // wid_n
    copies, loads = Copies(R.send_sem, R.recv_sem), Loads(R.load_sem)
    my_cols = aligned(place.wid * col, col, 128)
    my_rows = aligned(place.wid * sub, sub, sub)

    load_xv = loads.start(R.x, R.x_v)
    load_x = [loads.start(R.x, R.xall.at[:, my_cols]), loads.start(R.gains, R.gall.at[:, my_cols])]
    load_w = [loads.start(a, b) for a, b in ((R.wv, R.wv_s), (R.wq, R.wq_s), (R.wk, R.wk_s), (R.wr, R.wr_s))]
    load_dy = loads.start(R.dy, R.dyall.at[:, my_cols])
    load_o = loads.start(R.wo, R.wo_s)
    load_f = [loads.start(R.wg, R.wg_s.at[:, pl.ds(0, ff)]), loads.start(R.wu, R.wu_s.at[:, pl.ds(0, ff)]),
              loads.start(R.wd, R.wd_s.at[pl.ds(0, ff), :])]
    place.barrier()

    order = sorted(range(1, wid_n), key=lambda i: -min(i, wid_n - i))
    to_wid = [{"wid": place.wid_peer(i)} for i in order]
    get_x = [copies.start(R.x, R.xall.at[:, my_cols], d) for d in to_wid]
    get_x += [copies.start(R.gains, R.gall.at[:, my_cols], d) for d in to_wid]

    part_c, part_f = model // seq_n, ff // seq_n
    mine_c = aligned(place.seq * part_c, part_c, 16)
    mine_f = aligned(place.seq * part_f, part_f, 16)

    def slot_f(j):
        return aligned(j * ff + place.seq * part_f, part_f, 16)

    get_gu = []
    for src, dst in ((R.wg, R.wg_s), (R.wu, R.wu_s)):
        get_gu += [copies.start(src.at[mine_c, :], dst.at[mine_c, pl.ds(j * ff, ff)], {"hid": place.hid_peer(j)})
                   for j in range(1, hid_n)]

    load_xv.wait()
    for copy in load_x:
        copy.wait()
    for copy in get_x:
        copy.wait_recv()
    get_dy = [copies.start(R.dy, R.dyall.at[:, my_cols], d) for d in to_wid]
    xf = R.xall[...].astype(F32)
    inv_rms = lax.rsqrt(jnp.mean(xf * xf, -1, keepdims=True) + eps_norm)
    R.act[...] = (xf * inv_rms * R.gall[0:1, :]).astype(BF)
    for copy in load_w:
        copy.wait()
    act = R.act[...]
    R.v[...] = dot(act, R.wv_s[...], 1, 0).astype(BF)
    get_v = [copies.start(R.v, R.fv.at[i - 1], place.row_peer(i)) for i in range(1, hops + 1)]
    R.q[...] = dot(act, R.wq_s[...], 1, 0)
    R.k[...] = dot(act, R.wk_s[...], 1, 0)
    R.r[...] = dot(act, R.wr_s[...], 1, 0)
    R.c[...] = dot(act, R.wb[...], 1, 0)

    get_k = [[] for _ in range(heads)]
    get_p = [[] for _ in range(heads)]

    def send_head(h):
        cs = head_cols(h)
        for i in range(1, hops + 1):
            get_k[h].append(copies.start(R.kt_s.at[:, cs], R.chain.at[chain_slot(i, 0), :, cs], place.row_peer(i)))
        for i in range(1, hops):
            get_p[h].append(copies.start(R.prod_s.at[h], R.fp.at[i - 1, h], place.row_peer(i)))

    path_fwd_stage(heads, R.q, R.k, R.r, R.c, R.qt, R.kt_s, R.near_s, R.prod_s,
                   R.u, R.inv, R.psi, R.x1, R.y1, send_head)

    for copy in get_gu:
        copy.wait_recv()
    pass_gu = []
    for dst in (R.wg_s, R.wu_s):
        for i in range(1, seq_n):
            there = dst.at[mine_c, pl.ds(ff, (hid_n - 1) * ff)]
            pass_gu.append(copies.start(there, there, {"seq": place.seq_peer(i)}))
    get_d = [copies.start(R.wd.at[mine_f, :], R.wd_s.at[slot_f(j), :], {"hid": place.hid_peer(j)})
             for j in range(1, hid_n)]

    for copy in get_v:
        copy.wait_recv()
    attn_fwd_stage(heads, hops, place.row, R.lengths, R.qt, R.near_s, R.v, R.fv, R.fp, R.chain,
                   R.o, R.probs, R.s_s, get_k, get_p)

    load_o.wait()
    get_a = []
    for slot, i in enumerate(order):
        peer = place.wid_peer(i)
        rows = aligned(peer * sub, sub, sub)
        R.part_s[rows, :] = dot(R.o[rows, :], R.wo_s[...], 1, 0).astype(BF)
        get_a.append(copies.start(R.part_s.at[rows, :], R.recv_s.at[slot], {"wid": peer}))
    R.part_s[my_rows, :] = dot(R.o[my_rows, :], R.wo_s[...], 1, 0).astype(BF)
    mixed = R.xall[my_rows, :].astype(F32) + R.part_s[my_rows, :].astype(F32)
    for copy in get_d:
        copy.wait_recv()
    pass_d = []
    for i in range(1, seq_n):
        for j in range(1, hid_n):
            there = R.wd_s.at[slot_f(j), :]
            pass_d.append(copies.start(there, there, {"seq": place.seq_peer(i)}))
    for slot, copy in enumerate(get_a):
        copy.wait_recv()
        mixed = mixed + R.recv_s[slot].astype(F32)
    R.mixed[...] = mixed
    inv_two = lax.rsqrt(jnp.mean(mixed * mixed, -1, keepdims=True) + eps_norm)
    R.row_s[...] = (mixed * inv_two * R.gall[1:2, :]).astype(BF)
    get_i = [copies.start(R.row_s, R.inner.at[my_rows, :], d) for d in to_wid]
    R.inner[my_rows, :] = R.row_s[...]
    load_dy.wait()
    for copy in load_f:
        copy.wait()
    for copy in get_dy + pass_gu + pass_d + get_i:
        copy.wait_recv()

    def hidden_tile(t, carry):
        cs = aligned(t * ff, ff, 128)
        gate = dot(R.inner[...], R.wg_s[:, cs], 1, 0)
        up = dot(R.inner[...], R.wu_s[:, cs], 1, 0)
        g_hidden = dot(R.dyall[...], R.wd_s[cs, :], 1, 1)
        sig = 1.0 / (1.0 + jnp.exp(-gate))
        silu = gate * sig
        R.hidden[0:n, cs] = (silu * up).astype(BF)
        R.ggate[0:n, cs] = (g_hidden * up * sig * (1.0 + gate * (1.0 - sig))).astype(BF)
        R.gup[0:n, cs] = (g_hidden * silu).astype(BF)
        return carry

    lax.fori_loop(0, hid_n, hidden_tile, 0)

    half = model // seq_n
    mine = aligned(place.seq * half, half, 128)
    other = aligned((1 - place.seq) * half, half, 128)
    sibling = {"seq": 1 - place.seq}
    hid_peers = [{"hid": place.hid_peer(i)} for i in range(hid_n)]

    twin = [copies.start(ref.at[pl.ds(0, n), :], ref.at[pl.ds(n, n), :], sibling)
            for ref in (R.hidden, R.ggate, R.gup)]
    twin += [copies.start(R.inner.at[:, other], R.twin_inner, sibling),
             copies.start(R.dyall.at[:, other], R.twin_dy, sibling)]
    twin_a = [copies.start(R.act.at[:, other], R.twin_act, sibling),
              copies.start(R.o, R.twin_o, sibling)]

    def grad_tile(t, carry):
        cs = aligned(t * col, col, 128)
        R.gin[:, cs] = (dot(R.ggate[0:n, :], R.wg_s[cs, :], 1, 1)
                        + dot(R.gup[0:n, :], R.wu_s[cs, :], 1, 1)).astype(BF)
        return carry

    lax.fori_loop(0, wid_n, grad_tile, 0)
    get_g = []
    for slot, i in enumerate(order):
        peer = place.wid_peer(i)
        rows = aligned(peer * sub, sub, sub)
        get_g.append(copies.start(R.gin.at[rows, :], R.recv_s.at[slot], {"wid": peer}))

    copies.sent(pass_gu + pass_d + get_a)
    for copy in twin:
        copy.wait_recv()
    R.left_t[:, 0:n] = R.inner[:, mine].T
    R.left_t[:, n:2 * n] = R.twin_inner[...].T

    def ffn_grads(j):
        cs = pl.ds(j * ff, ff)
        gate = dot(R.left_t[...], R.ggate[:, cs], 1, 0)
        up = dot(R.left_t[...], R.gup[:, cs], 1, 0)
        down = dot(R.hidden[0:n, cs], R.dyall[:, mine], 0, 0) + dot(R.hidden[n:2 * n, cs], R.twin_dy[...], 0, 0)
        return gate, up, down

    get_w = []
    for j in range(1, hid_n):
        gate, up, down = ffn_grads(j)
        lanes, tops = pl.ds((j - 1) * ff, ff), pl.ds((j - 1) * ff, ff)
        R.wg_s[0:half, lanes] = gate.astype(BF)
        R.wg_s[half:2 * half, lanes] = up.astype(BF)
        R.wu_s[tops, 0:half] = down.astype(BF)
        to = hid_peers[hid_n - j]
        get_w.append(copies.start(R.wg_s.at[:, lanes], R.recv_gu.at[j - 1], to))
        get_w.append(copies.start(R.wu_s.at[tops, pl.ds(0, half)], R.recv_dn.at[j - 1], to))
    gate, up, down = ffn_grads(0)
    R.d_gate[...] = gate
    R.d_up[...] = up
    R.d_down[...] = down

    def out_tile(t, carry):
        cs = aligned(t * col, col, 128)
        R.part_s[:, cs] = (dot(R.hidden[0:n, :], R.wd_s[:, cs], 1, 0) + R.part_s[:, cs].astype(F32)).astype(BF)
        return carry

    lax.fori_loop(0, wid_n, out_tile, 0)

    g_inner = R.gin[my_rows, :].astype(F32)
    for slot, copy in enumerate(get_g):
        copy.wait_recv()
        g_inner = g_inner + R.recv_s[slot].astype(F32)
    mixed = R.mixed[...]
    inv_two = lax.rsqrt(jnp.mean(mixed * mixed, -1, keepdims=True) + eps_norm)
    n_two = mixed * inv_two
    scaled = g_inner * R.gall[1:2, :]
    g_mixed = (R.dyall[my_rows, :].astype(F32)
               + inv_two * (scaled - n_two * jnp.mean(scaled * n_two, -1, keepdims=True)))
    R.row_g[...] = g_mixed.astype(BF)
    get_z = [copies.start(R.row_g, R.gz.at[my_rows, :], d) for d in to_wid]
    R.gz[my_rows, :] = R.row_g[...]
    R.gpart[1:2, :] = jnp.sum(g_inner * n_two, 0, keepdims=True)
    get_f = []
    for slot, i in enumerate(order):
        peer = place.wid_peer(i)
        get_f.append(copies.start(R.part_s.at[:, aligned(peer * col, col, 128)], R.recv_f.at[slot], {"wid": peer}))
    for copy in twin_a:
        copy.wait_recv()
    R.left_t[:, 0:n] = R.act[:, mine].T
    R.left_t[:, n:2 * n] = R.twin_act[...].T
    for copy in get_z:
        copy.wait_recv()
    twin_z = copies.start(R.gz.at[:, other], R.twin_gz, sibling)

    gets = [[] for _ in range(heads)]
    for h in range(heads):
        cs = head_cols(h)
        go = dot(R.gz[...], R.wo_s[cs, :], 1, 1).astype(BF)
        attn_bwd_head(hops, h, R.probs, go, R.qt, R.v, R.fv, R.fp, R.chain,
                      R.gqt, R.near_s, R.gv, R.sendk, R.sendv, R.sendp, R.s_s)
        for i in range(1, hops + 1):
            to = place.row_peer(-i)
            gets[h].append(copies.start(R.sendv.at[i - 1, :, cs], R.recvv.at[i - 1, :, cs], to))
            gets[h].append(copies.start(R.sendk.at[i - 1, :, cs], R.recvk.at[i - 1, :, cs], to))
        for i in range(1, hops):
            gets[h].append(copies.start(R.sendp.at[i - 1, h], R.recvp.at[i - 1, h], place.row_peer(-i)))

    twin_z.wait_recv()
    piece = model // place.rows_n

    def window(p):
        return aligned(p * piece // 128 * 128, 2 * 128, 128)

    base = place.seq * half

    def out_grad(p):
        start = p * piece // 128 * 128
        return (dot(R.o[...], R.gz[:, aligned(base + start, 256, 128)], 0, 0)
                + dot(R.twin_o[...], R.twin_gz[:, aligned(start, 256, 128)], 0, 0))

    get_o = []
    for i in range(1, hid_n):
        R.send_o[i - 1] = out_grad(place.hid_peer(i)).astype(BF)
        get_o.append(copies.start(R.send_o.at[i - 1], R.recv_o.at[i - 1], hid_peers[i]))
    R.dout_s[...] = out_grad(place.hid)

    lane = lax.broadcasted_iota(jnp.int32, (n, HDIM), 1)
    gc_all = jnp.zeros((n, HDIM), F32)
    twin_h = []
    get_h = []
    half_rows = model // seq_n // hid_n

    def head_weights(h):
        twin_h[h].wait_recv()
        span = 4 * HDIM
        for two, pair in enumerate(((R.d_query, R.d_key), (R.d_house, R.d_value))):
            part = slice(h * span + two * 2 * HDIM, h * span + (two + 1) * 2 * HDIM)
            R.s_s[0:half, :] = dot(R.left_t[...], R.grads[:, part], 1, 0)
            R.wd_s[0:half, part] = R.s_s[0:half, :].astype(BF)
            own = R.s_s[aligned(place.hid * half_rows, half_rows, half_rows), :]
            for m, ref in enumerate(pair):
                ref[:, head_cols(h)] = own[:, head_cols(m)]
        for i in range(1, hid_n):
            peer = aligned(place.hid_peer(i) * half_rows, half_rows, half_rows)
            get_h.append(copies.start(R.wd_s.at[peer, pl.ds(h * span, span)], R.recv_q.at[i - 1, :, pl.ds(h * span, span)], hid_peers[i]))

    for h in range(heads):
        for copy in gets[h]:
            copy.wait_recv()
        cs = head_cols(h)
        gkt = R.recvk[0, :, cs].astype(F32)
        gv = R.gv[:, cs] + R.recvv[0, :, cs].astype(F32)
        for i in range(1, hops):
            gkt = gkt + R.recvk[i, :, cs].astype(F32)
            gv = gv + R.recvv[i, :, cs].astype(F32)
        gp = R.recvp[0, h].astype(F32)
        for i in range(1, hops - 1):
            gp = gp + R.recvp[i, h].astype(F32)
        gq, gk, gr, gc = path_bwd_head(h, heads, R.q, R.k, R.r, R.c, R.u, R.inv, R.psi, R.x1, R.y1,
                                       R.gqt[:, cs], gkt, R.near_s[h], gp)
        gc_all = jnp.where(lane == h, gc, gc_all)
        base = 4 * HDIM * h
        for m, val in enumerate((gq, gk, gr, gv.astype(BF))):
            R.grads[0:n, base + m * HDIM:base + (m + 1) * HDIM] = val
        gs = pl.ds(base, 4 * HDIM)
        twin_h.append(copies.start(R.grads.at[pl.ds(0, n), gs], R.grads.at[pl.ds(n, n), gs], sibling))
        if h > 0:
            head_weights(h - 1)
    R.gcs[0:n, :] = gc_all.astype(BF)
    twin_c = copies.start(R.gcs.at[pl.ds(0, n), :], R.gcs.at[pl.ds(n, n), :], sibling)

    xf = R.xall[...].astype(F32)
    inv_rms = lax.rsqrt(jnp.mean(xf * xf, -1, keepdims=True) + eps_norm)
    stat = jnp.zeros((n, 1), F32)
    get_n = []
    for slot, i in enumerate(order + [0]):
        peer = place.wid_peer(i)
        cs = aligned(peer * col, col, 128)
        g_act = dot(R.gcs[0:n, 0:heads], R.wb[cs, :], 1, 1)
        for h in range(heads):
            for m, w in enumerate((R.wq_s, R.wk_s, R.wr_s, R.wv_s)):
                base = (4 * h + m) * HDIM
                g_act = g_act + dot(R.grads[0:n, base:base + HDIM], w[cs, head_cols(h)], 1, 1)
        normed = R.xall[:, cs].astype(F32) * inv_rms
        both = g_act * normed
        stat = stat + jnp.sum(both * R.gall[0:1, cs], 1, keepdims=True)
        R.gpart[0:1, cs] = jnp.sum(both, 0, keepdims=True)
        if i == 0:
            R.own_n[...] = g_act
        else:
            R.send_n[slot] = g_act.astype(BF)
            get_n.append(copies.start(R.send_n.at[slot], R.recv_n.at[slot], {"wid": peer}))
    R.stat_s[...] = jnp.broadcast_to(stat, (n, HDIM)).T[0:8, :]
    get_s = [copies.start(R.stat_s, R.recv_st.at[slot], d) for slot, d in enumerate(to_wid)]
    get_gain = [copies.start(R.gpart.at[:, window(lax.rem(place.row + i, place.rows_n))], R.recv_gain.at[i - 1],
                             place.row_peer(i)) for i in range(1, place.rows_n)]
    head_weights(heads - 1)
    twin_c.wait_recv()
    R.db_s[...] = dot(R.left_t[...], R.gcs[...], 1, 0)
    R.send_b[...] = R.db_s[...].astype(BF)
    get_b = []
    for i in range(1, hid_n):
        peer = aligned(place.hid_peer(i) * half_rows, half_rows, half_rows)
        get_b.append(copies.start(R.send_b.at[peer, :], R.recv_b.at[i - 1], hid_peers[i]))

    gain = R.gpart[:, window(place.row)]
    for i, copy in enumerate(get_gain):
        copy.wait_recv()
        gain = gain + R.recv_gain[i]
    R.gain_s[...] = gain
    get_gain2 = [copies.start(R.gain_s, R.recv_gain2.at[slot], d) for slot, d in enumerate(to_wid)]
    for copy in get_w:
        copy.wait_recv()
    for j in range(hid_n - 1):
        R.d_gate[...] += R.recv_gu[j, 0:half].astype(F32)
        R.d_up[...] += R.recv_gu[j, half:2 * half].astype(F32)
        R.d_down[...] += R.recv_dn[j].astype(F32)
    out = R.x_v[...].astype(F32) + R.part_s[:, my_cols].astype(F32)
    for slot, copy in enumerate(get_f):
        copy.wait_recv()
        out = out + R.recv_f[slot].astype(F32)
    R.output[...] = out.astype(BF)
    dout = R.dout_s[...]
    for i, copy in enumerate(get_o):
        copy.wait_recv()
        dout = dout + R.recv_o[i].astype(F32)
    R.d_out[...] = jnp.where(lax.rem(place.hid, 2) == 1, dout[:, 64:64 + piece], dout[:, 0:piece])
    g_act = R.own_n[...]
    stats = R.stat_s[...]
    for slot in range(wid_n - 1):
        get_s[slot].wait_recv()
        get_n[slot].wait_recv()
        g_act = g_act + R.recv_n[slot].astype(F32)
        stats = stats + R.recv_st[slot]
    mean = stats.T[:, 0:1] / model
    normed = R.xall[:, my_cols].astype(F32) * inv_rms
    R.d_inputs[...] = (R.gz[:, my_cols].astype(F32)
                       + inv_rms * (g_act * R.gall[0:1, my_cols] - normed * mean))
    for copy in get_h + get_b:
        copy.wait_recv()
    for h in range(heads):
        for m, ref in enumerate((R.d_query, R.d_key, R.d_house, R.d_value)):
            base = (4 * h + m) * HDIM
            total = ref[:, head_cols(h)]
            for i in range(hid_n - 1):
                total = total + R.recv_q[i, :, base:base + HDIM].astype(F32)
            ref[:, head_cols(h)] = total
    d_beta = R.db_s[aligned(place.hid * half_rows, half_rows, half_rows), :]
    for i in range(hid_n - 1):
        d_beta = d_beta + R.recv_b[i].astype(F32)
    R.d_beta[...] = d_beta[:, 0:heads]
    gain = R.gain_s[...]
    for slot, copy in enumerate(get_gain2):
        copy.wait_recv()
        gain = gain + R.recv_gain2[slot]
    R.gain_out[...] = jnp.where(lax.rem(place.row, 2) == 1, gain[:, 64:64 + piece], gain[:, 0:piece])
    copies.sent(copies.open)


def step(args, heads, hops, sizes):
    lengths, x, dy, gains, wq, wk, wv, wr, wb, wo, wg, wu, wd = args
    n, col = x.shape
    seq_n, hid_n, wid_n = sizes
    model, ff = wq.shape[0], wg.shape[1]
    width = wq.shape[1]
    sub = n // wid_n
    rows_n = seq_n * hid_n
    half = model // seq_n
    piece = model // rows_n
    slots = hops * (hops + 1) // 2
    S = jax.ShapeDtypeStruct
    V = pltpu.VMEM
    outs = dict(
        output=S((n, col), BF), d_inputs=S((n, col), F32), gain_out=S((8, piece), F32),
        d_query=S((piece, width), F32), d_key=S((piece, width), F32), d_value=S((piece, width), F32),
        d_house=S((piece, width), F32), d_beta=S((piece, heads), F32), d_out=S((width, piece), F32),
        d_gate=S((half, ff), F32), d_up=S((half, ff), F32), d_down=S((ff, half), F32),
    )
    peers_w, peers_h = wid_n - 1, hid_n - 1
    scratch = dict(
        act=V((n, model), BF), xall=V((n, model), BF), gall=V((8, model), F32), dyall=V((n, model), BF),
        q=V((n, width), F32), k=V((n, width), F32), r=V((n, width), F32), c=V((n, heads), F32), v=V((n, width), BF),
        qt=V((n, width), BF), u=V((n, width), F32), inv=V((heads, n, n), F32), psi=V((heads, n, n), F32),
        x1=V((n, width), F32), y1=V((n, width), F32),
        fv=V((hops, n, width), BF), fp=V((hops - 1, heads, HDIM, HDIM), F32), chain=V((slots, n, width), BF),
        probs=V((hops + 1, heads, n, n), BF), o=V((n, width), BF), mixed=V((sub, model), F32),
        inner=V((n, model), BF), hidden=V((2 * n, hid_n * ff), BF), ggate=V((2 * n, hid_n * ff), BF),
        gup=V((2 * n, hid_n * ff), BF), gin=V((n, model), BF),
        wq_s=V((model, width), BF), wk_s=V((model, width), BF), wv_s=V((model, width), BF),
        wr_s=V((model, width), BF), wo_s=V((width, model), BF),
        wg_s=V((model, hid_n * ff), BF), wu_s=V((model, hid_n * ff), BF), wd_s=V((hid_n * ff, model), BF),
        kt_s=V((n, width), BF), near_s=V((heads, n, n), F32), prod_s=V((heads, HDIM, HDIM), F32),
        s_s=V((max((hops + 1) * n, half), n), F32), part_s=V((n, model), BF), recv_s=V((peers_w, sub, model), BF),
        row_s=V((sub, model), BF), row_g=V((sub, model), BF),
        x_v=V((n, col), BF),
        twin_inner=V((n, half), BF), twin_dy=V((n, half), BF), twin_act=V((n, half), BF), twin_o=V((n, width), BF),
        twin_gz=V((n, half), BF), left_t=V((half, 2 * n), BF),
        recv_gu=V((peers_h, 2 * half, ff), BF), recv_dn=V((peers_h, ff, half), BF),
        gz=V((n, model), BF), gpart=V((8, model), F32), recv_f=V((peers_w, n, col), BF),
        gqt=V((n, width), F32), gv=V((n, width), F32),
        sendk=V((hops, n, width), BF), sendv=V((hops, n, width), BF), sendp=V((hops - 1, heads, HDIM, HDIM), BF),
        recvk=V((hops, n, width), BF), recvv=V((hops, n, width), BF), recvp=V((hops - 1, heads, HDIM, HDIM), BF),
        dout_s=V((width, 256), F32), send_o=V((peers_h, width, 256), BF), recv_o=V((peers_h, width, 256), BF),
        grads=V((2 * n, 4 * width), BF), gcs=V((2 * n, HDIM), BF),
        recv_q=V((peers_h, piece, 4 * width), BF),
        db_s=V((half, HDIM), F32), send_b=V((half, HDIM), BF), recv_b=V((peers_h, piece, HDIM), BF),
        own_n=V((n, col), F32), send_n=V((peers_w, n, col), BF), recv_n=V((peers_w, n, col), BF),
        stat_s=V((8, n), F32), recv_st=V((peers_w, 8, n), F32),
        recv_gain=V((rows_n - 1, 8, 256), F32), gain_s=V((8, 256), F32), recv_gain2=V((peers_w, 8, 256), F32),
    )
    n_copies = 320
    scratch.update(load_sem=pltpu.SemaphoreType.DMA((12,)), send_sem=pltpu.SemaphoreType.DMA((n_copies,)),
                   recv_sem=pltpu.SemaphoreType.DMA((n_copies,)))
    ins = ("lengths", "x", "dy", "gains", "wq", "wk", "wv", "wr", "wb", "wo", "wg", "wu", "wd")
    any_spec = pl.BlockSpec(memory_space=pl.ANY)
    vmem = pl.BlockSpec(memory_space=pltpu.VMEM)
    smem = pl.BlockSpec(memory_space=pltpu.SMEM)
    names = ins + tuple(outs) + tuple(scratch)
    res = pl.pallas_call(
        functools.partial(step_kernel, (heads, hops, sizes), names),
        in_specs=[smem, any_spec, any_spec, any_spec] + [any_spec] * 4 + [vmem] + [any_spec] * 4,
        out_shape=tuple(outs.values()),
        out_specs=tuple(vmem for _ in outs),
        scratch_shapes=list(scratch.values()),
        compiler_params=pltpu.CompilerParams(
            vmem_limit_bytes=VMEM_ALL, collective_id=1, has_side_effects=True),
        name="step",
    )(*args)
    return dict(zip(outs, res))


def shifted(array, axis, by):
    peers = lax.axis_size(axis)
    pairs = [(i, i + by) for i in range(peers) if 0 <= i + by < peers]
    return lax.ppermute(array, axis, pairs)


def norm_rows(hidden_f):
    inverse = lax.rsqrt(jnp.mean(hidden_f * hidden_f, -1, keepdims=True) + eps_norm)
    return (hidden_f * inverse, inverse)


def norm_back(grad_out, normed, inverse, gain_vec):
    scaled_grad = grad_out * gain_vec
    grad_gain = jnp.sum(grad_out * normed, 0)
    grad_in = inverse * (scaled_grad - normed * jnp.mean(scaled_grad * normed, -1, keepdims=True))
    return (grad_in, grad_gain)


ROWS = ("seq", "hid")


def body(inputs, gain_attn, gain_ffn, w_query, w_key, w_value, w_house, w_beta, w_out,
         w_gate, w_up, w_down, lengths, cotangent):
    tok, col = inputs.shape
    row_devs = lax.axis_size(ROWS)
    my_row = lax.axis_index(ROWS)
    my_wid = lax.axis_index("wid")
    wid_n = lax.axis_size("wid")
    tokens_all = tok * row_devs
    most_len = max(LEAST, 2 * tokens_all // 5)
    hops = min((most_len - 2) // tok + 1, row_devs - 1)
    heads = w_query.shape[1] // HDIM
    ff = w_gate.shape[1]
    sub = tok // wid_n

    x_all = lax.all_gather(inputs, "wid", axis=1, tiled=True)
    gain_one = lax.all_gather(gain_attn, "wid", axis=0, tiled=True).astype(F32)
    gain_two = lax.all_gather(gain_ffn, "wid", axis=0, tiled=True).astype(F32)
    dy_all = lax.all_gather(cotangent, "wid", axis=1, tiled=True)
    w_gu = lax.all_gather(jnp.concatenate([w_gate, w_up], 1), "hid", axis=0)
    w_dn = lax.all_gather(w_down, "hid", axis=0)
    model = x_all.shape[1]

    residual = x_all.astype(F32)
    normed_one, inverse_one = norm_rows(residual)
    act = (normed_one * gain_one).astype(BF)

    def project(weight):
        return jnp.dot(act, weight, preferred_element_type=F32)

    q, k, r, c = project(w_query), project(w_key), project(w_house), project(w_beta)
    v = project(w_value).astype(BF)
    far_v = jnp.stack([shifted(v, ROWS, i) for i in range(1, hops + 1)])
    qt, kt, near, prod, *saved = path_fwd(q, k, r, c, heads)
    far_k = jnp.stack([shifted(kt, ROWS, i) for i in range(1, hops + 1)])
    far_p = jnp.stack([shifted(prod, ROWS, i) for i in range(1, hops)])
    row_arr = jnp.full((1,), my_row, jnp.int32)
    attended, probs, chain = attn_fwd(lengths, row_arr, qt, near, v, far_k, far_v, far_p, heads, hops)

    attn_part = jnp.dot(attended, w_out, preferred_element_type=F32).astype(BF)
    attn_rows = lax.psum_scatter(attn_part, "wid", scatter_dimension=0, tiled=True)
    x_rows = lax.dynamic_slice_in_dim(x_all, my_wid * sub, sub, 0).astype(F32)
    dy_rows = lax.dynamic_slice_in_dim(dy_all, my_wid * sub, sub, 0).astype(F32)
    mixed = x_rows + attn_rows.astype(F32)
    normed_two, inverse_two = norm_rows(mixed)
    inner = lax.all_gather((normed_two * gain_two).astype(BF), "wid", axis=0, tiled=True)

    pre = jnp.einsum("tc,hcf->htf", inner, w_gu, preferred_element_type=F32)
    gate, up = pre[:, :, :ff], pre[:, :, ff:]
    sig = jax.nn.sigmoid(gate)
    hidden = (gate * sig * up).astype(BF)
    ffn_part = jnp.einsum("htf,hfc->tc", hidden, w_dn, preferred_element_type=F32)
    ffn_part = (ffn_part + attn_part.astype(F32)).astype(BF)
    ffn_cols = lax.psum_scatter(ffn_part, "wid", scatter_dimension=1, tiled=True)
    output = (inputs.astype(F32) + ffn_cols.astype(F32)).astype(BF)

    g_hidden = jnp.einsum("tc,hfc->htf", dy_all, w_dn, preferred_element_type=F32)
    g_gate = g_hidden * up * sig * (1.0 + gate * (1.0 - sig))
    g_up = g_hidden * gate * sig
    g_pre = jnp.concatenate([g_gate, g_up], 2).astype(BF)
    g_inner = jnp.einsum("htf,hcf->tc", g_pre, w_gu, preferred_element_type=F32).astype(BF)
    g_inner = lax.psum_scatter(g_inner, "wid", scatter_dimension=0, tiled=True).astype(F32)
    g_mixed_n, g_gain_two = norm_back(g_inner, normed_two, inverse_two, gain_two)
    g_z = lax.all_gather((dy_rows + g_mixed_n).astype(BF), "wid", axis=0, tiled=True)

    d_gu = jnp.einsum("tc,htf->hcf", inner, g_pre, preferred_element_type=F32).astype(BF)
    d_dn = jnp.einsum("htf,tc->hfc", hidden, dy_all, preferred_element_type=F32).astype(BF)
    d_gu = lax.psum_scatter(d_gu, "seq", scatter_dimension=1, tiled=True)
    d_gu = lax.psum_scatter(d_gu, "hid", scatter_dimension=0)
    d_dn = lax.psum_scatter(d_dn, "seq", scatter_dimension=2, tiled=True)
    d_dn = lax.psum_scatter(d_dn, "hid", scatter_dimension=0)

    g_attn = jnp.einsum("tc,ic->ti", g_z, w_out, preferred_element_type=F32).astype(BF)
    d_out = jnp.einsum("ti,tc->ic", attended, g_z, preferred_element_type=F32).astype(BF)
    g_qt, g_near, gv, send_k, send_v, send_p = attn_bwd(probs, g_attn, qt, v, far_v, far_p, chain, heads, hops)
    g_kt = sum(shifted(send_k[i - 1], ROWS, -i).astype(F32) for i in range(1, hops + 1))
    gv = gv + sum(shifted(send_v[i - 1], ROWS, -i).astype(F32) for i in range(1, hops + 1))
    g_prod = sum(shifted(send_p[i - 1], ROWS, -i).astype(F32) for i in range(1, hops))
    g_q, g_k, g_r, g_c = path_bwd(q, k, r, c, saved, g_qt, g_kt, g_near, g_prod, heads)
    g_v = gv.astype(BF)

    def weight_grad(grad_low):
        return jnp.einsum("tc,ti->ci", act, grad_low, preferred_element_type=F32).astype(BF)

    def input_grad(grad_low, weight):
        return jnp.einsum("ti,ci->tc", grad_low, weight, preferred_element_type=F32)

    g_act = (input_grad(g_q, w_query) + input_grad(g_k, w_key) + input_grad(g_v, w_value)
             + input_grad(g_r, w_house) + input_grad(g_c, w_beta))
    g_act = lax.psum_scatter(g_act.astype(BF), "wid", scatter_dimension=0, tiled=True).astype(F32)
    normed_rows = lax.dynamic_slice_in_dim(normed_one, my_wid * sub, sub, 0)
    inverse_rows = lax.dynamic_slice_in_dim(inverse_one, my_wid * sub, sub, 0)
    g_resid, g_gain_one = norm_back(g_act, normed_rows, inverse_rows, gain_one)
    d_rows = dy_rows + g_mixed_n + g_resid
    d_inputs = lax.all_to_all(d_rows, "wid", split_axis=1, concat_axis=0, tiled=True)

    def scatter(x, dim):
        return lax.psum_scatter(x, ROWS, scatter_dimension=dim, tiled=True)

    gains = lax.psum(jnp.stack([g_gain_one, g_gain_two]), "wid")
    gains = scatter(gains, 1)
    return (
        output,
        d_inputs,
        gains[0],
        gains[1],
        scatter(weight_grad(g_q), 0).astype(F32),
        scatter(weight_grad(g_k), 0).astype(F32),
        scatter(weight_grad(g_v), 0).astype(F32),
        scatter(weight_grad(g_r), 0).astype(F32),
        scatter(weight_grad(g_c), 0).astype(F32),
        scatter(d_out, 1).astype(F32),
        d_gu[:, :ff].astype(F32),
        d_gu[:, ff:].astype(F32),
        d_dn.astype(F32),
    )


def fast_body(inputs, gain_attn, gain_ffn, w_query, w_key, w_value, w_house, w_beta, w_out,
              w_gate, w_up, w_down, lengths, cotangent):
    tok, col = inputs.shape
    row_devs = lax.axis_size(ROWS)
    sizes = tuple(lax.axis_size(i) for i in ("seq", "hid", "wid"))
    most_len = max(LEAST, 2 * tok * row_devs // 5)
    hops = min((most_len - 2) // tok + 1, row_devs - 1)
    heads = w_query.shape[1] // HDIM
    gains = jnp.zeros((8, col), F32).at[0].set(gain_attn.astype(F32)).at[1].set(gain_ffn.astype(F32))
    f = step((lengths, inputs, cotangent, gains, w_query, w_key, w_value, w_house, w_beta, w_out,
              w_gate, w_up, w_down), heads, hops, sizes)
    return (f["output"], f["d_inputs"], f["gain_out"][0], f["gain_out"][1], f["d_query"], f["d_key"], f["d_value"],
            f["d_house"], f["d_beta"], f["d_out"], f["d_gate"], f["d_up"], f["d_down"])


def slow(mesh):
    return mesh.shape["seq"] * mesh.shape["hid"] > 8


def solution(mesh):
    in_specs = (
        P(("seq", "hid"), "wid"), P("wid"), P("wid"),
        P(None, "wid"), P(None, "wid"), P(None, "wid"), P(None, "wid"), P(None, "wid"),
        P("wid", None), P(None, ("hid", "wid")), P(None, ("hid", "wid")), P(("hid", "wid"), None),
        P(), P(("seq", "hid"), "wid"),
    )
    out_specs = (
        P(("seq", "hid"), "wid"), P(("seq", "hid"), "wid"), P(("seq", "hid")), P(("seq", "hid")),
        P(("seq", "hid"), "wid"), P(("seq", "hid"), "wid"), P(("seq", "hid"), "wid"),
        P(("seq", "hid"), "wid"), P(("seq", "hid"), "wid"), P("wid", ("seq", "hid")),
        P("seq", ("hid", "wid")), P("seq", ("hid", "wid")), P(("hid", "wid"), "seq"),
    )
    return jax.shard_map(body if slow(mesh) else fast_body, mesh=mesh, in_specs=in_specs, out_specs=out_specs, check_vma=False)
```

```python
import functools
import types

import jax
import jax.numpy as jnp
from jax import lax
from jax.experimental import pallas as pl
from jax.experimental.pallas import tpu as pltpu
from jax.sharding import PartitionSpec as P

HDIM = 128
LEAST = 1024

eps_norm = 1e-06
neg_big = -1e30
BF = jnp.bfloat16
F32 = jnp.float32
VMEM_LIMIT = 60 * 1024 * 1024
VMEM_ALL = 67043328


def dot(a, b, ca, cb):
    return lax.dot_general(a, b, (((ca,), (cb,)), ((), ())), preferred_element_type=F32)


def split(a):
    hi = a.astype(BF)
    return hi, (a - hi.astype(F32)).astype(BF)


def dot3(a, b, ca, cb):
    return dot(a[0], b[0], ca, cb) + (dot(a[0], b[1], ca, cb) + dot(a[1], b[0], ca, cb))


def dot1(a, b, ca, cb):
    return dot(a.astype(BF), b.astype(BF), ca, cb)


def iotas(n):
    rows = lax.broadcasted_iota(jnp.int32, (n, n), 0)
    cols = lax.broadcasted_iota(jnp.int32, (n, n), 1)
    return rows, cols


def head_cols(h):
    return slice(h * HDIM, (h + 1) * HDIM)


def house_terms(raw, strength, heads, h):
    inv = lax.rsqrt(jnp.sum(raw * raw, -1, keepdims=True) + eps_norm)
    lane = lax.broadcasted_iota(jnp.int32, strength.shape, 1)
    c = jnp.sum(jnp.where(lane == h, strength, 0.0), 1, keepdims=True)
    root = jnp.sqrt(2.0 / (1.0 + jnp.exp(-c)))
    return inv, root


def path_fwd_stage(heads, q_ref, k_ref, r_ref, c_ref, qt_ref, kt_ref, near_ref, p_ref,
                   u_ref, inv_ref, psi_ref, x_ref, y_ref, done=None):
    n = c_ref.shape[0]
    rows, cols = iotas(n)
    strength = c_ref[...]
    us, us2, lows, invs = [], [], [], []
    for h in range(heads):
        raw = r_ref[:, head_cols(h)]
        inv, root = house_terms(raw, strength, heads, h)
        u = raw * (inv * root)
        u_ref[:, head_cols(h)] = u
        u2 = split(u)
        low = jnp.where(rows > cols, dot3(u2, u2, 1, 1), 0.0)
        us.append(u)
        us2.append(u2)
        lows.append(low)
        first = jnp.where(rows == cols, 1.0, 0.0) - jnp.where(rows // 2 == cols // 2, low, 0.0)
        invs.append(first)
    span = 2
    while span < n:
        pick = (rows // (2 * span) == cols // (2 * span)) & (rows // span != cols // span)
        halves = [split(m) for m in invs]
        mids = [dot3(split(jnp.where(pick, lows[h], 0.0)), halves[h], 1, 0) for h in range(heads)]
        invs = [invs[h] - dot3(halves[h], split(mids[h]), 1, 0) for h in range(heads)]
        span = span * 2
    for h in range(heads):
        inv_ref[h] = invs[h]
        kin = split(invs[h])
        q = q_ref[:, head_cols(h)]
        k = k_ref[:, head_cols(h)]
        q2, k2, u2 = split(q), split(k), us2[h]
        a = jnp.where(rows > cols, dot3(u2, k2, 1, 1), 0.0)
        aq = jnp.where(rows < cols, dot3(k2, u2, 1, 1), 0.0)
        fq = jnp.where(rows >= cols, dot3(q2, u2, 1, 1), 0.0)
        fq2 = split(fq)
        x = dot3(kin, u2, 1, 0)
        y = dot3(kin, u2, 0, 0)
        psi = dot3(kin, split(a), 1, 0)
        x2 = split(x)
        x_ref[:, head_cols(h)] = x
        y_ref[:, head_cols(h)] = y
        psi_ref[h] = psi
        qt_ref[:, head_cols(h)] = (q - dot3(fq2, x2, 1, 0)).astype(BF)
        kt_ref[:, head_cols(h)] = (k - dot3(split(aq), split(y), 1, 0)).astype(BF)
        near_ref[h] = dot3(q2, k2, 1, 1) - dot3(fq2, split(psi), 1, 0)
        er, ec = iotas(HDIM)
        p_ref[h] = (jnp.where(er == ec, 1.0, 0.0) - dot3(u2, x2, 0, 0)).astype(p_ref.dtype)
        if done is not None:
            done(h)


def path_fwd_kernel(heads, *refs):
    path_fwd_stage(heads, *refs)


def path_fwd(q, k, r, c, heads):
    n, width = q.shape
    flat = jax.ShapeDtypeStruct((n, width), F32)
    low = jax.ShapeDtypeStruct((n, width), BF)
    square = jax.ShapeDtypeStruct((heads, n, n), F32)
    return pl.pallas_call(
        functools.partial(path_fwd_kernel, heads),
        out_shape=(low, low, square, jax.ShapeDtypeStruct((heads, HDIM, HDIM), F32),
                   flat, square, square, flat, flat),
        compiler_params=pltpu.CompilerParams(vmem_limit_bytes=VMEM_LIMIT),
        name="path_fwd",
    )(q, k, r, c)


def doc_of(pos, len_ref):
    total = len_ref[0]
    doc = (pos >= total).astype(jnp.int32)
    for i in range(1, len_ref.shape[0]):
        total = total + len_ref[i]
        doc = doc + (pos >= total).astype(jnp.int32)
    return doc


def chain_slot(r, m):
    return r * (r - 1) // 2 + m


def attn_fwd_stage(heads, hops, row, len_ref, qt_ref, near_ref, v_ref, fv_ref, fp_ref, chain_ref,
                   o_ref, p_ref, s_ref, get_k, get_p):
    n = qt_ref.shape[0]
    scale = HDIM ** (-0.5)
    rows, cols = iotas(n)
    own = doc_of(row * n + rows, len_ref)
    near_ok = (rows >= cols) & (own == doc_of(row * n + cols, len_ref))
    for h in range(heads):
        cs = head_cols(h)
        q = qt_ref[:, cs]
        for copy in get_k[h] + get_p[h]:
            copy.wait_recv()
        s = jnp.where(near_ok, near_ref[h] * scale, neg_big)
        s_ref[0:n, :] = s
        top = jnp.max(s, 1, keepdims=True)
        for r in range(1, hops + 1):
            keys = chain_ref[chain_slot(r, 0), :, cs]
            for m in range(1, r):
                keys = dot(keys, fp_ref[r - m - 1, h].astype(BF), 1, 1).astype(BF)
                chain_ref[chain_slot(r, m), :, cs] = keys
            source = row - r
            docs = jnp.where(source >= 0, doc_of(source * n + cols, len_ref), -1)
            s = jnp.where(own == docs, dot(q, keys, 1, 1) * scale, neg_big)
            s_ref[r * n:(r + 1) * n, :] = s
            top = jnp.maximum(top, jnp.max(s, 1, keepdims=True))
        total = jnp.zeros((n, 1), F32)
        for r in range(hops + 1):
            e = jnp.exp(s_ref[r * n:(r + 1) * n, :] - top)
            s_ref[r * n:(r + 1) * n, :] = e
            total = total + jnp.sum(e, 1, keepdims=True)
        recip = 1.0 / total
        out = jnp.zeros((n, HDIM), F32)
        for r in range(hops + 1):
            p = (s_ref[r * n:(r + 1) * n, :] * recip).astype(BF)
            p_ref[r, h] = p
            vals = v_ref[:, cs] if r == 0 else fv_ref[r - 1, :, cs]
            out = out + dot(p, vals, 1, 0)
        o_ref[:, cs] = out.astype(BF)

def attn_fwd_kernel(heads, hops, len_ref, row_ref, qt_ref, near_ref, v_ref, fk_ref, fv_ref, fp_ref,
                    o_ref, p_ref, chain_ref, s_ref):
    for r in range(1, hops + 1):
        chain_ref[chain_slot(r, 0)] = fk_ref[r - 1]
    none = [[] for _ in range(heads)]
    attn_fwd_stage(heads, hops, row_ref[0], len_ref, qt_ref, near_ref, v_ref, fv_ref, fp_ref, chain_ref,
                   o_ref, p_ref, s_ref, none, none)


def attn_fwd(lengths, my_row, qt, near, v, far_k, far_v, far_p, heads, hops):
    n, width = qt.shape
    slots = hops * (hops + 1) // 2
    smem = pl.BlockSpec(memory_space=pltpu.SMEM)
    vmem = pl.BlockSpec(memory_space=pltpu.VMEM)
    return pl.pallas_call(
        functools.partial(attn_fwd_kernel, heads, hops),
        in_specs=[smem, smem] + [vmem] * 6,
        out_shape=(
            jax.ShapeDtypeStruct((n, width), BF),
            jax.ShapeDtypeStruct((hops + 1, heads, n, n), BF),
            jax.ShapeDtypeStruct((slots, n, width), BF),
        ),
        scratch_shapes=[pltpu.VMEM(((hops + 1) * n, n), F32)],
        compiler_params=pltpu.CompilerParams(vmem_limit_bytes=VMEM_LIMIT),
        name="attn_fwd",
    )(lengths, my_row, qt, near, v, far_k, far_v, far_p)


def attn_bwd_kernel(heads, hops, p_ref, go_ref, qt_ref, v_ref, fv_ref, fp_ref, chain_ref,
                    gqt_ref, gnear_ref, gv_ref, sendk_ref, sendv_ref, sendp_ref, dp_ref):
    n = qt_ref.shape[0]
    scale = HDIM ** (-0.5)
    for h in range(heads):
        cs = head_cols(h)
        go = go_ref[:, cs]
        q = qt_ref[:, cs]
        delta = jnp.zeros((n, 1), F32)
        for r in range(hops + 1):
            vals = v_ref[:, cs] if r == 0 else fv_ref[r - 1, :, cs]
            dp = dot(go, vals, 1, 1)
            dp_ref[r] = dp
            delta = delta + jnp.sum(p_ref[r, h].astype(F32) * dp, 1, keepdims=True)
            gv = dot(p_ref[r, h], go, 0, 0)
            if r == 0:
                gv_ref[:, cs] = gv
            else:
                sendv_ref[r - 1, :, cs] = gv.astype(BF)
        gnear_ref[h] = p_ref[0, h].astype(F32) * (dp_ref[0] - delta) * scale
        gq = jnp.zeros((n, HDIM), F32)
        gps = [jnp.zeros((HDIM, HDIM), F32) for _ in range(hops - 1)]
        for r in range(1, hops + 1):
            gs = (p_ref[r, h].astype(F32) * (dp_ref[r] - delta) * scale).astype(BF)
            gq = gq + dot(gs, chain_ref[chain_slot(r, r - 1), :, cs], 1, 0)
            gk = dot(gs, q, 0, 0)
            for m in range(r - 1, 0, -1):
                back = r - m - 1
                gkb = gk.astype(BF)
                gps[back] = gps[back] + dot(gkb, chain_ref[chain_slot(r, m - 1), :, cs], 0, 0)
                gk = dot(gkb, fp_ref[back, h].astype(BF), 1, 0)
            sendk_ref[r - 1, :, cs] = gk.astype(BF)
        gqt_ref[:, cs] = gq
        for i in range(hops - 1):
            sendp_ref[i, h] = gps[i].astype(BF)


def attn_bwd(p, go, qt, v, far_v, far_p, chain, heads, hops):
    n, width = qt.shape
    return pl.pallas_call(
        functools.partial(attn_bwd_kernel, heads, hops),
        out_shape=(
            jax.ShapeDtypeStruct((n, width), F32),
            jax.ShapeDtypeStruct((heads, n, n), F32),
            jax.ShapeDtypeStruct((n, width), F32),
            jax.ShapeDtypeStruct((hops, n, width), BF),
            jax.ShapeDtypeStruct((hops, n, width), BF),
            jax.ShapeDtypeStruct((hops - 1, heads, HDIM, HDIM), BF),
        ),
        scratch_shapes=[pltpu.VMEM((hops + 1, n, n), F32)],
        compiler_params=pltpu.CompilerParams(vmem_limit_bytes=VMEM_LIMIT),
        name="attn_bwd",
    )(p, go, qt, v, far_v, far_p, chain)


def path_bwd_kernel(heads, q_ref, k_ref, r_ref, c_ref, u_ref, inv_ref, psi_ref, x_ref, y_ref,
                    gqt_ref, gkt_ref, gnear_ref, gp_ref, gq_ref, gk_ref, gr_ref, gc_ref):
    n = q_ref.shape[0]
    rows, cols = iotas(n)
    strength = c_ref[...]
    lane = lax.broadcasted_iota(jnp.int32, strength.shape, 1)
    gc_all = jnp.zeros(strength.shape, F32)
    for h in range(heads):
        cs = head_cols(h)
        q, k, u = q_ref[:, cs], k_ref[:, cs], u_ref[:, cs]
        qb, kb, ub = q.astype(BF), k.astype(BF), u.astype(BF)
        kin = inv_ref[h].astype(BF)
        psi = psi_ref[h].astype(BF)
        x, y = x_ref[:, cs].astype(BF), y_ref[:, cs].astype(BF)
        gqt, gkt = gqt_ref[:, cs], gkt_ref[:, cs]
        gqtb, gktb = gqt.astype(BF), gkt.astype(BF)
        gs = gnear_ref[h]
        gsb = gs.astype(BF)
        gst = gs.T.astype(BF)
        gp = gp_ref[h].astype(BF)
        f = jnp.where(rows <= cols, dot(ub, qb, 1, 1), 0.0).astype(BF)
        fq = jnp.where(rows >= cols, dot(qb, ub, 1, 1), 0.0).astype(BF)
        a = jnp.where(rows > cols, dot(ub, kb, 1, 1), 0.0).astype(BF)
        gx = -(dot(f, gqtb, 1, 0) + dot(ub, gp, 1, 0))
        gy = -dot(a, gktb, 1, 0)
        phiq = dot(fq, kin, 1, 0).astype(BF)
        back = dot(gst, phiq, 1, 0)
        backb = back.astype(BF)
        gfq = jnp.where(rows >= cols, -(dot(gqtb, x, 1, 1) + dot(gsb, psi, 1, 1)), 0.0)
        gaq = jnp.where(rows < cols, -(dot(gktb, y, 1, 1) + back), 0.0)
        kgx = dot(kin, gx.astype(BF), 0, 0)
        kgy = dot(kin, gy.astype(BF), 1, 0)
        zt = dot(x, kgx.astype(BF), 1, 1) + dot(kgy.astype(BF), y, 1, 1) - dot(psi, backb, 1, 0)
        glt = jnp.where(rows < cols, -zt, 0.0)
        sym = (glt + glt.T).astype(BF)
        gfqb, gaqb = gfq.astype(BF), gaq.astype(BF)
        gu = (kgx + kgy - dot(x, gp, 1, 1) + dot(gfq.T.astype(BF), qb, 1, 0)
              + dot(gaq.T.astype(BF), kb, 1, 0) + dot(sym, ub, 1, 0))
        gq_ref[:, cs] = (gqt + dot(gsb, kb, 1, 0) + dot(gfqb, ub, 1, 0)).astype(BF)
        gk_ref[:, cs] = (gkt + dot(gst, qb, 1, 0) + dot(gaqb, ub, 1, 0)).astype(BF)
        raw = r_ref[:, cs]
        inv, root = house_terms(raw, strength, heads, h)
        gc = jnp.sum(gu * u, 1, keepdims=True) * (1.0 - 0.5 * root * root) * 0.5
        gun = gu * root
        un = raw * inv
        gr = inv * (gun - un * jnp.sum(gun * un, 1, keepdims=True))
        gr_ref[:, cs] = gr.astype(BF)
        gc_all = jnp.where(lane == h, gc, gc_all)
    gc_ref[...] = gc_all.astype(BF)


def path_bwd(q, k, r, c, saved, gqt, gkt, gnear, gp, heads):
    n, width = q.shape
    low = jax.ShapeDtypeStruct((n, width), BF)
    return pl.pallas_call(
        functools.partial(path_bwd_kernel, heads),
        out_shape=(low, low, low, jax.ShapeDtypeStruct((n, heads), BF)),
        compiler_params=pltpu.CompilerParams(vmem_limit_bytes=VMEM_LIMIT),
        name="path_bwd",
    )(q, k, r, c, *saved, gqt, gkt, gnear, gp)


MESH = pl.DeviceIdType.MESH


class Copies:
    def __init__(self, send, recv):
        self.send, self.recv, self.count, self.open = send, recv, 0, []

    def start(self, src, dst, device):
        i = self.count
        self.count = i + 1
        copy = pltpu.make_async_remote_copy(
            src_ref=src, dst_ref=dst, send_sem=self.send.at[i], recv_sem=self.recv.at[i],
            device_id=device, device_id_type=MESH)
        copy.start()
        self.open.append(copy)
        return copy

    def sent(self, some):
        for copy in some:
            copy.wait_send()
        self.open = [copy for copy in self.open if all(copy is not other for other in some)]


class Loads:
    def __init__(self, sems):
        self.sems, self.count = sems, 0

    def start(self, src, dst):
        copy = pltpu.make_async_copy(src, dst, self.sems.at[self.count])
        self.count = self.count + 1
        copy.start()
        return copy


class Place:
    def __init__(self, sizes):
        self.seq_n, self.hid_n, self.wid_n = sizes
        self.seq = lax.axis_index("seq")
        self.hid = lax.axis_index("hid")
        self.wid = lax.axis_index("wid")
        self.rows_n = self.seq_n * self.hid_n
        self.row = self.seq * self.hid_n + self.hid

    def wid_peer(self, i):
        return lax.rem(self.wid + i, self.wid_n)

    def hid_peer(self, i):
        return lax.rem(self.hid + i, self.hid_n)

    def seq_peer(self, i):
        return lax.rem(self.seq + i, self.seq_n)

    def row_peer(self, i):
        to = lax.rem(self.row + i + self.rows_n, self.rows_n)
        return {"seq": to // self.hid_n, "hid": lax.rem(to, self.hid_n)}

    def barrier(self):
        sem = pltpu.get_barrier_semaphore()
        for i in range(1, self.wid_n):
            pl.semaphore_signal(sem, inc=1, device_id={"wid": self.wid_peer(i)}, device_id_type=MESH)
        for i in range(1, self.rows_n):
            pl.semaphore_signal(sem, inc=1, device_id=self.row_peer(i), device_id_type=MESH)
        pl.semaphore_wait(sem, self.wid_n - 1 + self.rows_n - 1)


def aligned(start, size, step):
    return pl.ds(pl.multiple_of(start, step), size)


def attn_bwd_head(hops, h, p_ref, go, qt_ref, v_ref, fv_ref, fp_ref, chain_ref,
                  gqt_ref, gnear_ref, gv_ref, sendk_ref, sendv_ref, sendp_ref, dp_ref):
    n = qt_ref.shape[0]
    scale = HDIM ** (-0.5)
    cs = head_cols(h)
    q = qt_ref[:, cs]
    delta = jnp.zeros((n, 1), F32)
    for r in range(hops + 1):
        vals = v_ref[:, cs] if r == 0 else fv_ref[r - 1, :, cs]
        dp = dot(go, vals, 1, 1)
        dp_ref[r * n:(r + 1) * n, :] = dp
        delta = delta + jnp.sum(p_ref[r, h].astype(F32) * dp, 1, keepdims=True)
        gv = dot(p_ref[r, h], go, 0, 0)
        if r == 0:
            gv_ref[:, cs] = gv
        else:
            sendv_ref[r - 1, :, cs] = gv.astype(BF)
    gnear_ref[h] = p_ref[0, h].astype(F32) * (dp_ref[0:n, :] - delta) * scale
    gq = jnp.zeros((n, HDIM), F32)
    gps = [jnp.zeros((HDIM, HDIM), F32) for _ in range(hops - 1)]
    for r in range(1, hops + 1):
        gs = (p_ref[r, h].astype(F32) * (dp_ref[r * n:(r + 1) * n, :] - delta) * scale).astype(BF)
        gq = gq + dot(gs, chain_ref[chain_slot(r, r - 1), :, cs], 1, 0)
        gk = dot(gs, q, 0, 0)
        for m in range(r - 1, 0, -1):
            back = r - m - 1
            gkb = gk.astype(BF)
            gps[back] = gps[back] + dot(gkb, chain_ref[chain_slot(r, m - 1), :, cs], 0, 0)
            gk = dot(gkb, fp_ref[back, h].astype(BF), 1, 0)
        sendk_ref[r - 1, :, cs] = gk.astype(BF)
    gqt_ref[:, cs] = gq
    for i in range(hops - 1):
        sendp_ref[i, h] = gps[i].astype(BF)


def path_bwd_head(h, heads, q_ref, k_ref, r_ref, c_ref, u_ref, inv_ref, psi_ref, x_ref, y_ref,
                  gqt, gkt, gs, gp):
    n = c_ref.shape[0]
    rows, cols = iotas(n)
    cs = head_cols(h)
    q, k, u = q_ref[:, cs], k_ref[:, cs], u_ref[:, cs]
    qb, kb, ub = q.astype(BF), k.astype(BF), u.astype(BF)
    kin = inv_ref[h].astype(BF)
    psi = psi_ref[h].astype(BF)
    x, y = x_ref[:, cs].astype(BF), y_ref[:, cs].astype(BF)
    gqtb, gktb = gqt.astype(BF), gkt.astype(BF)
    gsb = gs.astype(BF)
    gst = gs.T.astype(BF)
    gp = gp.astype(BF)
    f = jnp.where(rows <= cols, dot(ub, qb, 1, 1), 0.0).astype(BF)
    fq = jnp.where(rows >= cols, dot(qb, ub, 1, 1), 0.0).astype(BF)
    a = jnp.where(rows > cols, dot(ub, kb, 1, 1), 0.0).astype(BF)
    gx = -(dot(f, gqtb, 1, 0) + dot(ub, gp, 1, 0))
    gy = -dot(a, gktb, 1, 0)
    phiq = dot(fq, kin, 1, 0).astype(BF)
    back = dot(gst, phiq, 1, 0)
    backb = back.astype(BF)
    gfq = jnp.where(rows >= cols, -(dot(gqtb, x, 1, 1) + dot(gsb, psi, 1, 1)), 0.0)
    gaq = jnp.where(rows < cols, -(dot(gktb, y, 1, 1) + back), 0.0)
    kgx = dot(kin, gx.astype(BF), 0, 0)
    kgy = dot(kin, gy.astype(BF), 1, 0)
    zt = dot(x, kgx.astype(BF), 1, 1) + dot(kgy.astype(BF), y, 1, 1) - dot(psi, backb, 1, 0)
    glt = jnp.where(rows < cols, -zt, 0.0)
    sym = (glt + glt.T).astype(BF)
    gfqb, gaqb = gfq.astype(BF), gaq.astype(BF)
    gu = (kgx + kgy - dot(x, gp, 1, 1) + dot(gfq.T.astype(BF), qb, 1, 0)
          + dot(gaq.T.astype(BF), kb, 1, 0) + dot(sym, ub, 1, 0))
    gq = (gqt + dot(gsb, kb, 1, 0) + dot(gfqb, ub, 1, 0)).astype(BF)
    gk = (gkt + dot(gst, qb, 1, 0) + dot(gaqb, ub, 1, 0)).astype(BF)
    raw = r_ref[:, cs]
    inv, root = house_terms(raw, c_ref[...], heads, h)
    gc = jnp.sum(gu * u, 1, keepdims=True) * (1.0 - 0.5 * root * root) * 0.5
    gun = gu * root
    un = raw * inv
    gr = (inv * (gun - un * jnp.sum(gun * un, 1, keepdims=True))).astype(BF)
    return gq, gk, gr, gc


class Heads:
    def __init__(self, ref, kind):
        self.ref, self.kind = ref, kind

    def __getitem__(self, index):
        base = 3 * index[1].start + self.kind * HDIM
        return self.ref[index[0], base:base + HDIM]


def turned(index, by):
    low = index % 2
    high = index // 2 % 2
    return index + (1 - 2 * low) * (by % 2) + (2 - 4 * high) * (by // 2)


def step_kernel(cfg, names, *refs):
    heads, hops, sizes = cfg
    R = types.SimpleNamespace(**dict(zip(names, refs)))
    place = Place(sizes)
    wid_n, hid_n, seq_n = place.wid_n, place.hid_n, place.seq_n
    n, col = R.x.shape
    width = heads * HDIM
    model = R.act.shape[1]
    ff = R.wg.shape[1]
    sub = n // wid_n
    half = model // seq_n
    piece = model // place.rows_n
    copies, loads = Copies(R.send_sem, R.recv_sem), Loads(R.load_sem)
    my_cols = aligned(place.wid * col, col, 128)
    my_rows = aligned(place.wid * sub, sub, sub)
    mine = aligned(place.seq * half, half, 128)
    other = aligned((1 - place.seq) * half, half, 128)
    sibling = {"seq": 1 - place.seq}
    order = sorted(range(1, wid_n), key=lambda i: -min(i, wid_n - i))
    to_wid = [{"wid": place.wid_peer(i)} for i in order]
    near = [{"hid": turned(place.hid, j)} for j in range(hid_n)]

    load_x = [loads.start(R.x, R.xall.at[:, my_cols])]
    load_v = loads.start(R.wv, R.w_s.at[:, pl.ds(3 * width, width)])
    load_w = [loads.start(w.at[:, pl.ds(h * HDIM, HDIM)], R.w_s.at[:, pl.ds((3 * h + m) * HDIM, HDIM)])
              for h in range(heads) for m, w in enumerate((R.wq, R.wk, R.wr))]
    load_dy = loads.start(R.dy, R.dyall.at[:, my_cols])
    load_o = loads.start(R.wo, R.wo_s)
    load_f = [loads.start(R.wg, R.wg_s.at[:, pl.ds(0, ff)]), loads.start(R.wu, R.wu_s.at[:, pl.ds(0, ff)]),
              loads.start(R.wd, R.wd_s.at[pl.ds(0, ff), :])]
    R.gain_in[0:1, :] = R.gain_attn[...].astype(F32).reshape(1, col)
    R.gain_in[1:2, :] = R.gain_ffn[...].astype(F32).reshape(1, col)
    place.barrier()

    get_x = [copies.start(R.x, R.xall.at[:, my_cols], d) for d in to_wid]
    get_x += [copies.start(R.gain_in, R.gall.at[:, my_cols], d) for d in to_wid]
    R.gall[:, my_cols] = R.gain_in[...]

    part_f = ff // seq_n
    mine_c = aligned(place.seq * half, half, 16)
    mine_f = aligned(place.seq * part_f, part_f, 16)

    def cols_of(j):
        return pl.ds(j * ff, ff)

    def down_rows(j, piece_i=0, pieces=1):
        size = part_f // pieces
        return aligned(j * ff + place.seq * part_f + piece_i * size, size, 16)

    def pass_on(ref, device):
        return copies.start(ref, ref, device)

    get_gate = [copies.start(R.wg.at[mine_c, :], R.wg_s.at[mine_c, cols_of(j)], near[j]) for j in (1, 2)]
    for copy in get_gate:
        copy.wait_recv()
    get_gate3 = copies.start(R.wg_s.at[mine_c, cols_of(1)], R.wg_s.at[mine_c, cols_of(3)], near[2])

    for copy in load_x:
        copy.wait()
    for copy in get_x:
        copy.wait_recv()
    get_dy = [copies.start(R.dy, R.dyall.at[:, my_cols], d) for d in to_wid]
    xf = R.xall[...].astype(F32)
    inv_rms = lax.rsqrt(jnp.mean(xf * xf, -1, keepdims=True) + eps_norm)
    R.inv_rms[...] = inv_rms
    R.act[...] = (xf * inv_rms * R.gall[0:1, :]).astype(BF)
    load_v.wait()
    R.v[...] = dot(R.act[...], R.w_s[:, 3 * width:4 * width], 1, 0).astype(BF)
    get_v = [copies.start(R.v, R.fv.at[i - 1], place.row_peer(i)) for i in range(1, hops + 1)]
    for copy in load_w:
        copy.wait()
    R.proj[...] = dot(R.act[...], R.w_s[:, 0:3 * width], 1, 0)
    R.c[...] = dot(R.act[...], R.wb[...], 1, 1)

    get_k = [[] for _ in range(heads)]
    get_p = [[] for _ in range(heads)]

    def send_head(h):
        cs = head_cols(h)
        for i in range(1, hops + 1):
            get_k[h].append(copies.start(R.kt_s.at[:, cs], R.chain.at[chain_slot(i, 0), :, cs], place.row_peer(i)))
        for i in range(1, hops):
            get_p[h].append(copies.start(R.prod_s.at[h], R.fp.at[i - 1, h], place.row_peer(i)))

    path_fwd_stage(heads, Heads(R.proj, 0), Heads(R.proj, 1), Heads(R.proj, 2), R.c, R.qt, R.kt_s, R.near_s, R.prod_s,
                   R.u, R.inv, R.psi, R.x1, R.y1, send_head)

    get_up = [copies.start(R.wu.at[mine_c, :], R.wu_s.at[mine_c, cols_of(j)], near[j]) for j in (1, 2)]
    get_down = [copies.start(R.wd.at[mine_f, :], R.wd_s.at[down_rows(j), :], near[j]) for j in (1, 2)]

    for copy in get_v:
        copy.wait_recv()
    attn_fwd_stage(heads, hops, place.row, R.lengths, R.qt, R.near_s, R.v, R.fv, R.fp, R.chain,
                   R.o, R.probs, R.s_s, get_k, get_p)

    load_o.wait()
    get_a = []
    for slot, i in enumerate(order):
        peer = place.wid_peer(i)
        rows = aligned(peer * sub, sub, sub)
        R.part_s[rows, :] = dot(R.o[rows, :], R.wo_s[...], 1, 0).astype(BF)
        get_a.append(copies.start(R.part_s.at[rows, :], R.recv_s.at[slot], {"wid": peer}))
    R.part_s[my_rows, :] = dot(R.o[my_rows, :], R.wo_s[...], 1, 0).astype(BF)
    for copy in get_up + get_down:
        copy.wait_recv()
    relay = [copies.start(R.wu_s.at[mine_c, cols_of(2)], R.wu_s.at[mine_c, cols_of(3)], near[1]),
             copies.start(R.wd_s.at[down_rows(1, 0, 2), :], R.wd_s.at[down_rows(3, 0, 2), :], near[2]),
             copies.start(R.wd_s.at[down_rows(2, 1, 2), :], R.wd_s.at[down_rows(3, 1, 2), :], near[1])]
    get_gate3.wait_recv()
    three = pl.ds(ff, 3 * ff)
    shared = [pass_on(R.wg_s.at[mine_c, three], sibling)]
    mixed = R.xall[my_rows, :].astype(F32) + R.part_s[my_rows, :].astype(F32)
    for slot, copy in enumerate(get_a):
        copy.wait_recv()
        mixed = mixed + R.recv_s[slot].astype(F32)
    R.mixed[...] = mixed
    inv_two = lax.rsqrt(jnp.mean(mixed * mixed, -1, keepdims=True) + eps_norm)
    R.row_s[...] = (mixed * inv_two * R.gall[1:2, :]).astype(BF)
    get_i = [copies.start(R.row_s, R.inner.at[my_rows, :], d) for d in to_wid]
    R.inner[my_rows, :] = R.row_s[...]
    for copy in relay:
        copy.wait_recv()
    shared.append(pass_on(R.wu_s.at[mine_c, three], sibling))
    shared += [pass_on(R.wd_s.at[down_rows(j), :], sibling) for j in (1, 2, 3)]
    twin_a = [copies.start(R.act.at[:, other], R.twin_act, sibling),
              copies.start(R.o, R.twin_o, sibling)]
    load_dy.wait()
    for copy in load_f:
        copy.wait()
    for copy in get_dy + shared + get_i:
        copy.wait_recv()

    def hidden_tile(t, carry):
        cs = aligned(t * ff, ff, 128)
        gate = dot(R.inner[...], R.wg_s[:, cs], 1, 0)
        up = dot(R.inner[...], R.wu_s[:, cs], 1, 0)
        g_hidden = dot(R.dyall[...], R.wd_s[cs, :], 1, 1)
        sig = 1.0 / (1.0 + jnp.exp(-gate))
        silu = gate * sig
        R.hidden[0:n, cs] = (silu * up).astype(BF)
        R.ggate[0:n, cs] = (g_hidden * up * sig * (1.0 + gate * (1.0 - sig))).astype(BF)
        R.gup[0:n, cs] = (g_hidden * silu).astype(BF)
        return carry

    lax.fori_loop(0, hid_n, hidden_tile, 0)

    twin = [copies.start(ref.at[pl.ds(0, n), :], ref.at[pl.ds(n, n), :], sibling)
            for ref in (R.hidden, R.ggate, R.gup)]
    twin += [copies.start(R.inner.at[:, other], R.twin_inner, sibling),
             copies.start(R.dyall.at[:, other], R.twin_dy, sibling)]

    def grad_tile(t, carry):
        cs = aligned(t * col, col, 128)
        R.gin[:, cs] = (dot(R.ggate[0:n, :], R.wg_s[cs, :], 1, 1)
                        + dot(R.gup[0:n, :], R.wu_s[cs, :], 1, 1)).astype(BF)
        return carry

    lax.fori_loop(0, wid_n, grad_tile, 0)
    get_g = []
    for slot, i in enumerate(order):
        peer = place.wid_peer(i)
        rows = aligned(peer * sub, sub, sub)
        get_g.append(copies.start(R.gin.at[rows, :], R.recv_s.at[slot], {"wid": peer}))

    copies.sent(shared + relay + [get_gate3] + get_a)
    for copy in twin:
        copy.wait_recv()
    R.left_t[:, 0:n] = R.inner[:, mine].T
    R.left_t[:, n:2 * n] = R.twin_inner[...].T
    down_a, down_b = pl.ds(0, half // 2), pl.ds(half // 2, half // 2)

    def grads_tile(j, carry):
        cs = aligned(j * ff, ff, 128)
        R.wg_s[0:half, cs] = dot(R.left_t[...], R.ggate[:, cs], 1, 0).astype(BF)
        R.wg_s[half:2 * half, cs] = dot(R.left_t[...], R.gup[:, cs], 1, 0).astype(BF)
        down = dot(R.hidden[0:n, cs], R.dyall[:, mine], 0, 0) + dot(R.hidden[n:2 * n, cs], R.twin_dy[...], 0, 0)
        R.wu_s[aligned(j * ff, ff, ff), 0:half] = down.astype(BF)
        return carry

    lax.fori_loop(0, hid_n, grads_tile, 0)
    upper, lower = pl.ds(0, half), pl.ds(half, half)

    def first_round(j, slot, rows, lanes, to, gus, downs):
        return [copies.start(R.wg_s.at[rows, cols_of(j)], gus.at[slot], to),
                copies.start(R.wu_s.at[cols_of(j), lanes], downs.at[slot], to)]

    get_r1 = (first_round(3, 1, upper, down_a, near[1], R.gu_x, R.dn_x)
              + first_round(3, 1, lower, down_b, near[2], R.gu_y, R.dn_y)
              + first_round(1, 0, upper, down_a, near[1], R.gu_x, R.dn_x)
              + first_round(2, 0, lower, down_b, near[2], R.gu_y, R.dn_y))

    def out_tile(t, carry):
        cs = aligned(t * col, col, 128)
        R.part_s[:, cs] = (dot(R.hidden[0:n, :], R.wd_s[:, cs], 1, 0) + R.part_s[:, cs].astype(F32)).astype(BF)
        return carry

    lax.fori_loop(0, wid_n, out_tile, 0)

    g_inner = R.gin[my_rows, :].astype(F32)
    for slot, copy in enumerate(get_g):
        copy.wait_recv()
        g_inner = g_inner + R.recv_s[slot].astype(F32)
    mixed = R.mixed[...]
    inv_two = lax.rsqrt(jnp.mean(mixed * mixed, -1, keepdims=True) + eps_norm)
    n_two = mixed * inv_two
    scaled = g_inner * R.gall[1:2, :]
    g_mixed = (R.dyall[my_rows, :].astype(F32)
               + inv_two * (scaled - n_two * jnp.mean(scaled * n_two, -1, keepdims=True)))
    R.row_g[...] = g_mixed.astype(BF)
    get_z = [copies.start(R.row_g, R.gz.at[my_rows, :], d) for d in to_wid]
    R.gz[my_rows, :] = R.row_g[...]
    R.gpart[1:2, :] = jnp.sum(g_inner * n_two, 0, keepdims=True)
    get_f = []
    for slot, i in enumerate(order):
        peer = place.wid_peer(i)
        get_f.append(copies.start(R.part_s.at[:, aligned(peer * col, col, 128)], R.recv_f.at[slot], {"wid": peer}))

    for copy in get_r1:
        copy.wait_recv()
    add_g = R.wg_s.at[upper, cols_of(2)]
    add_g[...] = (add_g[...].astype(F32) + R.gu_x[1].astype(F32)).astype(BF)
    add_u = R.wg_s.at[lower, cols_of(1)]
    add_u[...] = (add_u[...].astype(F32) + R.gu_y[1].astype(F32)).astype(BF)
    add_a = R.wu_s.at[cols_of(2), down_a]
    add_a[...] = (add_a[...].astype(F32) + R.dn_x[1].astype(F32)).astype(BF)
    add_b = R.wu_s.at[cols_of(1), down_b]
    add_b[...] = (add_b[...].astype(F32) + R.dn_y[1].astype(F32)).astype(BF)
    get_r2 = [copies.start(add_g, R.gu_x.at[2], near[2]), copies.start(add_a, R.dn_x.at[2], near[2]),
              copies.start(add_u, R.gu_y.at[2], near[1]), copies.start(add_b, R.dn_y.at[2], near[1])]

    for copy in twin_a:
        copy.wait_recv()
    for copy in get_z:
        copy.wait_recv()
    twin_z = copies.start(R.gz.at[:, other], R.twin_gz, sibling)

    gets = [[] for _ in range(heads)]
    for h in range(heads):
        cs = head_cols(h)
        go = dot(R.gz[...], R.wo_s[cs, :], 1, 1).astype(BF)
        attn_bwd_head(hops, h, R.probs, go, R.qt, R.v, R.fv, R.fp, R.chain,
                      R.gqt, R.near_s, R.gv, R.sendk, R.sendv, R.sendp, R.s_s)
        for i in range(1, hops + 1):
            to = place.row_peer(-i)
            gets[h].append(copies.start(R.sendv.at[i - 1, :, cs], R.recvv.at[i - 1, :, cs], to))
            gets[h].append(copies.start(R.sendk.at[i - 1, :, cs], R.recvk.at[i - 1, :, cs], to))
        for i in range(1, hops):
            gets[h].append(copies.start(R.sendp.at[i - 1, h], R.recvp.at[i - 1, h], place.row_peer(-i)))

    def left_of(ref, twin_ref):
        R.left_t[:, 0:n] = ref[:, mine].T
        R.left_t[:, n:2 * n] = twin_ref[...].T

    twin_z.wait_recv()
    left_of(R.gz, R.twin_gz)

    get_h = []

    def spread(src, dst):
        for j in range(1, hid_n):
            p = turned(place.hid, j)
            get_h.append(copies.start(src.at[aligned(p * piece, piece, 64), :], dst.at[j - 1], near[j]))

    R.wide_s[...] = dot(R.left_t[:, 0:n], R.o[...], 1, 0) + dot(R.left_t[:, n:2 * n], R.twin_o[...], 1, 0)
    R.d_out[...] = R.wide_s[aligned(place.hid * piece, piece, 64), :]
    R.send_o[...] = R.wide_s[...].astype(BF)
    spread(R.send_o, R.recv_o)
    left_of(R.act, R.twin_act)

    row8 = lax.broadcasted_iota(jnp.int32, (n, HDIM), 1)
    gc_all = jnp.zeros((n, HDIM), F32)
    for h in range(heads):
        for copy in gets[h]:
            copy.wait_recv()
        cs = head_cols(h)
        gv = R.gv[:, cs]
        for i in range(hops):
            gv = gv + R.recvv[i, :, cs].astype(F32)
        R.grads[0:n, (9 + h) * HDIM:(10 + h) * HDIM] = gv.astype(BF)
    val_cols = pl.ds(3 * width, width)
    twin_v = copies.start(R.grads.at[pl.ds(0, n), val_cols], R.grads.at[pl.ds(n, n), val_cols], sibling)
    twin_h = []

    def weights_of(slot, outs_of):
        cs = slice(slot * width, (slot + 1) * width)
        R.wide_s[...] = dot(R.left_t[...], R.grads[:, cs], 1, 0)
        R.wd_s[0:half, cs] = R.wide_s[...].astype(BF)
        own = R.wide_s[aligned(place.hid * piece, piece, 64), :]
        for m, (ref, at) in enumerate(outs_of):
            ref[:, at] = own[:, head_cols(m)]
        spread(R.wd_s.at[:, pl.ds(slot * width, width)], R.recv_q.at[:, :, pl.ds(slot * width, width)])

    def outs_of(h):
        return [(ref, head_cols(h)) for ref in (R.d_query, R.d_key, R.d_house)]

    val_outs = [(R.d_value, head_cols(m)) for m in range(heads)]
    for h in range(heads):
        cs = head_cols(h)
        gkt = R.recvk[0, :, cs].astype(F32)
        for i in range(1, hops):
            gkt = gkt + R.recvk[i, :, cs].astype(F32)
        gp = R.recvp[0, h].astype(F32)
        for i in range(1, hops - 1):
            gp = gp + R.recvp[i, h].astype(F32)
        gq, gk, gr, gc = path_bwd_head(h, heads, Heads(R.proj, 0), Heads(R.proj, 1), Heads(R.proj, 2), R.c,
                                       R.u, R.inv, R.psi, R.x1, R.y1, R.gqt[:, cs], gkt, R.near_s[h], gp)
        gc_all = jnp.where(row8 == h, gc, gc_all)
        for m, val in enumerate((gq, gk, gr)):
            R.grads[0:n, (3 * h + m) * HDIM:(3 * h + m + 1) * HDIM] = val
        gs = pl.ds(h * width, width)
        twin_h.append(copies.start(R.grads.at[pl.ds(0, n), gs], R.grads.at[pl.ds(n, n), gs], sibling))
        if h == 0:
            twin_v.wait_recv()
            weights_of(heads, val_outs)
        else:
            twin_h[h - 1].wait_recv()
            weights_of(h - 1, outs_of(h - 1))
    R.gcs[0:n, :] = gc_all.astype(BF)
    twin_c = copies.start(R.gcs.at[pl.ds(0, n), :], R.gcs.at[pl.ds(n, n), :], sibling)

    inv_rms = R.inv_rms[...]
    stat = jnp.zeros((n, 1), F32)
    get_n = []
    for slot, i in enumerate(order + [0]):
        peer = place.wid_peer(i)
        cs = aligned(peer * col, col, 128)
        g_act = dot(R.grads[0:n, :], R.w_s[cs, :], 1, 1) + dot(R.gcs[0:n, 0:heads], R.wb[:, cs], 1, 0)
        normed = R.xall[:, cs].astype(F32) * inv_rms
        both = g_act * normed
        stat = stat + jnp.sum(both * R.gall[0:1, cs], 1, keepdims=True)
        R.gpart[0:1, cs] = jnp.sum(both, 0, keepdims=True)
        if i == 0:
            R.own_n[...] = g_act
        else:
            R.send_n[slot] = g_act.astype(BF)
            get_n.append(copies.start(R.send_n.at[slot], R.recv_n.at[slot], {"wid": peer}))
    R.stat_s[...] = jnp.broadcast_to(stat, (n, HDIM)).T[0:8, :]
    get_s = [copies.start(R.stat_s, R.recv_st.at[slot], d) for slot, d in enumerate(to_wid)]
    twin_h[heads - 1].wait_recv()
    weights_of(heads - 1, outs_of(heads - 1))
    twin_c.wait_recv()
    d_beta = dot(R.gcs[0:n, :], R.act[:, mine], 0, 0) + dot(R.gcs[n:2 * n, :], R.twin_act[...], 0, 0)
    R.beta_s[...] = d_beta[0:8, :]

    def window(p):
        return aligned(p * piece // 128 * 128, 256, 128)

    get_b = [copies.start(R.beta_s.at[:, window(turned(place.hid, j))], R.recv_b.at[j - 1], near[j])
             for j in range(1, hid_n)]
    get_gain = [copies.start(R.gpart.at[:, window(lax.rem(place.row + i, place.rows_n))], R.recv_gain.at[i - 1],
                             place.row_peer(i)) for i in range(1, place.rows_n)]

    gain = R.gpart[:, window(place.row)]
    for i, copy in enumerate(get_gain):
        copy.wait_recv()
        gain = gain + R.recv_gain[i]
    R.gain_s[...] = gain
    get_gain2 = [copies.start(R.gain_s, R.recv_gain2.at[slot], d) for slot, d in enumerate(to_wid)]
    for copy in get_r2:
        copy.wait_recv()
    R.d_gate[...] = (R.wg_s[upper, 0:ff].astype(F32) + R.gu_x[0].astype(F32) + R.gu_x[2].astype(F32))
    R.d_up[...] = (R.wg_s[lower, 0:ff].astype(F32) + R.gu_y[0].astype(F32) + R.gu_y[2].astype(F32))
    for lanes, ref in ((down_a, R.dn_x), (down_b, R.dn_y)):
        R.d_down[:, lanes] = R.wu_s[0:ff, lanes].astype(F32) + ref[0].astype(F32) + ref[2].astype(F32)
    out = R.x[...].astype(F32) + R.part_s[:, my_cols].astype(F32)
    for slot, copy in enumerate(get_f):
        copy.wait_recv()
        out = out + R.recv_f[slot].astype(F32)
    R.output[...] = out.astype(BF)
    g_act = R.own_n[...]
    stats = R.stat_s[...]
    for slot in range(wid_n - 1):
        get_s[slot].wait_recv()
        get_n[slot].wait_recv()
        g_act = g_act + R.recv_n[slot].astype(F32)
        stats = stats + R.recv_st[slot]
    mean = stats.T[:, 0:1] / model
    normed = R.xall[:, my_cols].astype(F32) * inv_rms
    R.d_inputs[...] = (R.gz[:, my_cols].astype(F32)
                       + inv_rms * (g_act * R.gall[0:1, my_cols] - normed * mean))
    for copy in get_h + get_b:
        copy.wait_recv()
    for i in range(hid_n - 1):
        R.d_out[...] += R.recv_o[i].astype(F32)
    for slot, refs_of in [(heads, val_outs)] + [(h, outs_of(h)) for h in range(heads)]:
        for m, (ref, at) in enumerate(refs_of):
            base = slot * width + m * HDIM
            total = ref[:, at]
            for i in range(hid_n - 1):
                total = total + R.recv_q[i, :, base:base + HDIM].astype(F32)
            ref[:, at] = total
    d_beta = R.beta_s[:, window(place.hid)]
    for i in range(hid_n - 1):
        d_beta = d_beta + R.recv_b[i]
    gain = R.gain_s[...]
    for slot, copy in enumerate(get_gain2):
        copy.wait_recv()
        gain = gain + R.recv_gain2[slot]

    def exact(rows, at):
        return jnp.where(at % 2 == 1, rows[:, 64:64 + piece], rows[:, 0:piece])

    R.d_beta[...] = exact(d_beta, place.hid)[0:heads, :]
    R.gain_out[...] = exact(gain, place.row)
    copies.sent(copies.open)


def step(args, heads, hops, sizes):
    ins = ("lengths", "x", "dy", "gain_attn", "gain_ffn", "wq", "wk", "wv", "wr", "wb", "wo", "wg", "wu", "wd")
    shapes = dict(zip(ins, (a.shape for a in args)))
    n, col = shapes["x"]
    seq_n, hid_n, wid_n = sizes
    model, width = shapes["wq"]
    ff = shapes["wg"][1]
    sub = n // wid_n
    rows_n = seq_n * hid_n
    half = model // seq_n
    piece = model // rows_n
    slots = hops * (hops + 1) // 2
    S = jax.ShapeDtypeStruct
    V = pltpu.VMEM
    outs = dict(
        output=S((n, col), BF), d_inputs=S((n, col), F32), gain_out=S((8, piece), F32),
        d_query=S((piece, width), F32), d_key=S((piece, width), F32), d_value=S((piece, width), F32),
        d_house=S((piece, width), F32), d_beta=S((heads, piece), F32), d_out=S((piece, width), F32),
        d_gate=S((half, ff), F32), d_up=S((half, ff), F32), d_down=S((ff, half), F32),
    )
    peers_w, peers_h = wid_n - 1, hid_n - 1
    scratch = dict(
        gain_in=V((8, col), F32), gall=V((8, model), F32), inv_rms=V((n, 1), F32),
        act=V((n, model), BF), xall=V((n, model), BF), dyall=V((n, model), BF),
        proj=V((n, 3 * width), F32), c=V((n, heads), F32), v=V((n, width), BF),
        qt=V((n, width), BF), u=V((n, width), F32), inv=V((heads, n, n), F32), psi=V((heads, n, n), F32),
        x1=V((n, width), F32), y1=V((n, width), F32),
        fv=V((hops, n, width), BF), fp=V((hops - 1, heads, HDIM, HDIM), BF), chain=V((slots, n, width), BF),
        probs=V((hops + 1, heads, n, n), BF), o=V((n, width), BF), mixed=V((sub, model), F32),
        inner=V((n, model), BF), hidden=V((2 * n, hid_n * ff), BF), ggate=V((2 * n, hid_n * ff), BF),
        gup=V((2 * n, hid_n * ff), BF), gin=V((n, model), BF),
        w_s=V((model, 4 * width), BF), wo_s=V((width, model), BF),
        wg_s=V((model, hid_n * ff), BF), wu_s=V((model, hid_n * ff), BF), wd_s=V((hid_n * ff, model), BF),
        kt_s=V((n, width), BF), near_s=V((heads, n, n), F32), prod_s=V((heads, HDIM, HDIM), BF),
        s_s=V(((hops + 1) * n, n), F32), part_s=V((n, model), BF), recv_s=V((peers_w, sub, model), BF),
        row_s=V((sub, model), BF), row_g=V((sub, model), BF),
        twin_inner=V((n, half), BF), twin_dy=V((n, half), BF), twin_act=V((n, half), BF), twin_o=V((n, width), BF),
        twin_gz=V((n, half), BF), left_t=V((half, 2 * n), BF),
        gu_x=V((3, half, ff), BF), gu_y=V((3, half, ff), BF),
        dn_x=V((3, ff, half // 2), BF), dn_y=V((3, ff, half // 2), BF),
        gz=V((n, model), BF), gpart=V((8, model), F32), recv_f=V((peers_w, n, col), BF),
        gqt=V((n, width), F32), gv=V((n, width), F32),
        sendk=V((hops, n, width), BF), sendv=V((hops, n, width), BF), sendp=V((hops - 1, heads, HDIM, HDIM), BF),
        recvk=V((hops, n, width), BF), recvv=V((hops, n, width), BF), recvp=V((hops - 1, heads, HDIM, HDIM), BF),
        send_o=V((half, width), BF), recv_o=V((peers_h, piece, width), BF),
        grads=V((2 * n, 4 * width), BF), gcs=V((2 * n, HDIM), BF), wide_s=V((half, width), F32),
        recv_q=V((peers_h, piece, 4 * width), BF), beta_s=V((8, half), F32), recv_b=V((peers_h, 8, 256), F32),
        own_n=V((n, col), F32), send_n=V((peers_w, n, col), BF), recv_n=V((peers_w, n, col), BF),
        stat_s=V((8, n), F32), recv_st=V((peers_w, 8, n), F32),
        recv_gain=V((rows_n - 1, 8, 256), F32), gain_s=V((8, 256), F32), recv_gain2=V((peers_w, 8, 256), F32),
    )
    n_copies = 200
    scratch.update(load_sem=pltpu.SemaphoreType.DMA((24,)), send_sem=pltpu.SemaphoreType.DMA((n_copies,)),
                   recv_sem=pltpu.SemaphoreType.DMA((n_copies,)))
    spaces = {"lengths": pltpu.SMEM, "x": pltpu.VMEM, "gain_attn": pltpu.VMEM, "gain_ffn": pltpu.VMEM, "wb": pltpu.VMEM}
    vmem = pl.BlockSpec(memory_space=pltpu.VMEM)
    res = pl.pallas_call(
        functools.partial(step_kernel, (heads, hops, sizes), ins + tuple(outs) + tuple(scratch)),
        in_specs=[pl.BlockSpec(memory_space=spaces.get(i, pl.ANY)) for i in ins],
        out_shape=tuple(outs.values()),
        out_specs=tuple(vmem for _ in outs),
        scratch_shapes=list(scratch.values()),
        compiler_params=pltpu.CompilerParams(
            vmem_limit_bytes=VMEM_ALL, collective_id=1, has_side_effects=True),
        name="step",
    )(*args)
    return dict(zip(outs, res))


def finish_kernel(count, *refs):
    ins, outs, bufs, sems = refs[:count], refs[count:2 * count], refs[2 * count:3 * count], refs[3 * count]
    loads = [pltpu.make_async_copy(a, b, sems.at[0, i]) for i, (a, b) in enumerate(zip(ins, bufs))]
    stores = [pltpu.make_async_copy(b, c, sems.at[1, i]) for i, (b, c) in enumerate(zip(bufs, outs))]
    for copy in loads:
        copy.start()
    for load, store in zip(loads, stores):
        load.wait()
        store.start()
    for copy in stores:
        copy.wait()


def finish(arrays):
    count = len(arrays)
    spec = pl.BlockSpec(memory_space=pl.ANY)
    return pl.pallas_call(
        functools.partial(finish_kernel, count),
        in_specs=[spec] * count, out_specs=[spec] * count,
        out_shape=[jax.ShapeDtypeStruct(a.shape, a.dtype) for a in arrays],
        scratch_shapes=[pltpu.VMEM(a.shape, a.dtype) for a in arrays] + [pltpu.SemaphoreType.DMA((2, count))],
        compiler_params=pltpu.CompilerParams(vmem_limit_bytes=VMEM_ALL),
        name="finish",
    )(*arrays)


def shifted(array, axis, by):
    peers = lax.axis_size(axis)
    pairs = [(i, i + by) for i in range(peers) if 0 <= i + by < peers]
    return lax.ppermute(array, axis, pairs)


def norm_rows(hidden_f):
    inverse = lax.rsqrt(jnp.mean(hidden_f * hidden_f, -1, keepdims=True) + eps_norm)
    return (hidden_f * inverse, inverse)


def norm_back(grad_out, normed, inverse, gain_vec):
    scaled_grad = grad_out * gain_vec
    grad_gain = jnp.sum(grad_out * normed, 0)
    grad_in = inverse * (scaled_grad - normed * jnp.mean(scaled_grad * normed, -1, keepdims=True))
    return (grad_in, grad_gain)


ROWS = ("seq", "hid")


def body(inputs, gain_attn, gain_ffn, w_query, w_key, w_value, w_house, w_beta, w_out,
         w_gate, w_up, w_down, lengths, cotangent):
    tok, col = inputs.shape
    row_devs = lax.axis_size(ROWS)
    my_row = lax.axis_index(ROWS)
    my_wid = lax.axis_index("wid")
    wid_n = lax.axis_size("wid")
    tokens_all = tok * row_devs
    most_len = max(LEAST, 2 * tokens_all // 5)
    hops = min((most_len - 2) // tok + 1, row_devs - 1)
    heads = w_query.shape[1] // HDIM
    ff = w_gate.shape[1]
    sub = tok // wid_n

    x_all = lax.all_gather(inputs, "wid", axis=1, tiled=True)
    gain_one = lax.all_gather(gain_attn, "wid", axis=0, tiled=True).astype(F32)
    gain_two = lax.all_gather(gain_ffn, "wid", axis=0, tiled=True).astype(F32)
    dy_all = lax.all_gather(cotangent, "wid", axis=1, tiled=True)
    w_gu = lax.all_gather(jnp.concatenate([w_gate, w_up], 1), "hid", axis=0)
    w_dn = lax.all_gather(w_down, "hid", axis=0)
    model = x_all.shape[1]

    residual = x_all.astype(F32)
    normed_one, inverse_one = norm_rows(residual)
    act = (normed_one * gain_one).astype(BF)

    def project(weight):
        return jnp.dot(act, weight, preferred_element_type=F32)

    q, k, r, c = project(w_query), project(w_key), project(w_house), project(w_beta)
    v = project(w_value).astype(BF)
    far_v = jnp.stack([shifted(v, ROWS, i) for i in range(1, hops + 1)])
    qt, kt, near, prod, *saved = path_fwd(q, k, r, c, heads)
    far_k = jnp.stack([shifted(kt, ROWS, i) for i in range(1, hops + 1)])
    far_p = jnp.stack([shifted(prod, ROWS, i) for i in range(1, hops)])
    row_arr = jnp.full((1,), my_row, jnp.int32)
    attended, probs, chain = attn_fwd(lengths, row_arr, qt, near, v, far_k, far_v, far_p, heads, hops)

    attn_part = jnp.dot(attended, w_out, preferred_element_type=F32).astype(BF)
    attn_rows = lax.psum_scatter(attn_part, "wid", scatter_dimension=0, tiled=True)
    x_rows = lax.dynamic_slice_in_dim(x_all, my_wid * sub, sub, 0).astype(F32)
    dy_rows = lax.dynamic_slice_in_dim(dy_all, my_wid * sub, sub, 0).astype(F32)
    mixed = x_rows + attn_rows.astype(F32)
    normed_two, inverse_two = norm_rows(mixed)
    inner = lax.all_gather((normed_two * gain_two).astype(BF), "wid", axis=0, tiled=True)

    pre = jnp.einsum("tc,hcf->htf", inner, w_gu, preferred_element_type=F32)
    gate, up = pre[:, :, :ff], pre[:, :, ff:]
    sig = jax.nn.sigmoid(gate)
    hidden = (gate * sig * up).astype(BF)
    ffn_part = jnp.einsum("htf,hfc->tc", hidden, w_dn, preferred_element_type=F32)
    ffn_part = (ffn_part + attn_part.astype(F32)).astype(BF)
    ffn_cols = lax.psum_scatter(ffn_part, "wid", scatter_dimension=1, tiled=True)
    output = (inputs.astype(F32) + ffn_cols.astype(F32)).astype(BF)

    g_hidden = jnp.einsum("tc,hfc->htf", dy_all, w_dn, preferred_element_type=F32)
    g_gate = g_hidden * up * sig * (1.0 + gate * (1.0 - sig))
    g_up = g_hidden * gate * sig
    g_pre = jnp.concatenate([g_gate, g_up], 2).astype(BF)
    g_inner = jnp.einsum("htf,hcf->tc", g_pre, w_gu, preferred_element_type=F32).astype(BF)
    g_inner = lax.psum_scatter(g_inner, "wid", scatter_dimension=0, tiled=True).astype(F32)
    g_mixed_n, g_gain_two = norm_back(g_inner, normed_two, inverse_two, gain_two)
    g_z = lax.all_gather((dy_rows + g_mixed_n).astype(BF), "wid", axis=0, tiled=True)

    d_gu = jnp.einsum("tc,htf->hcf", inner, g_pre, preferred_element_type=F32).astype(BF)
    d_dn = jnp.einsum("htf,tc->hfc", hidden, dy_all, preferred_element_type=F32).astype(BF)
    d_gu = lax.psum_scatter(d_gu, "seq", scatter_dimension=1, tiled=True)
    d_gu = lax.psum_scatter(d_gu, "hid", scatter_dimension=0)
    d_dn = lax.psum_scatter(d_dn, "seq", scatter_dimension=2, tiled=True)
    d_dn = lax.psum_scatter(d_dn, "hid", scatter_dimension=0)

    g_attn = jnp.einsum("tc,ic->ti", g_z, w_out, preferred_element_type=F32).astype(BF)
    d_out = jnp.einsum("ti,tc->ic", attended, g_z, preferred_element_type=F32).astype(BF)
    g_qt, g_near, gv, send_k, send_v, send_p = attn_bwd(probs, g_attn, qt, v, far_v, far_p, chain, heads, hops)
    g_kt = sum(shifted(send_k[i - 1], ROWS, -i).astype(F32) for i in range(1, hops + 1))
    gv = gv + sum(shifted(send_v[i - 1], ROWS, -i).astype(F32) for i in range(1, hops + 1))
    g_prod = sum(shifted(send_p[i - 1], ROWS, -i).astype(F32) for i in range(1, hops))
    g_q, g_k, g_r, g_c = path_bwd(q, k, r, c, saved, g_qt, g_kt, g_near, g_prod, heads)
    g_v = gv.astype(BF)

    def weight_grad(grad_low):
        return jnp.einsum("tc,ti->ci", act, grad_low, preferred_element_type=F32).astype(BF)

    def input_grad(grad_low, weight):
        return jnp.einsum("ti,ci->tc", grad_low, weight, preferred_element_type=F32)

    g_act = (input_grad(g_q, w_query) + input_grad(g_k, w_key) + input_grad(g_v, w_value)
             + input_grad(g_r, w_house) + input_grad(g_c, w_beta))
    g_act = lax.psum_scatter(g_act.astype(BF), "wid", scatter_dimension=0, tiled=True).astype(F32)
    normed_rows = lax.dynamic_slice_in_dim(normed_one, my_wid * sub, sub, 0)
    inverse_rows = lax.dynamic_slice_in_dim(inverse_one, my_wid * sub, sub, 0)
    g_resid, g_gain_one = norm_back(g_act, normed_rows, inverse_rows, gain_one)
    d_rows = dy_rows + g_mixed_n + g_resid
    d_inputs = lax.all_to_all(d_rows, "wid", split_axis=1, concat_axis=0, tiled=True)

    def scatter(x, dim):
        return lax.psum_scatter(x, ROWS, scatter_dimension=dim, tiled=True)

    gains = lax.psum(jnp.stack([g_gain_one, g_gain_two]), "wid")
    gains = scatter(gains, 1)
    return (
        output,
        d_inputs,
        gains[0],
        gains[1],
        scatter(weight_grad(g_q), 0).astype(F32),
        scatter(weight_grad(g_k), 0).astype(F32),
        scatter(weight_grad(g_v), 0).astype(F32),
        scatter(weight_grad(g_r), 0).astype(F32),
        scatter(weight_grad(g_c), 0).astype(F32),
        scatter(d_out, 1).astype(F32),
        d_gu[:, :ff].astype(F32),
        d_gu[:, ff:].astype(F32),
        d_dn.astype(F32),
    )


def fast_body(inputs, gain_attn, gain_ffn, w_query, w_key, w_value, w_house, w_beta, w_out,
              w_gate, w_up, w_down, lengths, cotangent):
    tok, col = inputs.shape
    row_devs = lax.axis_size(ROWS)
    sizes = tuple(lax.axis_size(i) for i in ("seq", "hid", "wid"))
    most_len = max(LEAST, 2 * tok * row_devs // 5)
    hops = min((most_len - 2) // tok + 1, row_devs - 1)
    heads = w_query.shape[1] // HDIM
    f = step((lengths, inputs, cotangent, gain_attn, gain_ffn, w_query, w_key, w_value, w_house,
              w_beta.T, w_out, w_gate, w_up, w_down), heads, hops, sizes)
    names = [i for i in f if i != "gain_out"]
    f.update(zip(names, finish([f[i] for i in names])))
    return (f["output"], f["d_inputs"], f["gain_out"][0], f["gain_out"][1], f["d_query"], f["d_key"], f["d_value"],
            f["d_house"], f["d_beta"].T, f["d_out"].T, f["d_gate"], f["d_up"], f["d_down"])


def slow(mesh):
    return (mesh.shape["seq"], mesh.shape["hid"]) != (2, 4)


def solution(mesh):
    in_specs = (
        P(("seq", "hid"), "wid"), P("wid"), P("wid"),
        P(None, "wid"), P(None, "wid"), P(None, "wid"), P(None, "wid"), P(None, "wid"),
        P("wid", None), P(None, ("hid", "wid")), P(None, ("hid", "wid")), P(("hid", "wid"), None),
        P(), P(("seq", "hid"), "wid"),
    )
    out_specs = (
        P(("seq", "hid"), "wid"), P(("seq", "hid"), "wid"), P(("seq", "hid")), P(("seq", "hid")),
        P(("seq", "hid"), "wid"), P(("seq", "hid"), "wid"), P(("seq", "hid"), "wid"),
        P(("seq", "hid"), "wid"), P(("seq", "hid"), "wid"), P("wid", ("seq", "hid")),
        P("seq", ("hid", "wid")), P("seq", ("hid", "wid")), P(("hid", "wid"), "seq"),
    )
    return jax.shard_map(body if slow(mesh) else fast_body, mesh=mesh, in_specs=in_specs, out_specs=out_specs, check_vma=False)
```

```python
import functools
import types

import jax
import jax.numpy as jnp
from jax import lax
from jax.experimental import pallas as pl
from jax.experimental.pallas import tpu as pltpu
from jax.sharding import PartitionSpec as P

HDIM = 128
LEAST = 1024

eps_norm = 1e-06
neg_big = -1e30
BF = jnp.bfloat16
F32 = jnp.float32
VMEM_LIMIT = 60 * 1024 * 1024
VMEM_ALL = 67043328


def dot(a, b, ca, cb):
    return lax.dot_general(a, b, (((ca,), (cb,)), ((), ())), preferred_element_type=F32)


def split(a):
    hi = a.astype(BF)
    return hi, (a - hi.astype(F32)).astype(BF)


def dot3(a, b, ca, cb):
    return dot(a[0], b[0], ca, cb) + (dot(a[0], b[1], ca, cb) + dot(a[1], b[0], ca, cb))


def dot1(a, b, ca, cb):
    return dot(a.astype(BF), b.astype(BF), ca, cb)


def iotas(n):
    rows = lax.broadcasted_iota(jnp.int32, (n, n), 0)
    cols = lax.broadcasted_iota(jnp.int32, (n, n), 1)
    return rows, cols


def head_cols(h):
    return slice(h * HDIM, (h + 1) * HDIM)


def house_terms(raw, strength, heads, h):
    inv = lax.rsqrt(jnp.sum(raw * raw, -1, keepdims=True) + eps_norm)
    lane = lax.broadcasted_iota(jnp.int32, strength.shape, 1)
    c = jnp.sum(jnp.where(lane == h, strength, 0.0), 1, keepdims=True)
    root = jnp.sqrt(2.0 / (1.0 + jnp.exp(-c)))
    return inv, root


def path_fwd_stage(heads, q_ref, k_ref, r_ref, c_ref, qt_ref, kt_ref, near_ref, p_ref,
                   u_ref, inv_ref, psi_ref, x_ref, y_ref, done=None):
    n = c_ref.shape[0]
    rows, cols = iotas(n)
    strength = c_ref[...]
    us2 = []
    for h in range(heads):
        raw = r_ref[:, head_cols(h)]
        inv, root = house_terms(raw, strength, heads, h)
        u = raw * (inv * root)
        u_ref[:, head_cols(h)] = u
        u2 = split(u)
        us2.append(u2)
        low = jnp.where(rows > cols, dot3(u2, u2, 1, 1), 0.0)
        psi_ref[h] = low
        inv_ref[h] = jnp.where(rows == cols, 1.0, 0.0) - jnp.where(rows // 2 == cols // 2, low, 0.0)

    def double(step, carry):
        apart = jnp.right_shift(rows, step) != jnp.right_shift(cols, step)
        pick = apart & (jnp.right_shift(rows, step + 1) == jnp.right_shift(cols, step + 1))
        halves = [split(inv_ref[h]) for h in range(heads)]
        mids = [dot3(split(jnp.where(pick, psi_ref[h], 0.0)), halves[h], 1, 0) for h in range(heads)]
        for h in range(heads):
            inv_ref[h] = inv_ref[h] - dot3(halves[h], split(mids[h]), 1, 0)
        return carry

    lax.fori_loop(1, (n - 1).bit_length(), double, 0)
    for h in range(heads):
        kin = split(inv_ref[h])
        q = q_ref[:, head_cols(h)]
        k = k_ref[:, head_cols(h)]
        q2, k2, u2 = split(q), split(k), us2[h]
        a = jnp.where(rows > cols, dot3(u2, k2, 1, 1), 0.0)
        aq = jnp.where(rows < cols, dot3(k2, u2, 1, 1), 0.0)
        fq = jnp.where(rows >= cols, dot3(q2, u2, 1, 1), 0.0)
        fq2 = split(fq)
        x = dot3(kin, u2, 1, 0)
        y = dot3(kin, u2, 0, 0)
        psi = dot3(kin, split(a), 1, 0)
        x2 = split(x)
        x_ref[:, head_cols(h)] = x
        y_ref[:, head_cols(h)] = y
        psi_ref[h] = psi
        qt_ref[:, head_cols(h)] = (q - dot3(fq2, x2, 1, 0)).astype(BF)
        kt_ref[:, head_cols(h)] = (k - dot3(split(aq), split(y), 1, 0)).astype(BF)
        near_ref[h] = dot3(q2, k2, 1, 1) - dot3(fq2, split(psi), 1, 0)
        er, ec = iotas(HDIM)
        p_ref[h] = (jnp.where(er == ec, 1.0, 0.0) - dot3(u2, x2, 0, 0)).astype(p_ref.dtype)
        if done is not None:
            done(h)


def path_fwd_kernel(heads, *refs):
    path_fwd_stage(heads, *refs)


def path_fwd(q, k, r, c, heads):
    n, width = q.shape
    flat = jax.ShapeDtypeStruct((n, width), F32)
    low = jax.ShapeDtypeStruct((n, width), BF)
    square = jax.ShapeDtypeStruct((heads, n, n), F32)
    return pl.pallas_call(
        functools.partial(path_fwd_kernel, heads),
        out_shape=(low, low, square, jax.ShapeDtypeStruct((heads, HDIM, HDIM), F32),
                   flat, square, square, flat, flat),
        compiler_params=pltpu.CompilerParams(vmem_limit_bytes=VMEM_LIMIT),
        name="path_fwd",
    )(q, k, r, c)


def doc_of(pos, len_ref):
    total = len_ref[0]
    doc = (pos >= total).astype(jnp.int32)
    for i in range(1, len_ref.shape[0]):
        total = total + len_ref[i]
        doc = doc + (pos >= total).astype(jnp.int32)
    return doc


def chain_slot(r, m):
    return r * (r - 1) // 2 + m


def key_chain(hops, h, fp_ref, chain_ref):
    cs = head_cols(h)
    for r in range(2, hops + 1):
        keys = chain_ref[chain_slot(r, 0), :, cs]
        for m in range(1, r):
            keys = dot(keys, fp_ref[r - m - 1, h].astype(BF), 1, 1).astype(BF)
            chain_ref[chain_slot(r, m), :, cs] = keys


def attn_fwd_rows(hops, h, start, count, row, len_ref, qt_ref, near_ref, v_ref, fv_ref, chain_ref,
                  o_ref, p_ref, rcp_ref, s_ref):
    n = qt_ref.shape[0]
    scale = HDIM ** (-0.5)
    cs, rs = head_cols(h), slice(start, start + count)
    rows = start + lax.broadcasted_iota(jnp.int32, (count, n), 0)
    cols = lax.broadcasted_iota(jnp.int32, (count, n), 1)
    own = doc_of(row * n + rows, len_ref)
    near_ok = (rows >= cols) & (own == doc_of(row * n + cols, len_ref))
    q = qt_ref[rs, cs]
    s = jnp.where(near_ok, near_ref[h, rs, :] * scale, neg_big)
    s_ref[0:count, :] = s
    top = jnp.max(s, 1, keepdims=True)
    for r in range(1, hops + 1):
        source = row - r
        docs = jnp.where(source >= 0, doc_of(source * n + cols, len_ref), -1)
        keys = chain_ref[chain_slot(r, r - 1), :, cs]
        s = jnp.where(own == docs, dot(q, keys, 1, 1) * scale, neg_big)
        s_ref[r * count:(r + 1) * count, :] = s
        top = jnp.maximum(top, jnp.max(s, 1, keepdims=True))
    total = jnp.zeros((count, 1), F32)
    out = jnp.zeros((count, HDIM), F32)
    for r in range(hops + 1):
        e = jnp.exp(s_ref[r * count:(r + 1) * count, :] - top)
        total = total + jnp.sum(e, 1, keepdims=True)
        weights = e.astype(BF)
        p_ref[r, h, rs, :] = weights
        out = out + dot(weights, v_ref[:, cs] if r == 0 else fv_ref[r - 1, :, cs], 1, 0)
    recip = 1.0 / total
    rcp_ref[rs, h:h + 1] = recip
    o_ref[rs, cs] = (out * recip).astype(BF)


def attn_fwd_kernel(heads, hops, len_ref, row_ref, qt_ref, near_ref, v_ref, fk_ref, fv_ref, fp_ref,
                    o_ref, p_ref, chain_ref, rcp_ref, s_ref):
    for r in range(1, hops + 1):
        chain_ref[chain_slot(r, 0)] = fk_ref[r - 1]
    for h in range(heads):
        key_chain(hops, h, fp_ref, chain_ref)
        attn_fwd_rows(hops, h, 0, qt_ref.shape[0], row_ref[0], len_ref, qt_ref, near_ref, v_ref, fv_ref, chain_ref,
                      o_ref, p_ref, rcp_ref, s_ref)


def attn_fwd(lengths, my_row, qt, near, v, far_k, far_v, far_p, heads, hops):
    n, width = qt.shape
    slots = hops * (hops + 1) // 2
    smem = pl.BlockSpec(memory_space=pltpu.SMEM)
    vmem = pl.BlockSpec(memory_space=pltpu.VMEM)
    return pl.pallas_call(
        functools.partial(attn_fwd_kernel, heads, hops),
        in_specs=[smem, smem] + [vmem] * 6,
        out_shape=(
            jax.ShapeDtypeStruct((n, width), BF),
            jax.ShapeDtypeStruct((hops + 1, heads, n, n), BF),
            jax.ShapeDtypeStruct((slots, n, width), BF),
            jax.ShapeDtypeStruct((n, heads), F32),
        ),
        scratch_shapes=[pltpu.VMEM(((hops + 1) * n, n), F32)],
        compiler_params=pltpu.CompilerParams(vmem_limit_bytes=VMEM_LIMIT),
        name="attn_fwd",
    )(lengths, my_row, qt, near, v, far_k, far_v, far_p)


def attn_bwd_kernel(heads, hops, p_ref, rcp_ref, go_ref, qt_ref, v_ref, fv_ref, fp_ref, chain_ref,
                    gqt_ref, gnear_ref, gv_ref, sendk_ref, sendv_ref, sendp_ref, dp_ref):
    for h in range(heads):
        attn_bwd_head(hops, h, p_ref, rcp_ref, go_ref[:, head_cols(h)], qt_ref, v_ref, fv_ref, fp_ref, chain_ref,
                      gqt_ref, gnear_ref, gv_ref, sendk_ref, sendv_ref, sendp_ref, dp_ref)


def attn_bwd(p, rcp, go, qt, v, far_v, far_p, chain, heads, hops):
    n, width = qt.shape
    return pl.pallas_call(
        functools.partial(attn_bwd_kernel, heads, hops),
        out_shape=(
            jax.ShapeDtypeStruct((n, width), F32),
            jax.ShapeDtypeStruct((heads, n, n), F32),
            jax.ShapeDtypeStruct((n, width), F32),
            jax.ShapeDtypeStruct((hops, n, width), BF),
            jax.ShapeDtypeStruct((hops, n, width), BF),
            jax.ShapeDtypeStruct((hops - 1, heads, HDIM, HDIM), BF),
        ),
        scratch_shapes=[pltpu.VMEM(((hops + 1) * n, n), F32)],
        compiler_params=pltpu.CompilerParams(vmem_limit_bytes=VMEM_LIMIT),
        name="attn_bwd",
    )(p, rcp, go, qt, v, far_v, far_p, chain)


def path_bwd_kernel(heads, q_ref, k_ref, r_ref, c_ref, u_ref, inv_ref, psi_ref, x_ref, y_ref,
                    gqt_ref, gkt_ref, gnear_ref, gp_ref, gq_ref, gk_ref, gr_ref, gc_ref):
    lane = lax.broadcasted_iota(jnp.int32, c_ref.shape, 1)
    gc_all = jnp.zeros(c_ref.shape, F32)
    for h in range(heads):
        cs = head_cols(h)
        gq, gk, gr, gc = path_bwd_head(h, heads, q_ref, k_ref, r_ref, c_ref, u_ref, inv_ref, psi_ref, x_ref, y_ref,
                                       gqt_ref[:, cs], gkt_ref[:, cs], gnear_ref[h], gp_ref[h])
        gq_ref[:, cs] = gq
        gk_ref[:, cs] = gk
        gr_ref[:, cs] = gr
        gc_all = jnp.where(lane == h, gc, gc_all)
    gc_ref[...] = gc_all.astype(BF)


def path_bwd(q, k, r, c, saved, gqt, gkt, gnear, gp, heads):
    n, width = q.shape
    low = jax.ShapeDtypeStruct((n, width), BF)
    return pl.pallas_call(
        functools.partial(path_bwd_kernel, heads),
        out_shape=(low, low, low, jax.ShapeDtypeStruct((n, heads), BF)),
        compiler_params=pltpu.CompilerParams(vmem_limit_bytes=VMEM_LIMIT),
        name="path_bwd",
    )(q, k, r, c, *saved, gqt, gkt, gnear, gp)


MESH = pl.DeviceIdType.MESH


class Copies:
    def __init__(self, send, recv):
        self.send, self.recv, self.count, self.open = send, recv, 0, []

    def take(self):
        self.count = self.count + 1
        return self.count - 1

    def make(self, src, dst, device, send, recv):
        return pltpu.make_async_remote_copy(
            src_ref=src, dst_ref=dst, send_sem=self.send.at[send], recv_sem=self.recv.at[recv],
            device_id=device, device_id_type=MESH)

    def begin(self, copy):
        copy.start()
        self.open.append(copy)
        return copy

    def start(self, src, dst, device):
        i = self.take()
        return self.begin(self.make(src, dst, device, i, i))

    def sent(self, some):
        for copy in some:
            copy.wait_send()
        self.open = [copy for copy in self.open if all(copy is not other for other in some)]


class Loads:
    def __init__(self, sems):
        self.sems, self.count = sems, 0

    def start(self, src, dst):
        copy = pltpu.make_async_copy(src, dst, self.sems.at[self.count])
        self.count = self.count + 1
        copy.start()
        return copy


class Place:
    def __init__(self, sizes):
        self.seq_n, self.hid_n, self.wid_n = sizes
        self.seq = lax.axis_index("seq")
        self.hid = lax.axis_index("hid")
        self.wid = lax.axis_index("wid")
        self.rows_n = self.seq_n * self.hid_n
        self.row = self.seq * self.hid_n + self.hid

    def wid_peer(self, i):
        return lax.rem(self.wid + i, self.wid_n)

    def hid_peer(self, i):
        return lax.rem(self.hid + i, self.hid_n)

    def seq_peer(self, i):
        return lax.rem(self.seq + i, self.seq_n)

    def row_peer(self, i):
        to = lax.rem(self.row + i + self.rows_n, self.rows_n)
        return {"seq": to // self.hid_n, "hid": lax.rem(to, self.hid_n)}

    def barrier(self):
        sem = pltpu.get_barrier_semaphore()
        for i in range(1, self.wid_n):
            pl.semaphore_signal(sem, inc=1, device_id={"wid": self.wid_peer(i)}, device_id_type=MESH)
        for i in range(1, self.rows_n):
            pl.semaphore_signal(sem, inc=1, device_id=self.row_peer(i), device_id_type=MESH)
        pl.semaphore_wait(sem, self.wid_n - 1 + self.rows_n - 1)


class Sometimes:
    def __init__(self, copy, sends=None, gets=None):
        self.copy, self.sends, self.gets = copy, sends, gets

    def on(self, flag, act):
        if flag is None:
            act()
        else:
            pl.when(flag)(act)

    def start(self):
        self.on(self.sends, lambda: self.copy.start() and None)

    def wait_send(self):
        self.on(self.sends, self.copy.wait_send)

    def wait_recv(self):
        self.on(self.gets, self.copy.wait_recv)


class LineGather:
    def __init__(self, copies, place, src, view):
        me = place.wid
        self.me, self.copies, self.view = me, copies, view
        self.ids = [copies.take() for _ in range(3)]
        here = view(me)
        self.by = {i: copies.make(src, here, {"wid": place.wid_peer(i)}, self.ids[i - 1], self.ids[i - 1])
                   for i in (1, 2, 3)}
        self.by[1] = Sometimes(self.by[1], me != 3)
        self.by[3] = Sometimes(self.by[3], me != 0)
        for i in (2, 1, 3):
            copies.begin(self.by[i])

    def relay(self):
        self.by[2].wait_recv()
        for m, chunk, to, i in ((1, 3, 0, 1), (2, 0, 3, 3)):
            part = self.view(chunk)
            copy = self.copies.make(part, part, {"wid": to}, self.copies.take(), self.ids[i - 1])
            self.copies.begin(Sometimes(copy, self.me == m))

    def wait(self):
        self.by[1].wait_recv()
        self.by[3].wait_recv()


class LineSwap:
    def __init__(self, copies, place, piece, recv):
        self.copies, self.place, self.me, self.piece, self.recv = copies, place, place.wid, piece, recv
        self.ids = [copies.take() for _ in range(4)]
        me = self.me

        @pl.when(me == 0)
        def _():
            recv(0)[...] = jnp.zeros(recv(0).shape, BF)

        @pl.when(me == 3)
        def _():
            recv(2)[...] = jnp.zeros(recv(2).shape, BF)

    def make(self, src, i, slot, device, send):
        return self.copies.make(src, self.recv(slot), device, send, self.ids[slot])

    def start_far(self):
        self.far = []
        for end, far, middle in ((0, 3, 1), (3, 0, 2)):
            copy = Sometimes(self.make(self.piece(far), 0, 3, {"wid": middle}, self.copies.take()),
                             self.me == end, self.me == middle)
            self.copies.begin(copy)
            self.far.append(copy)

    def start(self):
        me, place = self.me, self.place
        to = [place.wid_peer(i) for i in range(4)]
        self.two = Sometimes(self.make(self.piece(to[2]), 2, 1, {"wid": to[2]}, self.ids[1]), (me == 0) | (me == 3))
        self.one = Sometimes(self.make(self.piece(to[1]), 1, 0, {"wid": to[1]}, self.ids[0]), me != 3, me != 0)
        self.three = Sometimes(self.make(self.piece(to[3]), 3, 2, {"wid": to[3]}, self.ids[2]), me != 0, me != 3)
        for copy in (self.two, self.one, self.three):
            self.copies.begin(copy)

    def combine(self):
        for copy in self.far:
            copy.wait_recv()
        mid = (self.me == 1) | (self.me == 2)
        far = 3 * (2 - jnp.minimum(jnp.maximum(self.me, 1), 2))

        @pl.when(mid)
        def _():
            at = self.recv(3)
            at[...] = (at[...].astype(F32) + self.piece(far)[...].astype(F32)).astype(BF)

        copy = self.make(self.recv(3), 2, 1, {"wid": far}, self.copies.take())
        self.copies.begin(Sometimes(copy, mid))

    def total(self, own):
        for copy in (self.two, self.one, self.three):
            copy.wait_recv()
        for slot in range(3):
            own = own + self.recv(slot)[...].astype(F32)
        return own


def aligned(start, size, step):
    return pl.ds(pl.multiple_of(start, step), size)


def attn_bwd_head(hops, h, p_ref, rcp_ref, go, qt_ref, v_ref, fv_ref, fp_ref, chain_ref,
                  gqt_ref, gnear_ref, gv_ref, sendk_ref, sendv_ref, sendp_ref, dp_ref):
    n = qt_ref.shape[0]
    scale = HDIM ** (-0.5)
    cs = head_cols(h)
    q = qt_ref[:, cs]
    recip = rcp_ref[:, h:h + 1]
    go_low = (go.astype(F32) * recip).astype(BF)
    delta = jnp.zeros((n, 1), F32)
    for r in range(hops + 1):
        vals = v_ref[:, cs] if r == 0 else fv_ref[r - 1, :, cs]
        dp = dot(go, vals, 1, 1)
        dp_ref[r * n:(r + 1) * n, :] = dp
        delta = delta + jnp.sum(p_ref[r, h].astype(F32) * dp, 1, keepdims=True)
        gv = dot(p_ref[r, h], go_low, 0, 0)
        if r == 0:
            gv_ref[:, cs] = gv
        else:
            sendv_ref[r - 1, :, cs] = gv.astype(BF)
    delta = delta * recip
    factor = recip * scale
    gnear_ref[h] = p_ref[0, h].astype(F32) * ((dp_ref[0:n, :] - delta) * factor)
    gq = jnp.zeros((n, HDIM), F32)
    gps = [jnp.zeros((HDIM, HDIM), F32) for _ in range(hops - 1)]
    for r in range(1, hops + 1):
        gs = (p_ref[r, h].astype(F32) * ((dp_ref[r * n:(r + 1) * n, :] - delta) * factor)).astype(BF)
        gq = gq + dot(gs, chain_ref[chain_slot(r, r - 1), :, cs], 1, 0)
        gk = dot(gs, q, 0, 0)
        for m in range(r - 1, 0, -1):
            back = r - m - 1
            gkb = gk.astype(BF)
            gps[back] = gps[back] + dot(gkb, chain_ref[chain_slot(r, m - 1), :, cs], 0, 0)
            gk = dot(gkb, fp_ref[back, h].astype(BF), 1, 0)
        sendk_ref[r - 1, :, cs] = gk.astype(BF)
    gqt_ref[:, cs] = gq
    for i in range(hops - 1):
        sendp_ref[i, h] = gps[i].astype(BF)


def path_bwd_head(h, heads, q_ref, k_ref, r_ref, c_ref, u_ref, inv_ref, psi_ref, x_ref, y_ref,
                  gqt, gkt, gs, gp):
    n = c_ref.shape[0]
    rows, cols = iotas(n)
    cs = head_cols(h)
    q, k, u = q_ref[:, cs], k_ref[:, cs], u_ref[:, cs]
    qb, kb, ub = q.astype(BF), k.astype(BF), u.astype(BF)
    kin = inv_ref[h].astype(BF)
    psi = psi_ref[h].astype(BF)
    x, y = x_ref[:, cs].astype(BF), y_ref[:, cs].astype(BF)
    gqtb, gktb = gqt.astype(BF), gkt.astype(BF)
    gsb = gs.astype(BF)
    gst = gs.T.astype(BF)
    gp = gp.astype(BF)
    f = jnp.where(rows <= cols, dot(ub, qb, 1, 1), 0.0).astype(BF)
    fq = jnp.where(rows >= cols, dot(qb, ub, 1, 1), 0.0).astype(BF)
    a = jnp.where(rows > cols, dot(ub, kb, 1, 1), 0.0).astype(BF)
    gx = -(dot(f, gqtb, 1, 0) + dot(ub, gp, 1, 0))
    gy = -dot(a, gktb, 1, 0)
    phiq = dot(fq, kin, 1, 0).astype(BF)
    back = dot(gst, phiq, 1, 0)
    backb = back.astype(BF)
    gfq = jnp.where(rows >= cols, -(dot(gqtb, x, 1, 1) + dot(gsb, psi, 1, 1)), 0.0)
    gaq = jnp.where(rows < cols, -(dot(gktb, y, 1, 1) + back), 0.0)
    kgx = dot(kin, gx.astype(BF), 0, 0)
    kgy = dot(kin, gy.astype(BF), 1, 0)
    zt = dot(x, kgx.astype(BF), 1, 1) + dot(kgy.astype(BF), y, 1, 1) - dot(psi, backb, 1, 0)
    glt = jnp.where(rows < cols, -zt, 0.0)
    sym = (glt + glt.T).astype(BF)
    gfqb, gaqb = gfq.astype(BF), gaq.astype(BF)
    gu = (kgx + kgy - dot(x, gp, 1, 1) + dot(gfq.T.astype(BF), qb, 1, 0)
          + dot(gaq.T.astype(BF), kb, 1, 0) + dot(sym, ub, 1, 0))
    gq = (gqt + dot(gsb, kb, 1, 0) + dot(gfqb, ub, 1, 0)).astype(BF)
    gk = (gkt + dot(gst, qb, 1, 0) + dot(gaqb, ub, 1, 0)).astype(BF)
    raw = r_ref[:, cs]
    inv, root = house_terms(raw, c_ref[...], heads, h)
    gc = jnp.sum(gu * u, 1, keepdims=True) * (1.0 - 0.5 * root * root) * 0.5
    gun = gu * root
    un = raw * inv
    gr = (inv * (gun - un * jnp.sum(gun * un, 1, keepdims=True))).astype(BF)
    return gq, gk, gr, gc


class Heads:
    def __init__(self, ref, kind):
        self.ref, self.kind = ref, kind

    def __getitem__(self, index):
        base = 3 * index[1].start + self.kind * HDIM
        return self.ref[index[0], base:base + HDIM]


def turned(index, by):
    low = index % 2
    high = index // 2 % 2
    return index + (1 - 2 * low) * (by % 2) + (2 - 4 * high) * (by // 2)


def step_kernel(cfg, names, *refs):
    heads, hops, sizes = cfg
    R = types.SimpleNamespace(**dict(zip(names, refs)))
    place = Place(sizes)
    wid_n, hid_n, seq_n = place.wid_n, place.hid_n, place.seq_n
    n, col = R.x.shape
    width = heads * HDIM
    model = R.act.shape[1]
    ff = R.wg.shape[1]
    sub = n // wid_n
    half = model // seq_n
    piece = model // place.rows_n
    copies, loads = Copies(R.send_sem, R.recv_sem), Loads(R.load_sem)
    my_cols = aligned(place.wid * col, col, 128)
    part_n = n // 2
    step_n = sub // 2

    def rows_of(w, hh):
        return aligned(hh * part_n + w * step_n, step_n, step_n)

    def half_of(hh):
        return slice(hh * step_n, (hh + 1) * step_n)

    def own_rows(ref):
        return jnp.concatenate([ref[rows_of(place.wid, hh), :].astype(F32) for hh in range(2)], 0)

    mine = aligned(place.seq * half, half, 128)
    other = aligned((1 - place.seq) * half, half, 128)
    sibling = {"seq": 1 - place.seq}
    order = sorted(range(1, wid_n), key=lambda i: -min(i, wid_n - i))
    to_wid = [{"wid": place.wid_peer(i)} for i in order]
    near = [{"hid": turned(place.hid, j)} for j in range(hid_n)]

    R.gain_in[0:1, :] = R.gain_attn[...].astype(F32).reshape(1, col)
    R.gain_in[1:2, :] = R.gain_ffn[...].astype(F32).reshape(1, col)
    R.xall[:, my_cols] = R.x[...]
    R.gall[:, my_cols] = R.gain_in[...]
    place.barrier()

    get_x = LineGather(copies, place, R.x, lambda c: R.xall.at[:, aligned(c * col, col, 128)])
    get_gains = [copies.start(R.gain_in, R.gall.at[:, my_cols], d) for d in to_wid]

    part_f = ff // seq_n
    mine_c = aligned(place.seq * half, half, 16)
    mine_f = aligned(place.seq * part_f, part_f, 16)

    def cols_of(j):
        return pl.ds(j * ff, ff)

    def down_rows(j, piece_i=0, pieces=1):
        size = part_f // pieces
        return aligned(j * ff + place.seq * part_f + piece_i * size, size, 16)

    def pass_on(ref, device):
        return copies.start(ref, ref, device)

    get_gate = [copies.start(R.wg.at[mine_c, :], R.wg_s.at[mine_c, cols_of(j)], near[j]) for j in (1, 2)]
    get_up = [copies.start(R.wu.at[mine_c, :], R.wu_s.at[mine_c, cols_of(j)], near[j]) for j in (1, 2)]
    load_v = loads.start(R.wv, R.w_s.at[:, pl.ds(3 * width, width)])
    load_w = [loads.start(w.at[:, pl.ds(h * HDIM, HDIM)], R.w_s.at[:, pl.ds((3 * h + m) * HDIM, HDIM)])
              for h in range(heads) for m, w in enumerate((R.wq, R.wk, R.wr))]
    load_dy = loads.start(R.dy, R.dyall.at[:, my_cols])
    load_o = loads.start(R.wo, R.wo_s)
    load_f = [loads.start(R.wg, R.wg_s.at[:, pl.ds(0, ff)]), loads.start(R.wu, R.wu_s.at[:, pl.ds(0, ff)]),
              loads.start(R.wd, R.wd_s.at[pl.ds(0, ff), :])]

    get_x.relay()
    get_x.wait()
    for copy in get_gains:
        copy.wait_recv()
    get_dy = [copies.start(R.dy, R.dyall.at[:, my_cols], d) for d in to_wid]
    xf = R.xall[...].astype(F32)
    inv_rms = lax.rsqrt(jnp.mean(xf * xf, -1, keepdims=True) + eps_norm)
    R.inv_rms[...] = inv_rms
    R.act[...] = (xf * inv_rms * R.gall[0:1, :]).astype(BF)
    load_v.wait()
    R.v[...] = dot(R.act[...], R.w_s[:, 3 * width:4 * width], 1, 0).astype(BF)
    get_v = [copies.start(R.v, R.fv.at[i - 1], place.row_peer(i)) for i in range(1, hops + 1)]
    for copy in load_w:
        copy.wait()
    R.proj[...] = dot(R.act[...], R.w_s[:, 0:3 * width], 1, 0)
    R.c[...] = dot(R.act[...], R.wb[...], 1, 1)

    get_k = [[] for _ in range(heads)]
    get_p = [[] for _ in range(heads)]

    def send_head(h):
        cs = head_cols(h)
        for i in range(1, hops + 1):
            get_k[h].append(copies.start(R.kt_s.at[:, cs], R.chain.at[chain_slot(i, 0), :, cs], place.row_peer(i)))
        for i in range(1, hops):
            get_p[h].append(copies.start(R.prod_s.at[h], R.fp.at[i - 1, h], place.row_peer(i)))

    path_fwd_stage(heads, Heads(R.proj, 0), Heads(R.proj, 1), Heads(R.proj, 2), R.c, R.qt, R.kt_s, R.near_s, R.prod_s,
                   R.u, R.inv, R.psi, R.x1, R.y1, send_head)

    for copy in get_gate + get_up:
        copy.wait_recv()
    relay = [copies.start(R.wg_s.at[mine_c, cols_of(1)], R.wg_s.at[mine_c, cols_of(3)], near[2]),
             copies.start(R.wu_s.at[mine_c, cols_of(2)], R.wu_s.at[mine_c, cols_of(3)], near[1])]
    get_down = [copies.start(R.wd.at[mine_f, :], R.wd_s.at[down_rows(j), :], near[j]) for j in (1, 2)]

    for copy in get_v:
        copy.wait_recv()
    load_o.wait()
    get_a = []
    for hh in range(2):
        for h in range(heads):
            if hh == 0:
                for copy in get_k[h] + get_p[h]:
                    copy.wait_recv()
                key_chain(hops, h, R.fp, R.chain)
            attn_fwd_rows(hops, h, hh * part_n, part_n, place.row, R.lengths, R.qt, R.near_s, R.v, R.fv, R.chain,
                          R.o, R.probs, R.rcp, R.s_s)
        rs = slice(hh * part_n, (hh + 1) * part_n)
        R.part_s[rs, :] = dot(R.o[rs, :], R.wo_s[...], 1, 0).astype(BF)
        get_a.append(LineSwap(copies, place, functools.partial(lambda hh, c: R.part_s.at[rows_of(c, hh), :], hh),
                              functools.partial(lambda hh, q: R.recv_s.at[q, pl.ds(hh * step_n, step_n), :], hh)))
        get_a[hh].start_far()
        get_a[hh].start()
    three = pl.ds(ff, 3 * ff)
    get_i = []

    def mix(hh):
        at, keep = rows_of(place.wid, hh), half_of(hh)
        mixed = get_a[hh].total(R.xall[at, :].astype(F32) + R.part_s[at, :].astype(F32))
        R.mixed[keep, :] = mixed
        inv_two = lax.rsqrt(jnp.mean(mixed * mixed, -1, keepdims=True) + eps_norm)
        R.row_s[keep, :] = (mixed * inv_two * R.gall[1:2, :]).astype(BF)
        get_i.append(LineGather(copies, place, R.row_s.at[pl.ds(hh * step_n, step_n), :],
                                functools.partial(lambda hh, c: R.inner.at[rows_of(c, hh), :], hh)))
        R.inner[at, :] = R.row_s[keep, :]

    get_a[0].combine()
    mix(0)
    get_a[1].combine()
    for copy in relay:
        copy.wait_recv()
    shared = [pass_on(ref.at[mine_c, three], sibling) for ref in (R.wg_s, R.wu_s)]
    for copy in get_down:
        copy.wait_recv()
    relay_d = [copies.start(R.wd_s.at[down_rows(1, 0, 2), :], R.wd_s.at[down_rows(3, 0, 2), :], near[2]),
               copies.start(R.wd_s.at[down_rows(2, 1, 2), :], R.wd_s.at[down_rows(3, 1, 2), :], near[1])]
    mix(1)
    get_i[0].relay()
    for copy in relay_d:
        copy.wait_recv()
    shared += [pass_on(R.wd_s.at[down_rows(j), :], sibling) for j in (1, 2, 3)]
    twin_a = [copies.start(R.act.at[:, other], R.twin_act, sibling),
              copies.start(R.o, R.twin_o, sibling)]
    load_dy.wait()
    for copy in load_f:
        copy.wait()
    get_i[1].relay()
    for copy in get_dy + shared:
        copy.wait_recv()
    for part in get_i:
        part.wait()
    twin = [copies.start(R.inner.at[:, other], R.twin_inner, sibling),
            copies.start(R.dyall.at[:, other], R.twin_dy, sibling)]

    def hidden_tile(t, carry):
        cs = aligned(t * ff, ff, 128)
        gate = dot(R.inner[...], R.wg_s[:, cs], 1, 0)
        up = dot(R.inner[...], R.wu_s[:, cs], 1, 0)
        g_hidden = dot(R.dyall[...], R.wd_s[cs, :], 1, 1)
        sig = 1.0 / (1.0 + jnp.exp(-gate))
        silu = gate * sig
        R.hidden[0:n, cs] = (silu * up).astype(BF)
        R.ggate[0:n, cs] = (g_hidden * up * sig * (1.0 + gate * (1.0 - sig))).astype(BF)
        R.gup[0:n, cs] = (g_hidden * silu).astype(BF)
        return carry

    lax.fori_loop(0, hid_n, hidden_tile, 0)

    twin += [copies.start(ref.at[pl.ds(0, n), :], ref.at[pl.ds(n, n), :], sibling)
            for ref in (R.hidden, R.ggate, R.gup)]

    def grad_tile(t, carry):
        cs = aligned(t * col, col, 128)
        tile = (dot(R.ggate[0:n, :], R.wg_s[cs, :], 1, 1) + dot(R.gup[0:n, :], R.wu_s[cs, :], 1, 1)).astype(BF)
        for w in range(wid_n):
            for hh in range(2):
                R.gin[w * sub + hh * step_n:w * sub + (hh + 1) * step_n, cs] = (
                    tile[hh * part_n + w * step_n:hh * part_n + (w + 1) * step_n, :])
        return carry

    lax.fori_loop(0, wid_n, grad_tile, 0)
    before = list(copies.open)
    get_g = LineSwap(copies, place, lambda c: R.gin.at[aligned(c * sub, sub, sub), :],
                     lambda q: R.recv_s.at[q] if q < 3 else R.recv_far)
    get_g.start_far()
    get_g.start()

    copies.sent(before)
    get_g.combine()
    for copy in twin:
        copy.wait_recv()
    R.left_t[:, 0:n] = R.inner[:, mine].T
    R.left_t[:, n:2 * n] = R.twin_inner[...].T
    down_a, down_b = pl.ds(0, half // 2), pl.ds(half // 2, half // 2)

    upper, lower = pl.ds(0, half), pl.ds(half, half)

    def ffn_grads(j):
        cs = slice(j * ff, (j + 1) * ff)
        R.wg_s[0:half, cs] = dot(R.left_t[...], R.ggate[:, cs], 1, 0).astype(BF)
        R.wg_s[half:2 * half, cs] = dot(R.left_t[...], R.gup[:, cs], 1, 0).astype(BF)
        down = dot(R.hidden[0:n, cs], R.dyall[:, mine], 0, 0) + dot(R.hidden[n:2 * n, cs], R.twin_dy[...], 0, 0)
        R.wu_s[cs, 0:half] = down.astype(BF)

    def first_round(j, slot, rows, lanes, to, gus, downs):
        return [copies.start(R.wg_s.at[rows, cols_of(j)], gus.at[slot], to),
                copies.start(R.wu_s.at[cols_of(j), lanes], downs.at[slot], to)]

    ffn_grads(3)
    get_r1 = (first_round(3, 1, upper, down_a, near[1], R.gu_x, R.dn_x)
              + first_round(3, 1, lower, down_b, near[2], R.gu_y, R.dn_y))
    ffn_grads(1)
    keep_r1 = first_round(1, 0, upper, down_a, near[1], R.gu_x, R.dn_x)
    ffn_grads(2)
    keep_r1 += first_round(2, 0, lower, down_b, near[2], R.gu_y, R.dn_y)
    ffn_grads(0)

    def out_tile(t, carry):
        cs = aligned(t * col, col, 128)
        R.part_s[:, cs] = (dot(R.hidden[0:n, :], R.wd_s[:, cs], 1, 0) + R.part_s[:, cs].astype(F32)).astype(BF)
        return carry

    lax.fori_loop(0, wid_n, out_tile, 0)

    g_inner = get_g.total(R.gin[aligned(place.wid * sub, sub, sub), :].astype(F32))
    mixed = R.mixed[...]
    inv_two = lax.rsqrt(jnp.mean(mixed * mixed, -1, keepdims=True) + eps_norm)
    n_two = mixed * inv_two
    scaled = g_inner * R.gall[1:2, :]
    g_mixed = (own_rows(R.dyall)
               + inv_two * (scaled - n_two * jnp.mean(scaled * n_two, -1, keepdims=True)))
    R.row_g[...] = g_mixed.astype(BF)
    get_z = []
    for hh in range(2):
        at = rows_of(place.wid, hh)
        get_z.append(LineGather(copies, place, R.row_g.at[pl.ds(hh * step_n, step_n), :],
                                functools.partial(lambda hh, c: R.gz.at[rows_of(c, hh), :], hh)))
        R.gz[at, :] = R.row_g[half_of(hh), :]
    R.gpart[1:2, :] = jnp.sum(g_inner * n_two, 0, keepdims=True)
    for copy in twin_a:
        copy.wait_recv()
    for part in get_z:
        part.relay()
    get_f = []
    for slot, i in enumerate(order):
        peer = place.wid_peer(i)
        get_f.append(copies.start(R.part_s.at[:, aligned(peer * col, col, 128)], R.recv_f.at[slot], {"wid": peer}))

    for copy in get_r1:
        copy.wait_recv()
    add_g = R.wg_s.at[upper, cols_of(2)]
    add_g[...] = (add_g[...].astype(F32) + R.gu_x[1].astype(F32)).astype(BF)
    add_u = R.wg_s.at[lower, cols_of(1)]
    add_u[...] = (add_u[...].astype(F32) + R.gu_y[1].astype(F32)).astype(BF)
    add_a = R.wu_s.at[cols_of(2), down_a]
    add_a[...] = (add_a[...].astype(F32) + R.dn_x[1].astype(F32)).astype(BF)
    add_b = R.wu_s.at[cols_of(1), down_b]
    add_b[...] = (add_b[...].astype(F32) + R.dn_y[1].astype(F32)).astype(BF)
    get_r2 = [copies.start(add_g, R.gu_x.at[2], near[2]), copies.start(add_a, R.dn_x.at[2], near[2]),
              copies.start(add_u, R.gu_y.at[2], near[1]), copies.start(add_b, R.dn_y.at[2], near[1])]

    for part in get_z:
        part.wait()
    twin_z = copies.start(R.gz.at[:, other], R.twin_gz, sibling)

    gets = [[] for _ in range(heads)]
    for h in range(heads):
        cs = head_cols(h)
        go = dot(R.gz[...], R.wo_s[cs, :], 1, 1).astype(BF)
        attn_bwd_head(hops, h, R.probs, R.rcp, go, R.qt, R.v, R.fv, R.fp, R.chain,
                      R.gqt, R.near_s, R.gv, R.sendk, R.sendv, R.sendp, R.s_s)
        for i in range(1, hops + 1):
            to = place.row_peer(-i)
            gets[h].append(copies.start(R.sendv.at[i - 1, :, cs], R.recvv.at[i - 1, :, cs], to))
            gets[h].append(copies.start(R.sendk.at[i - 1, :, cs], R.recvk.at[i - 1, :, cs], to))
        for i in range(1, hops):
            gets[h].append(copies.start(R.sendp.at[i - 1, h], R.recvp.at[i - 1, h], place.row_peer(-i)))

    def left_of(ref, twin_ref):
        R.left_t[:, 0:n] = ref[:, mine].T
        R.left_t[:, n:2 * n] = twin_ref[...].T

    twin_z.wait_recv()
    left_of(R.gz, R.twin_gz)

    fine = piece // 2
    get_h = []

    def rows_at(j, lot):
        return aligned(turned(place.hid, j) * piece + lot * fine, fine, 32)

    def round_one(src, slot):
        sent = [copies.start(src.at[rows_at(3, lot), :], R.recv_q.at[slot, 2 * lot + 1], near[lot + 1]) for lot in range(2)]
        keep = [copies.start(src.at[rows_at(lot + 1, lot), :], R.recv_q.at[slot, 2 * lot], near[lot + 1]) for lot in range(2)]
        get_h.extend(keep)
        return sent

    def round_two(src, slot, sent):
        for lot in range(2):
            sent[lot].wait_recv()
            at = src.at[rows_at(2 - lot, lot), :]
            at[...] = (at[...].astype(F32) + R.recv_q[slot, 2 * lot + 1].astype(F32)).astype(BF)
            get_h.append(copies.start(at, R.recv_q.at[slot, 4 + lot], near[2 - lot]))

    R.wide_s[...] = dot(R.left_t[:, 0:n], R.o[...], 1, 0) + dot(R.left_t[:, n:2 * n], R.twin_o[...], 1, 0)
    R.d_out[...] = R.wide_s[aligned(place.hid * piece, piece, 64), :]
    R.send_o[...] = R.wide_s[...].astype(BF)
    slot_o, slot_v = heads + 1, heads
    sent_o = round_one(R.send_o, slot_o)
    left_of(R.act, R.twin_act)

    row8 = lax.broadcasted_iota(jnp.int32, (n, HDIM), 1)
    gc_all = jnp.zeros((n, HDIM), F32)
    val_cols = pl.ds(3 * width, width)
    twin_h = []

    def grad_part(slot):
        return R.wd_s.at[:, pl.ds(slot * width, width)]

    def weights_of(slot, outs_of):
        cs = slice(slot * width, (slot + 1) * width)
        R.wide_s[...] = dot(R.left_t[...], R.grads[:, cs], 1, 0)
        R.wd_s[0:half, cs] = R.wide_s[...].astype(BF)
        own = R.wide_s[aligned(place.hid * piece, piece, 64), :]
        for m, (ref, at) in enumerate(outs_of):
            ref[:, at] = own[:, head_cols(m)]
        return round_one(grad_part(slot), slot)

    def outs_of(h):
        return [(ref, head_cols(h)) for ref in (R.d_query, R.d_key, R.d_house)]

    val_outs = [(R.d_value, head_cols(m)) for m in range(heads)]
    sent_h = []
    for h in range(heads):
        for copy in gets[h]:
            copy.wait_recv()
        cs = head_cols(h)
        gkt = R.recvk[0, :, cs].astype(F32)
        gv = R.gv[:, cs] + R.recvv[0, :, cs].astype(F32)
        for i in range(1, hops):
            gkt = gkt + R.recvk[i, :, cs].astype(F32)
            gv = gv + R.recvv[i, :, cs].astype(F32)
        gp = R.recvp[0, h].astype(F32)
        for i in range(1, hops - 1):
            gp = gp + R.recvp[i, h].astype(F32)
        R.grads[0:n, (9 + h) * HDIM:(10 + h) * HDIM] = gv.astype(BF)
        if h == heads - 1:
            twin_v = copies.start(R.grads.at[pl.ds(0, n), val_cols], R.grads.at[pl.ds(n, n), val_cols], sibling)
        gq, gk, gr, gc = path_bwd_head(h, heads, Heads(R.proj, 0), Heads(R.proj, 1), Heads(R.proj, 2), R.c,
                                       R.u, R.inv, R.psi, R.x1, R.y1, R.gqt[:, cs], gkt, R.near_s[h], gp)
        gc_all = jnp.where(row8 == h, gc, gc_all)
        for m, val in enumerate((gq, gk, gr)):
            R.grads[0:n, (3 * h + m) * HDIM:(3 * h + m + 1) * HDIM] = val
        gs = pl.ds(h * width, width)
        twin_h.append(copies.start(R.grads.at[pl.ds(0, n), gs], R.grads.at[pl.ds(n, n), gs], sibling))
        if 0 < h:
            twin_h[h - 1].wait_recv()
            sent_h.append(weights_of(h - 1, outs_of(h - 1)))
    R.gcs[0:n, :] = gc_all.astype(BF)
    twin_c = copies.start(R.gcs.at[pl.ds(0, n), :], R.gcs.at[pl.ds(n, n), :], sibling)

    inv_rms = R.inv_rms[...]
    stat = jnp.zeros((n, 1), F32)
    get_n = LineSwap(copies, place, lambda c: R.send_n.at[c], lambda q: R.recv_n.at[q])
    me, side = place.wid, place.wid // 2
    for turn, c in enumerate((3 * (1 - side), 2 - side, (1 - side) * (1 - me) + side * (5 - me), me)):
        cs = aligned(c * col, col, 128)
        g_act = dot(R.grads[0:n, :], R.w_s[cs, :], 1, 1) + dot(R.gcs[0:n, 0:heads], R.wb[:, cs], 1, 0)
        normed = R.xall[:, cs].astype(F32) * inv_rms
        both = g_act * normed
        stat = stat + jnp.sum(both * R.gall[0:1, cs], 1, keepdims=True)
        R.gpart[0:1, cs] = jnp.sum(both, 0, keepdims=True)
        if turn == 3:
            R.own_n[...] = g_act
        else:
            R.send_n[c] = g_act.astype(BF)
        if turn == 0:
            get_n.start_far()
        if turn == 2:
            get_n.start()
    R.stat_s[...] = jnp.broadcast_to(stat, (n, HDIM)).T[0:8, :]
    get_s = [copies.start(R.stat_s, R.recv_st.at[slot], d) for slot, d in enumerate(to_wid)]
    twin_v.wait_recv()
    sent_v = weights_of(slot_v, val_outs)
    get_n.combine()
    twin_h[heads - 1].wait_recv()
    sent_h.append(weights_of(heads - 1, outs_of(heads - 1)))
    round_two(R.send_o, slot_o, sent_o)
    for h in range(heads - 1):
        round_two(grad_part(h), h, sent_h[h])
    round_two(grad_part(slot_v), slot_v, sent_v)
    twin_c.wait_recv()
    d_beta = dot(R.gcs[0:n, :], R.act[:, mine], 0, 0) + dot(R.gcs[n:2 * n, :], R.twin_act[...], 0, 0)
    R.beta_s[...] = d_beta[0:8, :]

    def window(p):
        return aligned(p * piece // 128 * 128, 256, 128)

    get_b = [copies.start(R.beta_s.at[:, window(turned(place.hid, j))], R.recv_b.at[j - 1], near[j])
             for j in range(1, hid_n)]
    get_gain = [copies.start(R.gpart.at[:, window(lax.rem(place.row + i, place.rows_n))], R.recv_gain.at[i - 1],
                             place.row_peer(i)) for i in range(1, place.rows_n)]

    round_two(grad_part(heads - 1), heads - 1, sent_h[heads - 1])
    gain = R.gpart[:, window(place.row)]
    for i, copy in enumerate(get_gain):
        copy.wait_recv()
        gain = gain + R.recv_gain[i]
    R.gain_s[...] = gain
    get_gain2 = [copies.start(R.gain_s, R.recv_gain2.at[slot], d) for slot, d in enumerate(to_wid)]
    for copy in get_r2 + keep_r1:
        copy.wait_recv()
    R.d_gate[...] = (R.wg_s[upper, 0:ff].astype(F32) + R.gu_x[0].astype(F32) + R.gu_x[2].astype(F32))
    R.d_up[...] = (R.wg_s[lower, 0:ff].astype(F32) + R.gu_y[0].astype(F32) + R.gu_y[2].astype(F32))
    for lanes, ref in ((down_a, R.dn_x), (down_b, R.dn_y)):
        R.d_down[:, lanes] = R.wu_s[0:ff, lanes].astype(F32) + ref[0].astype(F32) + ref[2].astype(F32)
    out = R.x[...].astype(F32) + R.part_s[:, my_cols].astype(F32)
    for slot, copy in enumerate(get_f):
        copy.wait_recv()
        out = out + R.recv_f[slot].astype(F32)
    R.output[...] = out.astype(BF)
    g_act = get_n.total(R.own_n[...])
    stats = R.stat_s[...]
    for slot in range(wid_n - 1):
        get_s[slot].wait_recv()
        stats = stats + R.recv_st[slot]
    mean = stats.T[:, 0:1] / model
    normed = R.xall[:, my_cols].astype(F32) * inv_rms
    R.d_inputs[...] = (R.gz[:, my_cols].astype(F32)
                       + inv_rms * (g_act * R.gall[0:1, my_cols] - normed * mean))
    for copy in get_h + get_b:
        copy.wait_recv()
    out_outs = [(R.d_out, head_cols(m)) for m in range(heads)]
    for slot, refs_of in [(slot_o, out_outs), (slot_v, val_outs)] + [(h, outs_of(h)) for h in range(heads)]:
        for m, (ref, at) in enumerate(refs_of):
            for lot in range(2):
                rs = slice(lot * fine, (lot + 1) * fine)
                ref[rs, at] = (ref[rs, at] + R.recv_q[slot, 2 * lot, :, head_cols(m)].astype(F32)
                               + R.recv_q[slot, 4 + lot, :, head_cols(m)].astype(F32))
    d_beta = R.beta_s[:, window(place.hid)]
    for i in range(hid_n - 1):
        d_beta = d_beta + R.recv_b[i]
    gain = R.gain_s[...]
    for slot, copy in enumerate(get_gain2):
        copy.wait_recv()
        gain = gain + R.recv_gain2[slot]

    def exact(rows, at):
        return jnp.where(at % 2 == 1, rows[:, 64:64 + piece], rows[:, 0:piece])

    R.d_beta[...] = exact(d_beta, place.hid)[0:heads, :]
    R.gain_out[...] = exact(gain, place.row)
    copies.sent(copies.open)


def step(args, heads, hops, sizes):
    ins = ("lengths", "x", "dy", "gain_attn", "gain_ffn", "wq", "wk", "wv", "wr", "wb", "wo", "wg", "wu", "wd")
    shapes = dict(zip(ins, (a.shape for a in args)))
    n, col = shapes["x"]
    seq_n, hid_n, wid_n = sizes
    model, width = shapes["wq"]
    ff = shapes["wg"][1]
    sub = n // wid_n
    rows_n = seq_n * hid_n
    half = model // seq_n
    piece = model // rows_n
    slots = hops * (hops + 1) // 2
    S = jax.ShapeDtypeStruct
    V = pltpu.VMEM
    outs = dict(
        output=S((n, col), BF), d_inputs=S((n, col), F32), gain_out=S((8, piece), F32),
        d_query=S((piece, width), F32), d_key=S((piece, width), F32), d_value=S((piece, width), F32),
        d_house=S((piece, width), F32), d_beta=S((heads, piece), F32), d_out=S((piece, width), F32),
        d_gate=S((half, ff), F32), d_up=S((half, ff), F32), d_down=S((ff, half), F32),
    )
    peers_w, peers_h = wid_n - 1, hid_n - 1
    scratch = dict(
        gain_in=V((8, col), F32), gall=V((8, model), F32), inv_rms=V((n, 1), F32),
        act=V((n, model), BF), xall=V((n, model), BF), dyall=V((n, model), BF),
        proj=V((n, 3 * width), F32), c=V((n, heads), F32), v=V((n, width), BF),
        qt=V((n, width), BF), u=V((n, width), F32), inv=V((heads, n, n), F32), psi=V((heads, n, n), F32),
        x1=V((n, width), F32), y1=V((n, width), F32),
        fv=V((hops, n, width), BF), fp=V((hops - 1, heads, HDIM, HDIM), BF), chain=V((slots, n, width), BF),
        probs=V((hops + 1, heads, n, n), BF), rcp=V((n, heads), F32), o=V((n, width), BF), mixed=V((sub, model), F32),
        inner=V((n, model), BF), hidden=V((2 * n, hid_n * ff), BF), ggate=V((2 * n, hid_n * ff), BF),
        gup=V((2 * n, hid_n * ff), BF), gin=V((n, model), BF),
        w_s=V((model, 4 * width), BF), wo_s=V((width, model), BF),
        wg_s=V((model, hid_n * ff), BF), wu_s=V((model, hid_n * ff), BF), wd_s=V((hid_n * ff, model), BF),
        kt_s=V((n, width), BF), near_s=V((heads, n, n), F32), prod_s=V((heads, HDIM, HDIM), BF),
        s_s=V(((hops + 1) * n, n), F32), part_s=V((n, model), BF), recv_s=V((wid_n, sub, model), BF), recv_far=V((sub, model), BF),
        row_s=V((sub, model), BF), row_g=V((sub, model), BF),
        twin_inner=V((n, half), BF), twin_dy=V((n, half), BF), twin_act=V((n, half), BF), twin_o=V((n, width), BF),
        twin_gz=V((n, half), BF), left_t=V((half, 2 * n), BF),
        gu_x=V((3, half, ff), BF), gu_y=V((3, half, ff), BF),
        dn_x=V((3, ff, half // 2), BF), dn_y=V((3, ff, half // 2), BF),
        gz=V((n, model), BF), gpart=V((8, model), F32), recv_f=V((peers_w, n, col), BF),
        gqt=V((n, width), F32), gv=V((n, width), F32),
        sendk=V((hops, n, width), BF), sendv=V((hops, n, width), BF), sendp=V((hops - 1, heads, HDIM, HDIM), BF),
        recvk=V((hops, n, width), BF), recvv=V((hops, n, width), BF), recvp=V((hops - 1, heads, HDIM, HDIM), BF),
        send_o=V((half, width), BF),
        grads=V((2 * n, 4 * width), BF), gcs=V((2 * n, HDIM), BF), wide_s=V((half, width), F32),
        recv_q=V((heads + 2, 6, piece // 2, width), BF), beta_s=V((8, half), F32), recv_b=V((peers_h, 8, 256), F32),
        own_n=V((n, col), F32), send_n=V((wid_n, n, col), BF), recv_n=V((wid_n, n, col), BF),
        stat_s=V((8, n), F32), recv_st=V((peers_w, 8, n), F32),
        recv_gain=V((rows_n - 1, 8, 256), F32), gain_s=V((8, 256), F32), recv_gain2=V((peers_w, 8, 256), F32),
    )
    n_copies = 256
    scratch.update(load_sem=pltpu.SemaphoreType.DMA((24,)), send_sem=pltpu.SemaphoreType.DMA((n_copies,)),
                   recv_sem=pltpu.SemaphoreType.DMA((n_copies,)))
    spaces = {"lengths": pltpu.SMEM, "x": pltpu.VMEM, "gain_attn": pltpu.VMEM, "gain_ffn": pltpu.VMEM, "wb": pltpu.VMEM}
    vmem = pl.BlockSpec(memory_space=pltpu.VMEM)
    res = pl.pallas_call(
        functools.partial(step_kernel, (heads, hops, sizes), ins + tuple(outs) + tuple(scratch)),
        in_specs=[pl.BlockSpec(memory_space=spaces.get(i, pl.ANY)) for i in ins],
        out_shape=tuple(outs.values()),
        out_specs=tuple(vmem for _ in outs),
        scratch_shapes=list(scratch.values()),
        compiler_params=pltpu.CompilerParams(
            vmem_limit_bytes=VMEM_ALL, collective_id=1, has_side_effects=True),
        name="step",
    )(*args)
    return dict(zip(outs, res))


def finish_kernel(count, *refs):
    ins, outs, bufs, sems = refs[:count], refs[count:2 * count], refs[2 * count:3 * count], refs[3 * count]
    loads = [pltpu.make_async_copy(a, b, sems.at[0, i]) for i, (a, b) in enumerate(zip(ins, bufs))]
    stores = [pltpu.make_async_copy(b, c, sems.at[1, i]) for i, (b, c) in enumerate(zip(bufs, outs))]
    for copy in loads:
        copy.start()
    for load, store in zip(loads, stores):
        load.wait()
        store.start()
    for copy in stores:
        copy.wait()


def finish(arrays):
    count = len(arrays)
    spec = pl.BlockSpec(memory_space=pl.ANY)
    return pl.pallas_call(
        functools.partial(finish_kernel, count),
        in_specs=[spec] * count, out_specs=[spec] * count,
        out_shape=[jax.ShapeDtypeStruct(a.shape, a.dtype) for a in arrays],
        scratch_shapes=[pltpu.VMEM(a.shape, a.dtype) for a in arrays] + [pltpu.SemaphoreType.DMA((2, count))],
        compiler_params=pltpu.CompilerParams(vmem_limit_bytes=VMEM_ALL),
        name="finish",
    )(*arrays)


def shifted(array, axis, by):
    peers = lax.axis_size(axis)
    pairs = [(i, i + by) for i in range(peers) if 0 <= i + by < peers]
    return lax.ppermute(array, axis, pairs)


def norm_rows(hidden_f):
    inverse = lax.rsqrt(jnp.mean(hidden_f * hidden_f, -1, keepdims=True) + eps_norm)
    return (hidden_f * inverse, inverse)


def norm_back(grad_out, normed, inverse, gain_vec):
    scaled_grad = grad_out * gain_vec
    grad_gain = jnp.sum(grad_out * normed, 0)
    grad_in = inverse * (scaled_grad - normed * jnp.mean(scaled_grad * normed, -1, keepdims=True))
    return (grad_in, grad_gain)


ROWS = ("seq", "hid")


def body(inputs, gain_attn, gain_ffn, w_query, w_key, w_value, w_house, w_beta, w_out,
         w_gate, w_up, w_down, lengths, cotangent):
    tok, col = inputs.shape
    row_devs = lax.axis_size(ROWS)
    my_row = lax.axis_index(ROWS)
    my_wid = lax.axis_index("wid")
    wid_n = lax.axis_size("wid")
    tokens_all = tok * row_devs
    most_len = max(LEAST, 2 * tokens_all // 5)
    hops = min((most_len - 2) // tok + 1, row_devs - 1)
    heads = w_query.shape[1] // HDIM
    ff = w_gate.shape[1]
    sub = tok // wid_n

    x_all = lax.all_gather(inputs, "wid", axis=1, tiled=True)
    gain_one = lax.all_gather(gain_attn, "wid", axis=0, tiled=True).astype(F32)
    gain_two = lax.all_gather(gain_ffn, "wid", axis=0, tiled=True).astype(F32)
    dy_all = lax.all_gather(cotangent, "wid", axis=1, tiled=True)
    w_gu = lax.all_gather(jnp.concatenate([w_gate, w_up], 1), "hid", axis=0)
    w_dn = lax.all_gather(w_down, "hid", axis=0)
    model = x_all.shape[1]

    residual = x_all.astype(F32)
    normed_one, inverse_one = norm_rows(residual)
    act = (normed_one * gain_one).astype(BF)

    def project(weight):
        return jnp.dot(act, weight, preferred_element_type=F32)

    q, k, r, c = project(w_query), project(w_key), project(w_house), project(w_beta)
    v = project(w_value).astype(BF)
    far_v = jnp.stack([shifted(v, ROWS, i) for i in range(1, hops + 1)])
    qt, kt, near, prod, *saved = path_fwd(q, k, r, c, heads)
    far_k = jnp.stack([shifted(kt, ROWS, i) for i in range(1, hops + 1)])
    far_p = jnp.stack([shifted(prod, ROWS, i) for i in range(1, hops)])
    row_arr = jnp.full((1,), my_row, jnp.int32)
    attended, probs, chain, rcp = attn_fwd(lengths, row_arr, qt, near, v, far_k, far_v, far_p, heads, hops)

    attn_part = jnp.dot(attended, w_out, preferred_element_type=F32).astype(BF)
    attn_rows = lax.psum_scatter(attn_part, "wid", scatter_dimension=0, tiled=True)
    x_rows = lax.dynamic_slice_in_dim(x_all, my_wid * sub, sub, 0).astype(F32)
    dy_rows = lax.dynamic_slice_in_dim(dy_all, my_wid * sub, sub, 0).astype(F32)
    mixed = x_rows + attn_rows.astype(F32)
    normed_two, inverse_two = norm_rows(mixed)
    inner = lax.all_gather((normed_two * gain_two).astype(BF), "wid", axis=0, tiled=True)

    pre = jnp.einsum("tc,hcf->htf", inner, w_gu, preferred_element_type=F32)
    gate, up = pre[:, :, :ff], pre[:, :, ff:]
    sig = jax.nn.sigmoid(gate)
    hidden = (gate * sig * up).astype(BF)
    ffn_part = jnp.einsum("htf,hfc->tc", hidden, w_dn, preferred_element_type=F32)
    ffn_part = (ffn_part + attn_part.astype(F32)).astype(BF)
    ffn_cols = lax.psum_scatter(ffn_part, "wid", scatter_dimension=1, tiled=True)
    output = (inputs.astype(F32) + ffn_cols.astype(F32)).astype(BF)

    g_hidden = jnp.einsum("tc,hfc->htf", dy_all, w_dn, preferred_element_type=F32)
    g_gate = g_hidden * up * sig * (1.0 + gate * (1.0 - sig))
    g_up = g_hidden * gate * sig
    g_pre = jnp.concatenate([g_gate, g_up], 2).astype(BF)
    g_inner = jnp.einsum("htf,hcf->tc", g_pre, w_gu, preferred_element_type=F32).astype(BF)
    g_inner = lax.psum_scatter(g_inner, "wid", scatter_dimension=0, tiled=True).astype(F32)
    g_mixed_n, g_gain_two = norm_back(g_inner, normed_two, inverse_two, gain_two)
    g_z = lax.all_gather((dy_rows + g_mixed_n).astype(BF), "wid", axis=0, tiled=True)

    d_gu = jnp.einsum("tc,htf->hcf", inner, g_pre, preferred_element_type=F32).astype(BF)
    d_dn = jnp.einsum("htf,tc->hfc", hidden, dy_all, preferred_element_type=F32).astype(BF)
    d_gu = lax.psum_scatter(d_gu, "seq", scatter_dimension=1, tiled=True)
    d_gu = lax.psum_scatter(d_gu, "hid", scatter_dimension=0)
    d_dn = lax.psum_scatter(d_dn, "seq", scatter_dimension=2, tiled=True)
    d_dn = lax.psum_scatter(d_dn, "hid", scatter_dimension=0)

    g_attn = jnp.einsum("tc,ic->ti", g_z, w_out, preferred_element_type=F32).astype(BF)
    d_out = jnp.einsum("ti,tc->ic", attended, g_z, preferred_element_type=F32).astype(BF)
    g_qt, g_near, gv, send_k, send_v, send_p = attn_bwd(probs, rcp, g_attn, qt, v, far_v, far_p, chain, heads, hops)
    g_kt = sum(shifted(send_k[i - 1], ROWS, -i).astype(F32) for i in range(1, hops + 1))
    gv = gv + sum(shifted(send_v[i - 1], ROWS, -i).astype(F32) for i in range(1, hops + 1))
    g_prod = sum(shifted(send_p[i - 1], ROWS, -i).astype(F32) for i in range(1, hops))
    g_q, g_k, g_r, g_c = path_bwd(q, k, r, c, saved, g_qt, g_kt, g_near, g_prod, heads)
    g_v = gv.astype(BF)

    def weight_grad(grad_low):
        return jnp.einsum("tc,ti->ci", act, grad_low, preferred_element_type=F32).astype(BF)

    def input_grad(grad_low, weight):
        return jnp.einsum("ti,ci->tc", grad_low, weight, preferred_element_type=F32)

    g_act = (input_grad(g_q, w_query) + input_grad(g_k, w_key) + input_grad(g_v, w_value)
             + input_grad(g_r, w_house) + input_grad(g_c, w_beta))
    g_act = lax.psum_scatter(g_act.astype(BF), "wid", scatter_dimension=0, tiled=True).astype(F32)
    normed_rows = lax.dynamic_slice_in_dim(normed_one, my_wid * sub, sub, 0)
    inverse_rows = lax.dynamic_slice_in_dim(inverse_one, my_wid * sub, sub, 0)
    g_resid, g_gain_one = norm_back(g_act, normed_rows, inverse_rows, gain_one)
    d_rows = dy_rows + g_mixed_n + g_resid
    d_inputs = lax.all_to_all(d_rows, "wid", split_axis=1, concat_axis=0, tiled=True)

    def scatter(x, dim):
        return lax.psum_scatter(x, ROWS, scatter_dimension=dim, tiled=True)

    gains = lax.psum(jnp.stack([g_gain_one, g_gain_two]), "wid")
    gains = scatter(gains, 1)
    return (
        output,
        d_inputs,
        gains[0],
        gains[1],
        scatter(weight_grad(g_q), 0).astype(F32),
        scatter(weight_grad(g_k), 0).astype(F32),
        scatter(weight_grad(g_v), 0).astype(F32),
        scatter(weight_grad(g_r), 0).astype(F32),
        scatter(weight_grad(g_c), 0).astype(F32),
        scatter(d_out, 1).astype(F32),
        d_gu[:, :ff].astype(F32),
        d_gu[:, ff:].astype(F32),
        d_dn.astype(F32),
    )


def fast_body(inputs, gain_attn, gain_ffn, w_query, w_key, w_value, w_house, w_beta, w_out,
              w_gate, w_up, w_down, lengths, cotangent):
    tok, col = inputs.shape
    row_devs = lax.axis_size(ROWS)
    sizes = tuple(lax.axis_size(i) for i in ("seq", "hid", "wid"))
    most_len = max(LEAST, 2 * tok * row_devs // 5)
    hops = min((most_len - 2) // tok + 1, row_devs - 1)
    heads = w_query.shape[1] // HDIM
    f = step((lengths, inputs, cotangent, gain_attn, gain_ffn, w_query, w_key, w_value, w_house,
              w_beta.T, w_out, w_gate, w_up, w_down), heads, hops, sizes)
    names = [i for i in f if i != "gain_out"]
    f.update(zip(names, finish([f[i] for i in names])))
    return (f["output"], f["d_inputs"], f["gain_out"][0], f["gain_out"][1], f["d_query"], f["d_key"], f["d_value"],
            f["d_house"], f["d_beta"].T, f["d_out"].T, f["d_gate"], f["d_up"], f["d_down"])


def slow(mesh):
    return (mesh.shape["seq"], mesh.shape["hid"], mesh.shape["wid"]) != (2, 4, 4)


def solution(mesh):
    in_specs = (
        P(("seq", "hid"), "wid"), P("wid"), P("wid"),
        P(None, "wid"), P(None, "wid"), P(None, "wid"), P(None, "wid"), P(None, "wid"),
        P("wid", None), P(None, ("hid", "wid")), P(None, ("hid", "wid")), P(("hid", "wid"), None),
        P(), P(("seq", "hid"), "wid"),
    )
    out_specs = (
        P(("seq", "hid"), "wid"), P(("seq", "hid"), "wid"), P(("seq", "hid")), P(("seq", "hid")),
        P(("seq", "hid"), "wid"), P(("seq", "hid"), "wid"), P(("seq", "hid"), "wid"),
        P(("seq", "hid"), "wid"), P(("seq", "hid"), "wid"), P("wid", ("seq", "hid")),
        P("seq", ("hid", "wid")), P("seq", ("hid", "wid")), P(("hid", "wid"), "seq"),
    )
    return jax.shard_map(body if slow(mesh) else fast_body, mesh=mesh, in_specs=in_specs, out_specs=out_specs, check_vma=False)
```

```python
import functools
import types

import jax
import jax.numpy as jnp
from jax import lax
from jax.experimental import pallas as pl
from jax.experimental.pallas import tpu as pltpu
from jax.sharding import PartitionSpec as P

HDIM = 128
LEAST = 1024

eps_norm = 1e-06
neg_big = -1e30
BF = jnp.bfloat16
F32 = jnp.float32
VMEM_LIMIT = 60 * 1024 * 1024
VMEM_ALL = 67043328


def dot(a, b, ca, cb):
    return lax.dot_general(a, b, (((ca,), (cb,)), ((), ())), preferred_element_type=F32)


def split(a):
    hi = a.astype(BF)
    return hi, (a - hi.astype(F32)).astype(BF)


def dot3(a, b, ca, cb):
    return dot(a[0], b[0], ca, cb) + (dot(a[0], b[1], ca, cb) + dot(a[1], b[0], ca, cb))


def dot1(a, b, ca, cb):
    return dot(a.astype(BF), b.astype(BF), ca, cb)


def iotas(n):
    rows = lax.broadcasted_iota(jnp.int32, (n, n), 0)
    cols = lax.broadcasted_iota(jnp.int32, (n, n), 1)
    return rows, cols


def head_cols(h):
    return slice(h * HDIM, (h + 1) * HDIM)


def house_terms(raw, strength, heads, h):
    inv = lax.rsqrt(jnp.sum(raw * raw, -1, keepdims=True) + eps_norm)
    lane = lax.broadcasted_iota(jnp.int32, strength.shape, 1)
    c = jnp.sum(jnp.where(lane == h, strength, 0.0), 1, keepdims=True)
    root = jnp.sqrt(2.0 / (1.0 + jnp.exp(-c)))
    return inv, root


def path_fwd_stage(heads, q_ref, k_ref, r_ref, c_ref, qt_ref, kt_ref, near_ref, p_ref,
                   u_ref, inv_ref, psi_ref, x_ref, y_ref, done=None):
    n = c_ref.shape[0]
    rows, cols = iotas(n)
    strength = c_ref[...]
    us2 = []
    for h in range(heads):
        raw = r_ref[:, head_cols(h)]
        inv, root = house_terms(raw, strength, heads, h)
        u = raw * (inv * root)
        u_ref[:, head_cols(h)] = u
        u2 = split(u)
        us2.append(u2)
        low = jnp.where(rows > cols, dot3(u2, u2, 1, 1), 0.0)
        psi_ref[h] = low
        inv_ref[h] = jnp.where(rows == cols, 1.0, 0.0) - jnp.where(rows // 2 == cols // 2, low, 0.0)

    def double(step, carry):
        apart = jnp.right_shift(rows, step) != jnp.right_shift(cols, step)
        pick = apart & (jnp.right_shift(rows, step + 1) == jnp.right_shift(cols, step + 1))
        halves = [split(inv_ref[h]) for h in range(heads)]
        mids = [dot3(split(jnp.where(pick, psi_ref[h], 0.0)), halves[h], 1, 0) for h in range(heads)]
        for h in range(heads):
            inv_ref[h] = inv_ref[h] - dot3(halves[h], split(mids[h]), 1, 0)
        return carry

    lax.fori_loop(1, (n - 1).bit_length(), double, 0)
    er, ec = iotas(HDIM)
    for h in range(heads):
        kin = split(inv_ref[h])
        k = k_ref[:, head_cols(h)]
        u2 = us2[h]
        aq = jnp.where(rows < cols, dot3(split(k), u2, 1, 1), 0.0)
        y = dot3(kin, u2, 0, 0)
        y_ref[:, head_cols(h)] = y
        kt_ref[:, head_cols(h)] = (k - dot3(split(aq), split(y), 1, 0)).astype(BF)
        x = dot3(kin, u2, 1, 0)
        x_ref[:, head_cols(h)] = x
        p_ref[h] = (jnp.where(er == ec, 1.0, 0.0) - dot3(u2, split(x), 0, 0)).astype(p_ref.dtype)
        if done is not None:
            done(h)
    for h in range(heads):
        kin = split(inv_ref[h])
        q = q_ref[:, head_cols(h)]
        q2, k2, u2, x2 = split(q), split(k_ref[:, head_cols(h)]), us2[h], split(x_ref[:, head_cols(h)])
        fq2 = split(jnp.where(rows >= cols, dot3(q2, u2, 1, 1), 0.0))
        qt_ref[:, head_cols(h)] = (q - dot3(fq2, x2, 1, 0)).astype(BF)
        psi = dot3(kin, split(jnp.where(rows > cols, dot3(u2, k2, 1, 1), 0.0)), 1, 0)
        psi_ref[h] = psi
        near_ref[h] = dot3(q2, k2, 1, 1) - dot3(fq2, split(psi), 1, 0)


def path_fwd_kernel(heads, *refs):
    path_fwd_stage(heads, *refs)


def path_fwd(q, k, r, c, heads):
    n, width = q.shape
    flat = jax.ShapeDtypeStruct((n, width), F32)
    low = jax.ShapeDtypeStruct((n, width), BF)
    square = jax.ShapeDtypeStruct((heads, n, n), F32)
    return pl.pallas_call(
        functools.partial(path_fwd_kernel, heads),
        out_shape=(low, low, square, jax.ShapeDtypeStruct((heads, HDIM, HDIM), F32),
                   flat, square, square, flat, flat),
        compiler_params=pltpu.CompilerParams(vmem_limit_bytes=VMEM_LIMIT),
        name="path_fwd",
    )(q, k, r, c)


def doc_of(pos, len_ref):
    total = len_ref[0]
    doc = (pos >= total).astype(jnp.int32)
    for i in range(1, len_ref.shape[0]):
        total = total + len_ref[i]
        doc = doc + (pos >= total).astype(jnp.int32)
    return doc


def chain_slot(r, m):
    return r * (r - 1) // 2 + m


def key_chain(hops, h, fp_ref, chain_ref):
    cs = head_cols(h)
    for r in range(2, hops + 1):
        keys = chain_ref[chain_slot(r, 0), :, cs]
        for m in range(1, r):
            keys = dot(keys, fp_ref[r - m - 1, h].astype(BF), 1, 1).astype(BF)
            chain_ref[chain_slot(r, m), :, cs] = keys


def attn_fwd_rows(hops, h, start, count, row, len_ref, qt_ref, near_ref, v_ref, fv_ref, chain_ref,
                  o_ref, p_ref, rcp_ref, s_ref):
    n = qt_ref.shape[0]
    scale = HDIM ** (-0.5)
    cs, rs = head_cols(h), slice(start, start + count)
    rows = start + lax.broadcasted_iota(jnp.int32, (count, n), 0)
    cols = lax.broadcasted_iota(jnp.int32, (count, n), 1)
    own = doc_of(row * n + rows, len_ref)
    near_ok = (rows >= cols) & (own == doc_of(row * n + cols, len_ref))
    q = qt_ref[rs, cs]
    s = jnp.where(near_ok, near_ref[h, rs, :] * scale, neg_big)
    s_ref[0:count, :] = s
    top = jnp.max(s, 1, keepdims=True)
    for r in range(1, hops + 1):
        source = row - r
        docs = jnp.where(source >= 0, doc_of(source * n + cols, len_ref), -1)
        keys = chain_ref[chain_slot(r, r - 1), :, cs]
        s = jnp.where(own == docs, dot(q, keys, 1, 1) * scale, neg_big)
        s_ref[r * count:(r + 1) * count, :] = s
        top = jnp.maximum(top, jnp.max(s, 1, keepdims=True))
    total = jnp.zeros((count, 1), F32)
    out = jnp.zeros((count, HDIM), F32)
    for r in range(hops + 1):
        e = jnp.exp(s_ref[r * count:(r + 1) * count, :] - top)
        total = total + jnp.sum(e, 1, keepdims=True)
        weights = e.astype(BF)
        p_ref[r, h, rs, :] = weights
        out = out + dot(weights, v_ref[:, cs] if r == 0 else fv_ref[r - 1, :, cs], 1, 0)
    recip = 1.0 / total
    rcp_ref[rs, h:h + 1] = recip
    o_ref[rs, cs] = (out * recip).astype(BF)


def attn_fwd_kernel(heads, hops, len_ref, row_ref, qt_ref, near_ref, v_ref, fk_ref, fv_ref, fp_ref,
                    o_ref, p_ref, chain_ref, rcp_ref, s_ref):
    for r in range(1, hops + 1):
        chain_ref[chain_slot(r, 0)] = fk_ref[r - 1]
    for h in range(heads):
        key_chain(hops, h, fp_ref, chain_ref)
        attn_fwd_rows(hops, h, 0, qt_ref.shape[0], row_ref[0], len_ref, qt_ref, near_ref, v_ref, fv_ref, chain_ref,
                      o_ref, p_ref, rcp_ref, s_ref)


def attn_fwd(lengths, my_row, qt, near, v, far_k, far_v, far_p, heads, hops):
    n, width = qt.shape
    slots = hops * (hops + 1) // 2
    smem = pl.BlockSpec(memory_space=pltpu.SMEM)
    vmem = pl.BlockSpec(memory_space=pltpu.VMEM)
    return pl.pallas_call(
        functools.partial(attn_fwd_kernel, heads, hops),
        in_specs=[smem, smem] + [vmem] * 6,
        out_shape=(
            jax.ShapeDtypeStruct((n, width), BF),
            jax.ShapeDtypeStruct((hops + 1, heads, n, n), BF),
            jax.ShapeDtypeStruct((slots, n, width), BF),
            jax.ShapeDtypeStruct((n, heads), F32),
        ),
        scratch_shapes=[pltpu.VMEM(((hops + 1) * n, n), F32)],
        compiler_params=pltpu.CompilerParams(vmem_limit_bytes=VMEM_LIMIT),
        name="attn_fwd",
    )(lengths, my_row, qt, near, v, far_k, far_v, far_p)


def attn_bwd_kernel(heads, hops, p_ref, rcp_ref, go_ref, qt_ref, v_ref, fv_ref, fp_ref, chain_ref,
                    gqt_ref, gnear_ref, gv_ref, sendk_ref, sendv_ref, sendp_ref, dp_ref):
    for h in range(heads):
        attn_bwd_head(hops, h, p_ref, rcp_ref, go_ref[:, head_cols(h)], qt_ref, v_ref, fv_ref, fp_ref, chain_ref,
                      gqt_ref, gnear_ref, gv_ref, sendk_ref, sendv_ref, sendp_ref, dp_ref)


def attn_bwd(p, rcp, go, qt, v, far_v, far_p, chain, heads, hops):
    n, width = qt.shape
    return pl.pallas_call(
        functools.partial(attn_bwd_kernel, heads, hops),
        out_shape=(
            jax.ShapeDtypeStruct((n, width), F32),
            jax.ShapeDtypeStruct((heads, n, n), F32),
            jax.ShapeDtypeStruct((n, width), F32),
            jax.ShapeDtypeStruct((hops, n, width), BF),
            jax.ShapeDtypeStruct((hops, n, width), BF),
            jax.ShapeDtypeStruct((hops - 1, heads, HDIM, HDIM), BF),
        ),
        scratch_shapes=[pltpu.VMEM(((hops + 1) * n, n), F32)],
        compiler_params=pltpu.CompilerParams(vmem_limit_bytes=VMEM_LIMIT),
        name="attn_bwd",
    )(p, rcp, go, qt, v, far_v, far_p, chain)


def path_bwd_kernel(heads, q_ref, k_ref, r_ref, c_ref, u_ref, inv_ref, psi_ref, x_ref, y_ref,
                    gqt_ref, gkt_ref, gnear_ref, gp_ref, gq_ref, gk_ref, gr_ref, gc_ref):
    lane = lax.broadcasted_iota(jnp.int32, c_ref.shape, 1)
    gc_all = jnp.zeros(c_ref.shape, F32)
    for h in range(heads):
        cs = head_cols(h)
        gq, gk, gr, gc = path_bwd_head(h, heads, q_ref, k_ref, r_ref, c_ref, u_ref, inv_ref, psi_ref, x_ref, y_ref,
                                       gqt_ref[:, cs], gkt_ref[:, cs], gnear_ref[h], gp_ref[h])
        gq_ref[:, cs] = gq
        gk_ref[:, cs] = gk
        gr_ref[:, cs] = gr
        gc_all = jnp.where(lane == h, gc, gc_all)
    gc_ref[...] = gc_all.astype(BF)


def path_bwd(q, k, r, c, saved, gqt, gkt, gnear, gp, heads):
    n, width = q.shape
    low = jax.ShapeDtypeStruct((n, width), BF)
    return pl.pallas_call(
        functools.partial(path_bwd_kernel, heads),
        out_shape=(low, low, low, jax.ShapeDtypeStruct((n, heads), BF)),
        compiler_params=pltpu.CompilerParams(vmem_limit_bytes=VMEM_LIMIT),
        name="path_bwd",
    )(q, k, r, c, *saved, gqt, gkt, gnear, gp)


MESH = pl.DeviceIdType.MESH


class Copies:
    def __init__(self, send, recv):
        self.send, self.recv, self.count, self.open = send, recv, 0, []

    def take(self):
        self.count = self.count + 1
        return self.count - 1

    def make(self, src, dst, device, send, recv):
        return pltpu.make_async_remote_copy(
            src_ref=src, dst_ref=dst, send_sem=self.send.at[send], recv_sem=self.recv.at[recv],
            device_id=device, device_id_type=MESH)

    def begin(self, copy):
        copy.start()
        self.open.append(copy)
        return copy

    def start(self, src, dst, device):
        i = self.take()
        return self.begin(self.make(src, dst, device, i, i))

    def sent(self, some):
        for copy in some:
            copy.wait_send()
        self.open = [copy for copy in self.open if all(copy is not other for other in some)]


class Loads:
    def __init__(self, sems):
        self.sems, self.count = sems, 0

    def start(self, src, dst):
        copy = pltpu.make_async_copy(src, dst, self.sems.at[self.count])
        self.count = self.count + 1
        copy.start()
        return copy


class Place:
    def __init__(self, sizes):
        self.seq_n, self.hid_n, self.wid_n = sizes
        self.seq = lax.axis_index("seq")
        self.hid = lax.axis_index("hid")
        self.wid = lax.axis_index("wid")
        self.rows_n = self.seq_n * self.hid_n
        self.row = self.seq * self.hid_n + self.hid

    def wid_peer(self, i):
        return lax.rem(self.wid + i, self.wid_n)

    def hid_peer(self, i):
        return lax.rem(self.hid + i, self.hid_n)

    def seq_peer(self, i):
        return lax.rem(self.seq + i, self.seq_n)

    def row_peer(self, i):
        to = lax.rem(self.row + i + self.rows_n, self.rows_n)
        return {"seq": to // self.hid_n, "hid": lax.rem(to, self.hid_n)}

    def barrier(self):
        sem = pltpu.get_barrier_semaphore()
        for i in range(1, self.wid_n):
            pl.semaphore_signal(sem, inc=1, device_id={"wid": self.wid_peer(i)}, device_id_type=MESH)
        for i in range(1, self.rows_n):
            pl.semaphore_signal(sem, inc=1, device_id=self.row_peer(i), device_id_type=MESH)
        pl.semaphore_wait(sem, self.wid_n - 1 + self.rows_n - 1)


class Sometimes:
    def __init__(self, copy, sends=None, gets=None):
        self.copy, self.sends, self.gets = copy, sends, gets

    def on(self, flag, act):
        if flag is None:
            act()
        else:
            pl.when(flag)(act)

    def start(self):
        self.on(self.sends, lambda: self.copy.start() and None)

    def wait_send(self):
        self.on(self.sends, self.copy.wait_send)

    def wait_recv(self):
        self.on(self.gets, self.copy.wait_recv)


class LineGather:
    def __init__(self, copies, place, src, view):
        me = place.wid
        self.me, self.copies, self.view = me, copies, view
        self.ids = [copies.take() for _ in range(3)]
        here = view(me)
        self.by = {i: copies.make(src, here, {"wid": place.wid_peer(i)}, self.ids[i - 1], self.ids[i - 1])
                   for i in (1, 2, 3)}
        self.by[1] = Sometimes(self.by[1], me != 3)
        self.by[3] = Sometimes(self.by[3], me != 0)
        for i in (2, 1, 3):
            copies.begin(self.by[i])

    def relay(self):
        self.by[2].wait_recv()
        for m, chunk, to, i in ((1, 3, 0, 1), (2, 0, 3, 3)):
            part = self.view(chunk)
            copy = self.copies.make(part, part, {"wid": to}, self.copies.take(), self.ids[i - 1])
            self.copies.begin(Sometimes(copy, self.me == m))

    def wait(self):
        self.by[1].wait_recv()
        self.by[3].wait_recv()


class LineSwap:
    def __init__(self, copies, place, piece, recv):
        self.copies, self.place, self.me, self.piece, self.recv = copies, place, place.wid, piece, recv
        self.ids = [copies.take() for _ in range(4)]
        me = self.me

        @pl.when(me == 0)
        def _():
            recv(0)[...] = jnp.zeros(recv(0).shape, BF)

        @pl.when(me == 3)
        def _():
            recv(2)[...] = jnp.zeros(recv(2).shape, BF)

    def make(self, src, i, slot, device, send):
        return self.copies.make(src, self.recv(slot), device, send, self.ids[slot])

    def start_far(self):
        self.far = []
        for end, far, middle in ((0, 3, 1), (3, 0, 2)):
            copy = Sometimes(self.make(self.piece(far), 0, 3, {"wid": middle}, self.copies.take()),
                             self.me == end, self.me == middle)
            self.copies.begin(copy)
            self.far.append(copy)

    def start(self):
        me, place = self.me, self.place
        to = [place.wid_peer(i) for i in range(4)]
        self.two = Sometimes(self.make(self.piece(to[2]), 2, 1, {"wid": to[2]}, self.ids[1]), (me == 0) | (me == 3))
        self.one = Sometimes(self.make(self.piece(to[1]), 1, 0, {"wid": to[1]}, self.ids[0]), me != 3, me != 0)
        self.three = Sometimes(self.make(self.piece(to[3]), 3, 2, {"wid": to[3]}, self.ids[2]), me != 0, me != 3)
        for copy in (self.two, self.one, self.three):
            self.copies.begin(copy)

    def combine(self):
        for copy in self.far:
            copy.wait_recv()
        mid = (self.me == 1) | (self.me == 2)
        far = 3 * (2 - jnp.minimum(jnp.maximum(self.me, 1), 2))

        @pl.when(mid)
        def _():
            at = self.recv(3)
            at[...] = (at[...].astype(F32) + self.piece(far)[...].astype(F32)).astype(BF)

        copy = self.make(self.recv(3), 2, 1, {"wid": far}, self.copies.take())
        self.copies.begin(Sometimes(copy, mid))

    def total(self, own):
        for copy in (self.two, self.one, self.three):
            copy.wait_recv()
        for slot in range(3):
            own = own + self.recv(slot)[...].astype(F32)
        return own


def aligned(start, size, step):
    return pl.ds(pl.multiple_of(start, step), size)


def attn_bwd_head(hops, h, p_ref, rcp_ref, go, qt_ref, v_ref, fv_ref, fp_ref, chain_ref,
                  gqt_ref, gnear_ref, gv_ref, sendk_ref, sendv_ref, sendp_ref, dp_ref):
    n = qt_ref.shape[0]
    scale = HDIM ** (-0.5)
    cs = head_cols(h)
    q = qt_ref[:, cs]
    recip = rcp_ref[:, h:h + 1]
    go_low = (go.astype(F32) * recip).astype(BF)
    delta = jnp.zeros((n, 1), F32)
    for r in range(hops + 1):
        vals = v_ref[:, cs] if r == 0 else fv_ref[r - 1, :, cs]
        dp = dot(go, vals, 1, 1)
        dp_ref[r * n:(r + 1) * n, :] = dp
        delta = delta + jnp.sum(p_ref[r, h].astype(F32) * dp, 1, keepdims=True)
        gv = dot(p_ref[r, h], go_low, 0, 0)
        if r == 0:
            gv_ref[:, cs] = gv
        else:
            sendv_ref[r - 1, :, cs] = gv.astype(BF)
    delta = delta * recip
    factor = recip * scale
    gnear_ref[h] = p_ref[0, h].astype(F32) * ((dp_ref[0:n, :] - delta) * factor)
    gq = jnp.zeros((n, HDIM), F32)
    gps = [jnp.zeros((HDIM, HDIM), F32) for _ in range(hops - 1)]
    for r in range(1, hops + 1):
        gs = (p_ref[r, h].astype(F32) * ((dp_ref[r * n:(r + 1) * n, :] - delta) * factor)).astype(BF)
        gq = gq + dot(gs, chain_ref[chain_slot(r, r - 1), :, cs], 1, 0)
        gk = dot(gs, q, 0, 0)
        for m in range(r - 1, 0, -1):
            back = r - m - 1
            gkb = gk.astype(BF)
            gps[back] = gps[back] + dot(gkb, chain_ref[chain_slot(r, m - 1), :, cs], 0, 0)
            gk = dot(gkb, fp_ref[back, h].astype(BF), 1, 0)
        sendk_ref[r - 1, :, cs] = gk.astype(BF)
    gqt_ref[:, cs] = gq
    for i in range(hops - 1):
        sendp_ref[i, h] = gps[i].astype(BF)


def path_bwd_head(h, heads, q_ref, k_ref, r_ref, c_ref, u_ref, inv_ref, psi_ref, x_ref, y_ref,
                  gqt, gkt, gs, gp):
    n = c_ref.shape[0]
    rows, cols = iotas(n)
    cs = head_cols(h)
    q, k, u = q_ref[:, cs], k_ref[:, cs], u_ref[:, cs]
    qb, kb, ub = q.astype(BF), k.astype(BF), u.astype(BF)
    kin = inv_ref[h].astype(BF)
    psi = psi_ref[h].astype(BF)
    x, y = x_ref[:, cs].astype(BF), y_ref[:, cs].astype(BF)
    gqtb, gktb = gqt.astype(BF), gkt.astype(BF)
    gsb = gs.astype(BF)
    gst = gs.T.astype(BF)
    gp = gp.astype(BF)
    f = jnp.where(rows <= cols, dot(ub, qb, 1, 1), 0.0).astype(BF)
    fq = jnp.where(rows >= cols, dot(qb, ub, 1, 1), 0.0).astype(BF)
    a = jnp.where(rows > cols, dot(ub, kb, 1, 1), 0.0).astype(BF)
    gx = -(dot(f, gqtb, 1, 0) + dot(ub, gp, 1, 0))
    gy = -dot(a, gktb, 1, 0)
    phiq = dot(fq, kin, 1, 0).astype(BF)
    back = dot(gst, phiq, 1, 0)
    backb = back.astype(BF)
    gfq = jnp.where(rows >= cols, -(dot(gqtb, x, 1, 1) + dot(gsb, psi, 1, 1)), 0.0)
    gaq = jnp.where(rows < cols, -(dot(gktb, y, 1, 1) + back), 0.0)
    kgx = dot(kin, gx.astype(BF), 0, 0)
    kgy = dot(kin, gy.astype(BF), 1, 0)
    zt = dot(x, kgx.astype(BF), 1, 1) + dot(kgy.astype(BF), y, 1, 1) - dot(psi, backb, 1, 0)
    glt = jnp.where(rows < cols, -zt, 0.0)
    sym = (glt + glt.T).astype(BF)
    gfqb, gaqb = gfq.astype(BF), gaq.astype(BF)
    gu = (kgx + kgy - dot(x, gp, 1, 1) + dot(gfq.T.astype(BF), qb, 1, 0)
          + dot(gaq.T.astype(BF), kb, 1, 0) + dot(sym, ub, 1, 0))
    gq = (gqt + dot(gsb, kb, 1, 0) + dot(gfqb, ub, 1, 0)).astype(BF)
    gk = (gkt + dot(gst, qb, 1, 0) + dot(gaqb, ub, 1, 0)).astype(BF)
    raw = r_ref[:, cs]
    inv, root = house_terms(raw, c_ref[...], heads, h)
    gc = jnp.sum(gu * u, 1, keepdims=True) * (1.0 - 0.5 * root * root) * 0.5
    gun = gu * root
    un = raw * inv
    gr = (inv * (gun - un * jnp.sum(gun * un, 1, keepdims=True))).astype(BF)
    return gq, gk, gr, gc


class Heads:
    def __init__(self, ref, kind):
        self.ref, self.kind = ref, kind

    def __getitem__(self, index):
        base = 3 * index[1].start + self.kind * HDIM
        return self.ref[index[0], base:base + HDIM]


def turned(index, by):
    low = index % 2
    high = index // 2 % 2
    return index + (1 - 2 * low) * (by % 2) + (2 - 4 * high) * (by // 2)


def step_kernel(cfg, names, *refs):
    heads, hops, sizes = cfg
    R = types.SimpleNamespace(**dict(zip(names, refs)))
    place = Place(sizes)
    wid_n, hid_n, seq_n = place.wid_n, place.hid_n, place.seq_n
    n, col = R.x.shape
    width = heads * HDIM
    model = R.act.shape[1]
    ff = R.wg.shape[1]
    sub = n // wid_n
    half = model // seq_n
    piece = model // place.rows_n
    copies, loads = Copies(R.send_sem, R.recv_sem), Loads(R.load_sem)
    my_cols = aligned(place.wid * col, col, 128)
    part_n = n // 2
    step_n = sub // 2

    def rows_of(w, hh):
        return aligned(hh * part_n + w * step_n, step_n, step_n)

    def half_of(hh):
        return slice(hh * step_n, (hh + 1) * step_n)

    def own_rows(ref):
        return jnp.concatenate([ref[rows_of(place.wid, hh), :].astype(F32) for hh in range(2)], 0)

    mine = aligned(place.seq * half, half, 128)
    other = aligned((1 - place.seq) * half, half, 128)
    sibling = {"seq": 1 - place.seq}
    order = sorted(range(1, wid_n), key=lambda i: -min(i, wid_n - i))
    to_wid = [{"wid": place.wid_peer(i)} for i in order]
    near = [{"hid": turned(place.hid, j)} for j in range(hid_n)]

    R.gain_in[0:1, :] = R.gain_attn[...].astype(F32).reshape(1, col)
    R.gain_in[1:2, :] = R.gain_ffn[...].astype(F32).reshape(1, col)
    R.xall[:, my_cols] = R.x[...]
    R.gall[:, my_cols] = R.gain_in[...]
    place.barrier()

    get_x = LineGather(copies, place, R.x, lambda c: R.xall.at[:, aligned(c * col, col, 128)])
    get_gains = [copies.start(R.gain_in, R.gall.at[:, my_cols], d) for d in to_wid]

    part_f = ff // seq_n
    mine_c = aligned(place.seq * half, half, 16)
    mine_f = aligned(place.seq * part_f, part_f, 16)

    def cols_of(j):
        return pl.ds(j * ff, ff)

    def down_rows(j, piece_i=0, pieces=1):
        size = part_f // pieces
        return aligned(j * ff + place.seq * part_f + piece_i * size, size, 16)

    def pass_on(ref, device):
        return copies.start(ref, ref, device)

    get_gate = [copies.start(R.wg.at[mine_c, :], R.wg_s.at[mine_c, cols_of(j)], near[j]) for j in (1, 2)]
    get_up = [copies.start(R.wu.at[mine_c, :], R.wu_s.at[mine_c, cols_of(j)], near[j]) for j in (1, 2)]
    load_v = loads.start(R.wv, R.w_s.at[:, pl.ds(3 * width, width)])
    load_w = [loads.start(w.at[:, pl.ds(h * HDIM, HDIM)], R.w_s.at[:, pl.ds((3 * h + m) * HDIM, HDIM)])
              for h in range(heads) for m, w in enumerate((R.wq, R.wk, R.wr))]
    load_dy = loads.start(R.dy, R.dyall.at[:, my_cols])
    load_o = loads.start(R.wo, R.wo_s)
    load_f = [loads.start(R.wg, R.wg_s.at[:, pl.ds(0, ff)]), loads.start(R.wu, R.wu_s.at[:, pl.ds(0, ff)]),
              loads.start(R.wd, R.wd_s.at[pl.ds(0, ff), :])]

    get_x.relay()
    get_x.wait()
    for copy in get_gains:
        copy.wait_recv()
    get_dy = [copies.start(R.dy, R.dyall.at[:, my_cols], d) for d in to_wid]
    xf = R.xall[...].astype(F32)
    inv_rms = lax.rsqrt(jnp.mean(xf * xf, -1, keepdims=True) + eps_norm)
    R.inv_rms[...] = inv_rms
    R.act[...] = (xf * inv_rms * R.gall[0:1, :]).astype(BF)
    load_v.wait()
    R.v[...] = dot(R.act[...], R.w_s[:, 3 * width:4 * width], 1, 0).astype(BF)
    get_v = [copies.start(R.v, R.fv.at[i - 1], place.row_peer(i)) for i in range(1, hops + 1)]
    for copy in load_w:
        copy.wait()
    R.proj[...] = dot(R.act[...], R.w_s[:, 0:3 * width], 1, 0)
    R.c[...] = dot(R.act[...], R.wb[...], 1, 1)

    get_k = [[] for _ in range(heads)]
    get_p = [[] for _ in range(heads)]

    def send_head(h):
        cs = head_cols(h)
        for i in range(1, hops + 1):
            get_k[h].append(copies.start(R.kt_s.at[:, cs], R.chain.at[chain_slot(i, 0), :, cs], place.row_peer(i)))
        for i in range(1, hops):
            get_p[h].append(copies.start(R.prod_s.at[h], R.fp.at[i - 1, h], place.row_peer(i)))

    path_fwd_stage(heads, Heads(R.proj, 0), Heads(R.proj, 1), Heads(R.proj, 2), R.c, R.qt, R.kt_s, R.near_s, R.prod_s,
                   R.u, R.inv, R.psi, R.x1, R.y1, send_head)

    for copy in get_gate + get_up:
        copy.wait_recv()
    relay = [copies.start(R.wg_s.at[mine_c, cols_of(1)], R.wg_s.at[mine_c, cols_of(3)], near[2]),
             copies.start(R.wu_s.at[mine_c, cols_of(2)], R.wu_s.at[mine_c, cols_of(3)], near[1])]
    get_down = [copies.start(R.wd.at[mine_f, :], R.wd_s.at[down_rows(j), :], near[j]) for j in (1, 2)]

    for copy in get_v:
        copy.wait_recv()
    load_o.wait()
    get_a = []
    for hh in range(2):
        for h in range(heads):
            if hh == 0:
                for copy in get_k[h] + get_p[h]:
                    copy.wait_recv()
                key_chain(hops, h, R.fp, R.chain)
            attn_fwd_rows(hops, h, hh * part_n, part_n, place.row, R.lengths, R.qt, R.near_s, R.v, R.fv, R.chain,
                          R.o, R.probs, R.rcp, R.s_s)
        rs = slice(hh * part_n, (hh + 1) * part_n)
        R.part_s[rs, :] = dot(R.o[rs, :], R.wo_s[...], 1, 0).astype(BF)
        get_a.append(LineSwap(copies, place, functools.partial(lambda hh, c: R.part_s.at[rows_of(c, hh), :], hh),
                              functools.partial(lambda hh, q: R.recv_s.at[q, pl.ds(hh * step_n, step_n), :], hh)))
        get_a[hh].start_far()
        get_a[hh].start()
    three = pl.ds(ff, 3 * ff)
    get_i = []

    def mix(hh):
        at, keep = rows_of(place.wid, hh), half_of(hh)
        mixed = get_a[hh].total(R.xall[at, :].astype(F32) + R.part_s[at, :].astype(F32))
        R.mixed[keep, :] = mixed
        inv_two = lax.rsqrt(jnp.mean(mixed * mixed, -1, keepdims=True) + eps_norm)
        R.row_s[keep, :] = (mixed * inv_two * R.gall[1:2, :]).astype(BF)
        get_i.append(LineGather(copies, place, R.row_s.at[pl.ds(hh * step_n, step_n), :],
                                functools.partial(lambda hh, c: R.inner.at[rows_of(c, hh), :], hh)))
        R.inner[at, :] = R.row_s[keep, :]

    get_a[0].combine()
    mix(0)
    get_a[1].combine()
    for copy in relay:
        copy.wait_recv()
    shared = [pass_on(ref.at[mine_c, three], sibling) for ref in (R.wg_s, R.wu_s)]
    for copy in get_down:
        copy.wait_recv()
    relay_d = [copies.start(R.wd_s.at[down_rows(1, 0, 2), :], R.wd_s.at[down_rows(3, 0, 2), :], near[2]),
               copies.start(R.wd_s.at[down_rows(2, 1, 2), :], R.wd_s.at[down_rows(3, 1, 2), :], near[1])]
    mix(1)
    get_i[0].relay()
    for copy in relay_d:
        copy.wait_recv()
    shared += [pass_on(R.wd_s.at[down_rows(j), :], sibling) for j in (1, 2, 3)]
    twin_a = [copies.start(R.act.at[:, other], R.twin_act, sibling),
              copies.start(R.o, R.twin_o, sibling)]
    load_dy.wait()
    for copy in load_f:
        copy.wait()
    get_i[1].relay()
    for copy in get_dy + shared:
        copy.wait_recv()
    for part in get_i:
        part.wait()
    twin = [copies.start(R.inner.at[:, other], R.twin_inner, sibling),
            copies.start(R.dyall.at[:, other], R.twin_dy, sibling)]

    swapped = (R.hidden, R.ggate, R.gup)
    swap_ids = [copies.take() for _ in range(3 * hid_n)]

    def swap(m, cs, i):
        return copies.make(swapped[m].at[pl.ds(0, n), cs], swapped[m].at[pl.ds(n, n), cs], sibling, i, i)

    def hidden_tile(t, carry):
        j = hid_n - 1 - t
        cs = aligned(j * ff, ff, 128)
        gate = dot(R.inner[...], R.wg_s[:, cs], 1, 0)
        up = dot(R.inner[...], R.wu_s[:, cs], 1, 0)
        g_hidden = dot(R.dyall[...], R.wd_s[cs, :], 1, 1)
        sig = 1.0 / (1.0 + jnp.exp(-gate))
        silu = gate * sig
        R.hidden[0:n, cs] = (silu * up).astype(BF)
        R.ggate[0:n, cs] = (g_hidden * up * sig * (1.0 + gate * (1.0 - sig))).astype(BF)
        R.gup[0:n, cs] = (g_hidden * silu).astype(BF)
        for m in range(3):
            swap(m, cs, swap_ids[0] + 3 * j + m).start()
        return carry

    lax.fori_loop(0, hid_n, hidden_tile, 0)
    twin_tile = [[swap(m, cols_of(j), swap_ids[3 * j + m]) for m in range(3)] for j in range(hid_n)]
    for tile in twin_tile:
        copies.open.extend(tile)
    before = list(copies.open)

    for copy in twin:
        copy.wait_recv()
    R.left_t[:, 0:n] = R.inner[:, mine].T
    R.left_t[:, n:2 * n] = R.twin_inner[...].T
    down_a, down_b = pl.ds(0, half // 2), pl.ds(half // 2, half // 2)
    upper, lower = pl.ds(0, half), pl.ds(half, half)

    def ffn_grads(j, gate_up, down):
        for copy in twin_tile[j]:
            copy.wait_recv()
        cs = slice(j * ff, (j + 1) * ff)
        gate_up[0:half, :] = dot(R.left_t[...], R.ggate[:, cs], 1, 0).astype(BF)
        gate_up[half:2 * half, :] = dot(R.left_t[...], R.gup[:, cs], 1, 0).astype(BF)
        down[...] = (dot(R.hidden[0:n, cs], R.dyall[:, mine], 0, 0)
                     + dot(R.hidden[n:2 * n, cs], R.twin_dy[...], 0, 0)).astype(BF)

    def first_round(gate_up, down, slot, rows, lanes, to, gus, downs):
        return [copies.start(gate_up.at[rows, :], gus.at[slot], to),
                copies.start(down.at[:, lanes], downs.at[slot], to)]

    ffn_grads(3, R.far_gu, R.far_dn)
    get_r1 = (first_round(R.far_gu, R.far_dn, 1, upper, down_a, near[1], R.gu_x, R.dn_x)
              + first_round(R.far_gu, R.far_dn, 1, lower, down_b, near[2], R.gu_y, R.dn_y))

    def grad_tile(t, carry):
        cs = aligned(t * col, col, 128)
        tile = (dot(R.ggate[0:n, :], R.wg_s[cs, :], 1, 1) + dot(R.gup[0:n, :], R.wu_s[cs, :], 1, 1)).astype(BF)
        for w in range(wid_n):
            for hh in range(2):
                R.gin[w * sub + hh * step_n:w * sub + (hh + 1) * step_n, cs] = (
                    tile[hh * part_n + w * step_n:hh * part_n + (w + 1) * step_n, :])
        return carry

    lax.fori_loop(0, wid_n, grad_tile, 0)
    get_g = LineSwap(copies, place, lambda c: R.gin.at[aligned(c * sub, sub, sub), :],
                     lambda q: R.recv_s.at[q] if q < 3 else R.recv_far)
    get_g.start_far()
    get_g.start()
    copies.sent(before)

    def grads_of(j):
        return R.wg_s.at[:, cols_of(j)], R.wu_s.at[cols_of(j), pl.ds(0, half)]

    ffn_grads(2, *grads_of(2))
    keep_r1 = first_round(*grads_of(2), 0, lower, down_b, near[2], R.gu_y, R.dn_y)
    ffn_grads(1, *grads_of(1))
    keep_r1 += first_round(*grads_of(1), 0, upper, down_a, near[1], R.gu_x, R.dn_x)
    get_g.combine()
    ffn_grads(0, *grads_of(0))

    def out_tile(t, carry):
        cs = aligned(t * col, col, 128)
        R.part_s[:, cs] = (dot(R.hidden[0:n, :], R.wd_s[:, cs], 1, 0) + R.part_s[:, cs].astype(F32)).astype(BF)
        return carry

    lax.fori_loop(0, wid_n, out_tile, 0)

    for copy in get_r1:
        copy.wait_recv()
    add_g = R.wg_s.at[upper, cols_of(2)]
    add_g[...] = (add_g[...].astype(F32) + R.gu_x[1].astype(F32)).astype(BF)
    add_u = R.wg_s.at[lower, cols_of(1)]
    add_u[...] = (add_u[...].astype(F32) + R.gu_y[1].astype(F32)).astype(BF)
    add_a = R.wu_s.at[cols_of(2), down_a]
    add_a[...] = (add_a[...].astype(F32) + R.dn_x[1].astype(F32)).astype(BF)
    add_b = R.wu_s.at[cols_of(1), down_b]
    add_b[...] = (add_b[...].astype(F32) + R.dn_y[1].astype(F32)).astype(BF)
    get_r2 = [copies.start(add_g, R.gu_x.at[2], near[2]), copies.start(add_a, R.dn_x.at[2], near[2]),
              copies.start(add_u, R.gu_y.at[2], near[1]), copies.start(add_b, R.dn_y.at[2], near[1])]

    g_inner = get_g.total(R.gin[aligned(place.wid * sub, sub, sub), :].astype(F32))
    mixed = R.mixed[...]
    inv_two = lax.rsqrt(jnp.mean(mixed * mixed, -1, keepdims=True) + eps_norm)
    n_two = mixed * inv_two
    scaled = g_inner * R.gall[1:2, :]
    g_mixed = (own_rows(R.dyall)
               + inv_two * (scaled - n_two * jnp.mean(scaled * n_two, -1, keepdims=True)))
    R.row_g[...] = g_mixed.astype(BF)
    get_z = []
    for hh in range(2):
        at = rows_of(place.wid, hh)
        get_z.append(LineGather(copies, place, R.row_g.at[pl.ds(hh * step_n, step_n), :],
                                functools.partial(lambda hh, c: R.gz.at[rows_of(c, hh), :], hh)))
        R.gz[at, :] = R.row_g[half_of(hh), :]
    R.gpart[1:2, :] = jnp.sum(g_inner * n_two, 0, keepdims=True)
    for copy in twin_a:
        copy.wait_recv()
    for part in get_z:
        part.relay()
    get_f = []
    for slot, i in enumerate(order):
        peer = place.wid_peer(i)
        get_f.append(copies.start(R.part_s.at[:, aligned(peer * col, col, 128)], R.recv_f.at[slot], {"wid": peer}))

    for part in get_z:
        part.wait()
    twin_z = copies.start(R.gz.at[:, other], R.twin_gz, sibling)

    gets = [[] for _ in range(heads)]
    for h in range(heads):
        cs = head_cols(h)
        go = dot(R.gz[...], R.wo_s[cs, :], 1, 1).astype(BF)
        attn_bwd_head(hops, h, R.probs, R.rcp, go, R.qt, R.v, R.fv, R.fp, R.chain,
                      R.gqt, R.near_s, R.gv, R.sendk, R.sendv, R.sendp, R.s_s)
        for i in range(1, hops + 1):
            to = place.row_peer(-i)
            gets[h].append(copies.start(R.sendv.at[i - 1, :, cs], R.recvv.at[i - 1, :, cs], to))
            gets[h].append(copies.start(R.sendk.at[i - 1, :, cs], R.recvk.at[i - 1, :, cs], to))
        for i in range(1, hops):
            gets[h].append(copies.start(R.sendp.at[i - 1, h], R.recvp.at[i - 1, h], place.row_peer(-i)))

    def left_of(ref, twin_ref):
        R.left_t[:, 0:n] = ref[:, mine].T
        R.left_t[:, n:2 * n] = twin_ref[...].T

    twin_z.wait_recv()
    left_of(R.gz, R.twin_gz)

    fine = piece // 2
    get_h = []

    def rows_at(j, lot):
        return aligned(turned(place.hid, j) * piece + lot * fine, fine, 32)

    def round_one(src, slot):
        sent = [copies.start(src.at[rows_at(3, lot), :], R.recv_q.at[slot, 2 * lot + 1], near[lot + 1]) for lot in range(2)]
        keep = [copies.start(src.at[rows_at(lot + 1, lot), :], R.recv_q.at[slot, 2 * lot], near[lot + 1]) for lot in range(2)]
        get_h.extend(keep)
        return sent

    def round_two(src, slot, sent):
        for lot in range(2):
            sent[lot].wait_recv()
            at = src.at[rows_at(2 - lot, lot), :]
            at[...] = (at[...].astype(F32) + R.recv_q[slot, 2 * lot + 1].astype(F32)).astype(BF)
            get_h.append(copies.start(at, R.recv_q.at[slot, 4 + lot], near[2 - lot]))

    R.wide_s[...] = dot(R.left_t[:, 0:n], R.o[...], 1, 0) + dot(R.left_t[:, n:2 * n], R.twin_o[...], 1, 0)
    R.d_out[...] = R.wide_s[aligned(place.hid * piece, piece, 64), :]
    R.send_o[...] = R.wide_s[...].astype(BF)
    slot_o, slot_v = heads + 1, heads
    sent_o = round_one(R.send_o, slot_o)
    left_of(R.act, R.twin_act)
    for copy in get_r2 + keep_r1:
        copy.wait_recv()
    R.d_gate_s[...] = (R.wg_s[upper, 0:ff].astype(F32) + R.gu_x[0].astype(F32) + R.gu_x[2].astype(F32))
    R.d_up_s[...] = (R.wg_s[lower, 0:ff].astype(F32) + R.gu_y[0].astype(F32) + R.gu_y[2].astype(F32))
    for lanes, ref in ((down_a, R.dn_x), (down_b, R.dn_y)):
        R.d_down_s[:, lanes] = R.wu_s[0:ff, lanes].astype(F32) + ref[0].astype(F32) + ref[2].astype(F32)
    stores = [loads.start(R.d_gate_s, R.d_gate), loads.start(R.d_up_s, R.d_up), loads.start(R.d_down_s, R.d_down)]

    row8 = lax.broadcasted_iota(jnp.int32, (n, HDIM), 1)
    gc_all = jnp.zeros((n, HDIM), F32)
    val_cols = pl.ds(3 * width, width)
    twin_h = []

    def grad_part(slot):
        return R.wd_s.at[:, pl.ds(slot * width, width)]

    def weights_of(slot, outs_of):
        cs = slice(slot * width, (slot + 1) * width)
        R.wide_s[...] = dot(R.left_t[...], R.grads[:, cs], 1, 0)
        R.wd_s[0:half, cs] = R.wide_s[...].astype(BF)
        own = R.wide_s[aligned(place.hid * piece, piece, 64), :]
        for m, (ref, at) in enumerate(outs_of):
            ref[:, at] = own[:, head_cols(m)]
        return round_one(grad_part(slot), slot)

    def outs_of(h):
        return [(ref, head_cols(h)) for ref in (R.d_query, R.d_key, R.d_house)]

    val_outs = [(R.d_value, head_cols(m)) for m in range(heads)]
    sent_h = []
    for h in range(heads):
        for copy in gets[h]:
            copy.wait_recv()
        cs = head_cols(h)
        gkt = R.recvk[0, :, cs].astype(F32)
        gv = R.gv[:, cs] + R.recvv[0, :, cs].astype(F32)
        for i in range(1, hops):
            gkt = gkt + R.recvk[i, :, cs].astype(F32)
            gv = gv + R.recvv[i, :, cs].astype(F32)
        gp = R.recvp[0, h].astype(F32)
        for i in range(1, hops - 1):
            gp = gp + R.recvp[i, h].astype(F32)
        R.grads[0:n, (9 + h) * HDIM:(10 + h) * HDIM] = gv.astype(BF)
        if h == heads - 1:
            twin_v = copies.start(R.grads.at[pl.ds(0, n), val_cols], R.grads.at[pl.ds(n, n), val_cols], sibling)
        gq, gk, gr, gc = path_bwd_head(h, heads, Heads(R.proj, 0), Heads(R.proj, 1), Heads(R.proj, 2), R.c,
                                       R.u, R.inv, R.psi, R.x1, R.y1, R.gqt[:, cs], gkt, R.near_s[h], gp)
        gc_all = jnp.where(row8 == h, gc, gc_all)
        for m, val in enumerate((gq, gk, gr)):
            R.grads[0:n, (3 * h + m) * HDIM:(3 * h + m + 1) * HDIM] = val
        gs = pl.ds(h * width, width)
        twin_h.append(copies.start(R.grads.at[pl.ds(0, n), gs], R.grads.at[pl.ds(n, n), gs], sibling))
        if 0 < h < heads - 1:
            twin_h[h - 1].wait_recv()
            sent_h.append(weights_of(h - 1, outs_of(h - 1)))
    R.gcs[0:n, :] = gc_all.astype(BF)
    twin_c = copies.start(R.gcs.at[pl.ds(0, n), :], R.gcs.at[pl.ds(n, n), :], sibling)

    inv_rms = R.inv_rms[...]
    stat = jnp.zeros((n, 1), F32)
    get_n = LineSwap(copies, place, lambda c: R.send_n.at[c], lambda q: R.recv_n.at[q])
    me, side = place.wid, place.wid // 2
    for turn, c in enumerate((3 * (1 - side), 2 - side, (1 - side) * (1 - me) + side * (5 - me), me)):
        cs = aligned(c * col, col, 128)
        g_act = dot(R.grads[0:n, :], R.w_s[cs, :], 1, 1) + dot(R.gcs[0:n, 0:heads], R.wb[:, cs], 1, 0)
        normed = R.xall[:, cs].astype(F32) * inv_rms
        both = g_act * normed
        stat = stat + jnp.sum(both * R.gall[0:1, cs], 1, keepdims=True)
        R.gpart[0:1, cs] = jnp.sum(both, 0, keepdims=True)
        if turn == 3:
            R.own_n[...] = g_act
        else:
            R.send_n[c] = g_act.astype(BF)
        if turn == 0:
            get_n.start_far()
        if turn == 2:
            get_n.start()
    R.stat_s[...] = jnp.broadcast_to(stat, (n, HDIM)).T[0:8, :]
    get_s = [copies.start(R.stat_s, R.recv_st.at[slot], d) for slot, d in enumerate(to_wid)]

    def window(p):
        return aligned(p * piece // 128 * 128, 256, 128)

    get_gain = [copies.start(R.gpart.at[:, window(lax.rem(place.row + i, place.rows_n))], R.recv_gain.at[i - 1],
                             place.row_peer(i)) for i in range(1, place.rows_n)]
    twin_c.wait_recv()
    d_beta = dot(R.gcs[0:n, :], R.act[:, mine], 0, 0) + dot(R.gcs[n:2 * n, :], R.twin_act[...], 0, 0)
    R.beta_s[...] = d_beta[0:8, :]
    get_b = [copies.start(R.beta_s.at[:, window(turned(place.hid, j))], R.recv_b.at[j - 1], near[j])
             for j in range(1, hid_n)]
    for h in (heads - 2, heads - 1):
        twin_h[h].wait_recv()
        sent_h.append(weights_of(h, outs_of(h)))
    get_n.combine()
    twin_v.wait_recv()
    sent_v = weights_of(slot_v, val_outs)
    round_two(R.send_o, slot_o, sent_o)
    for h in range(heads - 1):
        round_two(grad_part(h), h, sent_h[h])
    out = R.x[...].astype(F32) + R.part_s[:, my_cols].astype(F32)
    for slot, copy in enumerate(get_f):
        copy.wait_recv()
        out = out + R.recv_f[slot].astype(F32)
    R.output_s[...] = out.astype(BF)
    stores.append(loads.start(R.output_s, R.output))
    gain = R.gpart[:, window(place.row)]
    for i, copy in enumerate(get_gain):
        copy.wait_recv()
        gain = gain + R.recv_gain[i]
    R.gain_s[...] = gain
    get_gain2 = [copies.start(R.gain_s, R.recv_gain2.at[slot], d) for slot, d in enumerate(to_wid)]
    round_two(grad_part(slot_v), slot_v, sent_v)

    round_two(grad_part(heads - 1), heads - 1, sent_h[heads - 1])
    g_act = get_n.total(R.own_n[...])
    stats = R.stat_s[...]
    for slot in range(wid_n - 1):
        get_s[slot].wait_recv()
        stats = stats + R.recv_st[slot]
    mean = stats.T[:, 0:1] / model
    normed = R.xall[:, my_cols].astype(F32) * inv_rms
    R.d_inputs[...] = (R.gz[:, my_cols].astype(F32)
                       + inv_rms * (g_act * R.gall[0:1, my_cols] - normed * mean))
    for copy in get_h + get_b:
        copy.wait_recv()
    out_outs = [(R.d_out, head_cols(m)) for m in range(heads)]
    for slot, refs_of in [(slot_o, out_outs), (slot_v, val_outs)] + [(h, outs_of(h)) for h in range(heads)]:
        for m, (ref, at) in enumerate(refs_of):
            for lot in range(2):
                rs = slice(lot * fine, (lot + 1) * fine)
                ref[rs, at] = (ref[rs, at] + R.recv_q[slot, 2 * lot, :, head_cols(m)].astype(F32)
                               + R.recv_q[slot, 4 + lot, :, head_cols(m)].astype(F32))
    d_beta = R.beta_s[:, window(place.hid)]
    for i in range(hid_n - 1):
        d_beta = d_beta + R.recv_b[i]
    gain = R.gain_s[...]
    for slot, copy in enumerate(get_gain2):
        copy.wait_recv()
        gain = gain + R.recv_gain2[slot]

    def exact(rows, at):
        return jnp.where(at % 2 == 1, rows[:, 64:64 + piece], rows[:, 0:piece])

    R.d_beta[...] = exact(d_beta, place.hid)[0:heads, :]
    R.gain_out[...] = exact(gain, place.row)
    for store in stores:
        store.wait()
    copies.sent(copies.open)


def step(args, heads, hops, sizes):
    ins = ("lengths", "x", "dy", "gain_attn", "gain_ffn", "wq", "wk", "wv", "wr", "wb", "wo", "wg", "wu", "wd")
    shapes = dict(zip(ins, (a.shape for a in args)))
    n, col = shapes["x"]
    seq_n, hid_n, wid_n = sizes
    model, width = shapes["wq"]
    ff = shapes["wg"][1]
    sub = n // wid_n
    rows_n = seq_n * hid_n
    half = model // seq_n
    piece = model // rows_n
    slots = hops * (hops + 1) // 2
    S = jax.ShapeDtypeStruct
    V = pltpu.VMEM
    outs = dict(
        output=S((n, col), BF), d_inputs=S((n, col), F32), gain_out=S((8, piece), F32),
        d_query=S((piece, width), F32), d_key=S((piece, width), F32), d_value=S((piece, width), F32),
        d_house=S((piece, width), F32), d_beta=S((heads, piece), F32), d_out=S((piece, width), F32),
        d_gate=S((half, ff), F32), d_up=S((half, ff), F32), d_down=S((ff, half), F32),
    )
    peers_w, peers_h = wid_n - 1, hid_n - 1
    scratch = dict(
        gain_in=V((8, col), F32), gall=V((8, model), F32), inv_rms=V((n, 1), F32),
        act=V((n, model), BF), xall=V((n, model), BF), dyall=V((n, model), BF),
        proj=V((n, 3 * width), F32), c=V((n, heads), F32), v=V((n, width), BF),
        qt=V((n, width), BF), u=V((n, width), F32), inv=V((heads, n, n), F32), psi=V((heads, n, n), F32),
        x1=V((n, width), F32), y1=V((n, width), F32),
        fv=V((hops, n, width), BF), fp=V((hops - 1, heads, HDIM, HDIM), BF), chain=V((slots, n, width), BF),
        probs=V((hops + 1, heads, n, n), BF), rcp=V((n, heads), F32), o=V((n, width), BF), mixed=V((sub, model), F32),
        inner=V((n, model), BF), hidden=V((2 * n, hid_n * ff), BF), ggate=V((2 * n, hid_n * ff), BF),
        gup=V((2 * n, hid_n * ff), BF), gin=V((n, model), BF),
        w_s=V((model, 4 * width), BF), wo_s=V((width, model), BF),
        wg_s=V((model, hid_n * ff), BF), wu_s=V((model, hid_n * ff), BF), wd_s=V((hid_n * ff, model), BF),
        kt_s=V((n, width), BF), near_s=V((heads, n, n), F32), prod_s=V((heads, HDIM, HDIM), BF),
        s_s=V(((hops + 1) * n, n), F32), part_s=V((n, model), BF), recv_s=V((wid_n, sub, model), BF), recv_far=V((sub, model), BF),
        far_gu=V((2 * half, ff), BF), far_dn=V((ff, half), BF),
        row_s=V((sub, model), BF), row_g=V((sub, model), BF),
        twin_inner=V((n, half), BF), twin_dy=V((n, half), BF), twin_act=V((n, half), BF), twin_o=V((n, width), BF),
        twin_gz=V((n, half), BF), left_t=V((half, 2 * n), BF),
        gu_x=V((3, half, ff), BF), gu_y=V((3, half, ff), BF),
        dn_x=V((3, ff, half // 2), BF), dn_y=V((3, ff, half // 2), BF),
        gz=V((n, model), BF), gpart=V((8, model), F32), recv_f=V((peers_w, n, col), BF),
        gqt=V((n, width), F32), gv=V((n, width), F32),
        sendk=V((hops, n, width), BF), sendv=V((hops, n, width), BF), sendp=V((hops - 1, heads, HDIM, HDIM), BF),
        recvk=V((hops, n, width), BF), recvv=V((hops, n, width), BF), recvp=V((hops - 1, heads, HDIM, HDIM), BF),
        send_o=V((half, width), BF),
        grads=V((2 * n, 4 * width), BF), gcs=V((2 * n, HDIM), BF), wide_s=V((half, width), F32),
        recv_q=V((heads + 2, 6, piece // 2, width), BF), beta_s=V((8, half), F32), recv_b=V((peers_h, 8, 256), F32),
        own_n=V((n, col), F32), send_n=V((wid_n, n, col), BF), recv_n=V((wid_n, n, col), BF),
        output_s=V((n, col), BF), d_gate_s=V((half, ff), F32), d_up_s=V((half, ff), F32), d_down_s=V((ff, half), F32),
        stat_s=V((8, n), F32), recv_st=V((peers_w, 8, n), F32),
        recv_gain=V((rows_n - 1, 8, 256), F32), gain_s=V((8, 256), F32), recv_gain2=V((peers_w, 8, 256), F32),
    )
    n_copies = 256
    scratch.update(load_sem=pltpu.SemaphoreType.DMA((24,)), send_sem=pltpu.SemaphoreType.DMA((n_copies,)),
                   recv_sem=pltpu.SemaphoreType.DMA((n_copies,)))
    spaces = {"lengths": pltpu.SMEM, "x": pltpu.VMEM, "gain_attn": pltpu.VMEM, "gain_ffn": pltpu.VMEM, "wb": pltpu.VMEM}
    vmem = pl.BlockSpec(memory_space=pltpu.VMEM)
    early = ("output", "d_gate", "d_up", "d_down")
    res = pl.pallas_call(
        functools.partial(step_kernel, (heads, hops, sizes), ins + tuple(outs) + tuple(scratch)),
        in_specs=[pl.BlockSpec(memory_space=spaces.get(i, pl.ANY)) for i in ins],
        out_shape=tuple(outs.values()),
        out_specs=tuple(pl.BlockSpec(memory_space=pl.ANY) if i in early else vmem for i in outs),
        scratch_shapes=list(scratch.values()),
        compiler_params=pltpu.CompilerParams(
            vmem_limit_bytes=VMEM_ALL, collective_id=1, has_side_effects=True),
        name="step",
    )(*args)
    return dict(zip(outs, res))


def finish_kernel(count, *refs):
    ins, outs, bufs = refs[:count + 1], refs[count + 1:2 * count + 3], refs[2 * count + 3:3 * count + 4]
    lines, sems = refs[3 * count + 4:3 * count + 6], refs[3 * count + 6]
    loads, stores = [], []
    for a, b, c in zip(ins[:count], bufs[:count], outs[:count]):
        rows = a.shape[0]
        cut = rows // 2 if rows >= 256 else rows
        for start in range(0, rows, cut):
            i, part = len(loads), pl.ds(start, cut)
            loads.append(pltpu.make_async_copy(a.at[part, :], b.at[part, :], sems.at[0, i]))
            stores.append(pltpu.make_async_copy(b.at[part, :], c.at[part, :], sems.at[1, i]))
    last = len(loads)
    loads.insert(0, pltpu.make_async_copy(ins[count], bufs[count], sems.at[0, last]))
    for copy in loads:
        copy.start()
    loads[0].wait()
    for m in range(2):
        lines[m][...] = bufs[count][m, :]
        stores.append(pltpu.make_async_copy(lines[m], outs[count + m], sems.at[1, last + m]))
        stores[-1].start()
    for load, store in zip(loads[1:], stores):
        load.wait()
        store.start()
    for copy in stores:
        copy.wait()


def finish(arrays, gains):
    count, size = len(arrays), gains.shape[1]
    spec = pl.BlockSpec(memory_space=pl.ANY)
    vector = jax.ShapeDtypeStruct((size,), F32)
    return pl.pallas_call(
        functools.partial(finish_kernel, count),
        in_specs=[spec] * (count + 1), out_specs=[spec] * (count + 2),
        out_shape=[jax.ShapeDtypeStruct(a.shape, a.dtype) for a in arrays] + [vector, vector],
        scratch_shapes=([pltpu.VMEM(a.shape, a.dtype) for a in arrays + [gains]]
                        + [pltpu.VMEM((size,), F32)] * 2 + [pltpu.SemaphoreType.DMA((2, 2 * count + 2))]),
        compiler_params=pltpu.CompilerParams(vmem_limit_bytes=VMEM_ALL),
        name="finish",
    )(*arrays, gains)


def shifted(array, axis, by):
    peers = lax.axis_size(axis)
    pairs = [(i, i + by) for i in range(peers) if 0 <= i + by < peers]
    return lax.ppermute(array, axis, pairs)


def norm_rows(hidden_f):
    inverse = lax.rsqrt(jnp.mean(hidden_f * hidden_f, -1, keepdims=True) + eps_norm)
    return (hidden_f * inverse, inverse)


def norm_back(grad_out, normed, inverse, gain_vec):
    scaled_grad = grad_out * gain_vec
    grad_gain = jnp.sum(grad_out * normed, 0)
    grad_in = inverse * (scaled_grad - normed * jnp.mean(scaled_grad * normed, -1, keepdims=True))
    return (grad_in, grad_gain)


ROWS = ("seq", "hid")


def body(inputs, gain_attn, gain_ffn, w_query, w_key, w_value, w_house, w_beta, w_out,
         w_gate, w_up, w_down, lengths, cotangent):
    tok, col = inputs.shape
    row_devs = lax.axis_size(ROWS)
    my_row = lax.axis_index(ROWS)
    my_wid = lax.axis_index("wid")
    wid_n = lax.axis_size("wid")
    tokens_all = tok * row_devs
    most_len = max(LEAST, 2 * tokens_all // 5)
    hops = min((most_len - 2) // tok + 1, row_devs - 1)
    heads = w_query.shape[1] // HDIM
    ff = w_gate.shape[1]
    sub = tok // wid_n

    x_all = lax.all_gather(inputs, "wid", axis=1, tiled=True)
    gain_one = lax.all_gather(gain_attn, "wid", axis=0, tiled=True).astype(F32)
    gain_two = lax.all_gather(gain_ffn, "wid", axis=0, tiled=True).astype(F32)
    dy_all = lax.all_gather(cotangent, "wid", axis=1, tiled=True)
    w_gu = lax.all_gather(jnp.concatenate([w_gate, w_up], 1), "hid", axis=0)
    w_dn = lax.all_gather(w_down, "hid", axis=0)
    model = x_all.shape[1]

    residual = x_all.astype(F32)
    normed_one, inverse_one = norm_rows(residual)
    act = (normed_one * gain_one).astype(BF)

    def project(weight):
        return jnp.dot(act, weight, preferred_element_type=F32)

    q, k, r, c = project(w_query), project(w_key), project(w_house), project(w_beta)
    v = project(w_value).astype(BF)
    far_v = jnp.stack([shifted(v, ROWS, i) for i in range(1, hops + 1)])
    qt, kt, near, prod, *saved = path_fwd(q, k, r, c, heads)
    far_k = jnp.stack([shifted(kt, ROWS, i) for i in range(1, hops + 1)])
    far_p = jnp.stack([shifted(prod, ROWS, i) for i in range(1, hops)])
    row_arr = jnp.full((1,), my_row, jnp.int32)
    attended, probs, chain, rcp = attn_fwd(lengths, row_arr, qt, near, v, far_k, far_v, far_p, heads, hops)

    attn_part = jnp.dot(attended, w_out, preferred_element_type=F32).astype(BF)
    attn_rows = lax.psum_scatter(attn_part, "wid", scatter_dimension=0, tiled=True)
    x_rows = lax.dynamic_slice_in_dim(x_all, my_wid * sub, sub, 0).astype(F32)
    dy_rows = lax.dynamic_slice_in_dim(dy_all, my_wid * sub, sub, 0).astype(F32)
    mixed = x_rows + attn_rows.astype(F32)
    normed_two, inverse_two = norm_rows(mixed)
    inner = lax.all_gather((normed_two * gain_two).astype(BF), "wid", axis=0, tiled=True)

    pre = jnp.einsum("tc,hcf->htf", inner, w_gu, preferred_element_type=F32)
    gate, up = pre[:, :, :ff], pre[:, :, ff:]
    sig = jax.nn.sigmoid(gate)
    hidden = (gate * sig * up).astype(BF)
    ffn_part = jnp.einsum("htf,hfc->tc", hidden, w_dn, preferred_element_type=F32)
    ffn_part = (ffn_part + attn_part.astype(F32)).astype(BF)
    ffn_cols = lax.psum_scatter(ffn_part, "wid", scatter_dimension=1, tiled=True)
    output = (inputs.astype(F32) + ffn_cols.astype(F32)).astype(BF)

    g_hidden = jnp.einsum("tc,hfc->htf", dy_all, w_dn, preferred_element_type=F32)
    g_gate = g_hidden * up * sig * (1.0 + gate * (1.0 - sig))
    g_up = g_hidden * gate * sig
    g_pre = jnp.concatenate([g_gate, g_up], 2).astype(BF)
    g_inner = jnp.einsum("htf,hcf->tc", g_pre, w_gu, preferred_element_type=F32).astype(BF)
    g_inner = lax.psum_scatter(g_inner, "wid", scatter_dimension=0, tiled=True).astype(F32)
    g_mixed_n, g_gain_two = norm_back(g_inner, normed_two, inverse_two, gain_two)
    g_z = lax.all_gather((dy_rows + g_mixed_n).astype(BF), "wid", axis=0, tiled=True)

    d_gu = jnp.einsum("tc,htf->hcf", inner, g_pre, preferred_element_type=F32).astype(BF)
    d_dn = jnp.einsum("htf,tc->hfc", hidden, dy_all, preferred_element_type=F32).astype(BF)
    d_gu = lax.psum_scatter(d_gu, "seq", scatter_dimension=1, tiled=True)
    d_gu = lax.psum_scatter(d_gu, "hid", scatter_dimension=0)
    d_dn = lax.psum_scatter(d_dn, "seq", scatter_dimension=2, tiled=True)
    d_dn = lax.psum_scatter(d_dn, "hid", scatter_dimension=0)

    g_attn = jnp.einsum("tc,ic->ti", g_z, w_out, preferred_element_type=F32).astype(BF)
    d_out = jnp.einsum("ti,tc->ic", attended, g_z, preferred_element_type=F32).astype(BF)
    g_qt, g_near, gv, send_k, send_v, send_p = attn_bwd(probs, rcp, g_attn, qt, v, far_v, far_p, chain, heads, hops)
    g_kt = sum(shifted(send_k[i - 1], ROWS, -i).astype(F32) for i in range(1, hops + 1))
    gv = gv + sum(shifted(send_v[i - 1], ROWS, -i).astype(F32) for i in range(1, hops + 1))
    g_prod = sum(shifted(send_p[i - 1], ROWS, -i).astype(F32) for i in range(1, hops))
    g_q, g_k, g_r, g_c = path_bwd(q, k, r, c, saved, g_qt, g_kt, g_near, g_prod, heads)
    g_v = gv.astype(BF)

    def weight_grad(grad_low):
        return jnp.einsum("tc,ti->ci", act, grad_low, preferred_element_type=F32).astype(BF)

    def input_grad(grad_low, weight):
        return jnp.einsum("ti,ci->tc", grad_low, weight, preferred_element_type=F32)

    g_act = (input_grad(g_q, w_query) + input_grad(g_k, w_key) + input_grad(g_v, w_value)
             + input_grad(g_r, w_house) + input_grad(g_c, w_beta))
    g_act = lax.psum_scatter(g_act.astype(BF), "wid", scatter_dimension=0, tiled=True).astype(F32)
    normed_rows = lax.dynamic_slice_in_dim(normed_one, my_wid * sub, sub, 0)
    inverse_rows = lax.dynamic_slice_in_dim(inverse_one, my_wid * sub, sub, 0)
    g_resid, g_gain_one = norm_back(g_act, normed_rows, inverse_rows, gain_one)
    d_rows = dy_rows + g_mixed_n + g_resid
    d_inputs = lax.all_to_all(d_rows, "wid", split_axis=1, concat_axis=0, tiled=True)

    def scatter(x, dim):
        return lax.psum_scatter(x, ROWS, scatter_dimension=dim, tiled=True)

    gains = lax.psum(jnp.stack([g_gain_one, g_gain_two]), "wid")
    gains = scatter(gains, 1)
    return (
        output,
        d_inputs,
        gains[0],
        gains[1],
        scatter(weight_grad(g_q), 0).astype(F32),
        scatter(weight_grad(g_k), 0).astype(F32),
        scatter(weight_grad(g_v), 0).astype(F32),
        scatter(weight_grad(g_r), 0).astype(F32),
        scatter(weight_grad(g_c), 0).astype(F32),
        scatter(d_out, 1).astype(F32),
        d_gu[:, :ff].astype(F32),
        d_gu[:, ff:].astype(F32),
        d_dn.astype(F32),
    )


def fast_body(inputs, gain_attn, gain_ffn, w_query, w_key, w_value, w_house, w_beta, w_out,
              w_gate, w_up, w_down, lengths, cotangent):
    tok, col = inputs.shape
    row_devs = lax.axis_size(ROWS)
    sizes = tuple(lax.axis_size(i) for i in ("seq", "hid", "wid"))
    most_len = max(LEAST, 2 * tok * row_devs // 5)
    hops = min((most_len - 2) // tok + 1, row_devs - 1)
    heads = w_query.shape[1] // HDIM
    f = step((lengths, inputs, cotangent, gain_attn, gain_ffn, w_query, w_key, w_value, w_house,
              w_beta.T, w_out, w_gate, w_up, w_down), heads, hops, sizes)
    names = [i for i in f if i != "gain_out"]
    f.update(zip(names + ["gain_one", "gain_two"], finish([f[i] for i in names], f["gain_out"])))
    return (f["output"], f["d_inputs"], f["gain_one"], f["gain_two"], f["d_query"], f["d_key"], f["d_value"],
            f["d_house"], f["d_beta"].T, f["d_out"].T, f["d_gate"], f["d_up"], f["d_down"])


def slow(mesh):
    return (mesh.shape["seq"], mesh.shape["hid"], mesh.shape["wid"]) != (2, 4, 4)


def solution(mesh):
    in_specs = (
        P(("seq", "hid"), "wid"), P("wid"), P("wid"),
        P(None, "wid"), P(None, "wid"), P(None, "wid"), P(None, "wid"), P(None, "wid"),
        P("wid", None), P(None, ("hid", "wid")), P(None, ("hid", "wid")), P(("hid", "wid"), None),
        P(), P(("seq", "hid"), "wid"),
    )
    out_specs = (
        P(("seq", "hid"), "wid"), P(("seq", "hid"), "wid"), P(("seq", "hid")), P(("seq", "hid")),
        P(("seq", "hid"), "wid"), P(("seq", "hid"), "wid"), P(("seq", "hid"), "wid"),
        P(("seq", "hid"), "wid"), P(("seq", "hid"), "wid"), P("wid", ("seq", "hid")),
        P("seq", ("hid", "wid")), P("seq", ("hid", "wid")), P(("hid", "wid"), "seq"),
    )
    return jax.shard_map(body if slow(mesh) else fast_body, mesh=mesh, in_specs=in_specs, out_specs=out_specs, check_vma=False)
```

```python
import functools
import types

import jax
import jax.numpy as jnp
from jax import lax
from jax.experimental import pallas as pl
from jax.experimental.pallas import tpu as pltpu
from jax.sharding import PartitionSpec as P

HDIM = 128
LEAST = 1024

eps_norm = 1e-06
neg_big = -1e30
BF = jnp.bfloat16
F32 = jnp.float32
VMEM_LIMIT = 60 * 1024 * 1024
VMEM_ALL = 67043328


def dot(a, b, ca, cb):
    return lax.dot_general(a, b, (((ca,), (cb,)), ((), ())), preferred_element_type=F32)


def split(a):
    hi = a.astype(BF)
    return hi, (a - hi.astype(F32)).astype(BF)


def dot3(a, b, ca, cb):
    return dot(a[0], b[0], ca, cb) + (dot(a[0], b[1], ca, cb) + dot(a[1], b[0], ca, cb))


def dot1(a, b, ca, cb):
    return dot(a.astype(BF), b.astype(BF), ca, cb)


def iotas(n):
    rows = lax.broadcasted_iota(jnp.int32, (n, n), 0)
    cols = lax.broadcasted_iota(jnp.int32, (n, n), 1)
    return rows, cols


def head_cols(h):
    return slice(h * HDIM, (h + 1) * HDIM)


def house_terms(raw, strength, heads, h):
    inv = lax.rsqrt(jnp.sum(raw * raw, -1, keepdims=True) + eps_norm)
    lane = lax.broadcasted_iota(jnp.int32, strength.shape, 1)
    c = jnp.sum(jnp.where(lane == h, strength, 0.0), 1, keepdims=True)
    root = jnp.sqrt(2.0 / (1.0 + jnp.exp(-c)))
    return inv, root


def path_fwd_stage(heads, q_ref, k_ref, r_ref, c_ref, qt_ref, kt_ref, near_ref, p_ref,
                   u_ref, inv_ref, psi_ref, x_ref, y_ref, done=None):
    n = c_ref.shape[0]
    rows, cols = iotas(n)
    strength = c_ref[...]
    m = n // 2
    side_rows = lax.broadcasted_iota(jnp.int32, (m, n), 0)
    wide_cols = lax.broadcasted_iota(jnp.int32, (m, n), 1)
    side_cols = wide_cols % m

    def diagonal(pair):
        return [jnp.concatenate([jnp.where(wide_cols < m, part, 0).astype(BF),
                                 jnp.where(wide_cols >= m, part, 0).astype(BF)], 0) for part in pair]

    us2 = []
    for h in range(heads):
        raw = r_ref[:, head_cols(h)]
        inv, root = house_terms(raw, strength, heads, h)
        u = raw * (inv * root)
        u_ref[:, head_cols(h)] = u
        u2 = split(u)
        us2.append(u2)
        low = jnp.where(rows > cols, dot3(u2, u2, 1, 1), 0.0)
        blocks = jnp.concatenate([low[0:m, 0:m], low[m:n, m:n]], 1)
        psi_ref[h, 0:m, :] = blocks
        psi_ref[h, m:n, 0:m] = low[m:n, 0:m]
        inv_ref[h, 0:m, :] = (jnp.where(side_rows == side_cols, 1.0, 0.0)
                              - jnp.where(side_rows // 2 == side_cols // 2, blocks, 0.0))

    def double(step, carry):
        apart = jnp.right_shift(side_rows, step) != jnp.right_shift(side_cols, step)
        pick = apart & (jnp.right_shift(side_rows, step + 1) == jnp.right_shift(side_cols, step + 1))
        now = [split(inv_ref[h, 0:m, :]) for h in range(heads)]
        mids = [dot3(split(jnp.where(pick, psi_ref[h, 0:m, :], 0.0)), diagonal(now[h]), 1, 0) for h in range(heads)]
        for h in range(heads):
            inv_ref[h, 0:m, :] = inv_ref[h, 0:m, :] - dot3(now[h], diagonal(split(mids[h])), 1, 0)
        return carry

    lax.fori_loop(1, (m - 1).bit_length(), double, 0)
    for h in range(heads):
        first, second = inv_ref[h, 0:m, 0:m], inv_ref[h, 0:m, m:n]
        corner = -dot3(split(second), split(dot3(split(psi_ref[h, m:n, 0:m]), split(first), 1, 0)), 1, 0)
        inv_ref[h, 0:m, m:n] = jnp.zeros((m, m), F32)
        inv_ref[h, m:n, 0:m] = corner
        inv_ref[h, m:n, m:n] = second
    er, ec = iotas(HDIM)
    for h in range(heads):
        kin = split(inv_ref[h])
        k = k_ref[:, head_cols(h)]
        u2 = us2[h]
        aq = jnp.where(rows < cols, dot3(split(k), u2, 1, 1), 0.0)
        y = dot3(kin, u2, 0, 0)
        y_ref[:, head_cols(h)] = y
        kt_ref[:, head_cols(h)] = (k - dot3(split(aq), split(y), 1, 0)).astype(BF)
        x = dot3(kin, u2, 1, 0)
        x_ref[:, head_cols(h)] = x
        p_ref[h] = (jnp.where(er == ec, 1.0, 0.0) - dot3(u2, split(x), 0, 0)).astype(p_ref.dtype)
        if done is not None:
            done(h)
    for h in range(heads):
        kin = split(inv_ref[h])
        q = q_ref[:, head_cols(h)]
        q2, k2, u2, x2 = split(q), split(k_ref[:, head_cols(h)]), us2[h], split(x_ref[:, head_cols(h)])
        fq2 = split(jnp.where(rows >= cols, dot3(q2, u2, 1, 1), 0.0))
        qt_ref[:, head_cols(h)] = (q - dot3(fq2, x2, 1, 0)).astype(BF)
        psi = dot3(kin, split(jnp.where(rows > cols, dot3(u2, k2, 1, 1), 0.0)), 1, 0)
        psi_ref[h] = psi
        near_ref[h] = dot3(q2, k2, 1, 1) - dot3(fq2, split(psi), 1, 0)


def path_fwd_kernel(heads, *refs):
    path_fwd_stage(heads, *refs)


def path_fwd(q, k, r, c, heads):
    n, width = q.shape
    flat = jax.ShapeDtypeStruct((n, width), F32)
    low = jax.ShapeDtypeStruct((n, width), BF)
    square = jax.ShapeDtypeStruct((heads, n, n), F32)
    return pl.pallas_call(
        functools.partial(path_fwd_kernel, heads),
        out_shape=(low, low, square, jax.ShapeDtypeStruct((heads, HDIM, HDIM), F32),
                   flat, square, square, flat, flat),
        compiler_params=pltpu.CompilerParams(vmem_limit_bytes=VMEM_LIMIT),
        name="path_fwd",
    )(q, k, r, c)


def doc_of(pos, len_ref):
    total = len_ref[0]
    doc = (pos >= total).astype(jnp.int32)
    for i in range(1, len_ref.shape[0]):
        total = total + len_ref[i]
        doc = doc + (pos >= total).astype(jnp.int32)
    return doc


def chain_slot(r, m):
    return r * (r - 1) // 2 + m


def key_chain(hops, h, fp_ref, chain_ref):
    cs = head_cols(h)
    for r in range(2, hops + 1):
        keys = chain_ref[chain_slot(r, 0), :, cs]
        for m in range(1, r):
            keys = dot(keys, fp_ref[r - m - 1, h].astype(BF), 1, 1).astype(BF)
            chain_ref[chain_slot(r, m), :, cs] = keys


def attn_fwd_rows(hops, h, start, count, row, len_ref, qt_ref, near_ref, v_ref, fv_ref, chain_ref,
                  o_ref, p_ref, rcp_ref, s_ref):
    n = qt_ref.shape[0]
    scale = HDIM ** (-0.5)
    cs, rs = head_cols(h), slice(start, start + count)
    rows = start + lax.broadcasted_iota(jnp.int32, (count, n), 0)
    cols = lax.broadcasted_iota(jnp.int32, (count, n), 1)
    key_at = lax.broadcasted_iota(jnp.int32, (1, n), 1)
    own = doc_of(row * n + start + lax.broadcasted_iota(jnp.int32, (count, 1), 0), len_ref)
    near_ok = (rows >= cols) & (own == doc_of(row * n + key_at, len_ref))
    q = qt_ref[rs, cs]
    s = jnp.where(near_ok, near_ref[h, rs, :] * scale, neg_big)
    s_ref[0:count, :] = s
    top = jnp.max(s, 1, keepdims=True)
    for r in range(1, hops + 1):
        source = row - r
        docs = jnp.where(source >= 0, doc_of(source * n + key_at, len_ref), -1)
        keys = chain_ref[chain_slot(r, r - 1), :, cs]
        s = jnp.where(own == docs, dot(q, keys, 1, 1) * scale, neg_big)
        s_ref[r * count:(r + 1) * count, :] = s
        top = jnp.maximum(top, jnp.max(s, 1, keepdims=True))
    total = jnp.zeros((count, 1), F32)
    out = jnp.zeros((count, HDIM), F32)
    for r in range(hops + 1):
        e = jnp.exp(s_ref[r * count:(r + 1) * count, :] - top)
        total = total + jnp.sum(e, 1, keepdims=True)
        weights = e.astype(BF)
        p_ref[r, h, rs, :] = weights
        out = out + dot(weights, v_ref[:, cs] if r == 0 else fv_ref[r - 1, :, cs], 1, 0)
    recip = 1.0 / total
    rcp_ref[rs, h:h + 1] = recip
    o_ref[rs, cs] = (out * recip).astype(BF)


def attn_fwd_kernel(heads, hops, len_ref, row_ref, qt_ref, near_ref, v_ref, fk_ref, fv_ref, fp_ref,
                    o_ref, p_ref, chain_ref, rcp_ref, s_ref):
    for r in range(1, hops + 1):
        chain_ref[chain_slot(r, 0)] = fk_ref[r - 1]
    for h in range(heads):
        key_chain(hops, h, fp_ref, chain_ref)
        attn_fwd_rows(hops, h, 0, qt_ref.shape[0], row_ref[0], len_ref, qt_ref, near_ref, v_ref, fv_ref, chain_ref,
                      o_ref, p_ref, rcp_ref, s_ref)


def attn_fwd(lengths, my_row, qt, near, v, far_k, far_v, far_p, heads, hops):
    n, width = qt.shape
    slots = hops * (hops + 1) // 2
    smem = pl.BlockSpec(memory_space=pltpu.SMEM)
    vmem = pl.BlockSpec(memory_space=pltpu.VMEM)
    return pl.pallas_call(
        functools.partial(attn_fwd_kernel, heads, hops),
        in_specs=[smem, smem] + [vmem] * 6,
        out_shape=(
            jax.ShapeDtypeStruct((n, width), BF),
            jax.ShapeDtypeStruct((hops + 1, heads, n, n), BF),
            jax.ShapeDtypeStruct((slots, n, width), BF),
            jax.ShapeDtypeStruct((n, heads), F32),
        ),
        scratch_shapes=[pltpu.VMEM(((hops + 1) * n, n), F32)],
        compiler_params=pltpu.CompilerParams(vmem_limit_bytes=VMEM_LIMIT),
        name="attn_fwd",
    )(lengths, my_row, qt, near, v, far_k, far_v, far_p)


def attn_bwd_kernel(heads, hops, p_ref, rcp_ref, go_ref, qt_ref, v_ref, fv_ref, fp_ref, chain_ref,
                    gqt_ref, gnear_ref, gv_ref, sendk_ref, sendv_ref, sendp_ref, dp_ref):
    for h in range(heads):
        attn_bwd_head(hops, h, p_ref, rcp_ref, go_ref[:, head_cols(h)], qt_ref, v_ref, fv_ref, fp_ref, chain_ref,
                      gqt_ref, gnear_ref, gv_ref, sendk_ref, sendv_ref, sendp_ref, dp_ref)


def attn_bwd(p, rcp, go, qt, v, far_v, far_p, chain, heads, hops):
    n, width = qt.shape
    return pl.pallas_call(
        functools.partial(attn_bwd_kernel, heads, hops),
        out_shape=(
            jax.ShapeDtypeStruct((n, width), F32),
            jax.ShapeDtypeStruct((heads, n, n), F32),
            jax.ShapeDtypeStruct((n, width), F32),
            jax.ShapeDtypeStruct((hops, n, width), BF),
            jax.ShapeDtypeStruct((hops, n, width), BF),
            jax.ShapeDtypeStruct((hops - 1, heads, HDIM, HDIM), BF),
        ),
        scratch_shapes=[pltpu.VMEM(((hops + 1) * n, n), F32)],
        compiler_params=pltpu.CompilerParams(vmem_limit_bytes=VMEM_LIMIT),
        name="attn_bwd",
    )(p, rcp, go, qt, v, far_v, far_p, chain)


def path_bwd_kernel(heads, q_ref, k_ref, r_ref, c_ref, u_ref, inv_ref, psi_ref, x_ref, y_ref,
                    gqt_ref, gkt_ref, gnear_ref, gp_ref, gq_ref, gk_ref, gr_ref, gc_ref):
    lane = lax.broadcasted_iota(jnp.int32, c_ref.shape, 1)
    gc_all = jnp.zeros(c_ref.shape, F32)
    for h in range(heads):
        cs = head_cols(h)
        gq, gk, gr, gc = path_bwd_head(h, heads, q_ref, k_ref, r_ref, c_ref, u_ref, inv_ref, psi_ref, x_ref, y_ref,
                                       gqt_ref[:, cs], gkt_ref[:, cs], gnear_ref[h], gp_ref[h])
        gq_ref[:, cs] = gq
        gk_ref[:, cs] = gk
        gr_ref[:, cs] = gr
        gc_all = jnp.where(lane == h, gc, gc_all)
    gc_ref[...] = gc_all.astype(BF)


def path_bwd(q, k, r, c, saved, gqt, gkt, gnear, gp, heads):
    n, width = q.shape
    low = jax.ShapeDtypeStruct((n, width), BF)
    return pl.pallas_call(
        functools.partial(path_bwd_kernel, heads),
        out_shape=(low, low, low, jax.ShapeDtypeStruct((n, heads), BF)),
        compiler_params=pltpu.CompilerParams(vmem_limit_bytes=VMEM_LIMIT),
        name="path_bwd",
    )(q, k, r, c, *saved, gqt, gkt, gnear, gp)


MESH = pl.DeviceIdType.MESH


class Copies:
    def __init__(self, send, recv):
        self.send, self.recv, self.count, self.open = send, recv, 0, []

    def take(self):
        self.count = self.count + 1
        return self.count - 1

    def make(self, src, dst, device, send, recv):
        return pltpu.make_async_remote_copy(
            src_ref=src, dst_ref=dst, send_sem=self.send.at[send], recv_sem=self.recv.at[recv],
            device_id=device, device_id_type=MESH)

    def begin(self, copy):
        copy.start()
        self.open.append(copy)
        return copy

    def start(self, src, dst, device):
        i = self.take()
        return self.begin(self.make(src, dst, device, i, i))

    def sent(self, some):
        for copy in some:
            copy.wait_send()
        self.open = [copy for copy in self.open if all(copy is not other for other in some)]


class Loads:
    def __init__(self, sems):
        self.sems, self.count = sems, 0

    def start(self, src, dst):
        copy = pltpu.make_async_copy(src, dst, self.sems.at[self.count])
        self.count = self.count + 1
        copy.start()
        return copy


class Place:
    def __init__(self, sizes):
        self.seq_n, self.hid_n, self.wid_n = sizes
        self.seq = lax.axis_index("seq")
        self.hid = lax.axis_index("hid")
        self.wid = lax.axis_index("wid")
        self.rows_n = self.seq_n * self.hid_n
        self.row = self.seq * self.hid_n + self.hid

    def wid_peer(self, i):
        return lax.rem(self.wid + i, self.wid_n)

    def hid_peer(self, i):
        return lax.rem(self.hid + i, self.hid_n)

    def seq_peer(self, i):
        return lax.rem(self.seq + i, self.seq_n)

    def row_peer(self, i):
        to = lax.rem(self.row + i + self.rows_n, self.rows_n)
        return {"seq": to // self.hid_n, "hid": lax.rem(to, self.hid_n)}

    def barrier(self):
        sem = pltpu.get_barrier_semaphore()
        for i in range(1, self.wid_n):
            pl.semaphore_signal(sem, inc=1, device_id={"wid": self.wid_peer(i)}, device_id_type=MESH)
        for i in range(1, self.rows_n):
            pl.semaphore_signal(sem, inc=1, device_id=self.row_peer(i), device_id_type=MESH)
        pl.semaphore_wait(sem, self.wid_n - 1 + self.rows_n - 1)


class Sometimes:
    def __init__(self, copy, sends=None, gets=None):
        self.copy, self.sends, self.gets = copy, sends, gets

    def on(self, flag, act):
        if flag is None:
            act()
        else:
            pl.when(flag)(act)

    def start(self):
        self.on(self.sends, lambda: self.copy.start() and None)

    def wait_send(self):
        self.on(self.sends, self.copy.wait_send)

    def wait_recv(self):
        self.on(self.gets, self.copy.wait_recv)


class LineGather:
    def __init__(self, copies, place, src, view):
        me = place.wid
        self.me, self.copies, self.view = me, copies, view
        self.ids = [copies.take() for _ in range(3)]
        here = view(me)
        self.by = {i: copies.make(src, here, {"wid": place.wid_peer(i)}, self.ids[i - 1], self.ids[i - 1])
                   for i in (1, 2, 3)}
        self.by[1] = Sometimes(self.by[1], me != 3)
        self.by[3] = Sometimes(self.by[3], me != 0)
        for i in (2, 1, 3):
            copies.begin(self.by[i])

    def relay(self):
        self.by[2].wait_recv()
        for m, chunk, to, i in ((1, 3, 0, 1), (2, 0, 3, 3)):
            part = self.view(chunk)
            copy = self.copies.make(part, part, {"wid": to}, self.copies.take(), self.ids[i - 1])
            self.copies.begin(Sometimes(copy, self.me == m))

    def wait(self):
        self.by[1].wait_recv()
        self.by[3].wait_recv()


class LineSwap:
    def __init__(self, copies, place, piece, recv):
        self.copies, self.place, self.me, self.piece, self.recv = copies, place, place.wid, piece, recv
        self.ids = [copies.take() for _ in range(4)]
        me = self.me

        @pl.when(me == 0)
        def _():
            recv(0)[...] = jnp.zeros(recv(0).shape, BF)

        @pl.when(me == 3)
        def _():
            recv(2)[...] = jnp.zeros(recv(2).shape, BF)

    def make(self, src, i, slot, device, send):
        return self.copies.make(src, self.recv(slot), device, send, self.ids[slot])

    def start_far(self):
        self.far = []
        for end, far, middle in ((0, 3, 1), (3, 0, 2)):
            copy = Sometimes(self.make(self.piece(far), 0, 3, {"wid": middle}, self.copies.take()),
                             self.me == end, self.me == middle)
            self.copies.begin(copy)
            self.far.append(copy)

    def start(self):
        me, place = self.me, self.place
        to = [place.wid_peer(i) for i in range(4)]
        self.two = Sometimes(self.make(self.piece(to[2]), 2, 1, {"wid": to[2]}, self.ids[1]), (me == 0) | (me == 3))
        self.one = Sometimes(self.make(self.piece(to[1]), 1, 0, {"wid": to[1]}, self.ids[0]), me != 3, me != 0)
        self.three = Sometimes(self.make(self.piece(to[3]), 3, 2, {"wid": to[3]}, self.ids[2]), me != 0, me != 3)
        for copy in (self.two, self.one, self.three):
            self.copies.begin(copy)

    def combine(self):
        for copy in self.far:
            copy.wait_recv()
        mid = (self.me == 1) | (self.me == 2)
        far = 3 * (2 - jnp.minimum(jnp.maximum(self.me, 1), 2))

        @pl.when(mid)
        def _():
            at = self.recv(3)
            at[...] = (at[...].astype(F32) + self.piece(far)[...].astype(F32)).astype(BF)

        copy = self.make(self.recv(3), 2, 1, {"wid": far}, self.copies.take())
        self.copies.begin(Sometimes(copy, mid))

    def total(self, own):
        for copy in (self.two, self.one, self.three):
            copy.wait_recv()
        for slot in range(3):
            own = own + self.recv(slot)[...].astype(F32)
        return own


def aligned(start, size, step):
    return pl.ds(pl.multiple_of(start, step), size)


def attn_bwd_head(hops, h, p_ref, rcp_ref, go, qt_ref, v_ref, fv_ref, fp_ref, chain_ref,
                  gqt_ref, gnear_ref, gv_ref, sendk_ref, sendv_ref, sendp_ref, dp_ref):
    n = qt_ref.shape[0]
    scale = HDIM ** (-0.5)
    cs = head_cols(h)
    q = qt_ref[:, cs]
    recip = rcp_ref[:, h:h + 1]
    go_low = (go.astype(F32) * recip).astype(BF)
    delta = jnp.zeros((n, 1), F32)
    for r in range(hops + 1):
        vals = v_ref[:, cs] if r == 0 else fv_ref[r - 1, :, cs]
        dp = dot(go, vals, 1, 1)
        dp_ref[r * n:(r + 1) * n, :] = dp
        delta = delta + jnp.sum(p_ref[r, h].astype(F32) * dp, 1, keepdims=True)
        gv = dot(p_ref[r, h], go_low, 0, 0)
        if r == 0:
            gv_ref[:, cs] = gv
        else:
            sendv_ref[r - 1, :, cs] = gv.astype(BF)
    delta = delta * recip
    factor = recip * scale
    gnear_ref[h] = p_ref[0, h].astype(F32) * ((dp_ref[0:n, :] - delta) * factor)
    gq = jnp.zeros((n, HDIM), F32)
    gps = [jnp.zeros((HDIM, HDIM), F32) for _ in range(hops - 1)]
    for r in range(1, hops + 1):
        gs = (p_ref[r, h].astype(F32) * ((dp_ref[r * n:(r + 1) * n, :] - delta) * factor)).astype(BF)
        gq = gq + dot(gs, chain_ref[chain_slot(r, r - 1), :, cs], 1, 0)
        gk = dot(gs, q, 0, 0)
        for m in range(r - 1, 0, -1):
            back = r - m - 1
            gkb = gk.astype(BF)
            gps[back] = gps[back] + dot(gkb, chain_ref[chain_slot(r, m - 1), :, cs], 0, 0)
            gk = dot(gkb, fp_ref[back, h].astype(BF), 1, 0)
        sendk_ref[r - 1, :, cs] = gk.astype(BF)
    gqt_ref[:, cs] = gq
    for i in range(hops - 1):
        sendp_ref[i, h] = gps[i].astype(BF)


def path_bwd_head(h, heads, q_ref, k_ref, r_ref, c_ref, u_ref, inv_ref, psi_ref, x_ref, y_ref,
                  gqt, gkt, gs, gp):
    n = c_ref.shape[0]
    rows, cols = iotas(n)
    cs = head_cols(h)
    q, k, u = q_ref[:, cs], k_ref[:, cs], u_ref[:, cs]
    qb, kb, ub = q.astype(BF), k.astype(BF), u.astype(BF)
    kin = inv_ref[h].astype(BF)
    psi = psi_ref[h].astype(BF)
    x, y = x_ref[:, cs].astype(BF), y_ref[:, cs].astype(BF)
    gqtb, gktb = gqt.astype(BF), gkt.astype(BF)
    gsb = gs.astype(BF)
    gst = gs.T.astype(BF)
    gp = gp.astype(BF)
    f = jnp.where(rows <= cols, dot(ub, qb, 1, 1), 0.0).astype(BF)
    fq = jnp.where(rows >= cols, dot(qb, ub, 1, 1), 0.0).astype(BF)
    a = jnp.where(rows > cols, dot(ub, kb, 1, 1), 0.0).astype(BF)
    gx = -(dot(f, gqtb, 1, 0) + dot(ub, gp, 1, 0))
    gy = -dot(a, gktb, 1, 0)
    phiq = dot(fq, kin, 1, 0).astype(BF)
    back = dot(gst, phiq, 1, 0)
    backb = back.astype(BF)
    gfq = jnp.where(rows >= cols, -(dot(gqtb, x, 1, 1) + dot(gsb, psi, 1, 1)), 0.0)
    gaq = jnp.where(rows < cols, -(dot(gktb, y, 1, 1) + back), 0.0)
    kgx = dot(kin, gx.astype(BF), 0, 0)
    kgy = dot(kin, gy.astype(BF), 1, 0)
    zt = dot(x, kgx.astype(BF), 1, 1) + dot(kgy.astype(BF), y, 1, 1) - dot(psi, backb, 1, 0)
    glt = jnp.where(rows < cols, -zt, 0.0)
    sym = (glt + glt.T).astype(BF)
    gfqb, gaqb = gfq.astype(BF), gaq.astype(BF)
    gu = (kgx + kgy - dot(x, gp, 1, 1) + dot(gfq.T.astype(BF), qb, 1, 0)
          + dot(gaq.T.astype(BF), kb, 1, 0) + dot(sym, ub, 1, 0))
    gq = (gqt + dot(gsb, kb, 1, 0) + dot(gfqb, ub, 1, 0)).astype(BF)
    gk = (gkt + dot(gst, qb, 1, 0) + dot(gaqb, ub, 1, 0)).astype(BF)
    raw = r_ref[:, cs]
    inv, root = house_terms(raw, c_ref[...], heads, h)
    gc = jnp.sum(gu * u, 1, keepdims=True) * (1.0 - 0.5 * root * root) * 0.5
    gun = gu * root
    un = raw * inv
    gr = (inv * (gun - un * jnp.sum(gun * un, 1, keepdims=True))).astype(BF)
    return gq, gk, gr, gc


class Heads:
    def __init__(self, ref, kind):
        self.ref, self.kind = ref, kind

    def __getitem__(self, index):
        base = 3 * index[1].start + self.kind * HDIM
        return self.ref[index[0], base:base + HDIM]


def turned(index, by):
    low = index % 2
    high = index // 2 % 2
    return index + (1 - 2 * low) * (by % 2) + (2 - 4 * high) * (by // 2)


def step_kernel(cfg, names, *refs):
    heads, hops, sizes = cfg
    R = types.SimpleNamespace(**dict(zip(names, refs)))
    place = Place(sizes)
    wid_n, hid_n, seq_n = place.wid_n, place.hid_n, place.seq_n
    n, col = R.x.shape
    width = heads * HDIM
    model = R.act.shape[1]
    ff = R.wg.shape[1]
    sub = n // wid_n
    half = model // seq_n
    piece = model // place.rows_n
    copies, loads = Copies(R.send_sem, R.recv_sem), Loads(R.load_sem)
    my_cols = aligned(place.wid * col, col, 128)
    part_n = n // 2
    step_n = sub // 2

    def rows_of(w, hh):
        return aligned(hh * part_n + w * step_n, step_n, step_n)

    def half_of(hh):
        return slice(hh * step_n, (hh + 1) * step_n)

    def own_rows(ref):
        return jnp.concatenate([ref[rows_of(place.wid, hh), :].astype(F32) for hh in range(2)], 0)

    mine = aligned(place.seq * half, half, 128)
    other = aligned((1 - place.seq) * half, half, 128)
    sibling = {"seq": 1 - place.seq}
    order = sorted(range(1, wid_n), key=lambda i: -min(i, wid_n - i))
    to_wid = [{"wid": place.wid_peer(i)} for i in order]
    near = [{"hid": turned(place.hid, j)} for j in range(hid_n)]

    R.gain_in[0:1, :] = R.gain_attn[...].astype(F32).reshape(1, col)
    R.gain_in[1:2, :] = R.gain_ffn[...].astype(F32).reshape(1, col)
    R.xall[:, my_cols] = R.x[...]
    R.gall[:, my_cols] = R.gain_in[...]
    place.barrier()

    get_x = LineGather(copies, place, R.x, lambda c: R.xall.at[:, aligned(c * col, col, 128)])
    get_gains = [copies.start(R.gain_in, R.gall.at[:, my_cols], d) for d in to_wid]

    part_f = ff // seq_n
    mine_c = aligned(place.seq * half, half, 16)
    mine_f = aligned(place.seq * part_f, part_f, 16)

    def cols_of(j):
        return pl.ds(j * ff, ff)

    def down_rows(j, piece_i=0, pieces=1):
        size = part_f // pieces
        return aligned(j * ff + place.seq * part_f + piece_i * size, size, 16)

    def pass_on(ref, device):
        return copies.start(ref, ref, device)

    get_gate = [copies.start(R.wg.at[mine_c, :], R.wg_s.at[mine_c, cols_of(j)], near[j]) for j in (1, 2)]
    load_v = loads.start(R.wv, R.w_s.at[:, pl.ds(3 * width, width)])
    load_w = [loads.start(w.at[:, pl.ds(h * HDIM, HDIM)], R.w_s.at[:, pl.ds((3 * h + m) * HDIM, HDIM)])
              for h in range(heads) for m, w in enumerate((R.wq, R.wk, R.wr))]
    load_dy = loads.start(R.dy, R.dyall.at[:, my_cols])
    load_o = loads.start(R.wo, R.wo_s)
    load_f = [loads.start(R.wg, R.wg_s.at[:, pl.ds(0, ff)]), loads.start(R.wu, R.wu_s.at[:, pl.ds(0, ff)]),
              loads.start(R.wd, R.wd_s.at[pl.ds(0, ff), :])]

    for copy in get_gate:
        copy.wait_recv()
    relay = [copies.start(R.wg_s.at[mine_c, cols_of(1)], R.wg_s.at[mine_c, cols_of(3)], near[2])]
    get_x.relay()
    get_x.wait()
    for copy in get_gains:
        copy.wait_recv()
    get_dy = [copies.start(R.dy, R.dyall.at[:, my_cols], d) for d in to_wid]
    xf = R.xall[...].astype(F32)
    inv_rms = lax.rsqrt(jnp.mean(xf * xf, -1, keepdims=True) + eps_norm)
    R.inv_rms[...] = inv_rms
    R.act[...] = (xf * inv_rms * R.gall[0:1, :]).astype(BF)
    load_v.wait()
    R.v[...] = dot(R.act[...], R.w_s[:, 3 * width:4 * width], 1, 0).astype(BF)
    get_v = [copies.start(R.v, R.fv.at[i - 1], place.row_peer(i)) for i in range(1, hops + 1)]
    for copy in load_w:
        copy.wait()
    R.proj[...] = dot(R.act[...], R.w_s[:, 0:3 * width], 1, 0)
    R.c[...] = dot(R.act[...], R.wb[...], 1, 1)

    get_k = [[] for _ in range(heads)]
    get_p = [[] for _ in range(heads)]

    def send_head(h):
        cs = head_cols(h)
        for i in range(1, hops + 1):
            get_k[h].append(copies.start(R.kt_s.at[:, cs], R.chain.at[chain_slot(i, 0), :, cs], place.row_peer(i)))
        for i in range(1, hops):
            get_p[h].append(copies.start(R.prod_s.at[h], R.fp.at[i - 1, h], place.row_peer(i)))

    path_fwd_stage(heads, Heads(R.proj, 0), Heads(R.proj, 1), Heads(R.proj, 2), R.c, R.qt, R.kt_s, R.near_s, R.prod_s,
                   R.u, R.inv, R.psi, R.x1, R.y1, send_head)

    get_up = [copies.start(R.wu.at[mine_c, :], R.wu_s.at[mine_c, cols_of(j)], near[j]) for j in (1, 2)]
    get_down = [copies.start(R.wd.at[mine_f, :], R.wd_s.at[down_rows(j), :], near[j]) for j in (1, 2)]

    for copy in get_v:
        copy.wait_recv()
    load_o.wait()
    get_a = []
    for hh in range(2):
        for h in range(heads):
            if hh == 0:
                for copy in get_k[h] + get_p[h]:
                    copy.wait_recv()
                key_chain(hops, h, R.fp, R.chain)
            attn_fwd_rows(hops, h, hh * part_n, part_n, place.row, R.lengths, R.qt, R.near_s, R.v, R.fv, R.chain,
                          R.o, R.probs, R.rcp, R.s_s)
        rs = slice(hh * part_n, (hh + 1) * part_n)
        R.part_s[rs, :] = dot(R.o[rs, :], R.wo_s[...], 1, 0).astype(BF)
        get_a.append(LineSwap(copies, place, functools.partial(lambda hh, c: R.part_s.at[rows_of(c, hh), :], hh),
                              functools.partial(lambda hh, q: R.recv_s.at[q, pl.ds(hh * step_n, step_n), :], hh)))
        get_a[hh].start_far()
        get_a[hh].start()
    three = pl.ds(ff, 3 * ff)
    get_i = []

    def mix(hh):
        at, keep = rows_of(place.wid, hh), half_of(hh)
        mixed = get_a[hh].total(R.xall[at, :].astype(F32) + R.part_s[at, :].astype(F32))
        R.mixed[keep, :] = mixed
        inv_two = lax.rsqrt(jnp.mean(mixed * mixed, -1, keepdims=True) + eps_norm)
        R.row_s[keep, :] = (mixed * inv_two * R.gall[1:2, :]).astype(BF)
        get_i.append(LineGather(copies, place, R.row_s.at[pl.ds(hh * step_n, step_n), :],
                                functools.partial(lambda hh, c: R.inner.at[rows_of(c, hh), :], hh)))
        R.inner[at, :] = R.row_s[keep, :]

    get_a[0].combine()
    mix(0)
    get_a[1].combine()
    for copy in get_up:
        copy.wait_recv()
    relay.append(copies.start(R.wu_s.at[mine_c, cols_of(2)], R.wu_s.at[mine_c, cols_of(3)], near[1]))
    for copy in get_down:
        copy.wait_recv()
    relay_d = [copies.start(R.wd_s.at[down_rows(1, 0, 2), :], R.wd_s.at[down_rows(3, 0, 2), :], near[2]),
               copies.start(R.wd_s.at[down_rows(2, 1, 2), :], R.wd_s.at[down_rows(3, 1, 2), :], near[1])]
    mix(1)
    get_i[0].relay()
    for copy in relay:
        copy.wait_recv()
    shared = [pass_on(ref.at[mine_c, three], sibling) for ref in (R.wg_s, R.wu_s)]
    for copy in relay_d:
        copy.wait_recv()
    shared += [pass_on(R.wd_s.at[down_rows(j), :], sibling) for j in (1, 2, 3)]
    twin_a = [copies.start(R.act.at[:, other], R.twin_act, sibling),
              copies.start(R.o, R.twin_o, sibling)]
    load_dy.wait()
    for copy in load_f:
        copy.wait()
    get_i[1].relay()
    for copy in get_dy + shared:
        copy.wait_recv()
    for part in get_i:
        part.wait()
    twin = [copies.start(R.inner.at[:, other], R.twin_inner, sibling),
            copies.start(R.dyall.at[:, other], R.twin_dy, sibling)]

    swapped = (R.hidden, R.ggate, R.gup)
    swap_ids = [copies.take() for _ in range(3 * hid_n)]

    def swap(m, cs, i):
        return copies.make(swapped[m].at[pl.ds(0, n), cs], swapped[m].at[pl.ds(n, n), cs], sibling, i, i)

    def hidden_tile(t, carry):
        j = hid_n - 1 - t
        cs = aligned(j * ff, ff, 128)
        gate = dot(R.inner[...], R.wg_s[:, cs], 1, 0)
        up = dot(R.inner[...], R.wu_s[:, cs], 1, 0)
        g_hidden = dot(R.dyall[...], R.wd_s[cs, :], 1, 1)
        sig = 1.0 / (1.0 + jnp.exp(-gate))
        silu = gate * sig
        R.hidden[0:n, cs] = (silu * up).astype(BF)
        R.ggate[0:n, cs] = (g_hidden * up * sig * (1.0 + gate * (1.0 - sig))).astype(BF)
        R.gup[0:n, cs] = (g_hidden * silu).astype(BF)
        for m in range(3):
            swap(m, cs, swap_ids[0] + 3 * j + m).start()
        return carry

    lax.fori_loop(0, hid_n, hidden_tile, 0)
    twin_tile = [[swap(m, cols_of(j), swap_ids[3 * j + m]) for m in range(3)] for j in range(hid_n)]
    for tile in twin_tile:
        copies.open.extend(tile)
    before = list(copies.open)

    for copy in twin:
        copy.wait_recv()
    R.left_t[:, 0:n] = R.inner[:, mine].T
    R.left_t[:, n:2 * n] = R.twin_inner[...].T
    down_a, down_b = pl.ds(0, half // 2), pl.ds(half // 2, half // 2)
    upper, lower = pl.ds(0, half), pl.ds(half, half)

    def ffn_grads(j, gate_up, down):
        for copy in twin_tile[j]:
            copy.wait_recv()
        cs = slice(j * ff, (j + 1) * ff)
        gate_up[0:half, :] = dot(R.left_t[...], R.ggate[:, cs], 1, 0).astype(BF)
        gate_up[half:2 * half, :] = dot(R.left_t[...], R.gup[:, cs], 1, 0).astype(BF)
        down[...] = (dot(R.hidden[0:n, cs], R.dyall[:, mine], 0, 0)
                     + dot(R.hidden[n:2 * n, cs], R.twin_dy[...], 0, 0)).astype(BF)

    def first_round(gate_up, down, slot, rows, lanes, to, gus, downs):
        return [copies.start(gate_up.at[rows, :], gus.at[slot], to),
                copies.start(down.at[:, lanes], downs.at[slot], to)]

    ffn_grads(3, R.far_gu, R.far_dn)
    get_r1 = (first_round(R.far_gu, R.far_dn, 1, upper, down_a, near[1], R.gu_x, R.dn_x)
              + first_round(R.far_gu, R.far_dn, 1, lower, down_b, near[2], R.gu_y, R.dn_y))

    def grad_tile(t, carry):
        cs = aligned(t * col, col, 128)
        tile = (dot(R.ggate[0:n, :], R.wg_s[cs, :], 1, 1) + dot(R.gup[0:n, :], R.wu_s[cs, :], 1, 1)).astype(BF)
        for w in range(wid_n):
            for hh in range(2):
                R.gin[w * sub + hh * step_n:w * sub + (hh + 1) * step_n, cs] = (
                    tile[hh * part_n + w * step_n:hh * part_n + (w + 1) * step_n, :])
        return carry

    lax.fori_loop(0, wid_n, grad_tile, 0)
    get_g = LineSwap(copies, place, lambda c: R.gin.at[aligned(c * sub, sub, sub), :],
                     lambda q: R.recv_s.at[q] if q < 3 else R.recv_far)
    get_g.start_far()
    get_g.start()
    copies.sent(before)

    def grads_of(j):
        return R.wg_s.at[:, cols_of(j)], R.wu_s.at[cols_of(j), pl.ds(0, half)]

    ffn_grads(2, *grads_of(2))
    keep_r1 = first_round(*grads_of(2), 0, lower, down_b, near[2], R.gu_y, R.dn_y)
    ffn_grads(1, *grads_of(1))
    keep_r1 += first_round(*grads_of(1), 0, upper, down_a, near[1], R.gu_x, R.dn_x)
    get_g.combine()
    ffn_grads(0, *grads_of(0))

    def out_tile(t, carry):
        cs = aligned(t * col, col, 128)
        R.part_s[:, cs] = (dot(R.hidden[0:n, :], R.wd_s[:, cs], 1, 0) + R.part_s[:, cs].astype(F32)).astype(BF)
        return carry

    lax.fori_loop(0, wid_n, out_tile, 0)

    for copy in get_r1:
        copy.wait_recv()
    add_g = R.wg_s.at[upper, cols_of(2)]
    add_g[...] = (add_g[...].astype(F32) + R.gu_x[1].astype(F32)).astype(BF)
    add_u = R.wg_s.at[lower, cols_of(1)]
    add_u[...] = (add_u[...].astype(F32) + R.gu_y[1].astype(F32)).astype(BF)
    add_a = R.wu_s.at[cols_of(2), down_a]
    add_a[...] = (add_a[...].astype(F32) + R.dn_x[1].astype(F32)).astype(BF)
    add_b = R.wu_s.at[cols_of(1), down_b]
    add_b[...] = (add_b[...].astype(F32) + R.dn_y[1].astype(F32)).astype(BF)
    get_r2 = [copies.start(add_g, R.gu_x.at[2], near[2]), copies.start(add_a, R.dn_x.at[2], near[2]),
              copies.start(add_u, R.gu_y.at[2], near[1]), copies.start(add_b, R.dn_y.at[2], near[1])]

    g_inner = get_g.total(R.gin[aligned(place.wid * sub, sub, sub), :].astype(F32))
    mixed = R.mixed[...]
    inv_two = lax.rsqrt(jnp.mean(mixed * mixed, -1, keepdims=True) + eps_norm)
    n_two = mixed * inv_two
    scaled = g_inner * R.gall[1:2, :]
    g_mixed = (own_rows(R.dyall)
               + inv_two * (scaled - n_two * jnp.mean(scaled * n_two, -1, keepdims=True)))
    R.row_g[...] = g_mixed.astype(BF)
    get_z = []
    for hh in range(2):
        at = rows_of(place.wid, hh)
        get_z.append(LineGather(copies, place, R.row_g.at[pl.ds(hh * step_n, step_n), :],
                                functools.partial(lambda hh, c: R.gz.at[rows_of(c, hh), :], hh)))
        R.gz[at, :] = R.row_g[half_of(hh), :]
    R.gpart[1:2, :] = jnp.sum(g_inner * n_two, 0, keepdims=True)
    for copy in twin_a:
        copy.wait_recv()
    for part in get_z:
        part.relay()
    get_f = []
    for slot, i in enumerate(order):
        peer = place.wid_peer(i)
        get_f.append(copies.start(R.part_s.at[:, aligned(peer * col, col, 128)], R.recv_f.at[slot], {"wid": peer}))

    for part in get_z:
        part.wait()
    twin_z = copies.start(R.gz.at[:, other], R.twin_gz, sibling)

    gets = [[] for _ in range(heads)]
    for h in range(heads):
        cs = head_cols(h)
        go = dot(R.gz[...], R.wo_s[cs, :], 1, 1).astype(BF)
        attn_bwd_head(hops, h, R.probs, R.rcp, go, R.qt, R.v, R.fv, R.fp, R.chain,
                      R.gqt, R.near_s, R.gv, R.sendk, R.sendv, R.sendp, R.s_s)
        for i in range(1, hops + 1):
            to = place.row_peer(-i)
            gets[h].append(copies.start(R.sendv.at[i - 1, :, cs], R.recvv.at[i - 1, :, cs], to))
            gets[h].append(copies.start(R.sendk.at[i - 1, :, cs], R.recvk.at[i - 1, :, cs], to))
        for i in range(1, hops):
            gets[h].append(copies.start(R.sendp.at[i - 1, h], R.recvp.at[i - 1, h], place.row_peer(-i)))

    def left_of(ref, twin_ref):
        R.left_t[:, 0:n] = ref[:, mine].T
        R.left_t[:, n:2 * n] = twin_ref[...].T

    twin_z.wait_recv()
    left_of(R.gz, R.twin_gz)

    fine = piece // 2
    get_h = {}

    def rows_at(j, lot):
        return aligned(turned(place.hid, j) * piece + lot * fine, fine, 32)

    def round_one(src, slot):
        sent = [copies.start(src.at[rows_at(3, lot), :], R.recv_q.at[slot, 2 * lot + 1], near[lot + 1]) for lot in range(2)]
        keep = [copies.start(src.at[rows_at(lot + 1, lot), :], R.recv_q.at[slot, 2 * lot], near[lot + 1]) for lot in range(2)]
        get_h[slot] = keep
        return sent

    def round_two(src, slot, sent):
        for lot in range(2):
            sent[lot].wait_recv()
            at = src.at[rows_at(2 - lot, lot), :]
            at[...] = (at[...].astype(F32) + R.recv_q[slot, 2 * lot + 1].astype(F32)).astype(BF)
            get_h[slot].append(copies.start(at, R.recv_q.at[slot, 4 + lot], near[2 - lot]))

    R.wide_s[...] = dot(R.left_t[:, 0:n], R.o[...], 1, 0) + dot(R.left_t[:, n:2 * n], R.twin_o[...], 1, 0)
    R.d_out[...] = R.wide_s[aligned(place.hid * piece, piece, 64), :]
    R.send_o[...] = R.wide_s[...].astype(BF)
    slot_o, slot_v = heads + 1, heads
    sent_o = round_one(R.send_o, slot_o)
    left_of(R.act, R.twin_act)
    for copy in get_r2 + keep_r1:
        copy.wait_recv()
    R.d_gate_s[...] = (R.wg_s[upper, 0:ff].astype(F32) + R.gu_x[0].astype(F32) + R.gu_x[2].astype(F32))
    R.d_up_s[...] = (R.wg_s[lower, 0:ff].astype(F32) + R.gu_y[0].astype(F32) + R.gu_y[2].astype(F32))
    for lanes, ref in ((down_a, R.dn_x), (down_b, R.dn_y)):
        R.d_down_s[:, lanes] = R.wu_s[0:ff, lanes].astype(F32) + ref[0].astype(F32) + ref[2].astype(F32)
    stores = [loads.start(R.d_gate_s, R.d_gate), loads.start(R.d_up_s, R.d_up), loads.start(R.d_down_s, R.d_down)]

    row8 = lax.broadcasted_iota(jnp.int32, (n, HDIM), 1)
    gc_all = jnp.zeros((n, HDIM), F32)
    val_cols = pl.ds(3 * width, width)
    twin_h = []

    def grad_part(slot):
        return R.wd_s.at[:, pl.ds(slot * width, width)]

    def weights_of(slot, outs_of):
        cs = slice(slot * width, (slot + 1) * width)
        R.wide_s[...] = dot(R.left_t[...], R.grads[:, cs], 1, 0)
        R.wd_s[0:half, cs] = R.wide_s[...].astype(BF)
        own = R.wide_s[aligned(place.hid * piece, piece, 64), :]
        for m, (ref, at) in enumerate(outs_of):
            ref[:, at] = own[:, head_cols(m)]
        return round_one(grad_part(slot), slot)

    def outs_of(h):
        return [(ref, head_cols(h)) for ref in (R.d_query, R.d_key, R.d_house)]

    val_outs = [(R.d_value, head_cols(m)) for m in range(heads)]
    sent_h = []
    for h in range(heads):
        for copy in gets[h]:
            copy.wait_recv()
        cs = head_cols(h)
        gkt = R.recvk[0, :, cs].astype(F32)
        gv = R.gv[:, cs] + R.recvv[0, :, cs].astype(F32)
        for i in range(1, hops):
            gkt = gkt + R.recvk[i, :, cs].astype(F32)
            gv = gv + R.recvv[i, :, cs].astype(F32)
        gp = R.recvp[0, h].astype(F32)
        for i in range(1, hops - 1):
            gp = gp + R.recvp[i, h].astype(F32)
        R.grads[0:n, (9 + h) * HDIM:(10 + h) * HDIM] = gv.astype(BF)
        if h == heads - 1:
            twin_v = copies.start(R.grads.at[pl.ds(0, n), val_cols], R.grads.at[pl.ds(n, n), val_cols], sibling)
        gq, gk, gr, gc = path_bwd_head(h, heads, Heads(R.proj, 0), Heads(R.proj, 1), Heads(R.proj, 2), R.c,
                                       R.u, R.inv, R.psi, R.x1, R.y1, R.gqt[:, cs], gkt, R.near_s[h], gp)
        gc_all = jnp.where(row8 == h, gc, gc_all)
        for m, val in enumerate((gq, gk, gr)):
            R.grads[0:n, (3 * h + m) * HDIM:(3 * h + m + 1) * HDIM] = val
        gs = pl.ds(h * width, width)
        twin_h.append(copies.start(R.grads.at[pl.ds(0, n), gs], R.grads.at[pl.ds(n, n), gs], sibling))
        if 0 < h < heads - 1:
            twin_h[h - 1].wait_recv()
            sent_h.append(weights_of(h - 1, outs_of(h - 1)))
    R.gcs[0:n, :] = gc_all.astype(BF)
    twin_c = copies.start(R.gcs.at[pl.ds(0, n), :], R.gcs.at[pl.ds(n, n), :], sibling)

    inv_rms = R.inv_rms[...]
    stat = jnp.zeros((n, 1), F32)
    get_n = LineSwap(copies, place, lambda c: R.send_n.at[c], lambda q: R.recv_n.at[q])
    me, side = place.wid, place.wid // 2
    for turn, c in enumerate((3 * (1 - side), 2 - side, (1 - side) * (1 - me) + side * (5 - me), me)):
        cs = aligned(c * col, col, 128)
        g_act = dot(R.grads[0:n, :], R.w_s[cs, :], 1, 1) + dot(R.gcs[0:n, 0:heads], R.wb[:, cs], 1, 0)
        normed = R.xall[:, cs].astype(F32) * inv_rms
        both = g_act * normed
        stat = stat + jnp.sum(both * R.gall[0:1, cs], 1, keepdims=True)
        R.gpart[0:1, cs] = jnp.sum(both, 0, keepdims=True)
        if turn == 3:
            R.own_n[...] = g_act
        else:
            R.send_n[c] = g_act.astype(BF)
        if turn == 0:
            get_n.start_far()
        if turn == 2:
            get_n.start()
    R.stat_s[...] = jnp.broadcast_to(stat, (n, HDIM)).T[0:8, :]
    get_s = [copies.start(R.stat_s, R.recv_st.at[slot], d) for slot, d in enumerate(to_wid)]

    def window(p):
        return aligned(p * piece // 128 * 128, 256, 128)

    get_gain = [copies.start(R.gpart.at[:, window(lax.rem(place.row + i, place.rows_n))], R.recv_gain.at[i - 1],
                             place.row_peer(i)) for i in range(1, place.rows_n)]
    twin_c.wait_recv()
    d_beta = dot(R.gcs[0:n, :], R.act[:, mine], 0, 0) + dot(R.gcs[n:2 * n, :], R.twin_act[...], 0, 0)
    R.beta_s[...] = d_beta[0:8, :]
    get_b = [copies.start(R.beta_s.at[:, window(turned(place.hid, j))], R.recv_b.at[j - 1], near[j])
             for j in range(1, hid_n)]
    for h in (heads - 2, heads - 1):
        twin_h[h].wait_recv()
        sent_h.append(weights_of(h, outs_of(h)))
    get_n.combine()
    twin_v.wait_recv()
    sent_v = weights_of(slot_v, val_outs)
    round_two(R.send_o, slot_o, sent_o)
    for h in range(heads - 1):
        round_two(grad_part(h), h, sent_h[h])
    out = R.x[...].astype(F32) + R.part_s[:, my_cols].astype(F32)
    for slot, copy in enumerate(get_f):
        copy.wait_recv()
        out = out + R.recv_f[slot].astype(F32)
    R.output_s[...] = out.astype(BF)
    stores.append(loads.start(R.output_s, R.output))
    def final(slot, refs_of):
        for copy in get_h[slot]:
            copy.wait_recv()
        for m, (ref, at) in enumerate(refs_of):
            for lot in range(2):
                rs = slice(lot * fine, (lot + 1) * fine)
                ref[rs, at] = (ref[rs, at] + R.recv_q[slot, 2 * lot, :, head_cols(m)].astype(F32)
                               + R.recv_q[slot, 4 + lot, :, head_cols(m)].astype(F32))

    final(slot_o, [(R.d_out, head_cols(m)) for m in range(heads)])
    gain = R.gpart[:, window(place.row)]
    for i, copy in enumerate(get_gain):
        copy.wait_recv()
        gain = gain + R.recv_gain[i]
    R.gain_s[...] = gain
    get_gain2 = [copies.start(R.gain_s, R.recv_gain2.at[slot], d) for slot, d in enumerate(to_wid)]
    round_two(grad_part(heads - 1), heads - 1, sent_h[heads - 1])
    round_two(grad_part(slot_v), slot_v, sent_v)

    g_act = get_n.total(R.own_n[...])
    stats = R.stat_s[...]
    for slot in range(wid_n - 1):
        get_s[slot].wait_recv()
        stats = stats + R.recv_st[slot]
    mean = stats.T[:, 0:1] / model
    normed = R.xall[:, my_cols].astype(F32) * inv_rms
    R.d_inputs[...] = (R.gz[:, my_cols].astype(F32)
                       + inv_rms * (g_act * R.gall[0:1, my_cols] - normed * mean))
    for h in range(heads - 1):
        final(h, outs_of(h))
    final(heads - 1, outs_of(heads - 1))
    final(slot_v, val_outs)
    for copy in get_b:
        copy.wait_recv()
    d_beta = R.beta_s[:, window(place.hid)]
    for i in range(hid_n - 1):
        d_beta = d_beta + R.recv_b[i]
    gain = R.gain_s[...]
    for slot, copy in enumerate(get_gain2):
        copy.wait_recv()
        gain = gain + R.recv_gain2[slot]

    def exact(rows, at):
        return jnp.where(at % 2 == 1, rows[:, 64:64 + piece], rows[:, 0:piece])

    R.d_beta[...] = exact(d_beta, place.hid)[0:heads, :]
    R.gain_out[...] = exact(gain, place.row)
    for store in stores:
        store.wait()
    copies.sent(copies.open)


def step(args, heads, hops, sizes):
    ins = ("lengths", "x", "dy", "gain_attn", "gain_ffn", "wq", "wk", "wv", "wr", "wb", "wo", "wg", "wu", "wd")
    shapes = dict(zip(ins, (a.shape for a in args)))
    n, col = shapes["x"]
    seq_n, hid_n, wid_n = sizes
    model, width = shapes["wq"]
    ff = shapes["wg"][1]
    sub = n // wid_n
    rows_n = seq_n * hid_n
    half = model // seq_n
    piece = model // rows_n
    slots = hops * (hops + 1) // 2
    S = jax.ShapeDtypeStruct
    V = pltpu.VMEM
    outs = dict(
        output=S((n, col), BF), d_inputs=S((n, col), F32), gain_out=S((8, piece), F32),
        d_query=S((piece, width), F32), d_key=S((piece, width), F32), d_value=S((piece, width), F32),
        d_house=S((piece, width), F32), d_beta=S((heads, piece), F32), d_out=S((piece, width), F32),
        d_gate=S((half, ff), F32), d_up=S((half, ff), F32), d_down=S((ff, half), F32),
    )
    peers_w, peers_h = wid_n - 1, hid_n - 1
    scratch = dict(
        gain_in=V((8, col), F32), gall=V((8, model), F32), inv_rms=V((n, 1), F32),
        act=V((n, model), BF), xall=V((n, model), BF), dyall=V((n, model), BF),
        proj=V((n, 3 * width), F32), c=V((n, heads), F32), v=V((n, width), BF),
        qt=V((n, width), BF), u=V((n, width), F32), inv=V((heads, n, n), F32), psi=V((heads, n, n), F32),
        x1=V((n, width), F32), y1=V((n, width), F32),
        fv=V((hops, n, width), BF), fp=V((hops - 1, heads, HDIM, HDIM), BF), chain=V((slots, n, width), BF),
        probs=V((hops + 1, heads, n, n), BF), rcp=V((n, heads), F32), o=V((n, width), BF), mixed=V((sub, model), F32),
        inner=V((n, model), BF), hidden=V((2 * n, hid_n * ff), BF), ggate=V((2 * n, hid_n * ff), BF),
        gup=V((2 * n, hid_n * ff), BF), gin=V((n, model), BF),
        w_s=V((model, 4 * width), BF), wo_s=V((width, model), BF),
        wg_s=V((model, hid_n * ff), BF), wu_s=V((model, hid_n * ff), BF), wd_s=V((hid_n * ff, model), BF),
        kt_s=V((n, width), BF), near_s=V((heads, n, n), F32), prod_s=V((heads, HDIM, HDIM), BF),
        s_s=V(((hops + 1) * n, n), F32), part_s=V((n, model), BF), recv_s=V((wid_n, sub, model), BF), recv_far=V((sub, model), BF),
        far_gu=V((2 * half, ff), BF), far_dn=V((ff, half), BF),
        row_s=V((sub, model), BF), row_g=V((sub, model), BF),
        twin_inner=V((n, half), BF), twin_dy=V((n, half), BF), twin_act=V((n, half), BF), twin_o=V((n, width), BF),
        twin_gz=V((n, half), BF), left_t=V((half, 2 * n), BF),
        gu_x=V((3, half, ff), BF), gu_y=V((3, half, ff), BF),
        dn_x=V((3, ff, half // 2), BF), dn_y=V((3, ff, half // 2), BF),
        gz=V((n, model), BF), gpart=V((8, model), F32), recv_f=V((peers_w, n, col), BF),
        gqt=V((n, width), F32), gv=V((n, width), F32),
        sendk=V((hops, n, width), BF), sendv=V((hops, n, width), BF), sendp=V((hops - 1, heads, HDIM, HDIM), BF),
        recvk=V((hops, n, width), BF), recvv=V((hops, n, width), BF), recvp=V((hops - 1, heads, HDIM, HDIM), BF),
        send_o=V((half, width), BF),
        grads=V((2 * n, 4 * width), BF), gcs=V((2 * n, HDIM), BF), wide_s=V((half, width), F32),
        recv_q=V((heads + 2, 6, piece // 2, width), BF), beta_s=V((8, half), F32), recv_b=V((peers_h, 8, 256), F32),
        own_n=V((n, col), F32), send_n=V((wid_n, n, col), BF), recv_n=V((wid_n, n, col), BF),
        output_s=V((n, col), BF), d_gate_s=V((half, ff), F32), d_up_s=V((half, ff), F32), d_down_s=V((ff, half), F32),
        stat_s=V((8, n), F32), recv_st=V((peers_w, 8, n), F32),
        recv_gain=V((rows_n - 1, 8, 256), F32), gain_s=V((8, 256), F32), recv_gain2=V((peers_w, 8, 256), F32),
    )
    n_copies = 256
    scratch.update(load_sem=pltpu.SemaphoreType.DMA((24,)), send_sem=pltpu.SemaphoreType.DMA((n_copies,)),
                   recv_sem=pltpu.SemaphoreType.DMA((n_copies,)))
    spaces = {"lengths": pltpu.SMEM, "x": pltpu.VMEM, "gain_attn": pltpu.VMEM, "gain_ffn": pltpu.VMEM, "wb": pltpu.VMEM}
    vmem = pl.BlockSpec(memory_space=pltpu.VMEM)
    early = ("output", "d_gate", "d_up", "d_down")
    res = pl.pallas_call(
        functools.partial(step_kernel, (heads, hops, sizes), ins + tuple(outs) + tuple(scratch)),
        in_specs=[pl.BlockSpec(memory_space=spaces.get(i, pl.ANY)) for i in ins],
        out_shape=tuple(outs.values()),
        out_specs=tuple(pl.BlockSpec(memory_space=pl.ANY) if i in early else vmem for i in outs),
        scratch_shapes=list(scratch.values()),
        compiler_params=pltpu.CompilerParams(
            vmem_limit_bytes=VMEM_ALL, collective_id=1, has_side_effects=True),
        name="step",
    )(*args)
    return dict(zip(outs, res))


def finish_kernel(count, *refs):
    ins, outs, bufs = refs[:count + 1], refs[count + 1:2 * count + 3], refs[2 * count + 3:3 * count + 4]
    lines, sems = refs[3 * count + 4:3 * count + 6], refs[3 * count + 6]
    loads, stores = [], []
    for a, b, c in zip(ins[:count], bufs[:count], outs[:count]):
        rows = a.shape[0]
        cut = rows // 2 if rows >= 768 else rows
        for start in range(0, rows, cut):
            i, part = len(loads), pl.ds(start, cut)
            loads.append(pltpu.make_async_copy(a.at[part, :], b.at[part, :], sems.at[0, i]))
            stores.append(pltpu.make_async_copy(b.at[part, :], c.at[part, :], sems.at[1, i]))
    last = len(loads)
    loads.insert(0, pltpu.make_async_copy(ins[count], bufs[count], sems.at[0, last]))
    for copy in loads:
        copy.start()
    loads[0].wait()
    for m in range(2):
        lines[m][...] = bufs[count][m, :]
        stores.append(pltpu.make_async_copy(lines[m], outs[count + m], sems.at[1, last + m]))
        stores[-1].start()
    for load, store in zip(loads[1:], stores):
        load.wait()
        store.start()
    for copy in stores:
        copy.wait()


def finish(arrays, gains):
    count, size = len(arrays), gains.shape[1]
    spec = pl.BlockSpec(memory_space=pl.ANY)
    vector = jax.ShapeDtypeStruct((size,), F32)
    return pl.pallas_call(
        functools.partial(finish_kernel, count),
        in_specs=[spec] * (count + 1), out_specs=[spec] * (count + 2),
        out_shape=[jax.ShapeDtypeStruct(a.shape, a.dtype) for a in arrays] + [vector, vector],
        scratch_shapes=([pltpu.VMEM(a.shape, a.dtype) for a in arrays + [gains]]
                        + [pltpu.VMEM((size,), F32)] * 2 + [pltpu.SemaphoreType.DMA((2, 2 * count + 2))]),
        compiler_params=pltpu.CompilerParams(vmem_limit_bytes=VMEM_ALL),
        name="finish",
    )(*arrays, gains)


def shifted(array, axis, by):
    peers = lax.axis_size(axis)
    pairs = [(i, i + by) for i in range(peers) if 0 <= i + by < peers]
    return lax.ppermute(array, axis, pairs)


def norm_rows(hidden_f):
    inverse = lax.rsqrt(jnp.mean(hidden_f * hidden_f, -1, keepdims=True) + eps_norm)
    return (hidden_f * inverse, inverse)


def norm_back(grad_out, normed, inverse, gain_vec):
    scaled_grad = grad_out * gain_vec
    grad_gain = jnp.sum(grad_out * normed, 0)
    grad_in = inverse * (scaled_grad - normed * jnp.mean(scaled_grad * normed, -1, keepdims=True))
    return (grad_in, grad_gain)


ROWS = ("seq", "hid")


def body(inputs, gain_attn, gain_ffn, w_query, w_key, w_value, w_house, w_beta, w_out,
         w_gate, w_up, w_down, lengths, cotangent):
    tok, col = inputs.shape
    row_devs = lax.axis_size(ROWS)
    my_row = lax.axis_index(ROWS)
    my_wid = lax.axis_index("wid")
    wid_n = lax.axis_size("wid")
    tokens_all = tok * row_devs
    most_len = max(LEAST, 2 * tokens_all // 5)
    hops = min((most_len - 2) // tok + 1, row_devs - 1)
    heads = w_query.shape[1] // HDIM
    ff = w_gate.shape[1]
    sub = tok // wid_n

    x_all = lax.all_gather(inputs, "wid", axis=1, tiled=True)
    gain_one = lax.all_gather(gain_attn, "wid", axis=0, tiled=True).astype(F32)
    gain_two = lax.all_gather(gain_ffn, "wid", axis=0, tiled=True).astype(F32)
    dy_all = lax.all_gather(cotangent, "wid", axis=1, tiled=True)
    w_gu = lax.all_gather(jnp.concatenate([w_gate, w_up], 1), "hid", axis=0)
    w_dn = lax.all_gather(w_down, "hid", axis=0)
    model = x_all.shape[1]

    residual = x_all.astype(F32)
    normed_one, inverse_one = norm_rows(residual)
    act = (normed_one * gain_one).astype(BF)

    def project(weight):
        return jnp.dot(act, weight, preferred_element_type=F32)

    q, k, r, c = project(w_query), project(w_key), project(w_house), project(w_beta)
    v = project(w_value).astype(BF)
    far_v = jnp.stack([shifted(v, ROWS, i) for i in range(1, hops + 1)])
    qt, kt, near, prod, *saved = path_fwd(q, k, r, c, heads)
    far_k = jnp.stack([shifted(kt, ROWS, i) for i in range(1, hops + 1)])
    far_p = jnp.stack([shifted(prod, ROWS, i) for i in range(1, hops)])
    row_arr = jnp.full((1,), my_row, jnp.int32)
    attended, probs, chain, rcp = attn_fwd(lengths, row_arr, qt, near, v, far_k, far_v, far_p, heads, hops)

    attn_part = jnp.dot(attended, w_out, preferred_element_type=F32).astype(BF)
    attn_rows = lax.psum_scatter(attn_part, "wid", scatter_dimension=0, tiled=True)
    x_rows = lax.dynamic_slice_in_dim(x_all, my_wid * sub, sub, 0).astype(F32)
    dy_rows = lax.dynamic_slice_in_dim(dy_all, my_wid * sub, sub, 0).astype(F32)
    mixed = x_rows + attn_rows.astype(F32)
    normed_two, inverse_two = norm_rows(mixed)
    inner = lax.all_gather((normed_two * gain_two).astype(BF), "wid", axis=0, tiled=True)

    pre = jnp.einsum("tc,hcf->htf", inner, w_gu, preferred_element_type=F32)
    gate, up = pre[:, :, :ff], pre[:, :, ff:]
    sig = jax.nn.sigmoid(gate)
    hidden = (gate * sig * up).astype(BF)
    ffn_part = jnp.einsum("htf,hfc->tc", hidden, w_dn, preferred_element_type=F32)
    ffn_part = (ffn_part + attn_part.astype(F32)).astype(BF)
    ffn_cols = lax.psum_scatter(ffn_part, "wid", scatter_dimension=1, tiled=True)
    output = (inputs.astype(F32) + ffn_cols.astype(F32)).astype(BF)

    g_hidden = jnp.einsum("tc,hfc->htf", dy_all, w_dn, preferred_element_type=F32)
    g_gate = g_hidden * up * sig * (1.0 + gate * (1.0 - sig))
    g_up = g_hidden * gate * sig
    g_pre = jnp.concatenate([g_gate, g_up], 2).astype(BF)
    g_inner = jnp.einsum("htf,hcf->tc", g_pre, w_gu, preferred_element_type=F32).astype(BF)
    g_inner = lax.psum_scatter(g_inner, "wid", scatter_dimension=0, tiled=True).astype(F32)
    g_mixed_n, g_gain_two = norm_back(g_inner, normed_two, inverse_two, gain_two)
    g_z = lax.all_gather((dy_rows + g_mixed_n).astype(BF), "wid", axis=0, tiled=True)

    d_gu = jnp.einsum("tc,htf->hcf", inner, g_pre, preferred_element_type=F32).astype(BF)
    d_dn = jnp.einsum("htf,tc->hfc", hidden, dy_all, preferred_element_type=F32).astype(BF)
    d_gu = lax.psum_scatter(d_gu, "seq", scatter_dimension=1, tiled=True)
    d_gu = lax.psum_scatter(d_gu, "hid", scatter_dimension=0)
    d_dn = lax.psum_scatter(d_dn, "seq", scatter_dimension=2, tiled=True)
    d_dn = lax.psum_scatter(d_dn, "hid", scatter_dimension=0)

    g_attn = jnp.einsum("tc,ic->ti", g_z, w_out, preferred_element_type=F32).astype(BF)
    d_out = jnp.einsum("ti,tc->ic", attended, g_z, preferred_element_type=F32).astype(BF)
    g_qt, g_near, gv, send_k, send_v, send_p = attn_bwd(probs, rcp, g_attn, qt, v, far_v, far_p, chain, heads, hops)
    g_kt = sum(shifted(send_k[i - 1], ROWS, -i).astype(F32) for i in range(1, hops + 1))
    gv = gv + sum(shifted(send_v[i - 1], ROWS, -i).astype(F32) for i in range(1, hops + 1))
    g_prod = sum(shifted(send_p[i - 1], ROWS, -i).astype(F32) for i in range(1, hops))
    g_q, g_k, g_r, g_c = path_bwd(q, k, r, c, saved, g_qt, g_kt, g_near, g_prod, heads)
    g_v = gv.astype(BF)

    def weight_grad(grad_low):
        return jnp.einsum("tc,ti->ci", act, grad_low, preferred_element_type=F32).astype(BF)

    def input_grad(grad_low, weight):
        return jnp.einsum("ti,ci->tc", grad_low, weight, preferred_element_type=F32)

    g_act = (input_grad(g_q, w_query) + input_grad(g_k, w_key) + input_grad(g_v, w_value)
             + input_grad(g_r, w_house) + input_grad(g_c, w_beta))
    g_act = lax.psum_scatter(g_act.astype(BF), "wid", scatter_dimension=0, tiled=True).astype(F32)
    normed_rows = lax.dynamic_slice_in_dim(normed_one, my_wid * sub, sub, 0)
    inverse_rows = lax.dynamic_slice_in_dim(inverse_one, my_wid * sub, sub, 0)
    g_resid, g_gain_one = norm_back(g_act, normed_rows, inverse_rows, gain_one)
    d_rows = dy_rows + g_mixed_n + g_resid
    d_inputs = lax.all_to_all(d_rows, "wid", split_axis=1, concat_axis=0, tiled=True)

    def scatter(x, dim):
        return lax.psum_scatter(x, ROWS, scatter_dimension=dim, tiled=True)

    gains = lax.psum(jnp.stack([g_gain_one, g_gain_two]), "wid")
    gains = scatter(gains, 1)
    return (
        output,
        d_inputs,
        gains[0],
        gains[1],
        scatter(weight_grad(g_q), 0).astype(F32),
        scatter(weight_grad(g_k), 0).astype(F32),
        scatter(weight_grad(g_v), 0).astype(F32),
        scatter(weight_grad(g_r), 0).astype(F32),
        scatter(weight_grad(g_c), 0).astype(F32),
        scatter(d_out, 1).astype(F32),
        d_gu[:, :ff].astype(F32),
        d_gu[:, ff:].astype(F32),
        d_dn.astype(F32),
    )


def fast_body(inputs, gain_attn, gain_ffn, w_query, w_key, w_value, w_house, w_beta, w_out,
              w_gate, w_up, w_down, lengths, cotangent):
    tok, col = inputs.shape
    row_devs = lax.axis_size(ROWS)
    sizes = tuple(lax.axis_size(i) for i in ("seq", "hid", "wid"))
    most_len = max(LEAST, 2 * tok * row_devs // 5)
    hops = min((most_len - 2) // tok + 1, row_devs - 1)
    heads = w_query.shape[1] // HDIM
    f = step((lengths, inputs, cotangent, gain_attn, gain_ffn, w_query, w_key, w_value, w_house,
              w_beta.T, w_out, w_gate, w_up, w_down), heads, hops, sizes)
    names = [i for i in f if i != "gain_out"]
    f.update(zip(names + ["gain_one", "gain_two"], finish([f[i] for i in names], f["gain_out"])))
    return (f["output"], f["d_inputs"], f["gain_one"], f["gain_two"], f["d_query"], f["d_key"], f["d_value"],
            f["d_house"], f["d_beta"].T, f["d_out"].T, f["d_gate"], f["d_up"], f["d_down"])


def slow(mesh):
    return (mesh.shape["seq"], mesh.shape["hid"], mesh.shape["wid"]) != (2, 4, 4)


def solution(mesh):
    in_specs = (
        P(("seq", "hid"), "wid"), P("wid"), P("wid"),
        P(None, "wid"), P(None, "wid"), P(None, "wid"), P(None, "wid"), P(None, "wid"),
        P("wid", None), P(None, ("hid", "wid")), P(None, ("hid", "wid")), P(("hid", "wid"), None),
        P(), P(("seq", "hid"), "wid"),
    )
    out_specs = (
        P(("seq", "hid"), "wid"), P(("seq", "hid"), "wid"), P(("seq", "hid")), P(("seq", "hid")),
        P(("seq", "hid"), "wid"), P(("seq", "hid"), "wid"), P(("seq", "hid"), "wid"),
        P(("seq", "hid"), "wid"), P(("seq", "hid"), "wid"), P("wid", ("seq", "hid")),
        P("seq", ("hid", "wid")), P("seq", ("hid", "wid")), P(("hid", "wid"), "seq"),
    )
    return jax.shard_map(body if slow(mesh) else fast_body, mesh=mesh, in_specs=in_specs, out_specs=out_specs, check_vma=False)
```

```python
import functools
import types

import jax
import jax.numpy as jnp
from jax import lax
from jax.experimental import pallas as pl
from jax.experimental.pallas import tpu as pltpu
from jax.sharding import PartitionSpec as P

HDIM = 128
LEAST = 1024

eps_norm = 1e-06
neg_big = -1e30
BF = jnp.bfloat16
F32 = jnp.float32
VMEM_LIMIT = 60 * 1024 * 1024
VMEM_ALL = 67043328


def dot(a, b, ca, cb):
    return lax.dot_general(a, b, (((ca,), (cb,)), ((), ())), preferred_element_type=F32)


def split(a):
    hi = a.astype(BF)
    return hi, (a - hi.astype(F32)).astype(BF)


def dot3(a, b, ca, cb):
    return dot(a[0], b[0], ca, cb) + (dot(a[0], b[1], ca, cb) + dot(a[1], b[0], ca, cb))


def dot1(a, b, ca, cb):
    return dot(a.astype(BF), b.astype(BF), ca, cb)


def iotas(n):
    rows = lax.broadcasted_iota(jnp.int32, (n, n), 0)
    cols = lax.broadcasted_iota(jnp.int32, (n, n), 1)
    return rows, cols


def head_cols(h):
    return slice(h * HDIM, (h + 1) * HDIM)


def house_terms(raw, strength, heads, h):
    inv = lax.rsqrt(jnp.sum(raw * raw, -1, keepdims=True) + eps_norm)
    lane = lax.broadcasted_iota(jnp.int32, strength.shape, 1)
    c = jnp.sum(jnp.where(lane == h, strength, 0.0), 1, keepdims=True)
    root = jnp.sqrt(2.0 / (1.0 + jnp.exp(-c)))
    return inv, root


def path_fwd_stage(heads, q_ref, k_ref, r_ref, c_ref, qt_ref, kt_ref, near_ref, p_ref,
                   u_ref, inv_ref, psi_ref, x_ref, y_ref, done=None):
    n = c_ref.shape[0]
    rows, cols = iotas(n)
    strength = c_ref[...]
    m = n // 2
    side_rows = lax.broadcasted_iota(jnp.int32, (m, n), 0)
    wide_cols = lax.broadcasted_iota(jnp.int32, (m, n), 1)
    side_cols = wide_cols % m

    def diagonal(pair):
        return [jnp.concatenate([jnp.where(wide_cols < m, part, 0).astype(BF),
                                 jnp.where(wide_cols >= m, part, 0).astype(BF)], 0) for part in pair]

    us2 = []
    for h in range(heads):
        raw = r_ref[:, head_cols(h)]
        inv, root = house_terms(raw, strength, heads, h)
        u = raw * (inv * root)
        u_ref[:, head_cols(h)] = u
        u2 = split(u)
        us2.append(u2)
        low = jnp.where(rows > cols, dot3(u2, u2, 1, 1), 0.0)
        blocks = jnp.concatenate([low[0:m, 0:m], low[m:n, m:n]], 1)
        psi_ref[h, 0:m, :] = blocks
        psi_ref[h, m:n, 0:m] = low[m:n, 0:m]
        inv_ref[h, 0:m, :] = (jnp.where(side_rows == side_cols, 1.0, 0.0)
                              - jnp.where(side_rows // 2 == side_cols // 2, blocks, 0.0))

    def double(step, carry):
        apart = jnp.right_shift(side_rows, step) != jnp.right_shift(side_cols, step)
        pick = apart & (jnp.right_shift(side_rows, step + 1) == jnp.right_shift(side_cols, step + 1))
        now = [split(inv_ref[h, 0:m, :]) for h in range(heads)]
        mids = [dot3(split(jnp.where(pick, psi_ref[h, 0:m, :], 0.0)), diagonal(now[h]), 1, 0) for h in range(heads)]
        for h in range(heads):
            inv_ref[h, 0:m, :] = inv_ref[h, 0:m, :] - dot3(now[h], diagonal(split(mids[h])), 1, 0)
        return carry

    lax.fori_loop(1, (m - 1).bit_length(), double, 0)
    for h in range(heads):
        first, second = inv_ref[h, 0:m, 0:m], inv_ref[h, 0:m, m:n]
        corner = -dot3(split(second), split(dot3(split(psi_ref[h, m:n, 0:m]), split(first), 1, 0)), 1, 0)
        inv_ref[h, 0:m, m:n] = jnp.zeros((m, m), F32)
        inv_ref[h, m:n, 0:m] = corner
        inv_ref[h, m:n, m:n] = second
    er, ec = iotas(HDIM)
    for h in range(heads):
        kin = split(inv_ref[h])
        k = k_ref[:, head_cols(h)]
        u2 = us2[h]
        aq = jnp.where(rows < cols, dot3(split(k), u2, 1, 1), 0.0)
        y = dot3(kin, u2, 0, 0)
        y_ref[:, head_cols(h)] = y
        kt_ref[:, head_cols(h)] = (k - dot3(split(aq), split(y), 1, 0)).astype(BF)
        x = dot3(kin, u2, 1, 0)
        x_ref[:, head_cols(h)] = x
        p_ref[h] = (jnp.where(er == ec, 1.0, 0.0) - dot3(u2, split(x), 0, 0)).astype(p_ref.dtype)
        if done is not None:
            done(h)
    for h in range(heads):
        kin = split(inv_ref[h])
        q = q_ref[:, head_cols(h)]
        q2, k2, u2, x2 = split(q), split(k_ref[:, head_cols(h)]), us2[h], split(x_ref[:, head_cols(h)])
        fq2 = split(jnp.where(rows >= cols, dot3(q2, u2, 1, 1), 0.0))
        qt_ref[:, head_cols(h)] = (q - dot3(fq2, x2, 1, 0)).astype(BF)
        psi = dot3(kin, split(jnp.where(rows > cols, dot3(u2, k2, 1, 1), 0.0)), 1, 0)
        psi_ref[h] = psi
        near_ref[h] = dot3(q2, k2, 1, 1) - dot3(fq2, split(psi), 1, 0)


def path_fwd_kernel(heads, *refs):
    path_fwd_stage(heads, *refs)


def path_fwd(q, k, r, c, heads):
    n, width = q.shape
    flat = jax.ShapeDtypeStruct((n, width), F32)
    low = jax.ShapeDtypeStruct((n, width), BF)
    square = jax.ShapeDtypeStruct((heads, n, n), F32)
    return pl.pallas_call(
        functools.partial(path_fwd_kernel, heads),
        out_shape=(low, low, square, jax.ShapeDtypeStruct((heads, HDIM, HDIM), F32),
                   flat, square, square, flat, flat),
        compiler_params=pltpu.CompilerParams(vmem_limit_bytes=VMEM_LIMIT),
        name="path_fwd",
    )(q, k, r, c)


def doc_of(pos, len_ref):
    total = len_ref[0]
    doc = (pos >= total).astype(jnp.int32)
    for i in range(1, len_ref.shape[0]):
        total = total + len_ref[i]
        doc = doc + (pos >= total).astype(jnp.int32)
    return doc


def chain_slot(r, m):
    return r * (r - 1) // 2 + m


def key_chain(hops, h, fp_ref, chain_ref):
    cs = head_cols(h)
    for r in range(2, hops + 1):
        keys = chain_ref[chain_slot(r, 0), :, cs]
        for m in range(1, r):
            keys = dot(keys, fp_ref[r - m - 1, h].astype(BF), 1, 1).astype(BF)
            chain_ref[chain_slot(r, m), :, cs] = keys


def attn_fwd_rows(hops, h, start, count, row, len_ref, qt_ref, near_ref, v_ref, fv_ref, chain_ref,
                  o_ref, p_ref, rcp_ref, s_ref):
    n = qt_ref.shape[0]
    scale = HDIM ** (-0.5)
    cs, rs = head_cols(h), slice(start, start + count)
    rows = start + lax.broadcasted_iota(jnp.int32, (count, n), 0)
    cols = lax.broadcasted_iota(jnp.int32, (count, n), 1)
    key_at = lax.broadcasted_iota(jnp.int32, (1, n), 1)
    own = doc_of(row * n + start + lax.broadcasted_iota(jnp.int32, (count, 1), 0), len_ref)
    near_ok = (rows >= cols) & (own == doc_of(row * n + key_at, len_ref))
    q = qt_ref[rs, cs]
    s = jnp.where(near_ok, near_ref[h, rs, :] * scale, neg_big)
    s_ref[0:count, :] = s
    top = jnp.max(s, 1, keepdims=True)
    for r in range(1, hops + 1):
        source = row - r
        docs = jnp.where(source >= 0, doc_of(source * n + key_at, len_ref), -1)
        keys = chain_ref[chain_slot(r, r - 1), :, cs]
        s = jnp.where(own == docs, dot(q, keys, 1, 1) * scale, neg_big)
        s_ref[r * count:(r + 1) * count, :] = s
        top = jnp.maximum(top, jnp.max(s, 1, keepdims=True))
    total = jnp.zeros((count, 1), F32)
    out = jnp.zeros((count, HDIM), F32)
    for r in range(hops + 1):
        e = jnp.exp(s_ref[r * count:(r + 1) * count, :] - top)
        total = total + jnp.sum(e, 1, keepdims=True)
        weights = e.astype(BF)
        p_ref[r, h, rs, :] = weights
        out = out + dot(weights, v_ref[:, cs] if r == 0 else fv_ref[r - 1, :, cs], 1, 0)
    recip = 1.0 / total
    rcp_ref[rs, h:h + 1] = recip
    o_ref[rs, cs] = (out * recip).astype(BF)


def attn_fwd_kernel(heads, hops, len_ref, row_ref, qt_ref, near_ref, v_ref, fk_ref, fv_ref, fp_ref,
                    o_ref, p_ref, chain_ref, rcp_ref, s_ref):
    for r in range(1, hops + 1):
        chain_ref[chain_slot(r, 0)] = fk_ref[r - 1]
    for h in range(heads):
        key_chain(hops, h, fp_ref, chain_ref)
        attn_fwd_rows(hops, h, 0, qt_ref.shape[0], row_ref[0], len_ref, qt_ref, near_ref, v_ref, fv_ref, chain_ref,
                      o_ref, p_ref, rcp_ref, s_ref)


def attn_fwd(lengths, my_row, qt, near, v, far_k, far_v, far_p, heads, hops):
    n, width = qt.shape
    slots = hops * (hops + 1) // 2
    smem = pl.BlockSpec(memory_space=pltpu.SMEM)
    vmem = pl.BlockSpec(memory_space=pltpu.VMEM)
    return pl.pallas_call(
        functools.partial(attn_fwd_kernel, heads, hops),
        in_specs=[smem, smem] + [vmem] * 6,
        out_shape=(
            jax.ShapeDtypeStruct((n, width), BF),
            jax.ShapeDtypeStruct((hops + 1, heads, n, n), BF),
            jax.ShapeDtypeStruct((slots, n, width), BF),
            jax.ShapeDtypeStruct((n, heads), F32),
        ),
        scratch_shapes=[pltpu.VMEM(((hops + 1) * n, n), F32)],
        compiler_params=pltpu.CompilerParams(vmem_limit_bytes=VMEM_LIMIT),
        name="attn_fwd",
    )(lengths, my_row, qt, near, v, far_k, far_v, far_p)


def attn_bwd_kernel(heads, hops, p_ref, rcp_ref, go_ref, qt_ref, v_ref, fv_ref, fp_ref, chain_ref,
                    gqt_ref, gnear_ref, gv_ref, sendk_ref, sendv_ref, sendp_ref, dp_ref):
    for h in range(heads):
        attn_bwd_head(hops, h, p_ref, rcp_ref, go_ref[:, head_cols(h)], qt_ref, v_ref, fv_ref, fp_ref, chain_ref,
                      gqt_ref, gnear_ref, gv_ref, sendk_ref, sendv_ref, sendp_ref, dp_ref)


def attn_bwd(p, rcp, go, qt, v, far_v, far_p, chain, heads, hops):
    n, width = qt.shape
    return pl.pallas_call(
        functools.partial(attn_bwd_kernel, heads, hops),
        out_shape=(
            jax.ShapeDtypeStruct((n, width), F32),
            jax.ShapeDtypeStruct((heads, n, n), F32),
            jax.ShapeDtypeStruct((n, width), F32),
            jax.ShapeDtypeStruct((hops, n, width), BF),
            jax.ShapeDtypeStruct((hops, n, width), BF),
            jax.ShapeDtypeStruct((hops - 1, heads, HDIM, HDIM), BF),
        ),
        scratch_shapes=[pltpu.VMEM(((hops + 1) * n, n), F32)],
        compiler_params=pltpu.CompilerParams(vmem_limit_bytes=VMEM_LIMIT),
        name="attn_bwd",
    )(p, rcp, go, qt, v, far_v, far_p, chain)


def path_bwd_kernel(heads, q_ref, k_ref, r_ref, c_ref, u_ref, inv_ref, psi_ref, x_ref, y_ref,
                    gqt_ref, gkt_ref, gnear_ref, gp_ref, gq_ref, gk_ref, gr_ref, gc_ref):
    lane = lax.broadcasted_iota(jnp.int32, c_ref.shape, 1)
    gc_all = jnp.zeros(c_ref.shape, F32)
    for h in range(heads):
        cs = head_cols(h)
        gq, gk, gr, gc = path_bwd_head(h, heads, q_ref, k_ref, r_ref, c_ref, u_ref, inv_ref, psi_ref, x_ref, y_ref,
                                       gqt_ref[:, cs], gkt_ref[:, cs], gnear_ref[h], gp_ref[h])
        gq_ref[:, cs] = gq
        gk_ref[:, cs] = gk
        gr_ref[:, cs] = gr
        gc_all = jnp.where(lane == h, gc, gc_all)
    gc_ref[...] = gc_all.astype(BF)


def path_bwd(q, k, r, c, saved, gqt, gkt, gnear, gp, heads):
    n, width = q.shape
    low = jax.ShapeDtypeStruct((n, width), BF)
    return pl.pallas_call(
        functools.partial(path_bwd_kernel, heads),
        out_shape=(low, low, low, jax.ShapeDtypeStruct((n, heads), BF)),
        compiler_params=pltpu.CompilerParams(vmem_limit_bytes=VMEM_LIMIT),
        name="path_bwd",
    )(q, k, r, c, *saved, gqt, gkt, gnear, gp)


MESH = pl.DeviceIdType.MESH


class Copies:
    def __init__(self, send, recv):
        self.send, self.recv, self.count, self.open = send, recv, 0, []

    def take(self):
        self.count = self.count + 1
        return self.count - 1

    def make(self, src, dst, device, send, recv):
        return pltpu.make_async_remote_copy(
            src_ref=src, dst_ref=dst, send_sem=self.send.at[send], recv_sem=self.recv.at[recv],
            device_id=device, device_id_type=MESH)

    def begin(self, copy):
        copy.start()
        self.open.append(copy)
        return copy

    def start(self, src, dst, device):
        i = self.take()
        return self.begin(self.make(src, dst, device, i, i))

    def sent(self, some):
        for copy in some:
            copy.wait_send()
        self.open = [copy for copy in self.open if all(copy is not other for other in some)]


class Loads:
    def __init__(self, sems):
        self.sems, self.count = sems, 0

    def start(self, src, dst):
        copy = pltpu.make_async_copy(src, dst, self.sems.at[self.count])
        self.count = self.count + 1
        copy.start()
        return copy


class Place:
    def __init__(self, sizes):
        self.seq_n, self.hid_n, self.wid_n = sizes
        self.seq = lax.axis_index("seq")
        self.hid = lax.axis_index("hid")
        self.wid = lax.axis_index("wid")
        self.rows_n = self.seq_n * self.hid_n
        self.row = self.seq * self.hid_n + self.hid

    def wid_peer(self, i):
        return lax.rem(self.wid + i, self.wid_n)

    def hid_peer(self, i):
        return lax.rem(self.hid + i, self.hid_n)

    def seq_peer(self, i):
        return lax.rem(self.seq + i, self.seq_n)

    def row_peer(self, i):
        to = lax.rem(self.row + i + self.rows_n, self.rows_n)
        return {"seq": to // self.hid_n, "hid": lax.rem(to, self.hid_n)}

    def barrier(self):
        sem = pltpu.get_barrier_semaphore()
        for i in range(1, self.wid_n):
            pl.semaphore_signal(sem, inc=1, device_id={"wid": self.wid_peer(i)}, device_id_type=MESH)
        for i in range(1, self.rows_n):
            pl.semaphore_signal(sem, inc=1, device_id=self.row_peer(i), device_id_type=MESH)
        pl.semaphore_wait(sem, self.wid_n - 1 + self.rows_n - 1)


class Sometimes:
    def __init__(self, copy, sends=None, gets=None):
        self.copy, self.sends, self.gets = copy, sends, gets

    def on(self, flag, act):
        if flag is None:
            act()
        else:
            pl.when(flag)(act)

    def start(self):
        self.on(self.sends, lambda: self.copy.start() and None)

    def wait_send(self):
        self.on(self.sends, self.copy.wait_send)

    def wait_recv(self):
        self.on(self.gets, self.copy.wait_recv)


class LineGather:
    def __init__(self, copies, place, src, view):
        me = place.wid
        self.me, self.copies, self.view = me, copies, view
        self.ids = [copies.take() for _ in range(3)]
        here = view(me)
        self.by = {i: copies.make(src, here, {"wid": place.wid_peer(i)}, self.ids[i - 1], self.ids[i - 1])
                   for i in (1, 2, 3)}
        self.by[1] = Sometimes(self.by[1], me != 3)
        self.by[3] = Sometimes(self.by[3], me != 0)
        for i in (2, 1, 3):
            copies.begin(self.by[i])

    def relay(self):
        self.by[2].wait_recv()
        for m, chunk, to, i in ((1, 3, 0, 1), (2, 0, 3, 3)):
            part = self.view(chunk)
            copy = self.copies.make(part, part, {"wid": to}, self.copies.take(), self.ids[i - 1])
            self.copies.begin(Sometimes(copy, self.me == m))

    def wait(self):
        self.by[1].wait_recv()
        self.by[3].wait_recv()


class LineSwap:
    def __init__(self, copies, place, piece, recv):
        self.copies, self.place, self.me, self.piece, self.recv = copies, place, place.wid, piece, recv
        self.ids = [copies.take() for _ in range(4)]
        me = self.me

        @pl.when(me == 0)
        def _():
            recv(0)[...] = jnp.zeros(recv(0).shape, BF)

        @pl.when(me == 3)
        def _():
            recv(2)[...] = jnp.zeros(recv(2).shape, BF)

    def make(self, src, i, slot, device, send):
        return self.copies.make(src, self.recv(slot), device, send, self.ids[slot])

    def start_far(self):
        self.far = []
        for end, far, middle in ((0, 3, 1), (3, 0, 2)):
            copy = Sometimes(self.make(self.piece(far), 0, 3, {"wid": middle}, self.copies.take()),
                             self.me == end, self.me == middle)
            self.copies.begin(copy)
            self.far.append(copy)

    def start(self):
        me, place = self.me, self.place
        to = [place.wid_peer(i) for i in range(4)]
        self.two = Sometimes(self.make(self.piece(to[2]), 2, 1, {"wid": to[2]}, self.ids[1]), (me == 0) | (me == 3))
        self.one = Sometimes(self.make(self.piece(to[1]), 1, 0, {"wid": to[1]}, self.ids[0]), me != 3, me != 0)
        self.three = Sometimes(self.make(self.piece(to[3]), 3, 2, {"wid": to[3]}, self.ids[2]), me != 0, me != 3)
        for copy in (self.two, self.one, self.three):
            self.copies.begin(copy)

    def combine(self):
        for copy in self.far:
            copy.wait_recv()
        mid = (self.me == 1) | (self.me == 2)
        far = 3 * (2 - jnp.minimum(jnp.maximum(self.me, 1), 2))

        @pl.when(mid)
        def _():
            at = self.recv(3)
            at[...] = (at[...].astype(F32) + self.piece(far)[...].astype(F32)).astype(BF)

        copy = self.make(self.recv(3), 2, 1, {"wid": far}, self.copies.take())
        self.copies.begin(Sometimes(copy, mid))

    def total(self, own):
        for copy in (self.two, self.one, self.three):
            copy.wait_recv()
        for slot in range(3):
            own = own + self.recv(slot)[...].astype(F32)
        return own


def aligned(start, size, step):
    return pl.ds(pl.multiple_of(start, step), size)


def attn_bwd_head(hops, h, p_ref, rcp_ref, go, qt_ref, v_ref, fv_ref, fp_ref, chain_ref,
                  gqt_ref, gnear_ref, gv_ref, sendk_ref, sendv_ref, sendp_ref, dp_ref):
    n = qt_ref.shape[0]
    scale = HDIM ** (-0.5)
    cs = head_cols(h)
    q = qt_ref[:, cs]
    recip = rcp_ref[:, h:h + 1]
    go_low = (go.astype(F32) * recip).astype(BF)
    delta = jnp.zeros((n, 1), F32)
    for r in range(hops + 1):
        vals = v_ref[:, cs] if r == 0 else fv_ref[r - 1, :, cs]
        dp = dot(go, vals, 1, 1)
        dp_ref[r * n:(r + 1) * n, :] = dp
        delta = delta + jnp.sum(p_ref[r, h].astype(F32) * dp, 1, keepdims=True)
        gv = dot(p_ref[r, h], go_low, 0, 0)
        if r == 0:
            gv_ref[:, cs] = gv
        else:
            sendv_ref[r - 1, :, cs] = gv.astype(BF)
    delta = delta * recip
    factor = recip * scale
    gnear_ref[h] = p_ref[0, h].astype(F32) * ((dp_ref[0:n, :] - delta) * factor)
    gq = jnp.zeros((n, HDIM), F32)
    gps = [jnp.zeros((HDIM, HDIM), F32) for _ in range(hops - 1)]
    for r in range(1, hops + 1):
        gs = (p_ref[r, h].astype(F32) * ((dp_ref[r * n:(r + 1) * n, :] - delta) * factor)).astype(BF)
        gq = gq + dot(gs, chain_ref[chain_slot(r, r - 1), :, cs], 1, 0)
        gk = dot(gs, q, 0, 0)
        for m in range(r - 1, 0, -1):
            back = r - m - 1
            gkb = gk.astype(BF)
            gps[back] = gps[back] + dot(gkb, chain_ref[chain_slot(r, m - 1), :, cs], 0, 0)
            gk = dot(gkb, fp_ref[back, h].astype(BF), 1, 0)
        sendk_ref[r - 1, :, cs] = gk.astype(BF)
    gqt_ref[:, cs] = gq
    for i in range(hops - 1):
        sendp_ref[i, h] = gps[i].astype(BF)


def path_bwd_head(h, heads, q_ref, k_ref, r_ref, c_ref, u_ref, inv_ref, psi_ref, x_ref, y_ref,
                  gqt, gkt, gs, gp):
    n = c_ref.shape[0]
    rows, cols = iotas(n)
    cs = head_cols(h)
    q, k, u = q_ref[:, cs], k_ref[:, cs], u_ref[:, cs]
    qb, kb, ub = q.astype(BF), k.astype(BF), u.astype(BF)
    kin = inv_ref[h].astype(BF)
    psi = psi_ref[h].astype(BF)
    x, y = x_ref[:, cs].astype(BF), y_ref[:, cs].astype(BF)
    gqtb, gktb = gqt.astype(BF), gkt.astype(BF)
    gsb = gs.astype(BF)
    gst = gs.T.astype(BF)
    gp = gp.astype(BF)
    f = jnp.where(rows <= cols, dot(ub, qb, 1, 1), 0.0).astype(BF)
    fq = jnp.where(rows >= cols, dot(qb, ub, 1, 1), 0.0).astype(BF)
    a = jnp.where(rows > cols, dot(ub, kb, 1, 1), 0.0).astype(BF)
    gx = -(dot(f, gqtb, 1, 0) + dot(ub, gp, 1, 0))
    gy = -dot(a, gktb, 1, 0)
    phiq = dot(fq, kin, 1, 0).astype(BF)
    back = dot(gst, phiq, 1, 0)
    backb = back.astype(BF)
    gfq = jnp.where(rows >= cols, -(dot(gqtb, x, 1, 1) + dot(gsb, psi, 1, 1)), 0.0)
    gaq = jnp.where(rows < cols, -(dot(gktb, y, 1, 1) + back), 0.0)
    kgx = dot(kin, gx.astype(BF), 0, 0)
    kgy = dot(kin, gy.astype(BF), 1, 0)
    zt = dot(x, kgx.astype(BF), 1, 1) + dot(kgy.astype(BF), y, 1, 1) - dot(psi, backb, 1, 0)
    glt = jnp.where(rows < cols, -zt, 0.0)
    sym = (glt + glt.T).astype(BF)
    gfqb, gaqb = gfq.astype(BF), gaq.astype(BF)
    gu = (kgx + kgy - dot(x, gp, 1, 1) + dot(gfq.T.astype(BF), qb, 1, 0)
          + dot(gaq.T.astype(BF), kb, 1, 0) + dot(sym, ub, 1, 0))
    gq = (gqt + dot(gsb, kb, 1, 0) + dot(gfqb, ub, 1, 0)).astype(BF)
    gk = (gkt + dot(gst, qb, 1, 0) + dot(gaqb, ub, 1, 0)).astype(BF)
    raw = r_ref[:, cs]
    inv, root = house_terms(raw, c_ref[...], heads, h)
    gc = jnp.sum(gu * u, 1, keepdims=True) * (1.0 - 0.5 * root * root) * 0.5
    gun = gu * root
    un = raw * inv
    gr = (inv * (gun - un * jnp.sum(gun * un, 1, keepdims=True))).astype(BF)
    return gq, gk, gr, gc


class Heads:
    def __init__(self, ref, kind):
        self.ref, self.kind = ref, kind

    def __getitem__(self, index):
        base = 3 * index[1].start + self.kind * HDIM
        return self.ref[index[0], base:base + HDIM]


def turned(index, by):
    low = index % 2
    high = index // 2 % 2
    return index + (1 - 2 * low) * (by % 2) + (2 - 4 * high) * (by // 2)


def step_kernel(cfg, names, *refs):
    heads, hops, sizes = cfg
    R = types.SimpleNamespace(**dict(zip(names, refs)))
    place = Place(sizes)
    wid_n, hid_n, seq_n = place.wid_n, place.hid_n, place.seq_n
    n, col = R.x.shape
    width = heads * HDIM
    model = R.act.shape[1]
    ff = R.wg.shape[1]
    sub = n // wid_n
    half = model // seq_n
    piece = model // place.rows_n
    copies, loads = Copies(R.send_sem, R.recv_sem), Loads(R.load_sem)
    my_cols = aligned(place.wid * col, col, 128)
    part_n = n // 2
    step_n = sub // 2

    def rows_of(w, hh):
        return aligned(hh * part_n + w * step_n, step_n, step_n)

    def half_of(hh):
        return slice(hh * step_n, (hh + 1) * step_n)

    def own_rows(ref):
        return jnp.concatenate([ref[rows_of(place.wid, hh), :].astype(F32) for hh in range(2)], 0)

    mine = aligned(place.seq * half, half, 128)
    other = aligned((1 - place.seq) * half, half, 128)
    sibling = {"seq": 1 - place.seq}
    order = sorted(range(1, wid_n), key=lambda i: -min(i, wid_n - i))
    to_wid = [{"wid": place.wid_peer(i)} for i in order]
    near = [{"hid": turned(place.hid, j)} for j in range(hid_n)]

    R.gain_in[0:1, :] = R.gain_attn[...].astype(F32).reshape(1, col)
    R.gain_in[1:2, :] = R.gain_ffn[...].astype(F32).reshape(1, col)
    R.xall[:, my_cols] = R.x[...]
    R.gall[:, my_cols] = R.gain_in[...]
    place.barrier()

    get_x = LineGather(copies, place, R.x, lambda c: R.xall.at[:, aligned(c * col, col, 128)])
    get_gains = [copies.start(R.gain_in, R.gall.at[:, my_cols], d) for d in to_wid]

    part_f = ff // seq_n
    mine_c = aligned(place.seq * half, half, 16)
    mine_f = aligned(place.seq * part_f, part_f, 16)

    def cols_of(j):
        return pl.ds(j * ff, ff)

    def down_rows(j, piece_i=0, pieces=1):
        size = part_f // pieces
        return aligned(j * ff + place.seq * part_f + piece_i * size, size, 16)

    def pass_on(ref, device):
        return copies.start(ref, ref, device)

    get_gate = [copies.start(R.wg.at[mine_c, :], R.wg_s.at[mine_c, cols_of(j)], near[j]) for j in (1, 2)]
    load_v = loads.start(R.wv, R.w_s.at[:, pl.ds(3 * width, width)])
    load_w = [loads.start(w.at[:, pl.ds(h * HDIM, HDIM)], R.w_s.at[:, pl.ds((3 * h + m) * HDIM, HDIM)])
              for h in range(heads) for m, w in enumerate((R.wq, R.wk, R.wr))]
    load_dy = loads.start(R.dy, R.dyall.at[:, my_cols])
    load_o = loads.start(R.wo, R.wo_s)
    load_f = [loads.start(R.wg, R.wg_s.at[:, pl.ds(0, ff)]), loads.start(R.wu, R.wu_s.at[:, pl.ds(0, ff)]),
              loads.start(R.wd, R.wd_s.at[pl.ds(0, ff), :])]

    for copy in get_gate:
        copy.wait_recv()
    relay = [copies.start(R.wg_s.at[mine_c, cols_of(1)], R.wg_s.at[mine_c, cols_of(3)], near[2])]
    get_x.relay()
    get_x.wait()
    for copy in get_gains:
        copy.wait_recv()
    get_dy = [copies.start(R.dy, R.dyall.at[:, my_cols], d) for d in to_wid]
    xf = R.xall[...].astype(F32)
    inv_rms = lax.rsqrt(jnp.mean(xf * xf, -1, keepdims=True) + eps_norm)
    R.inv_rms[...] = inv_rms
    R.act[...] = (xf * inv_rms * R.gall[0:1, :]).astype(BF)
    load_v.wait()
    R.v[...] = dot(R.act[...], R.w_s[:, 3 * width:4 * width], 1, 0).astype(BF)
    get_v = [copies.start(R.v, R.fv.at[i - 1], place.row_peer(i)) for i in range(1, hops + 1)]
    for copy in load_w:
        copy.wait()
    R.proj[...] = dot(R.act[...], R.w_s[:, 0:3 * width], 1, 0)
    R.c[...] = dot(R.act[...], R.wb[...], 1, 1)

    get_k = [[] for _ in range(heads)]
    get_p = [[] for _ in range(heads)]

    def send_head(h):
        cs = head_cols(h)
        for i in range(1, hops + 1):
            get_k[h].append(copies.start(R.kt_s.at[:, cs], R.chain.at[chain_slot(i, 0), :, cs], place.row_peer(i)))
        for i in range(1, hops):
            get_p[h].append(copies.start(R.prod_s.at[h], R.fp.at[i - 1, h], place.row_peer(i)))

    path_fwd_stage(heads, Heads(R.proj, 0), Heads(R.proj, 1), Heads(R.proj, 2), R.c, R.qt, R.kt_s, R.near_s, R.prod_s,
                   R.u, R.inv, R.psi, R.x1, R.y1, send_head)

    get_up = [copies.start(R.wu.at[mine_c, :], R.wu_s.at[mine_c, cols_of(j)], near[j]) for j in (1, 2)]
    get_down = [copies.start(R.wd.at[mine_f, :], R.wd_s.at[down_rows(j), :], near[j]) for j in (1, 2)]

    for copy in get_v:
        copy.wait_recv()
    load_o.wait()
    get_a = []
    for hh in range(2):
        for h in range(heads):
            if hh == 0:
                for copy in get_k[h] + get_p[h]:
                    copy.wait_recv()
                key_chain(hops, h, R.fp, R.chain)
            attn_fwd_rows(hops, h, hh * part_n, part_n, place.row, R.lengths, R.qt, R.near_s, R.v, R.fv, R.chain,
                          R.o, R.probs, R.rcp, R.s_s)
        rs = slice(hh * part_n, (hh + 1) * part_n)
        R.part_s[rs, :] = dot(R.o[rs, :], R.wo_s[...], 1, 0).astype(BF)
        get_a.append(LineSwap(copies, place, functools.partial(lambda hh, c: R.part_s.at[rows_of(c, hh), :], hh),
                              functools.partial(lambda hh, q: R.recv_s.at[q, pl.ds(hh * step_n, step_n), :], hh)))
        get_a[hh].start_far()
        get_a[hh].start()
    three = pl.ds(ff, 3 * ff)
    get_i = []

    def mix(hh):
        at, keep = rows_of(place.wid, hh), half_of(hh)
        mixed = get_a[hh].total(R.xall[at, :].astype(F32) + R.part_s[at, :].astype(F32))
        R.mixed[keep, :] = mixed
        inv_two = lax.rsqrt(jnp.mean(mixed * mixed, -1, keepdims=True) + eps_norm)
        R.row_s[keep, :] = (mixed * inv_two * R.gall[1:2, :]).astype(BF)
        get_i.append(LineGather(copies, place, R.row_s.at[pl.ds(hh * step_n, step_n), :],
                                functools.partial(lambda hh, c: R.inner.at[rows_of(c, hh), :], hh)))
        R.inner[at, :] = R.row_s[keep, :]

    get_a[0].combine()
    mix(0)
    get_a[1].combine()
    for copy in get_up:
        copy.wait_recv()
    relay.append(copies.start(R.wu_s.at[mine_c, cols_of(2)], R.wu_s.at[mine_c, cols_of(3)], near[1]))
    for copy in get_down:
        copy.wait_recv()
    relay_d = [copies.start(R.wd_s.at[down_rows(1, 0, 2), :], R.wd_s.at[down_rows(3, 0, 2), :], near[2]),
               copies.start(R.wd_s.at[down_rows(2, 1, 2), :], R.wd_s.at[down_rows(3, 1, 2), :], near[1])]
    mix(1)
    get_i[0].relay()
    for copy in relay:
        copy.wait_recv()
    shared = [pass_on(ref.at[mine_c, three], sibling) for ref in (R.wg_s, R.wu_s)]
    for copy in relay_d:
        copy.wait_recv()
    shared += [pass_on(R.wd_s.at[down_rows(j), :], sibling) for j in (1, 2, 3)]
    twin_a = [copies.start(R.act.at[:, other], R.twin_act, sibling),
              copies.start(R.o, R.twin_o, sibling)]
    load_dy.wait()
    for copy in load_f:
        copy.wait()
    get_i[1].relay()
    for copy in get_dy + shared:
        copy.wait_recv()
    for part in get_i:
        part.wait()
    twin = [copies.start(R.inner.at[:, other], R.twin_inner, sibling),
            copies.start(R.dyall.at[:, other], R.twin_dy, sibling)]

    swapped = (R.hidden, R.ggate, R.gup)
    swap_ids = [copies.take() for _ in range(3 * hid_n)]

    def swap(m, cs, i):
        return copies.make(swapped[m].at[pl.ds(0, n), cs], swapped[m].at[pl.ds(n, n), cs], sibling, i, i)

    def hidden_tile(t, carry):
        j = hid_n - 1 - t
        cs = aligned(j * ff, ff, 128)
        gate = dot(R.inner[...], R.wg_s[:, cs], 1, 0)
        up = dot(R.inner[...], R.wu_s[:, cs], 1, 0)
        g_hidden = dot(R.dyall[...], R.wd_s[cs, :], 1, 1)
        sig = 1.0 / (1.0 + jnp.exp(-gate))
        silu = gate * sig
        R.hidden[0:n, cs] = (silu * up).astype(BF)
        R.ggate[0:n, cs] = (g_hidden * up * sig * (1.0 + gate * (1.0 - sig))).astype(BF)
        R.gup[0:n, cs] = (g_hidden * silu).astype(BF)
        for m in range(3):
            swap(m, cs, swap_ids[0] + 3 * j + m).start()
        return carry

    lax.fori_loop(0, hid_n, hidden_tile, 0)
    twin_tile = [[swap(m, cols_of(j), swap_ids[3 * j + m]) for m in range(3)] for j in range(hid_n)]
    for tile in twin_tile:
        copies.open.extend(tile)
    before = list(copies.open)

    for copy in twin:
        copy.wait_recv()
    R.left_t[:, 0:n] = R.inner[:, mine].T
    R.left_t[:, n:2 * n] = R.twin_inner[...].T
    down_a, down_b = pl.ds(0, half // 2), pl.ds(half // 2, half // 2)
    upper, lower = pl.ds(0, half), pl.ds(half, half)

    def ffn_grads(j, gate_up, down):
        for copy in twin_tile[j]:
            copy.wait_recv()
        cs = slice(j * ff, (j + 1) * ff)
        gate_up[0:half, :] = dot(R.left_t[...], R.ggate[:, cs], 1, 0).astype(BF)
        gate_up[half:2 * half, :] = dot(R.left_t[...], R.gup[:, cs], 1, 0).astype(BF)
        down[...] = (dot(R.hidden[0:n, cs], R.dyall[:, mine], 0, 0)
                     + dot(R.hidden[n:2 * n, cs], R.twin_dy[...], 0, 0)).astype(BF)

    def first_round(gate_up, down, slot, rows, lanes, to, gus, downs):
        return [copies.start(gate_up.at[rows, :], gus.at[slot], to),
                copies.start(down.at[:, lanes], downs.at[slot], to)]

    ffn_grads(3, R.far_gu, R.far_dn)
    get_r1 = (first_round(R.far_gu, R.far_dn, 1, upper, down_a, near[1], R.gu_x, R.dn_x)
              + first_round(R.far_gu, R.far_dn, 1, lower, down_b, near[2], R.gu_y, R.dn_y))

    def grad_tile(t, carry):
        cs = aligned(t * col, col, 128)
        tile = (dot(R.ggate[0:n, :], R.wg_s[cs, :], 1, 1) + dot(R.gup[0:n, :], R.wu_s[cs, :], 1, 1)).astype(BF)
        for w in range(wid_n):
            for hh in range(2):
                R.gin[w * sub + hh * step_n:w * sub + (hh + 1) * step_n, cs] = (
                    tile[hh * part_n + w * step_n:hh * part_n + (w + 1) * step_n, :])
        return carry

    lax.fori_loop(0, wid_n, grad_tile, 0)
    get_g = LineSwap(copies, place, lambda c: R.gin.at[aligned(c * sub, sub, sub), :],
                     lambda q: R.recv_s.at[q] if q < 3 else R.recv_far)
    get_g.start_far()
    get_g.start()
    copies.sent(before)

    def grads_of(j):
        return R.wg_s.at[:, cols_of(j)], R.wu_s.at[cols_of(j), pl.ds(0, half)]

    ffn_grads(2, *grads_of(2))
    keep_r1 = first_round(*grads_of(2), 0, lower, down_b, near[2], R.gu_y, R.dn_y)
    ffn_grads(1, *grads_of(1))
    keep_r1 += first_round(*grads_of(1), 0, upper, down_a, near[1], R.gu_x, R.dn_x)
    get_g.combine()
    ffn_grads(0, *grads_of(0))

    def out_tile(t, carry):
        cs = aligned(t * col, col, 128)
        R.part_s[:, cs] = (dot(R.hidden[0:n, :], R.wd_s[:, cs], 1, 0) + R.part_s[:, cs].astype(F32)).astype(BF)
        return carry

    lax.fori_loop(0, wid_n, out_tile, 0)

    for copy in get_r1:
        copy.wait_recv()
    add_g = R.wg_s.at[upper, cols_of(2)]
    add_g[...] = (add_g[...].astype(F32) + R.gu_x[1].astype(F32)).astype(BF)
    add_u = R.wg_s.at[lower, cols_of(1)]
    add_u[...] = (add_u[...].astype(F32) + R.gu_y[1].astype(F32)).astype(BF)
    add_a = R.wu_s.at[cols_of(2), down_a]
    add_a[...] = (add_a[...].astype(F32) + R.dn_x[1].astype(F32)).astype(BF)
    add_b = R.wu_s.at[cols_of(1), down_b]
    add_b[...] = (add_b[...].astype(F32) + R.dn_y[1].astype(F32)).astype(BF)
    get_r2 = [copies.start(add_g, R.gu_x.at[2], near[2]), copies.start(add_a, R.dn_x.at[2], near[2]),
              copies.start(add_u, R.gu_y.at[2], near[1]), copies.start(add_b, R.dn_y.at[2], near[1])]

    g_inner = get_g.total(R.gin[aligned(place.wid * sub, sub, sub), :].astype(F32))
    mixed = R.mixed[...]
    inv_two = lax.rsqrt(jnp.mean(mixed * mixed, -1, keepdims=True) + eps_norm)
    n_two = mixed * inv_two
    scaled = g_inner * R.gall[1:2, :]
    g_mixed = (own_rows(R.dyall)
               + inv_two * (scaled - n_two * jnp.mean(scaled * n_two, -1, keepdims=True)))
    R.row_g[...] = g_mixed.astype(BF)
    get_z = []
    for hh in range(2):
        at = rows_of(place.wid, hh)
        get_z.append(LineGather(copies, place, R.row_g.at[pl.ds(hh * step_n, step_n), :],
                                functools.partial(lambda hh, c: R.gz.at[rows_of(c, hh), :], hh)))
        R.gz[at, :] = R.row_g[half_of(hh), :]
    R.gpart[1:2, :] = jnp.sum(g_inner * n_two, 0, keepdims=True)
    for copy in twin_a:
        copy.wait_recv()
    for part in get_z:
        part.relay()
    get_f = []
    for slot, i in enumerate(order):
        peer = place.wid_peer(i)
        get_f.append(copies.start(R.part_s.at[:, aligned(peer * col, col, 128)], R.recv_f.at[slot], {"wid": peer}))

    for part in get_z:
        part.wait()
    twin_z = copies.start(R.gz.at[:, other], R.twin_gz, sibling)

    gets = [[] for _ in range(heads)]
    for h in range(heads):
        cs = head_cols(h)
        go = dot(R.gz[...], R.wo_s[cs, :], 1, 1).astype(BF)
        attn_bwd_head(hops, h, R.probs, R.rcp, go, R.qt, R.v, R.fv, R.fp, R.chain,
                      R.gqt, R.near_s, R.gv, R.sendk, R.sendv, R.sendp, R.s_s)
        for i in range(1, hops + 1):
            to = place.row_peer(-i)
            gets[h].append(copies.start(R.sendv.at[i - 1, :, cs], R.recvv.at[i - 1, :, cs], to))
            gets[h].append(copies.start(R.sendk.at[i - 1, :, cs], R.recvk.at[i - 1, :, cs], to))
        for i in range(1, hops):
            gets[h].append(copies.start(R.sendp.at[i - 1, h], R.recvp.at[i - 1, h], place.row_peer(-i)))

    def left_of(ref, twin_ref):
        R.left_t[:, 0:n] = ref[:, mine].T
        R.left_t[:, n:2 * n] = twin_ref[...].T

    twin_z.wait_recv()
    left_of(R.gz, R.twin_gz)

    fine = piece // 2
    get_h = {}

    def rows_at(j, lot):
        return aligned(turned(place.hid, j) * piece + lot * fine, fine, 32)

    def round_one(src, slot):
        sent = [copies.start(src.at[rows_at(3, lot), :], R.recv_q.at[slot, 2 * lot + 1], near[lot + 1]) for lot in range(2)]
        keep = [copies.start(src.at[rows_at(lot + 1, lot), :], R.recv_q.at[slot, 2 * lot], near[lot + 1]) for lot in range(2)]
        get_h[slot] = keep
        return sent

    def round_two(src, slot, sent):
        for lot in range(2):
            sent[lot].wait_recv()
            at = src.at[rows_at(2 - lot, lot), :]
            at[...] = (at[...].astype(F32) + R.recv_q[slot, 2 * lot + 1].astype(F32)).astype(BF)
            get_h[slot].append(copies.start(at, R.recv_q.at[slot, 4 + lot], near[2 - lot]))

    R.wide_s[...] = dot(R.left_t[:, 0:n], R.o[...], 1, 0) + dot(R.left_t[:, n:2 * n], R.twin_o[...], 1, 0)
    R.d_out[...] = R.wide_s[aligned(place.hid * piece, piece, 64), :]
    R.send_o[...] = R.wide_s[...].astype(BF)
    slot_o, slot_v = heads + 1, heads
    sent_o = round_one(R.send_o, slot_o)
    left_of(R.act, R.twin_act)
    for copy in get_r2 + keep_r1:
        copy.wait_recv()
    R.d_gate_s[...] = (R.wg_s[upper, 0:ff].astype(F32) + R.gu_x[0].astype(F32) + R.gu_x[2].astype(F32))
    R.d_up_s[...] = (R.wg_s[lower, 0:ff].astype(F32) + R.gu_y[0].astype(F32) + R.gu_y[2].astype(F32))
    for lanes, ref in ((down_a, R.dn_x), (down_b, R.dn_y)):
        R.d_down_s[:, lanes] = R.wu_s[0:ff, lanes].astype(F32) + ref[0].astype(F32) + ref[2].astype(F32)
    stores = [loads.start(R.d_gate_s, R.d_gate), loads.start(R.d_up_s, R.d_up), loads.start(R.d_down_s, R.d_down)]

    row8 = lax.broadcasted_iota(jnp.int32, (n, HDIM), 1)
    gc_all = jnp.zeros((n, HDIM), F32)
    val_cols = pl.ds(3 * width, width)
    twin_h = []

    def grad_part(slot):
        return R.wd_s.at[:, pl.ds(slot * width, width)]

    def weights_of(slot, outs_of):
        cs = slice(slot * width, (slot + 1) * width)
        R.wide_s[...] = dot(R.left_t[...], R.grads[:, cs], 1, 0)
        R.wd_s[0:half, cs] = R.wide_s[...].astype(BF)
        own = R.wide_s[aligned(place.hid * piece, piece, 64), :]
        for m, (ref, at) in enumerate(outs_of):
            ref[:, at] = own[:, head_cols(m)]
        return round_one(grad_part(slot), slot)

    def outs_of(h):
        return [(ref, head_cols(h)) for ref in (R.d_query, R.d_key, R.d_house)]

    val_outs = [(R.d_value, head_cols(m)) for m in range(heads)]
    sent_h = []
    for h in range(heads):
        for copy in gets[h]:
            copy.wait_recv()
        cs = head_cols(h)
        gkt = R.recvk[0, :, cs].astype(F32)
        gv = R.gv[:, cs] + R.recvv[0, :, cs].astype(F32)
        for i in range(1, hops):
            gkt = gkt + R.recvk[i, :, cs].astype(F32)
            gv = gv + R.recvv[i, :, cs].astype(F32)
        gp = R.recvp[0, h].astype(F32)
        for i in range(1, hops - 1):
            gp = gp + R.recvp[i, h].astype(F32)
        R.grads[0:n, (9 + h) * HDIM:(10 + h) * HDIM] = gv.astype(BF)
        if h == heads - 1:
            twin_v = copies.start(R.grads.at[pl.ds(0, n), val_cols], R.grads.at[pl.ds(n, n), val_cols], sibling)
        gq, gk, gr, gc = path_bwd_head(h, heads, Heads(R.proj, 0), Heads(R.proj, 1), Heads(R.proj, 2), R.c,
                                       R.u, R.inv, R.psi, R.x1, R.y1, R.gqt[:, cs], gkt, R.near_s[h], gp)
        gc_all = jnp.where(row8 == h, gc, gc_all)
        for m, val in enumerate((gq, gk, gr)):
            R.grads[0:n, (3 * h + m) * HDIM:(3 * h + m + 1) * HDIM] = val
        gs = pl.ds(h * width, width)
        twin_h.append(copies.start(R.grads.at[pl.ds(0, n), gs], R.grads.at[pl.ds(n, n), gs], sibling))
        if 0 < h:
            twin_h[h - 1].wait_recv()
            sent_h.append(weights_of(h - 1, outs_of(h - 1)))
    R.gcs[0:n, :] = gc_all.astype(BF)
    twin_c = copies.start(R.gcs.at[pl.ds(0, n), :], R.gcs.at[pl.ds(n, n), :], sibling)

    inv_rms = R.inv_rms[...]
    stat = jnp.zeros((n, 1), F32)
    get_n = LineSwap(copies, place, lambda c: R.send_n.at[c], lambda q: R.recv_n.at[q])
    me, side = place.wid, place.wid // 2
    for turn, c in enumerate((3 * (1 - side), 2 - side, (1 - side) * (1 - me) + side * (5 - me), me)):
        cs = aligned(c * col, col, 128)
        g_act = dot(R.grads[0:n, :], R.w_s[cs, :], 1, 1) + dot(R.gcs[0:n, 0:heads], R.wb[:, cs], 1, 0)
        normed = R.xall[:, cs].astype(F32) * inv_rms
        both = g_act * normed
        stat = stat + jnp.sum(both * R.gall[0:1, cs], 1, keepdims=True)
        R.gpart[0:1, cs] = jnp.sum(both, 0, keepdims=True)
        if turn == 3:
            R.own_n[...] = g_act
        else:
            R.send_n[c] = g_act.astype(BF)
        if turn == 0:
            get_n.start_far()
        if turn == 2:
            get_n.start()
    R.stat_s[...] = jnp.broadcast_to(stat, (n, HDIM)).T[0:8, :]
    get_s = [copies.start(R.stat_s, R.recv_st.at[slot], d) for slot, d in enumerate(to_wid)]

    def window(p):
        return aligned(p * piece // 128 * 128, 256, 128)

    get_gain = [copies.start(R.gpart.at[:, window(lax.rem(place.row + i, place.rows_n))], R.recv_gain.at[i - 1],
                             place.row_peer(i)) for i in range(1, place.rows_n)]
    twin_c.wait_recv()
    d_beta = dot(R.gcs[0:n, :], R.act[:, mine], 0, 0) + dot(R.gcs[n:2 * n, :], R.twin_act[...], 0, 0)
    R.beta_s[...] = d_beta[0:8, :]
    get_b = [copies.start(R.beta_s.at[:, window(turned(place.hid, j))], R.recv_b.at[j - 1], near[j])
             for j in range(1, hid_n)]
    for h in (heads - 1,):
        twin_h[h].wait_recv()
        sent_h.append(weights_of(h, outs_of(h)))
    get_n.combine()
    twin_v.wait_recv()
    sent_v = weights_of(slot_v, val_outs)
    round_two(R.send_o, slot_o, sent_o)
    for h in range(heads - 1):
        round_two(grad_part(h), h, sent_h[h])
    out = R.x[...].astype(F32) + R.part_s[:, my_cols].astype(F32)
    for slot, copy in enumerate(get_f):
        copy.wait_recv()
        out = out + R.recv_f[slot].astype(F32)
    R.output_s[...] = out.astype(BF)
    stores.append(loads.start(R.output_s, R.output))
    def final(slot, refs_of):
        for copy in get_h[slot]:
            copy.wait_recv()
        for m, (ref, at) in enumerate(refs_of):
            for lot in range(2):
                rs = slice(lot * fine, (lot + 1) * fine)
                ref[rs, at] = (ref[rs, at] + R.recv_q[slot, 2 * lot, :, head_cols(m)].astype(F32)
                               + R.recv_q[slot, 4 + lot, :, head_cols(m)].astype(F32))

    final(slot_o, [(R.d_out, head_cols(m)) for m in range(heads)])
    gain = R.gpart[:, window(place.row)]
    for i, copy in enumerate(get_gain):
        copy.wait_recv()
        gain = gain + R.recv_gain[i]
    R.gain_s[...] = gain
    get_gain2 = [copies.start(R.gain_s, R.recv_gain2.at[slot], d) for slot, d in enumerate(to_wid)]
    round_two(grad_part(heads - 1), heads - 1, sent_h[heads - 1])
    round_two(grad_part(slot_v), slot_v, sent_v)

    g_act = get_n.total(R.own_n[...])
    stats = R.stat_s[...]
    for slot in range(wid_n - 1):
        get_s[slot].wait_recv()
        stats = stats + R.recv_st[slot]
    mean = stats.T[:, 0:1] / model
    normed = R.xall[:, my_cols].astype(F32) * inv_rms
    R.d_inputs[...] = (R.gz[:, my_cols].astype(F32)
                       + inv_rms * (g_act * R.gall[0:1, my_cols] - normed * mean))
    for h in range(heads - 1):
        final(h, outs_of(h))
    final(heads - 1, outs_of(heads - 1))
    final(slot_v, val_outs)
    for copy in get_b:
        copy.wait_recv()
    d_beta = R.beta_s[:, window(place.hid)]
    for i in range(hid_n - 1):
        d_beta = d_beta + R.recv_b[i]
    gain = R.gain_s[...]
    for slot, copy in enumerate(get_gain2):
        copy.wait_recv()
        gain = gain + R.recv_gain2[slot]

    def exact(rows, at):
        return jnp.where(at % 2 == 1, rows[:, 64:64 + piece], rows[:, 0:piece])

    R.d_beta[...] = exact(d_beta, place.hid)[0:heads, :]
    R.gain_out[...] = exact(gain, place.row)
    for store in stores:
        store.wait()
    copies.sent(copies.open)


def step(args, heads, hops, sizes):
    ins = ("lengths", "x", "dy", "gain_attn", "gain_ffn", "wq", "wk", "wv", "wr", "wb", "wo", "wg", "wu", "wd")
    shapes = dict(zip(ins, (a.shape for a in args)))
    n, col = shapes["x"]
    seq_n, hid_n, wid_n = sizes
    model, width = shapes["wq"]
    ff = shapes["wg"][1]
    sub = n // wid_n
    rows_n = seq_n * hid_n
    half = model // seq_n
    piece = model // rows_n
    slots = hops * (hops + 1) // 2
    S = jax.ShapeDtypeStruct
    V = pltpu.VMEM
    outs = dict(
        output=S((n, col), BF), d_inputs=S((n, col), F32), gain_out=S((8, piece), F32),
        d_query=S((piece, width), F32), d_key=S((piece, width), F32), d_value=S((piece, width), F32),
        d_house=S((piece, width), F32), d_beta=S((heads, piece), F32), d_out=S((piece, width), F32),
        d_gate=S((half, ff), F32), d_up=S((half, ff), F32), d_down=S((ff, half), F32),
    )
    peers_w, peers_h = wid_n - 1, hid_n - 1
    scratch = dict(
        gain_in=V((8, col), F32), gall=V((8, model), F32), inv_rms=V((n, 1), F32),
        act=V((n, model), BF), xall=V((n, model), BF), dyall=V((n, model), BF),
        proj=V((n, 3 * width), F32), c=V((n, heads), F32), v=V((n, width), BF),
        qt=V((n, width), BF), u=V((n, width), F32), inv=V((heads, n, n), F32), psi=V((heads, n, n), F32),
        x1=V((n, width), F32), y1=V((n, width), F32),
        fv=V((hops, n, width), BF), fp=V((hops - 1, heads, HDIM, HDIM), BF), chain=V((slots, n, width), BF),
        probs=V((hops + 1, heads, n, n), BF), rcp=V((n, heads), F32), o=V((n, width), BF), mixed=V((sub, model), F32),
        inner=V((n, model), BF), hidden=V((2 * n, hid_n * ff), BF), ggate=V((2 * n, hid_n * ff), BF),
        gup=V((2 * n, hid_n * ff), BF), gin=V((n, model), BF),
        w_s=V((model, 4 * width), BF), wo_s=V((width, model), BF),
        wg_s=V((model, hid_n * ff), BF), wu_s=V((model, hid_n * ff), BF), wd_s=V((hid_n * ff, model), BF),
        kt_s=V((n, width), BF), near_s=V((heads, n, n), F32), prod_s=V((heads, HDIM, HDIM), BF),
        s_s=V(((hops + 1) * n, n), F32), part_s=V((n, model), BF), recv_s=V((wid_n, sub, model), BF), recv_far=V((sub, model), BF),
        far_gu=V((2 * half, ff), BF), far_dn=V((ff, half), BF),
        row_s=V((sub, model), BF), row_g=V((sub, model), BF),
        twin_inner=V((n, half), BF), twin_dy=V((n, half), BF), twin_act=V((n, half), BF), twin_o=V((n, width), BF),
        twin_gz=V((n, half), BF), left_t=V((half, 2 * n), BF),
        gu_x=V((3, half, ff), BF), gu_y=V((3, half, ff), BF),
        dn_x=V((3, ff, half // 2), BF), dn_y=V((3, ff, half // 2), BF),
        gz=V((n, model), BF), gpart=V((8, model), F32), recv_f=V((peers_w, n, col), BF),
        gqt=V((n, width), F32), gv=V((n, width), F32),
        sendk=V((hops, n, width), BF), sendv=V((hops, n, width), BF), sendp=V((hops - 1, heads, HDIM, HDIM), BF),
        recvk=V((hops, n, width), BF), recvv=V((hops, n, width), BF), recvp=V((hops - 1, heads, HDIM, HDIM), BF),
        send_o=V((half, width), BF),
        grads=V((2 * n, 4 * width), BF), gcs=V((2 * n, HDIM), BF), wide_s=V((half, width), F32),
        recv_q=V((heads + 2, 6, piece // 2, width), BF), beta_s=V((8, half), F32), recv_b=V((peers_h, 8, 256), F32),
        own_n=V((n, col), F32), send_n=V((wid_n, n, col), BF), recv_n=V((wid_n, n, col), BF),
        output_s=V((n, col), BF), d_gate_s=V((half, ff), F32), d_up_s=V((half, ff), F32), d_down_s=V((ff, half), F32),
        stat_s=V((8, n), F32), recv_st=V((peers_w, 8, n), F32),
        recv_gain=V((rows_n - 1, 8, 256), F32), gain_s=V((8, 256), F32), recv_gain2=V((peers_w, 8, 256), F32),
    )
    n_copies = 256
    scratch.update(load_sem=pltpu.SemaphoreType.DMA((24,)), send_sem=pltpu.SemaphoreType.DMA((n_copies,)),
                   recv_sem=pltpu.SemaphoreType.DMA((n_copies,)))
    spaces = {"lengths": pltpu.SMEM, "x": pltpu.VMEM, "gain_attn": pltpu.VMEM, "gain_ffn": pltpu.VMEM, "wb": pltpu.VMEM}
    vmem = pl.BlockSpec(memory_space=pltpu.VMEM)
    early = ("output", "d_gate", "d_up", "d_down")
    res = pl.pallas_call(
        functools.partial(step_kernel, (heads, hops, sizes), ins + tuple(outs) + tuple(scratch)),
        in_specs=[pl.BlockSpec(memory_space=spaces.get(i, pl.ANY)) for i in ins],
        out_shape=tuple(outs.values()),
        out_specs=tuple(pl.BlockSpec(memory_space=pl.ANY) if i in early else vmem for i in outs),
        scratch_shapes=list(scratch.values()),
        compiler_params=pltpu.CompilerParams(
            vmem_limit_bytes=VMEM_ALL, collective_id=1, has_side_effects=True),
        name="step",
    )(*args)
    return dict(zip(outs, res))


def finish_kernel(count, *refs):
    ins, outs, bufs = refs[:count + 1], refs[count + 1:2 * count + 3], refs[2 * count + 3:3 * count + 4]
    lines, sems = refs[3 * count + 4:3 * count + 6], refs[3 * count + 6]
    loads, stores = [], []
    for a, b, c in zip(ins[:count], bufs[:count], outs[:count]):
        rows = a.shape[0]
        cut = rows // 2 if rows >= 768 else rows
        for start in range(0, rows, cut):
            i, part = len(loads), pl.ds(start, cut)
            loads.append(pltpu.make_async_copy(a.at[part, :], b.at[part, :], sems.at[0, i]))
            stores.append(pltpu.make_async_copy(b.at[part, :], c.at[part, :], sems.at[1, i]))
    last = len(loads)
    loads.insert(0, pltpu.make_async_copy(ins[count], bufs[count], sems.at[0, last]))
    for copy in loads:
        copy.start()
    loads[0].wait()
    for m in range(2):
        lines[m][...] = bufs[count][m, :]
        stores.append(pltpu.make_async_copy(lines[m], outs[count + m], sems.at[1, last + m]))
        stores[-1].start()
    for load, store in zip(loads[1:], stores):
        load.wait()
        store.start()
    for copy in stores:
        copy.wait()


def finish(arrays, gains):
    count, size = len(arrays), gains.shape[1]
    spec = pl.BlockSpec(memory_space=pl.ANY)
    vector = jax.ShapeDtypeStruct((size,), F32)
    return pl.pallas_call(
        functools.partial(finish_kernel, count),
        in_specs=[spec] * (count + 1), out_specs=[spec] * (count + 2),
        out_shape=[jax.ShapeDtypeStruct(a.shape, a.dtype) for a in arrays] + [vector, vector],
        scratch_shapes=([pltpu.VMEM(a.shape, a.dtype) for a in arrays + [gains]]
                        + [pltpu.VMEM((size,), F32)] * 2 + [pltpu.SemaphoreType.DMA((2, 2 * count + 2))]),
        compiler_params=pltpu.CompilerParams(vmem_limit_bytes=VMEM_ALL),
        name="finish",
    )(*arrays, gains)


def shifted(array, axis, by):
    peers = lax.axis_size(axis)
    pairs = [(i, i + by) for i in range(peers) if 0 <= i + by < peers]
    return lax.ppermute(array, axis, pairs)


def norm_rows(hidden_f):
    inverse = lax.rsqrt(jnp.mean(hidden_f * hidden_f, -1, keepdims=True) + eps_norm)
    return (hidden_f * inverse, inverse)


def norm_back(grad_out, normed, inverse, gain_vec):
    scaled_grad = grad_out * gain_vec
    grad_gain = jnp.sum(grad_out * normed, 0)
    grad_in = inverse * (scaled_grad - normed * jnp.mean(scaled_grad * normed, -1, keepdims=True))
    return (grad_in, grad_gain)


ROWS = ("seq", "hid")


def body(inputs, gain_attn, gain_ffn, w_query, w_key, w_value, w_house, w_beta, w_out,
         w_gate, w_up, w_down, lengths, cotangent):
    tok, col = inputs.shape
    row_devs = lax.axis_size(ROWS)
    my_row = lax.axis_index(ROWS)
    my_wid = lax.axis_index("wid")
    wid_n = lax.axis_size("wid")
    tokens_all = tok * row_devs
    most_len = max(LEAST, 2 * tokens_all // 5)
    hops = min((most_len - 2) // tok + 1, row_devs - 1)
    heads = w_query.shape[1] // HDIM
    ff = w_gate.shape[1]
    sub = tok // wid_n

    x_all = lax.all_gather(inputs, "wid", axis=1, tiled=True)
    gain_one = lax.all_gather(gain_attn, "wid", axis=0, tiled=True).astype(F32)
    gain_two = lax.all_gather(gain_ffn, "wid", axis=0, tiled=True).astype(F32)
    dy_all = lax.all_gather(cotangent, "wid", axis=1, tiled=True)
    w_gu = lax.all_gather(jnp.concatenate([w_gate, w_up], 1), "hid", axis=0)
    w_dn = lax.all_gather(w_down, "hid", axis=0)
    model = x_all.shape[1]

    residual = x_all.astype(F32)
    normed_one, inverse_one = norm_rows(residual)
    act = (normed_one * gain_one).astype(BF)

    def project(weight):
        return jnp.dot(act, weight, preferred_element_type=F32)

    q, k, r, c = project(w_query), project(w_key), project(w_house), project(w_beta)
    v = project(w_value).astype(BF)
    far_v = jnp.stack([shifted(v, ROWS, i) for i in range(1, hops + 1)])
    qt, kt, near, prod, *saved = path_fwd(q, k, r, c, heads)
    far_k = jnp.stack([shifted(kt, ROWS, i) for i in range(1, hops + 1)])
    far_p = jnp.stack([shifted(prod, ROWS, i) for i in range(1, hops)])
    row_arr = jnp.full((1,), my_row, jnp.int32)
    attended, probs, chain, rcp = attn_fwd(lengths, row_arr, qt, near, v, far_k, far_v, far_p, heads, hops)

    attn_part = jnp.dot(attended, w_out, preferred_element_type=F32).astype(BF)
    attn_rows = lax.psum_scatter(attn_part, "wid", scatter_dimension=0, tiled=True)
    x_rows = lax.dynamic_slice_in_dim(x_all, my_wid * sub, sub, 0).astype(F32)
    dy_rows = lax.dynamic_slice_in_dim(dy_all, my_wid * sub, sub, 0).astype(F32)
    mixed = x_rows + attn_rows.astype(F32)
    normed_two, inverse_two = norm_rows(mixed)
    inner = lax.all_gather((normed_two * gain_two).astype(BF), "wid", axis=0, tiled=True)

    pre = jnp.einsum("tc,hcf->htf", inner, w_gu, preferred_element_type=F32)
    gate, up = pre[:, :, :ff], pre[:, :, ff:]
    sig = jax.nn.sigmoid(gate)
    hidden = (gate * sig * up).astype(BF)
    ffn_part = jnp.einsum("htf,hfc->tc", hidden, w_dn, preferred_element_type=F32)
    ffn_part = (ffn_part + attn_part.astype(F32)).astype(BF)
    ffn_cols = lax.psum_scatter(ffn_part, "wid", scatter_dimension=1, tiled=True)
    output = (inputs.astype(F32) + ffn_cols.astype(F32)).astype(BF)

    g_hidden = jnp.einsum("tc,hfc->htf", dy_all, w_dn, preferred_element_type=F32)
    g_gate = g_hidden * up * sig * (1.0 + gate * (1.0 - sig))
    g_up = g_hidden * gate * sig
    g_pre = jnp.concatenate([g_gate, g_up], 2).astype(BF)
    g_inner = jnp.einsum("htf,hcf->tc", g_pre, w_gu, preferred_element_type=F32).astype(BF)
    g_inner = lax.psum_scatter(g_inner, "wid", scatter_dimension=0, tiled=True).astype(F32)
    g_mixed_n, g_gain_two = norm_back(g_inner, normed_two, inverse_two, gain_two)
    g_z = lax.all_gather((dy_rows + g_mixed_n).astype(BF), "wid", axis=0, tiled=True)

    d_gu = jnp.einsum("tc,htf->hcf", inner, g_pre, preferred_element_type=F32).astype(BF)
    d_dn = jnp.einsum("htf,tc->hfc", hidden, dy_all, preferred_element_type=F32).astype(BF)
    d_gu = lax.psum_scatter(d_gu, "seq", scatter_dimension=1, tiled=True)
    d_gu = lax.psum_scatter(d_gu, "hid", scatter_dimension=0)
    d_dn = lax.psum_scatter(d_dn, "seq", scatter_dimension=2, tiled=True)
    d_dn = lax.psum_scatter(d_dn, "hid", scatter_dimension=0)

    g_attn = jnp.einsum("tc,ic->ti", g_z, w_out, preferred_element_type=F32).astype(BF)
    d_out = jnp.einsum("ti,tc->ic", attended, g_z, preferred_element_type=F32).astype(BF)
    g_qt, g_near, gv, send_k, send_v, send_p = attn_bwd(probs, rcp, g_attn, qt, v, far_v, far_p, chain, heads, hops)
    g_kt = sum(shifted(send_k[i - 1], ROWS, -i).astype(F32) for i in range(1, hops + 1))
    gv = gv + sum(shifted(send_v[i - 1], ROWS, -i).astype(F32) for i in range(1, hops + 1))
    g_prod = sum(shifted(send_p[i - 1], ROWS, -i).astype(F32) for i in range(1, hops))
    g_q, g_k, g_r, g_c = path_bwd(q, k, r, c, saved, g_qt, g_kt, g_near, g_prod, heads)
    g_v = gv.astype(BF)

    def weight_grad(grad_low):
        return jnp.einsum("tc,ti->ci", act, grad_low, preferred_element_type=F32).astype(BF)

    def input_grad(grad_low, weight):
        return jnp.einsum("ti,ci->tc", grad_low, weight, preferred_element_type=F32)

    g_act = (input_grad(g_q, w_query) + input_grad(g_k, w_key) + input_grad(g_v, w_value)
             + input_grad(g_r, w_house) + input_grad(g_c, w_beta))
    g_act = lax.psum_scatter(g_act.astype(BF), "wid", scatter_dimension=0, tiled=True).astype(F32)
    normed_rows = lax.dynamic_slice_in_dim(normed_one, my_wid * sub, sub, 0)
    inverse_rows = lax.dynamic_slice_in_dim(inverse_one, my_wid * sub, sub, 0)
    g_resid, g_gain_one = norm_back(g_act, normed_rows, inverse_rows, gain_one)
    d_rows = dy_rows + g_mixed_n + g_resid
    d_inputs = lax.all_to_all(d_rows, "wid", split_axis=1, concat_axis=0, tiled=True)

    def scatter(x, dim):
        return lax.psum_scatter(x, ROWS, scatter_dimension=dim, tiled=True)

    gains = lax.psum(jnp.stack([g_gain_one, g_gain_two]), "wid")
    gains = scatter(gains, 1)
    return (
        output,
        d_inputs,
        gains[0],
        gains[1],
        scatter(weight_grad(g_q), 0).astype(F32),
        scatter(weight_grad(g_k), 0).astype(F32),
        scatter(weight_grad(g_v), 0).astype(F32),
        scatter(weight_grad(g_r), 0).astype(F32),
        scatter(weight_grad(g_c), 0).astype(F32),
        scatter(d_out, 1).astype(F32),
        d_gu[:, :ff].astype(F32),
        d_gu[:, ff:].astype(F32),
        d_dn.astype(F32),
    )


def fast_body(inputs, gain_attn, gain_ffn, w_query, w_key, w_value, w_house, w_beta, w_out,
              w_gate, w_up, w_down, lengths, cotangent):
    tok, col = inputs.shape
    row_devs = lax.axis_size(ROWS)
    sizes = tuple(lax.axis_size(i) for i in ("seq", "hid", "wid"))
    most_len = max(LEAST, 2 * tok * row_devs // 5)
    hops = min((most_len - 2) // tok + 1, row_devs - 1)
    heads = w_query.shape[1] // HDIM
    f = step((lengths, inputs, cotangent, gain_attn, gain_ffn, w_query, w_key, w_value, w_house,
              w_beta.T, w_out, w_gate, w_up, w_down), heads, hops, sizes)
    names = [i for i in f if i != "gain_out"]
    f.update(zip(names + ["gain_one", "gain_two"], finish([f[i] for i in names], f["gain_out"])))
    return (f["output"], f["d_inputs"], f["gain_one"], f["gain_two"], f["d_query"], f["d_key"], f["d_value"],
            f["d_house"], f["d_beta"].T, f["d_out"].T, f["d_gate"], f["d_up"], f["d_down"])


def slow(mesh):
    return (mesh.shape["seq"], mesh.shape["hid"], mesh.shape["wid"]) != (2, 4, 4)


def solution(mesh):
    in_specs = (
        P(("seq", "hid"), "wid"), P("wid"), P("wid"),
        P(None, "wid"), P(None, "wid"), P(None, "wid"), P(None, "wid"), P(None, "wid"),
        P("wid", None), P(None, ("hid", "wid")), P(None, ("hid", "wid")), P(("hid", "wid"), None),
        P(), P(("seq", "hid"), "wid"),
    )
    out_specs = (
        P(("seq", "hid"), "wid"), P(("seq", "hid"), "wid"), P(("seq", "hid")), P(("seq", "hid")),
        P(("seq", "hid"), "wid"), P(("seq", "hid"), "wid"), P(("seq", "hid"), "wid"),
        P(("seq", "hid"), "wid"), P(("seq", "hid"), "wid"), P("wid", ("seq", "hid")),
        P("seq", ("hid", "wid")), P("seq", ("hid", "wid")), P(("hid", "wid"), "seq"),
    )
    return jax.shard_map(body if slow(mesh) else fast_body, mesh=mesh, in_specs=in_specs, out_specs=out_specs, check_vma=False)
```
